32 devices in a mesh: dp: 16 (over z, y, x), seq: 2 (over core).
Axes of the slice: x: 2, y: 2, z: 4, core: 2. Of those that a mesh axis runs over, the one named last changes fastest.
Arguments:
- patches: bfloat16 [64, 280, 768], P('dp', 'seq'), may hold values from -6 to 6
- pos_index: int32 [64, 280], P('dp', 'seq'), may hold values from 0 to 197, as said below
- valid: int32 [64], P('dp'), may hold values from 70 to 280, as said below
- classes: int32 [64, 3], P('dp'), may hold values from 0 to 999
- mixing: int32 [64], P('dp'), may hold values from 1 to 15
- image_weight: int32 [64], P('dp'), may hold values from 1 to 4
- drop_keep: int32 [64, 2], P('dp'), may hold values 0 or 1
- patch_weight: float32 [768, 768], P(('dp', 'seq')), may hold values from -0.21875 to 0.21875
- patch_mean: float32 [768, 768], P(('dp', 'seq')), may hold values from -3.8146973e-06 to 3.8146973e-06
- patch_square: float32 [768, 768], P(('dp', 'seq')), may hold values from 4.2685643e-14 to 1.7074257e-13
- block_weight: float32 [768, 6144], P(('dp', 'seq')), may hold values from -0.21875 to 0.21875
- block_mean: float32 [768, 6144], P(('dp', 'seq')), may hold values from -3.8146973e-06 to 3.8146973e-06
- block_square: float32 [768, 6144], P(('dp', 'seq')), may hold values from 4.2685643e-14 to 1.7074257e-13
- down_weight: float32 [3072, 768], P(('dp', 'seq')), may hold values from -0.109375 to 0.109375
- down_mean: float32 [3072, 768], P(('dp', 'seq')), may hold values from -3.8146973e-06 to 3.8146973e-06
- down_square: float32 [3072, 768], P(('dp', 'seq')), may hold values from 4.2685643e-14 to 1.7074257e-13
- heads_weight: float32 [768, 2000], P(('dp', 'seq')), may hold values from -0.21875 to 0.21875
- heads_mean: float32 [768, 2000], P(('dp', 'seq')), may hold values from -3.8146973e-06 to 3.8146973e-06
- heads_square: float32 [768, 2000], P(('dp', 'seq')), may hold values from 4.2685643e-14 to 1.7074257e-13
- small_rows: float32 [211, 768], replicated, may hold values from -4 to 4
- rows_mean: float32 [211, 768], replicated, may hold values from -1.1444092e-05 to 1.1444092e-05
- rows_square: float32 [211, 768], replicated, may hold values from 3.841708e-13 to 1.5366832e-12
- small_long: float32 [5072], replicated, may hold values from -1.75 to 1.75
- long_mean: float32 [5072], replicated, may hold values from -1.1444092e-05 to 1.1444092e-05
- long_square: float32 [5072], replicated, may hold values from 3.841708e-13 to 1.5366832e-12
Outputs:
- loss: float32 [], replicated
- grad_norm: float32 [], replicated
- patch_new: float32 [768, 768], P(('dp', 'seq'))
- patch_mean_new: float32 [768, 768], P(('dp', 'seq'))
- patch_square_new: float32 [768, 768], P(('dp', 'seq'))
- block_new: float32 [768, 6144], P(('dp', 'seq'))
- block_mean_new: float32 [768, 6144], P(('dp', 'seq'))
- block_square_new: float32 [768, 6144], P(('dp', 'seq'))
- down_new: float32 [3072, 768], P(('dp', 'seq'))
- down_mean_new: float32 [3072, 768], P(('dp', 'seq'))
- down_square_new: float32 [3072, 768], P(('dp', 'seq'))
- heads_new: float32 [768, 2000], P(('dp', 'seq'))
- heads_mean_new: float32 [768, 2000], P(('dp', 'seq'))
- heads_square_new: float32 [768, 2000], P(('dp', 'seq'))
- rows_new: float32 [211, 768], replicated
- rows_mean_new: float32 [211, 768], replicated
- rows_square_new: float32 [211, 768], replicated
- long_new: float32 [5072], replicated
- long_mean_new: float32 [5072], replicated
- long_square_new: float32 [5072], replicated
- vectors_grad: float32 [13, 768], replicated
The draws below stay inside these ranges and needn't reach their ends.
Inputs may be any that keep to these rules, and one draw needn't show every extreme that they name: `pos_index`: slot 0 maps to row 0, slot 1 to row 1, every other slot to a row of 2 to 197. `valid`: used slots come first; some image uses all 280.
All inputs are finite; a program needn't handle non-finite values. No bound on the sum of `drop_keep` on one device may be relied on, other than what follows from the above.
Results may differ from the reference program's by a relative error of at most 0.009.
Values may be sent and summed in bfloat16 or wider, within the bound.
No kernel may reach another device: no remote copies, remote signals or barrier semaphores. Data moves between devices by JAX's collectives and lax.ppermute only.
A program may use at most 192 MiB of HBM per device.

```python
import math
import jax
import jax.numpy as jnp
from jax import lax

D = 768
HEADS = 12
HD = 64
FF = 3072
PD = 768
CLS = 1000
POS = 198
SLOTS = 280
NVEC = 13
STEP = 7
IMAGES = 64
PARAMS = 9370832


def draw_pos_index(key, part):
    others = jax.random.randint(key, (IMAGES, SLOTS), 2, POS)
    slot_ids = lax.broadcasted_iota(jnp.int32, (IMAGES, SLOTS), 1)
    return jnp.where(slot_ids < 2, slot_ids, others).astype(jnp.int32)


def draw_valid(key, part):
    lengths = jax.random.randint(key, (IMAGES,), SLOTS // 4, SLOTS + 1)
    leading = lax.broadcasted_iota(jnp.int32, (IMAGES,), 0) == 0
    return jnp.where(leading, SLOTS, lengths).astype(jnp.int32)


def draw_small_rows(key, part):
    base = jnp.clip(jax.random.normal(key, (POS + NVEC, D), jnp.float32), -4.0, 4.0)
    row_ids = lax.broadcasted_iota(jnp.int32, (POS + NVEC, D), 0) - POS
    is_gain = (row_ids == 3) | (row_ids == 8) | (row_ids == 11)
    is_token = (row_ids == 1) | (row_ids == 2)
    scale = jnp.where(row_ids < 0, 0.5, jnp.where(is_token, 1.0, jnp.where(is_gain, 0.1, 0.3)))
    return (base * scale + jnp.where(is_gain, 1.0, 0.0)).astype(jnp.float32)


def with_ends(drawn, rng, low, largest):
    longest = drawn.shape.index(max(drawn.shape))
    spots = []
    for shift in (0, 1):
        where = [jax.random.randint(jax.random.fold_in(rng, axis), (), 0, length) for axis, length in enumerate(drawn.shape)]
        where[longest] = (where[longest] + shift) % drawn.shape[longest]
        spots.append(tuple(where))
    return drawn.at[spots[0]].set(low).at[spots[1]].set(largest)


def shard_levels(key, dims, shards, smallest, largest):
    level, own = 1.0, jax.random.fold_in(key, 6)
    for position, shards_of in shards:
        draws = jnp.exp(jax.random.uniform(jax.random.fold_in(own, position), (shards_of,), jnp.float32, smallest / len(shards), largest / len(shards)))
        level = level * jnp.repeat(draws, dims[position] // shards_of).reshape([-1 if axis == position else 1 for axis in range(len(dims))])
    return level


def gaussian(rng, dims, deviation, most, cuts=(), kind=jnp.bfloat16):
    factor_of = shard_levels(rng, dims, cuts, -0.22, 0.18) if cuts else 1.0
    values = jax.random.normal(rng, dims, jnp.float32) * deviation * factor_of
    return jnp.minimum(jnp.maximum(values, -most), most).astype(kind)


def setup_inputs(seed: int = 0) -> dict:
    arg_keys = jax.random.split(jax.random.key(seed), 26)
    return {
        "patches": gaussian(arg_keys[0], (IMAGES, SLOTS, PD), 1.0, 6.0, ((0, 16), (1, 2))),
        "pos_index": draw_pos_index(jax.random.fold_in(arg_keys[25], 71), 0),
        "valid": draw_valid(jax.random.fold_in(arg_keys[25], 71), 0),
        "classes": with_ends(jax.random.randint(arg_keys[3], (IMAGES, 3), 0, CLS), jax.random.fold_in(arg_keys[3], 1), 0, CLS - 1).astype(jnp.int32),
        "mixing": with_ends(jax.random.randint(arg_keys[4], (IMAGES,), 1, 16), jax.random.fold_in(arg_keys[4], 1), 1, 15).astype(jnp.int32),
        "image_weight": with_ends(jax.random.randint(arg_keys[5], (IMAGES,), 1, 5), jax.random.fold_in(arg_keys[5], 1), 1, 4).astype(jnp.int32),
        "drop_keep": with_ends((jax.random.randint(arg_keys[6], (IMAGES, 2), 0, 10) < 9).astype(jnp.int32), jax.random.fold_in(arg_keys[6], 1), 0, 1),
        "patch_weight": gaussian(arg_keys[7], (PD, D), PD ** -0.5, 0.21875, ((0, 32),), jnp.float32),
        "patch_mean": gaussian(arg_keys[8], (PD, D), (0.002 / PARAMS ** 0.5), 3.814697265625e-06, ((0, 32),), jnp.float32),
        "patch_square": jnp.clip(jnp.exp(math.log(1.7074257047285102e-13) - 1.3862944 * jax.random.uniform(arg_keys[9], (PD, D), jnp.float32) ** shard_levels(arg_keys[9], (PD, D), ((0, 32),), -0.2, 0.2)), 4.2685642618212755e-14, 1.7074257047285102e-13),
        "block_weight": gaussian(arg_keys[10], (D, 4 * D + FF), D ** -0.5, 0.21875, ((0, 32),), jnp.float32),
        "block_mean": gaussian(arg_keys[11], (D, 4 * D + FF), (0.002 / PARAMS ** 0.5), 3.814697265625e-06, ((0, 32),), jnp.float32),
        "block_square": jnp.clip(jnp.exp(math.log(1.7074257047285102e-13) - 1.3862944 * jax.random.uniform(arg_keys[12], (D, 4 * D + FF), jnp.float32) ** shard_levels(arg_keys[12], (D, 4 * D + FF), ((0, 32),), -0.2, 0.2)), 4.2685642618212755e-14, 1.7074257047285102e-13),
        "down_weight": gaussian(arg_keys[13], (FF, D), FF ** -0.5, 0.109375, ((0, 32),), jnp.float32),
        "down_mean": gaussian(arg_keys[14], (FF, D), (0.002 / PARAMS ** 0.5), 3.814697265625e-06, ((0, 32),), jnp.float32),
        "down_square": jnp.clip(jnp.exp(math.log(1.7074257047285102e-13) - 1.3862944 * jax.random.uniform(arg_keys[15], (FF, D), jnp.float32) ** shard_levels(arg_keys[15], (FF, D), ((0, 32),), -0.2, 0.2)), 4.2685642618212755e-14, 1.7074257047285102e-13),
        "heads_weight": gaussian(arg_keys[16], (D, 2 * CLS), D ** -0.5, 0.21875, ((0, 32),), jnp.float32),
        "heads_mean": gaussian(arg_keys[17], (D, 2 * CLS), (0.002 / PARAMS ** 0.5), 3.814697265625e-06, ((0, 32),), jnp.float32),
        "heads_square": jnp.clip(jnp.exp(math.log(1.7074257047285102e-13) - 1.3862944 * jax.random.uniform(arg_keys[18], (D, 2 * CLS), jnp.float32) ** shard_levels(arg_keys[18], (D, 2 * CLS), ((0, 32),), -0.2, 0.2)), 4.2685642618212755e-14, 1.7074257047285102e-13),
        "small_rows": draw_small_rows(jax.random.fold_in(arg_keys[25], 71), 0),
        "rows_mean": gaussian(arg_keys[20], (POS + NVEC, D), (0.006 / PARAMS ** 0.5), 1.1444091796875e-05, (), jnp.float32),
        "rows_square": jnp.clip(jnp.exp(jax.random.uniform(arg_keys[21], (POS + NVEC, D), jnp.float32, math.log(3.8417080389270553e-13), math.log(1.5366832155708221e-12))), 3.8417080389270553e-13, 1.5366832155708221e-12),
        "small_long": gaussian(arg_keys[22], (FF + 2 * CLS,), 0.3, 1.75, (), jnp.float32),
        "long_mean": gaussian(arg_keys[23], (FF + 2 * CLS,), (0.006 / PARAMS ** 0.5), 1.1444091796875e-05, (), jnp.float32),
        "long_square": jnp.clip(jnp.exp(jax.random.uniform(arg_keys[24], (FF + 2 * CLS,), jnp.float32, math.log(3.8417080389270553e-13), math.log(1.5366832155708221e-12))), 3.8417080389270553e-13, 1.5366832155708221e-12),
    }


@jax.custom_vjp
def low(v):
    return lax.optimization_barrier(v.astype(jnp.bfloat16)).astype(jnp.float32)

@jax.custom_vjp
def low_back(v):
    return v

def low_keep(v):
    return (low(v), None)

def low_pass(kept, grad):
    return (grad,)

def back_keep(v):
    return (v, None)

def back_low(kept, grad):
    return (low(grad),)
low.defvjp(low_keep, low_pass)
low_back.defvjp(back_keep, back_low)
highest = lax.Precision.HIGHEST

def dense(left, right):
    return jnp.dot(left, right, precision=highest)

def layer_norm(values, gain, shift):
    centered = values - lax.optimization_barrier(jnp.mean(values, -1, keepdims=True))
    variance = lax.optimization_barrier(jnp.mean(centered * centered, -1, keepdims=True))
    return centered * lax.rsqrt(variance + 1e-06) * gain + shift

def group_loss(params, batch, weight_sum):
    patch_weight, block_weight, down_weight, heads_weight, small_rows, small_long = params
    patches, pos_index, valid, classes, mixing, image_weight, drop_keep = batch
    count = patches.shape[0]
    table = small_rows[:POS]
    vectors = small_rows[POS:]
    block_low = low(block_weight)
    embedded = low_back(dense(low(patches.reshape(count * SLOTS, PD)), low(patch_weight))).reshape(count, SLOTS, D)
    slot_ids = jnp.arange(SLOTS, dtype=jnp.int32)[None, :, None]
    stream = jnp.where(slot_ids == 0, vectors[1], jnp.where(slot_ids == 1, vectors[2], embedded + vectors[0])) + table[pos_index]
    first = low(layer_norm(stream, vectors[3], vectors[4])).reshape(count * SLOTS, D)
    qkv_bias = jnp.concatenate([vectors[5], jnp.zeros((D,), jnp.float32), vectors[6]])
    projected = low_back(low(dense(first, block_low[:, :3 * D]) + qkv_bias)).reshape(count, SLOTS, 3, HEADS, HD)
    scores = jnp.einsum('nqhd,nkhd->nhqk', projected[:, :, 0], projected[:, :, 1], precision=highest) * HD ** (-0.5)
    key_mask = jnp.arange(SLOTS, dtype=jnp.int32)[None, :] < valid[:, None]
    scores = low_back(jnp.where(key_mask[:, None, None, :], scores, -1e+30))
    probs = jax.nn.softmax(scores, -1)
    attended = jnp.einsum('nhqk,nkhd->nqhd', low(probs), projected[:, :, 2], precision=highest)
    attended = low_back(low(attended)).reshape(count * SLOTS, D)
    attn_out = low_back(dense(attended, block_low[:, 3 * D:4 * D]) + vectors[7]).reshape(count, SLOTS, D)
    keep_scales = drop_keep.astype(jnp.float32) / 0.9
    stream = stream + keep_scales[:, 0, None, None] * attn_out
    second = low(layer_norm(stream, vectors[8], vectors[9])).reshape(count * SLOTS, D)
    hidden = low_back(dense(second, block_low[:, 4 * D:]) + small_long[:FF])
    activated = low(jax.nn.gelu(hidden, approximate=False))
    mlp_out = low_back(dense(activated, low(down_weight)) + vectors[10]).reshape(count, SLOTS, D)
    stream = stream + keep_scales[:, 1, None, None] * mlp_out
    head = low(layer_norm(stream[:, :2], vectors[11], vectors[12]))
    heads_low = low(heads_weight)
    logits_cls = low_back(dense(head[:, 0], heads_low[:, :CLS]) + small_long[FF:FF + CLS])
    logits_dist = low_back(dense(head[:, 1], heads_low[:, CLS:]) + small_long[FF + CLS:])
    columns = jnp.arange(CLS, dtype=jnp.int32)[None, :]
    share = mixing.astype(jnp.float32)[:, None] / 16.0
    target = share * (classes[:, 0:1] == columns).astype(jnp.float32) + (1.0 - share) * (classes[:, 1:2] == columns).astype(jnp.float32)
    teacher = (classes[:, 2:3] == columns).astype(jnp.float32)
    terms = -0.5 * (lax.optimization_barrier(jnp.sum(target * jax.nn.log_softmax(logits_cls, -1), -1)) + lax.optimization_barrier(jnp.sum(teacher * jax.nn.log_softmax(logits_dist, -1), -1)))
    return jnp.sum(image_weight.astype(jnp.float32) * terms) / weight_sum

def adam_update(weight, first, second, gradient, factor, decay, rate):
    clipped = gradient * factor
    first_new = 0.9 * first + 0.1 * clipped
    second_new = 0.999 * second + 0.001 * clipped * clipped
    first_hat = first_new / (1.0 - 0.9 ** STEP)
    second_hat = second_new / (1.0 - 0.999 ** STEP)
    weight_new = weight - rate * (first_hat / (jnp.sqrt(second_hat) + 1e-08) + decay * weight)
    return (weight_new, first_new, second_new)

def reference(patches, pos_index, valid, classes, mixing, image_weight, drop_keep, patch_weight, patch_mean, patch_square, block_weight, block_mean, block_square, down_weight, down_mean, down_square, heads_weight, heads_mean, heads_square, small_rows, rows_mean, rows_square, small_long, long_mean, long_square):
    params = (patch_weight, block_weight, down_weight, heads_weight, small_rows, small_long)
    groups = IMAGES // 16
    batch_all = (patches.astype(jnp.float32), pos_index, valid, classes, mixing, image_weight, drop_keep)
    batches = jax.tree.map(lambda array: array.reshape((groups, 16) + array.shape[1:]), batch_all)
    weight_sum = jnp.sum(image_weight.astype(jnp.float32))

    def accumulate(carry, batch):
        loss_now, grads_now = carry
        value, pullback = jax.vjp(lambda inner: group_loss(inner, batch, weight_sum), params)
        gradients, = pullback(jnp.ones_like(value))
        return ((loss_now + value, jax.tree.map(jnp.add, grads_now, gradients)), None)
    zeros = jax.tree.map(jnp.zeros_like, params)
    (loss, gradients), _ = lax.scan(accumulate, (jnp.zeros((), jnp.float32), zeros), batches)
    square = jnp.zeros((), jnp.float32)
    for gradient in gradients:
        square = square + jnp.sum(gradient * gradient)
    grad_norm = jnp.sqrt(square)
    factor = jnp.minimum(1.0, 0.02 / (grad_norm + 1e-06))
    vectors_grad = factor * gradients[4][POS:]
    patch_new, patch_mean_new, patch_square_new = adam_update(patch_weight, patch_mean, patch_square, gradients[0], factor, 0.05, 0.02)
    block_new, block_mean_new, block_square_new = adam_update(block_weight, block_mean, block_square, gradients[1], factor, 0.05, 0.02)
    down_new, down_mean_new, down_square_new = adam_update(down_weight, down_mean, down_square, gradients[2], factor, 0.05, 0.02)
    heads_new, heads_mean_new, heads_square_new = adam_update(heads_weight, heads_mean, heads_square, gradients[3], factor, 0.05, 0.02)
    rows_new, rows_mean_new, rows_square_new = adam_update(small_rows, rows_mean, rows_square, gradients[4], factor, 0.0, 0.15)
    long_new, long_mean_new, long_square_new = adam_update(small_long, long_mean, long_square, gradients[5], factor, 0.0, 0.15)
    return (loss, grad_norm, patch_new, patch_mean_new, patch_square_new, block_new, block_mean_new, block_square_new, down_new, down_mean_new, down_square_new, heads_new, heads_mean_new, heads_square_new, rows_new, rows_mean_new, rows_square_new, long_new, long_mean_new, long_square_new, vectors_grad)
```

```python
import jax
import jax.numpy as jnp
from jax import lax
from jax.sharding import PartitionSpec as P

D = 768
HEADS = 12
HD = 64
FF = 3072
CLS = 1000
POS = 198
STEP = 7


NORM_EPS = 1e-06
DROP_SCALE = 1.0 / 0.9
CLIP_NORM = 0.02
LEARN_RATE = 0.02
SMALL_RATE = 0.15
BETA_FIRST = 0.9
BETA_SECOND = 0.999
ADAM_EPS = 1e-08
DECAY_RATE = 0.05
MASK_FILL = -1e30
highest = lax.Precision.HIGHEST


def matmul(left, right):
    return jnp.dot(left, right, preferred_element_type=jnp.float32)


def matmul_tn(left, right):
    return lax.dot_general(
        left, right, (((0,), (0,)), ((), ())), preferred_element_type=jnp.float32
    )


def matmul_nt(left, right):
    return lax.dot_general(
        left, right, (((1,), (1,)), ((), ())), preferred_element_type=jnp.float32
    )


def norm_forward(values, gain, shift):
    centered = values - jnp.mean(values, -1, keepdims=True)
    inverse = lax.rsqrt(jnp.mean(centered * centered, -1, keepdims=True) + NORM_EPS)
    normed = centered * inverse
    return (normed * gain + shift, normed, inverse)


def norm_backward(grad_out, normed, inverse, gain):
    scaled = grad_out * gain
    grad_in = inverse * (
        scaled
        - jnp.mean(scaled, -1, keepdims=True)
        - normed * jnp.mean(scaled * normed, -1, keepdims=True)
    )
    leading = tuple(range(grad_out.ndim - 1))
    return (grad_in, jnp.sum(grad_out * normed, leading), jnp.sum(grad_out, leading))


def gelu_parts(values):
    cumulative = 0.5 * (1.0 + jax.scipy.special.erf(values * 0.7071067811865476))
    density = 0.3989422804014327 * jnp.exp(-0.5 * values * values)
    return (values * cumulative, cumulative + values * density)


def adam_update(weight, first, second, gradient, factor, decay, rate):
    clipped = gradient * factor
    first_new = BETA_FIRST * first + (1.0 - BETA_FIRST) * clipped
    second_new = BETA_SECOND * second + (1.0 - BETA_SECOND) * clipped * clipped
    first_hat = first_new / (1.0 - BETA_FIRST**STEP)
    second_hat = second_new / (1.0 - BETA_SECOND**STEP)
    weight_new = weight - rate * (first_hat / (jnp.sqrt(second_hat) + ADAM_EPS) + decay * weight)
    return (weight_new, first_new, second_new)


ALL = ("dp", "seq")


def exchange(blocks, axes=ALL):
    return lax.all_to_all(blocks, axes, 0, 0, tiled=True)


def gather_blocks(block, axes=ALL):
    count = lax.axis_size(axes)
    return exchange(jnp.broadcast_to(block[None], (count,) + block.shape), axes)


def swap_cores(value):
    return lax.ppermute(value, "seq", [(0, 1), (1, 0)])


def join_cores(value, seq_index, axis):
    other = swap_cores(value)
    first = jnp.where(seq_index == 0, value, other)
    second = jnp.where(seq_index == 0, other, value)
    return jnp.stack([first, second], axis)


def split_low(value):
    high = value.astype(jnp.bfloat16)
    rest = (value - high.astype(jnp.float32)).astype(jnp.bfloat16)
    return high, rest


def shards(
    patches,
    pos_index,
    valid,
    classes,
    mixing,
    image_weight,
    drop_keep,
    patch_weight,
    patch_mean,
    patch_square,
    block_weight,
    block_mean,
    block_square,
    down_weight,
    down_mean,
    down_square,
    heads_weight,
    heads_mean,
    heads_square,
    small_rows,
    rows_mean,
    rows_square,
    small_long,
    long_mean,
    long_square,
):
    low = jnp.bfloat16
    f32 = jnp.float32
    images, local_slots, patch_dim = patches.shape
    row_count = images * local_slots
    dp_size = lax.axis_size("dp")
    seq_size = lax.axis_size("seq")
    devices = dp_size * seq_size
    seq_index = lax.axis_index("seq")
    device = lax.axis_index("dp") * seq_size + seq_index
    own_rows = patch_weight.shape[0]
    own_hidden = down_weight.shape[0]
    own_images = images // seq_size
    all_images = dp_size * images
    pairs = 2 * HEADS
    table = small_rows[:POS]
    vectors = small_rows[POS:]

    gathered_late = lax.all_gather(
        jnp.concatenate([block_weight[:, 2 * D : 4 * D], heads_weight], 1).astype(low),
        ALL,
        axis=0,
        tiled=True,
    )
    gathered_query_key = lax.all_gather(
        lax.optimization_barrier((block_weight[:, : 2 * D].astype(low), gathered_late[:8, :128]))[0],
        ALL,
        axis=0,
        tiled=True,
    )

    tokens = vectors[1:3] + table[0:2]
    token_out, token_normed, token_inverse = norm_forward(tokens, vectors[3], vectors[4])
    token_low = token_out.astype(low)
    select_own = (
        lax.broadcasted_iota(jnp.int32, (own_rows, D), 0) + device * own_rows
        == lax.broadcasted_iota(jnp.int32, (own_rows, D), 1)
    ).astype(low)
    token_own = matmul_nt(token_low, select_own).astype(low)
    query_partial = matmul(token_own, block_weight[:, :D].astype(low))
    query = jnp.sum(gather_blocks(query_partial), 0) + vectors[5]
    query_low = query.astype(low)
    head_of = lax.broadcasted_iota(jnp.int32, (HEADS, D), 1) // HD
    head_mask = head_of == lax.broadcasted_iota(jnp.int32, (HEADS, D), 0)
    query_blocks = jnp.where(head_mask[None], query_low[:, None, :], 0).reshape(pairs, D)
    key_own = matmul_nt(block_weight[:, D : 2 * D].astype(low), query_blocks.astype(low)) * HD ** (
        -0.5
    )
    meta = jnp.concatenate(
        [
            (classes // 32),
            (classes % 32),
            mixing[:, None],
            image_weight[:, None],
            drop_keep,
        ],
        1,
    )
    meta_width = meta.shape[1]
    meta_columns = -(-images * meta_width // own_rows)
    meta = jnp.pad(meta.reshape(-1), (0, own_rows * meta_columns - images * meta_width))
    meta = meta.reshape(own_rows, meta_columns).astype(low)
    extra = -(-(pairs + meta_columns) // 128) * 128
    early = jnp.concatenate(
        [
            patch_weight.astype(low),
            key_own.astype(low),
            meta,
            jnp.zeros((own_rows, extra - pairs - meta_columns), low),
        ],
        1,
    )
    early = gather_blocks(early, "dp").reshape(dp_size, own_rows, D + extra)
    early = join_cores(early, seq_index, 1)
    metas = early[:, 0, :, D + pairs : D + pairs + meta_columns].astype(f32)
    metas = metas.reshape(dp_size, own_rows * meta_columns)[:, : images * meta_width]
    metas = metas.reshape(all_images, meta_width)
    early = early.reshape(D, D + extra)
    full_patch = early[:, :D]
    key_vectors = early[:, D : D + pairs]

    slot_global = seq_index * local_slots + lax.broadcasted_iota(jnp.int32, (1, local_slots, 1), 1)
    is_class = slot_global == 0
    is_distill = slot_global == 1
    special = is_class | is_distill
    key_mask = slot_global < valid[:, None, None]
    flat_patches = patches.reshape(row_count, patch_dim)
    onehot_pos = (
        pos_index.reshape(row_count)[:, None]
        == lax.broadcasted_iota(jnp.int32, (1, POS), 1)
    ).astype(low)
    table_high, table_rest = split_low(table)
    embedded = matmul(flat_patches, full_patch)
    positions = matmul(onehot_pos, table_high) + matmul(onehot_pos, table_rest)
    embedded = (embedded + positions + vectors[0]).reshape(images, local_slots, D)
    stream = jnp.where(is_class, tokens[0], jnp.where(is_distill, tokens[1], embedded))
    first_out, first_normed, first_inverse = norm_forward(stream, vectors[3], vectors[4])
    first_low = first_out.astype(low)
    flat_first = first_low.reshape(row_count, D)
    scores = matmul(flat_first, key_vectors).reshape(images, local_slots, pairs)
    scores = jnp.where(key_mask, scores, MASK_FILL)
    local_peak = jnp.max(scores, 1, keepdims=True)
    exponent = jnp.exp(scores - local_peak)
    local_total = jnp.sum(exponent, 1, keepdims=True)
    local_pooled = jnp.einsum(
        "nlm,nld->nmd", exponent.astype(low), first_low, preferred_element_type=f32
    )
    packed = jnp.concatenate(
        [
            local_pooled,
            jnp.broadcast_to(local_peak.transpose(0, 2, 1), (images, pairs, 64)),
            jnp.broadcast_to(local_total.transpose(0, 2, 1), (images, pairs, 64)),
        ],
        2,
    )
    other = swap_cores(packed)
    other_pooled = other[:, :, :D]
    peak_here = local_peak.transpose(0, 2, 1)
    peak_there = other[:, :, D : D + 1]
    peak = jnp.maximum(peak_here, peak_there)
    scale_here = jnp.exp(peak_here - peak)
    scale_there = jnp.exp(peak_there - peak)
    total = (
        scale_here * local_total.transpose(0, 2, 1) + scale_there * other[:, :, D + 64 : D + 65]
    )
    pooled = (scale_here * local_pooled + scale_there * other_pooled) / total
    probs = exponent * (scale_here / total).transpose(0, 2, 1)
    pooled_low = pooled.astype(low)
    own_pooled = lax.dynamic_slice_in_dim(pooled_low, seq_index * own_images, own_images, 0)

    up_blocks = (
        block_weight[:, 4 * D :]
        .astype(low)
        .reshape(own_rows, devices, own_hidden)
        .transpose(1, 0, 2)
        .reshape(devices, own_rows * own_hidden)
    )
    pooled_blocks = (
        own_pooled.reshape(own_images * pairs, devices, own_rows)
        .transpose(1, 0, 2)
        .reshape(devices, own_images * pairs * own_rows)
    )
    received = exchange(jnp.concatenate([up_blocks, pooled_blocks], 1))
    up_own = received[:, : own_rows * own_hidden].reshape(D, own_hidden)
    pooled_own = received[:, own_rows * own_hidden :].reshape(all_images, 2, HEADS, own_rows)

    full_value = gathered_late[:, :D]
    full_out = gathered_late[:, D : 2 * D]
    full_heads = gathered_late[:, 2 * D :]
    mixed = matmul(own_pooled.reshape(own_images * pairs, D), full_value)
    attended = jnp.sum(
        jnp.where(head_mask, mixed.reshape(own_images * 2, HEADS, D), 0.0), 1
    ) + vectors[6]
    attended = attended.astype(low)
    rows = all_images * 2
    attended = gather_blocks(attended).reshape(rows, D)
    keep_float = metas[:, 8:10] * DROP_SCALE
    keep_rows = jnp.repeat(keep_float, 2, axis=0)
    keep_first = keep_rows[:, 0:1]
    keep_second = keep_rows[:, 1:2]
    middle = jnp.tile(tokens, (all_images, 1)) + keep_first * (
        matmul(attended, full_out) + vectors[7]
    )
    second_out, second_normed, second_inverse = norm_forward(middle, vectors[8], vectors[9])
    second_low = second_out.astype(low)
    hidden_bias = lax.dynamic_slice_in_dim(small_long, device * own_hidden, own_hidden, 0)
    hidden = matmul(second_low, up_own) + hidden_bias
    activated, gelu_slope = gelu_parts(hidden)
    activated = activated.astype(low)
    down_low = down_weight.astype(low)
    mlp_partial = matmul(activated, down_low).astype(low)
    row_share = own_images * 2
    mlp_own = jnp.sum(
        exchange(mlp_partial.reshape(devices, row_share, D)).astype(f32), 0
    )
    mlp_rows = gather_blocks(mlp_own.astype(low)).reshape(rows, D).astype(f32)
    result = middle + keep_second * (mlp_rows + vectors[10])

    head_out, head_normed, head_inverse = norm_forward(result, vectors[11], vectors[12])
    head_low = head_out.astype(low).reshape(all_images, 2, D)
    logits_class = matmul(head_low[:, 0], full_heads[:, :CLS]) + small_long[FF : FF + CLS]
    logits_distill = matmul(head_low[:, 1], full_heads[:, CLS:]) + small_long[FF + CLS :]
    columns = lax.broadcasted_iota(jnp.int32, (1, CLS), 1)
    labels = (metas[:, 0:3] * 32.0 + metas[:, 3:6]).astype(jnp.int32)
    share = metas[:, 6:7] / 16.0
    weights = metas[:, 7]
    weight_sum = jnp.sum(weights)
    target = share * (labels[:, 0:1] == columns).astype(f32) + (1.0 - share) * (
        labels[:, 1:2] == columns
    ).astype(f32)
    teacher = (labels[:, 2:3] == columns).astype(f32)
    log_class = jax.nn.log_softmax(logits_class, -1)
    log_distill = jax.nn.log_softmax(logits_distill, -1)
    terms = -0.5 * (jnp.sum(target * log_class, -1) + jnp.sum(teacher * log_distill, -1))
    loss = jnp.sum(weights * terms) / weight_sum
    scale_rows = (weights * 0.5 / weight_sum)[:, None]
    grad_class = (scale_rows * (jnp.exp(log_class) - target)).astype(low)
    grad_distill = (scale_rows * (jnp.exp(log_distill) - teacher)).astype(low)
    head_own = matmul_nt(select_own, head_low.reshape(rows, D)).astype(low)
    head_own = head_own.reshape(own_rows, all_images, 2)
    owned_heads = jnp.concatenate(
        [matmul(head_own[:, :, 0], grad_class), matmul(head_own[:, :, 1], grad_distill)], 1
    )
    head_bias = jnp.concatenate(
        [jnp.sum(grad_class.astype(f32), 0), jnp.sum(grad_distill.astype(f32), 0)]
    )
    grad_head_rows = jnp.stack(
        [matmul_nt(grad_class, full_heads[:, :CLS]), matmul_nt(grad_distill, full_heads[:, CLS:])],
        1,
    ).reshape(rows, D)
    grad_result, final_gain, final_shift = norm_backward(
        grad_head_rows, head_normed, head_inverse, vectors[11]
    )

    grad_mlp = (keep_second * grad_result).astype(low)
    owned_down = matmul_tn(activated, grad_mlp)
    down_bias = jnp.sum(grad_mlp.astype(f32), 0)
    grad_hidden = (matmul_nt(grad_mlp, down_low) * gelu_slope).astype(low)
    up_bias = jnp.sum(grad_hidden.astype(f32), 0)
    grad_up = matmul_tn(second_low, grad_hidden).astype(low)
    grad_second_partial = matmul_nt(grad_hidden, up_own).astype(low)
    received = exchange(
        jnp.concatenate(
            [
                grad_second_partial.reshape(devices, row_share * D),
                grad_up.reshape(devices, own_rows * own_hidden),
            ],
            1,
        )
    )
    grad_second = jnp.sum(
        received[:, : row_share * D].astype(f32).reshape(devices, row_share, D), 0
    )
    owned_up = (
        received[:, row_share * D :]
        .reshape(devices, own_rows, own_hidden)
        .transpose(1, 0, 2)
        .reshape(own_rows, FF)
        .astype(f32)
    )
    row_start = device * row_share
    own_normed = lax.dynamic_slice_in_dim(second_normed, row_start, row_share, 0)
    own_inverse = lax.dynamic_slice_in_dim(second_inverse, row_start, row_share, 0)
    own_result = lax.dynamic_slice_in_dim(grad_result, row_start, row_share, 0)
    own_keep = lax.dynamic_slice_in_dim(keep_first, row_start, row_share, 0)
    grad_second_in, second_gain, second_shift = norm_backward(
        grad_second, own_normed, own_inverse, vectors[8]
    )
    grad_middle = own_result + grad_second_in
    grad_attn_own = (own_keep * grad_middle).astype(low)
    out_bias = jnp.sum(grad_attn_own.astype(f32), 0)
    grad_attn = join_cores(grad_attn_own, seq_index, 0).reshape(images * 2, D)
    grad_att = matmul_nt(grad_attn, full_out).astype(low)
    value_bias = jnp.sum(
        lax.dynamic_slice_in_dim(grad_att, seq_index * row_share, row_share, 0).astype(f32), 0
    )
    grad_att_blocks = jnp.where(
        head_mask, grad_att.reshape(images * 2, 1, D), jnp.zeros((), low)
    ).reshape(images * pairs, D)
    value_vectors = matmul_nt(grad_att_blocks, full_value).astype(low)
    value_const = jnp.sum(grad_att_blocks.astype(f32) * vectors[6], -1).reshape(images, pairs)
    value_vectors = value_vectors.reshape(images, pairs, D)
    mean_grad = jnp.sum(pooled * value_vectors.astype(f32), -1) + value_const
    grad_probs = (
        jnp.einsum("nld,nmd->nlm", first_low, value_vectors, preferred_element_type=f32)
        + value_const[:, None, :]
    )
    grad_scores = (probs * (grad_probs - mean_grad[:, None, :])).astype(low)
    key_rows = jnp.broadcast_to(key_vectors.T[None], (images, pairs, D))
    grad_first = jnp.einsum(
        "nlk,nkd->nld",
        jnp.concatenate([grad_scores, probs.astype(low)], 2),
        jnp.concatenate([key_rows, value_vectors], 1),
        preferred_element_type=f32,
    )
    grad_stream, first_gain, first_shift = norm_backward(
        grad_first, first_normed, first_inverse, vectors[3]
    )
    pooled_grad = matmul_tn(grad_scores.reshape(row_count, pairs), flat_first)
    query_grad_blocks = matmul(pooled_grad.astype(low), gathered_query_key[:, D:]) * HD ** (-0.5)
    grad_query = jnp.sum(
        jnp.where(head_mask, query_grad_blocks.reshape(2, HEADS, D), 0.0), 1
    )
    token_grad = matmul_nt(grad_query.astype(low), gathered_query_key[:, :D])
    token_grad_in, token_gain, token_shift = norm_backward(
        token_grad, token_normed, token_inverse, vectors[3]
    )
    grad_tokens = (
        token_grad_in
        + jnp.sum(grad_middle.reshape(own_images, 2, D), 0)
        + jnp.stack(
            [
                jnp.sum(jnp.where(is_class, grad_stream, 0.0), (0, 1)),
                jnp.sum(jnp.where(is_distill, grad_stream, 0.0), (0, 1)),
            ]
        )
    )
    grad_embed = jnp.where(special, 0.0, grad_stream)
    embed_low = grad_embed.astype(low).reshape(row_count, D)
    grad_patch = matmul_tn(flat_patches, embed_low)
    grad_table = matmul_tn(onehot_pos, embed_low)
    patch_bias = jnp.sum(grad_embed, (0, 1))
    leader = (device == 0).astype(f32)
    small_terms = jnp.concatenate(
        [
            grad_tokens,
            grad_table[2:],
            patch_bias[None],
            grad_tokens,
            (first_gain + token_gain)[None],
            (first_shift + token_shift)[None],
            jnp.sum(grad_query, 0)[None],
            value_bias[None],
            out_bias[None],
            second_gain[None],
            second_shift[None],
            leader * down_bias[None],
            leader * final_gain[None],
            leader * final_shift[None],
        ],
        0,
    )
    small_count = POS + 13
    small_share = -(-small_count // devices)
    small_terms = jnp.pad(small_terms, ((0, small_share * devices - small_count), (0, 0)))

    key_terms = (
        pooled_grad.reshape(pairs, devices, own_rows)
        .transpose(1, 0, 2)
        .reshape(devices, pairs * own_rows)
    )
    key_share = -(-pairs * own_rows // D)
    key_terms = jnp.pad(key_terms, ((0, 0), (0, key_share * D - pairs * own_rows)))
    terms_rows = jnp.concatenate(
        [
            grad_patch.reshape(dp_size, seq_size, own_rows, D),
            small_terms.reshape(dp_size, seq_size, small_share, D),
            key_terms.reshape(dp_size, seq_size, key_share, D),
            jnp.broadcast_to(grad_query, (dp_size, seq_size, 2, D)),
        ],
        2,
    )
    mine = lax.dynamic_index_in_dim(terms_rows, seq_index, 1, keepdims=False)
    theirs = lax.dynamic_index_in_dim(terms_rows, 1 - seq_index, 1, keepdims=False)
    chip_terms = mine + swap_cores(theirs.astype(low)).astype(f32)
    pair_share = 2 * row_share
    grad_att_own = lax.dynamic_slice_in_dim(grad_att, seq_index * row_share, row_share, 0)
    pair_own = jnp.concatenate([grad_attn_own, grad_att_own], 0)
    sent = jnp.concatenate(
        [chip_terms.astype(low), jnp.broadcast_to(pair_own, (dp_size, pair_share, D))], 1
    )
    received = exchange(sent, "dp")
    summed_share = chip_terms.shape[1]
    reduced = jnp.sum(received[:, :summed_share].astype(f32), 0)
    pair_rows = join_cores(received[:, summed_share:], seq_index, 1)
    pair_rows = pair_rows.reshape(devices, 2, row_share, D)
    owned_patch = reduced[:own_rows]
    owned_small = reduced[own_rows : own_rows + small_share]
    key_start = own_rows + small_share
    key_reduced = reduced[key_start : key_start + key_share].reshape(-1)[: pairs * own_rows]
    key_reduced = key_reduced.reshape(2, HEADS, own_rows)
    query_reduced = reduced[key_start + key_share :]

    owned_query = matmul_tn(token_own, query_reduced.astype(low))
    key_left = jnp.repeat(
        key_reduced.transpose(2, 0, 1), HD, axis=2
    )
    owned_key = jnp.sum(key_left * query_low.astype(f32)[None], 1) * HD ** (-0.5)
    grad_attn_rows = pair_rows[:, 0].reshape(rows, D)
    grad_att_rows = pair_rows[:, 1].reshape(all_images, 2, HEADS, HD)
    owned_value = jnp.einsum(
        "nihd,nihc->dhc", pooled_own, grad_att_rows, preferred_element_type=f32
    ).reshape(own_rows, D)
    attended_own = matmul_nt(select_own, attended).astype(low)
    owned_out = matmul(attended_own, grad_attn_rows)
    owned_block = jnp.concatenate([owned_query, owned_key, owned_value, owned_out, owned_up], 1)

    shard_square = (
        jnp.sum(owned_patch * owned_patch)
        + jnp.sum(owned_block * owned_block)
        + jnp.sum(owned_down * owned_down)
        + jnp.sum(owned_heads * owned_heads)
        + jnp.sum(owned_small * owned_small)
        + jnp.sum(up_bias * up_bias)
    )
    square_high, square_rest = split_low(shard_square)
    square_rest, square_last = split_low(shard_square - square_high.astype(f32))
    tail_row = jnp.concatenate(
        [
            jnp.stack([square_high, square_rest, square_last]),
            up_bias.astype(low),
            jnp.zeros((D - 3 - own_hidden,), low),
        ]
    )
    final = gather_blocks(
        jnp.concatenate([owned_small.astype(low), tail_row[None]], 0), "dp"
    ).reshape(dp_size, small_share + 1, D)
    final = join_cores(final, seq_index, 1).reshape(devices, small_share + 1, D)
    summed_rows = final[:, :small_share].astype(f32).reshape(devices * small_share, D)[:small_count]
    global_square = jnp.sum(final[:, small_share, 0:3].astype(f32))
    up_bias_all = final[:, small_share, 3 : 3 + own_hidden].astype(f32).reshape(FF)
    summed_long = jnp.concatenate([up_bias_all, head_bias])
    total_square = global_square + jnp.sum(head_bias * head_bias)
    grad_norm = jnp.sqrt(total_square)
    factor = jnp.minimum(1.0, CLIP_NORM / (grad_norm + 1e-06))
    vectors_grad = factor * summed_rows[POS:]
    patch_new, patch_mean_new, patch_square_new = adam_update(
        patch_weight, patch_mean, patch_square, owned_patch, factor, DECAY_RATE, LEARN_RATE
    )
    block_new, block_mean_new, block_square_new = adam_update(
        block_weight, block_mean, block_square, owned_block, factor, DECAY_RATE, LEARN_RATE
    )
    down_new, down_mean_new, down_square_new = adam_update(
        down_weight, down_mean, down_square, owned_down, factor, DECAY_RATE, LEARN_RATE
    )
    heads_new, heads_mean_new, heads_square_new = adam_update(
        heads_weight, heads_mean, heads_square, owned_heads, factor, DECAY_RATE, LEARN_RATE
    )
    rows_new, rows_mean_new, rows_square_new = adam_update(
        small_rows, rows_mean, rows_square, summed_rows, factor, 0.0, SMALL_RATE
    )
    long_new, long_mean_new, long_square_new = adam_update(
        small_long, long_mean, long_square, summed_long, factor, 0.0, SMALL_RATE
    )
    return (
        loss,
        grad_norm,
        patch_new,
        patch_mean_new,
        patch_square_new,
        block_new,
        block_mean_new,
        block_square_new,
        down_new,
        down_mean_new,
        down_square_new,
        heads_new,
        heads_mean_new,
        heads_square_new,
        rows_new,
        rows_mean_new,
        rows_square_new,
        long_new,
        long_mean_new,
        long_square_new,
        vectors_grad,
    )


def solution(mesh):
    placed = (
        P("dp", "seq", None),
        P("dp", "seq"),
        P("dp"),
        P("dp", None),
        P("dp"),
        P("dp"),
        P("dp", None),
        P(("dp", "seq"), None),
        P(("dp", "seq"), None),
        P(("dp", "seq"), None),
        P(("dp", "seq"), None),
        P(("dp", "seq"), None),
        P(("dp", "seq"), None),
        P(("dp", "seq"), None),
        P(("dp", "seq"), None),
        P(("dp", "seq"), None),
        P(("dp", "seq"), None),
        P(("dp", "seq"), None),
        P(("dp", "seq"), None),
        P(),
        P(),
        P(),
        P(),
        P(),
        P(),
    )
    return jax.shard_map(
        shards,
        mesh=mesh,
        in_specs=placed,
        out_specs=(
            P(),
            P(),
            P(("dp", "seq"), None),
            P(("dp", "seq"), None),
            P(("dp", "seq"), None),
            P(("dp", "seq"), None),
            P(("dp", "seq"), None),
            P(("dp", "seq"), None),
            P(("dp", "seq"), None),
            P(("dp", "seq"), None),
            P(("dp", "seq"), None),
            P(("dp", "seq"), None),
            P(("dp", "seq"), None),
            P(("dp", "seq"), None),
            P(),
            P(),
            P(),
            P(),
            P(),
            P(),
            P(),
        ),
        check_vma=False,
    )
```

```python
import math

import jax
import jax.numpy as jnp
from jax import lax
from jax.experimental import pallas as pl
from jax.experimental.pallas import tpu as pltpu
from jax.sharding import PartitionSpec as P

D = 768
HEADS = 12
HD = 64
FF = 3072
CLS = 1000
POS = 198
STEP = 7


NORM_EPS = 1e-06
DROP_SCALE = 1.0 / 0.9
CLIP_NORM = 0.02
LEARN_RATE = 0.02
SMALL_RATE = 0.15
BETA_FIRST = 0.9
BETA_SECOND = 0.999
ADAM_EPS = 1e-08
DECAY_RATE = 0.05
MASK_FILL = -1e30
highest = lax.Precision.HIGHEST


def matmul(left, right):
    return jnp.dot(left, right, preferred_element_type=jnp.float32)


def matmul_tn(left, right):
    return lax.dot_general(
        left, right, (((0,), (0,)), ((), ())), preferred_element_type=jnp.float32
    )


def matmul_nt(left, right):
    return lax.dot_general(
        left, right, (((1,), (1,)), ((), ())), preferred_element_type=jnp.float32
    )


def norm_forward(values, gain, shift):
    centered = values - jnp.mean(values, -1, keepdims=True)
    inverse = lax.rsqrt(jnp.mean(centered * centered, -1, keepdims=True) + NORM_EPS)
    normed = centered * inverse
    return (normed * gain + shift, normed, inverse)


def norm_backward(grad_out, normed, inverse, gain):
    scaled = grad_out * gain
    grad_in = inverse * (
        scaled
        - jnp.mean(scaled, -1, keepdims=True)
        - normed * jnp.mean(scaled * normed, -1, keepdims=True)
    )
    leading = tuple(range(grad_out.ndim - 1))
    return (grad_in, jnp.sum(grad_out * normed, leading), jnp.sum(grad_out, leading))


def gelu_parts(values):
    cumulative = 0.5 * (1.0 + jax.scipy.special.erf(values * 0.7071067811865476))
    density = 0.3989422804014327 * jnp.exp(-0.5 * values * values)
    return (values * cumulative, cumulative + values * density)


def adam_update(weight, first, second, gradient, factor, decay, rate):
    clipped = gradient * factor
    first_new = BETA_FIRST * first + (1.0 - BETA_FIRST) * clipped
    second_new = BETA_SECOND * second + (1.0 - BETA_SECOND) * clipped * clipped
    first_hat = first_new / (1.0 - BETA_FIRST**STEP)
    second_hat = second_new / (1.0 - BETA_SECOND**STEP)
    weight_new = weight - rate * (first_hat / (jnp.sqrt(second_hat) + ADAM_EPS) + decay * weight)
    return (weight_new, first_new, second_new)


ALL = ("dp", "seq")


def exchange(blocks, axes=ALL):
    return lax.all_to_all(blocks, axes, 0, 0, tiled=True)


def gather_blocks(block, axes=ALL):
    count = lax.axis_size(axes)
    return exchange(jnp.broadcast_to(block[None], (count,) + block.shape), axes)


def swap_cores(value):
    return lax.ppermute(value, "seq", [(0, 1), (1, 0)])


def join_cores(value, seq_index, axis):
    other = swap_cores(value)
    first = jnp.where(seq_index == 0, value, other)
    second = jnp.where(seq_index == 0, other, value)
    return jnp.stack([first, second], axis)


def split_low(value):
    high = value.astype(jnp.bfloat16)
    rest = (value - high.astype(jnp.float32)).astype(jnp.bfloat16)
    return high, rest


PADDED = 16
PAIR = 2 * PADDED
CHUNK = 112


def whole(shape, columns=None):
    if columns is None:
        return pl.BlockSpec(shape, lambda *_: (0,) * len(shape))
    return pl.BlockSpec(shape, lambda *_: (0, columns))


def kernel_call(body, outputs, inputs, specs=None, scratch=(), flops=1_000_000):
    specs = specs or {}
    in_specs = []
    moved = 0
    for position, value in enumerate(inputs):
        if value.ndim == 1:
            in_specs.append(pl.BlockSpec(memory_space=pltpu.SMEM))
            continue
        in_specs.append(specs.get(position, whole(value.shape)))
        moved += math.prod(in_specs[-1].block_shape) * value.dtype.itemsize
    moved += sum(math.prod(shape) * jnp.dtype(kind).itemsize for shape, kind in outputs)
    return pl.pallas_call(
        body,
        grid=(1,),
        in_specs=in_specs,
        out_specs=[whole(shape) for shape, _ in outputs],
        out_shape=[jax.ShapeDtypeStruct(shape, kind) for shape, kind in outputs],
        scratch_shapes=list(scratch),
        cost_estimate=pl.CostEstimate(flops=flops, bytes_accessed=moved, transcendentals=0),
        compiler_params=pltpu.CompilerParams(vmem_limit_bytes=48 * 1024 * 1024),
    )(*inputs)


def iota(shape, axis):
    return lax.broadcasted_iota(jnp.int32, shape, axis)


def own_selector(device, count):
    return jnp.where(
        iota((count, D), 0) + device * count == iota((count, D), 1), 1.0, 0.0
    ).astype(jnp.bfloat16)


def pair_mask(rows):
    return (iota((rows, D), 0) & (PADDED - 1)) == (iota((rows, D), 1) >> 6)


def token_rows(small_ref):
    tokens = small_ref[POS + 1 : POS + 3, :] + small_ref[0:2, :]
    return jnp.concatenate([tokens, jnp.zeros((6, D), jnp.float32)], 0)


def vector(small_ref, index):
    return small_ref[POS + index : POS + index + 1, :]


def norm_in(grad_out, normed, inverse, gain):
    scaled = grad_out * gain
    return inverse * (
        scaled
        - jnp.mean(scaled, -1, keepdims=True)
        - normed * jnp.mean(scaled * normed, -1, keepdims=True)
    )


def spread_pairs(values):
    count = values.shape[0]
    spread = jnp.broadcast_to(values[:, None, :], (count, PADDED, D)).reshape(count * PADDED, D)
    return jnp.where(pair_mask(count * PADDED), spread, 0.0)


def collect_pairs(values):
    count = values.shape[0] // PADDED
    kept = jnp.where(pair_mask(values.shape[0]), values, 0.0)
    return jnp.sum(kept.reshape(count, PADDED, D), 1)


def prepare_kernel(device_ref, small_ref, query_weight_ref, meta_ref, out_ref):
    own = query_weight_ref.shape[0]
    token_out, _, _ = norm_forward(token_rows(small_ref), vector(small_ref, 3), vector(small_ref, 4))
    token_own = matmul_nt(token_out.astype(jnp.bfloat16), own_selector(device_ref[0], own))
    partial = matmul(token_own.astype(jnp.bfloat16), query_weight_ref[...].astype(jnp.bfloat16))
    high, rest = split_low(partial)
    half = D // 2
    pieces = [part[i : i + 1, j * half : (j + 1) * half].astype(jnp.float32)
              for part in (high, rest) for i in range(2) for j in range(2)]
    block = jnp.concatenate([jnp.concatenate(pieces, 0), meta_ref[...]], 1).astype(jnp.bfloat16)
    out_ref[...] = jnp.broadcast_to(block[None], out_ref.shape)


def query_kernel(received_ref, key_weight_ref, patch_ref, small_ref, early_ref, query_ref):
    total = jnp.sum(received_ref[:, :, : D // 2].astype(jnp.float32), 0)
    halves = total[0:4] + total[4:8]
    query = jnp.concatenate(
        [
            jnp.concatenate([halves[0:1], halves[1:2]], 1),
            jnp.concatenate([halves[2:3], halves[3:4]], 1),
        ],
        0,
    ) + vector(small_ref, 5)
    query = query.astype(jnp.bfloat16).astype(jnp.float32)
    blocks = spread_pairs(jnp.concatenate([query] * 4, 0))
    query_ref[...] = blocks[:PAIR]
    keys = matmul_nt(key_weight_ref[...].astype(jnp.bfloat16), blocks.astype(jnp.bfloat16))
    keys = keys * HD ** (-0.5)
    block = jnp.concatenate([patch_ref[...], keys], 1).astype(jnp.bfloat16)
    early_ref[...] = jnp.broadcast_to(block[None], early_ref.shape)


def row_ids(start, rows, images, local_slots, seq_index):
    ids = iota((rows, 1), 0) + start
    shift = images.bit_length() - 1
    return ids & (images - 1), (ids >> shift) + seq_index * local_slots


def join_weights(seq_index, own_ref, other_ref, weights):
    count = own_ref.shape[1]
    first_core = seq_index == 0
    for block in range(own_ref.shape[0]):
        here = own_ref[block].astype(jnp.float32)
        there = other_ref[block].astype(jnp.float32)
        start = block * 2 * count
        weights[start : start + count, :] = jnp.where(first_core, here, there).astype(jnp.bfloat16)
        weights[start + count : start + 2 * count, :] = jnp.where(first_core, there, here).astype(
            jnp.bfloat16
        )


def slots_kernel(
    seq_ref, own_ref, other_ref, patches_ref, pos_ref, valid_ref, small_ref,
    packed_ref, exponent_ref, first_ref, normed_ref, inverse_ref, keys_ref,
    weights, high, rest,
):
    images = exponent_ref.shape[1] // PAIR
    row_count = patches_ref.shape[0]
    local_slots = row_count // images
    columns = exponent_ref.shape[1]
    seq_index = seq_ref[0]
    join_weights(seq_index, own_ref, other_ref, weights)
    keys_ref[...] = weights[:, D:]
    tokens = token_rows(small_ref)
    table_high, table_rest = split_low(small_ref[0:POS, :])
    high[...] = table_high
    rest[...] = table_rest
    column_image = iota((CHUNK, columns), 1) >> 5

    def step(index, peak):
        rows = pl.ds(pl.multiple_of(index * CHUNK, CHUNK), CHUNK)
        onehot = jnp.where(pos_ref[rows, :] == iota((CHUNK, POS), 1), 1.0, 0.0).astype(jnp.bfloat16)
        embedded = (
            matmul(patches_ref[rows, :], weights[:, :D])
            + matmul(onehot, high[...])
            + matmul(onehot, rest[...])
            + vector(small_ref, 0)
        )
        image, slot = row_ids(index * CHUNK, CHUNK, images, local_slots, seq_index)
        stream = jnp.where(slot == 0, tokens[0:1], jnp.where(slot == 1, tokens[1:2], embedded))
        out, normed, inverse = norm_forward(stream, vector(small_ref, 3), vector(small_ref, 4))
        first = out.astype(jnp.bfloat16)
        first_ref[rows, :] = first
        normed_ref[rows, :] = normed
        inverse_ref[rows, :] = inverse
        scores = matmul(first, weights[:, D:])
        kept = (column_image == image) & (slot < valid_ref[0:1, :])
        scores = jnp.where(kept, scores, MASK_FILL)
        exponent_ref[rows, :] = scores
        return jnp.maximum(peak, jnp.max(scores, 0, keepdims=True))

    peak = lax.fori_loop(
        0, row_count // CHUNK, step, jnp.full((1, columns), MASK_FILL, jnp.float32)
    )
    exponent = jnp.exp(exponent_ref[...] - peak)
    exponent_ref[...] = exponent
    total = jnp.sum(exponent, 0, keepdims=True)
    packed_ref[0:columns, :] = matmul_tn(exponent.astype(jnp.bfloat16), first_ref[...])
    packed_ref[columns : columns + 8, :] = jnp.zeros((8, D), jnp.float32)
    packed_ref[columns : columns + 1, 0:columns] = peak
    packed_ref[columns + 1 : columns + 2, 0:columns] = total


def combine_kernel(seq_ref, own_ref, other_ref, pooled_ref, scale_ref, turned_ref, turned):
    columns = pooled_ref.shape[0]
    own = turned_ref.shape[1]
    peak_here = own_ref[columns : columns + 1, 0:columns]
    peak_there = other_ref[columns : columns + 1, 0:columns]
    peak = jnp.maximum(peak_here, peak_there)
    here = jnp.exp(peak_here - peak)
    there = jnp.exp(peak_there - peak)
    total = (
        here * own_ref[columns + 1 : columns + 2, 0:columns]
        + there * other_ref[columns + 1 : columns + 2, 0:columns]
    )
    here = here / total
    there = there / total
    scale_ref[...] = jnp.broadcast_to(here, (8, columns))
    here_rows = jnp.broadcast_to(here, (columns, columns)).T[:, 0:1]
    there_rows = jnp.broadcast_to(there, (columns, columns)).T[:, 0:1]
    pooled = own_ref[0:columns, :] * here_rows + other_ref[0:columns, :] * there_rows
    pooled_ref[...] = pooled
    turned[...] = pooled.T
    for block in range(turned_ref.shape[0]):
        start = pl.multiple_of(block * 2 * own + seq_ref[0] * own, 8)
        turned_ref[block] = turned[pl.ds(start, own), :].astype(jnp.bfloat16)


def attend_kernel(pooled_ref, value_weight_ref, small_ref, out_ref):
    mixed = matmul(pooled_ref[...].astype(jnp.bfloat16), value_weight_ref[...])
    attended = (collect_pairs(mixed) + vector(small_ref, 6)).astype(jnp.bfloat16)
    out_ref[...] = jnp.broadcast_to(attended[None], out_ref.shape)


def odd_row(shape):
    return (iota(shape, 0) & 1) == 1


def mlp_kernel(
    device_ref, attended_ref, out_weight_ref, up_ref, down_ref, small_ref, info_ref, bias_ref,
    partial_ref, second_ref, normed_ref, inverse_ref, slope_ref, act_ref, middle_ref, turned_ref,
):
    attended = attended_ref[...]
    own = turned_ref.shape[0]
    turned_ref[...] = matmul_nt(own_selector(device_ref[0], own), attended).astype(jnp.bfloat16)
    tokens = token_rows(small_ref)
    stream = jnp.where(odd_row(attended.shape), tokens[1:2], tokens[0:1])
    middle = stream + info_ref[:, 5:6] * (
        matmul(attended, out_weight_ref[...]) + vector(small_ref, 7)
    )
    middle_ref[...] = middle
    out, normed, inverse = norm_forward(middle, vector(small_ref, 8), vector(small_ref, 9))
    second = out.astype(jnp.bfloat16)
    second_ref[...] = second
    normed_ref[...] = normed
    inverse_ref[...] = inverse
    hidden = matmul(second, up_ref[...]) + bias_ref[...]
    act, slope = gelu_parts(hidden)
    act = act.astype(jnp.bfloat16)
    act_ref[...] = act
    slope_ref[...] = slope
    partial_ref[...] = matmul(act, down_ref[...].astype(jnp.bfloat16)).astype(jnp.bfloat16)


def heads_kernel(
    device_ref, mlp_ref, middle_ref, info_ref, small_ref,
    class_a_ref, class_b_ref, distill_a_ref, distill_b_ref, bias_ref,
    act_ref, slope_ref, second_ref, up_ref, down_ref,
    partial_ref, result_ref, heads_ref, sums_ref, bias_out_ref, down_out_ref, up_bias_ref, loss_ref,
):
    rows = mlp_ref.shape[0]
    half = class_a_ref.shape[1]
    low = jnp.bfloat16
    result = middle_ref[...] + info_ref[:, 6:7] * (
        mlp_ref[...].astype(jnp.float32) + vector(small_ref, 10)
    )
    out, normed, inverse = norm_forward(result, vector(small_ref, 11), vector(small_ref, 12))
    head = out.astype(low)
    columns = iota((rows, half), 1)
    odd = odd_row((rows, half))
    left, right, share_a, share_b = (info_ref[:, k : k + 1] for k in range(4))
    weight = info_ref[:, 4:5]
    logits, targets = [], []
    for part, (class_ref, distill_ref) in enumerate(
        ((class_a_ref, distill_a_ref), (class_b_ref, distill_b_ref))
    ):
        start = part * half
        piece = jnp.where(
            odd,
            matmul(head, distill_ref[...]) + bias_ref[1:2, start : start + half],
            matmul(head, class_ref[...]) + bias_ref[0:1, start : start + half],
        )
        where = (columns + start).astype(jnp.float32)
        logits.append(jnp.where(columns + start < CLS, piece, MASK_FILL))
        targets.append(
            share_a * jnp.where(where == left, 1.0, 0.0)
            + share_b * jnp.where(where == right, 1.0, 0.0)
        )
    peak = jnp.maximum(
        jnp.max(logits[0], -1, keepdims=True), jnp.max(logits[1], -1, keepdims=True)
    )
    exponents = [jnp.exp(piece - peak) for piece in logits]
    total = jnp.sum(exponents[0], -1, keepdims=True) + jnp.sum(exponents[1], -1, keepdims=True)
    log_total = peak + jnp.log(total)
    weight_sum = 0.5 * jnp.sum(weight, 0, keepdims=True)
    terms = jnp.zeros((rows, 1), jnp.float32)
    for piece, target in zip(logits, targets):
        terms = terms - 0.5 * jnp.sum(
            target * (piece - log_total), -1, keepdims=True
        )
    loss = jnp.sum(weight * terms, 0, keepdims=True) / weight_sum
    loss_ref[...] = jnp.broadcast_to(loss, loss_ref.shape)
    scale = weight * 0.5 / weight_sum
    head_own = matmul_nt(own_selector(device_ref[0], heads_ref.shape[1]), head).astype(low)
    grad_head = jnp.zeros((rows, D), jnp.float32)
    for part, (class_ref, distill_ref) in enumerate(
        ((class_a_ref, distill_a_ref), (class_b_ref, distill_b_ref))
    ):
        start = part * half
        grad = scale * (exponents[part] / total - targets[part])
        grad = grad.astype(low).astype(jnp.float32)
        for side, weight_ref in ((0, class_ref), (1, distill_ref)):
            mine = jnp.where(odd == (side == 1), grad, 0.0)
            bias_out_ref[side : side + 1, start : start + half] = jnp.sum(mine, 0, keepdims=True)
            mine = mine.astype(low)
            heads_ref[side, :, start : start + half] = matmul(head_own, mine)
            grad_head = grad_head + matmul_nt(mine, weight_ref[...])
    grad_result = norm_in(grad_head, normed, inverse, vector(small_ref, 11))
    result_ref[...] = grad_result
    grad_mlp = (info_ref[:, 6:7] * grad_result).astype(low)
    sums_ref[...] = jnp.zeros(sums_ref.shape, jnp.float32)
    sums_ref[0:1, :] = jnp.sum(grad_mlp.astype(jnp.float32), 0, keepdims=True)
    sums_ref[1:2, :] = jnp.sum(grad_head * normed, 0, keepdims=True)
    sums_ref[2:3, :] = jnp.sum(grad_head, 0, keepdims=True)
    down_out_ref[...] = matmul_tn(act_ref[...], grad_mlp)
    grad_hidden = (
        matmul_nt(grad_mlp, down_ref[...].astype(low)) * slope_ref[...]
    ).astype(low)
    up_bias_ref[...] = jnp.broadcast_to(
        jnp.sum(grad_hidden.astype(jnp.float32), 0, keepdims=True), up_bias_ref.shape
    )
    partial = matmul_nt(grad_hidden, up_ref[...])
    grad_up = matmul_tn(second_ref[...], grad_hidden)
    blocks = partial_ref.shape[0]
    per = rows // blocks
    own = D // blocks
    hidden = grad_up.shape[1]
    pad = jnp.zeros((D, 128 - hidden), jnp.float32)
    grad_up = jnp.concatenate([grad_up, pad], 1)
    for block in range(blocks):
        partial_ref[block, 0:per, :] = partial[block * per : (block + 1) * per].astype(low)
        pieces = [
            grad_up[block * own + 8 * j : block * own + 8 * (j + 1)] for j in range(own // 8)
        ]
        partial_ref[block, per : 2 * per, :] = jnp.concatenate(pieces, 1).astype(low)


def back_kernel(
    index_ref, second_ref, other_ref, normed2_ref, inverse2_ref, result_ref, info_ref, small_ref,
    out_weight_ref, value_weight_ref, query_weight_ref, key_weight_ref,
    pooled_ref, scale_ref, exponent_ref, first_ref, normed_ref, inverse_ref, keys_ref,
    patches_ref, pos_ref, sums_ref,
    mine_ref, theirs_ref,
    values, turned_keys, embed, scores, onehot, patch_out, small_out, pooled_grad,
):
    low = jnp.bfloat16
    columns = pooled_ref.shape[0]
    images = columns // PAIR
    row_count = patches_ref.shape[0]
    local_slots = row_count // images
    dp_index, seq_index = index_ref[0], index_ref[1]
    per = 2 * images
    own_rows = pl.ds(pl.multiple_of(dp_index * per, 8), per)
    grad_second = second_ref[...] + other_ref[...]
    normed2 = normed2_ref[own_rows, :]
    grad_middle = result_ref[own_rows, :] + norm_in(
        grad_second, normed2, inverse2_ref[own_rows, :], vector(small_ref, 8)
    )
    grad_attn = (info_ref[own_rows, 5:6] * grad_middle).astype(low)
    grad_att = matmul_nt(grad_attn, out_weight_ref[...]).astype(low)
    att_float = grad_att.astype(jnp.float32)
    att_blocks = spread_pairs(att_float)
    value_rows = matmul_nt(att_blocks.astype(low), value_weight_ref[...]).astype(low)
    values[...] = value_rows
    turned_keys[...] = keys_ref[...].astype(jnp.float32).T.astype(low)
    const = jnp.sum(att_blocks * vector(small_ref, 6), -1, keepdims=True)
    mean = jnp.sum(pooled_ref[...] * value_rows.astype(jnp.float32), -1, keepdims=True) + const
    const = jnp.broadcast_to(const, (columns, columns)).T[0:1, :]
    mean = jnp.broadcast_to(mean, (columns, columns)).T[0:1, :]
    gain = vector(small_ref, 3)

    def step(index, sums):
        gain_sum, shift_sum, embed_sum, class_sum, distill_sum = sums
        rows = pl.ds(pl.multiple_of(index * CHUNK, CHUNK), CHUNK)
        first = first_ref[rows, :]
        probs = exponent_ref[rows, :] * scale_ref[0:1, :]
        grad_probs = matmul_nt(first, values[...]) + const
        grad_scores = (probs * (grad_probs - mean)).astype(low)
        scores[rows, :] = grad_scores
        grad_first = matmul(grad_scores, turned_keys[...]) + matmul(probs.astype(low), values[...])
        normed = normed_ref[rows, :]
        grad_stream = norm_in(grad_first, normed, inverse_ref[rows, :], gain)
        _, slot = row_ids(index * CHUNK, CHUNK, images, local_slots, seq_index)
        grad_embed = jnp.where(slot < 2, 0.0, grad_stream)
        embed[rows, :] = grad_embed.astype(low)
        onehot[rows, :] = jnp.where(pos_ref[rows, :] == iota((CHUNK, POS), 1), 1.0, 0.0).astype(low)
        return (
            gain_sum + jnp.sum(grad_first * normed, 0, keepdims=True),
            shift_sum + jnp.sum(grad_first, 0, keepdims=True),
            embed_sum + jnp.sum(grad_embed, 0, keepdims=True),
            class_sum + jnp.sum(jnp.where(slot == 0, grad_stream, 0.0), 0, keepdims=True),
            distill_sum + jnp.sum(jnp.where(slot == 1, grad_stream, 0.0), 0, keepdims=True),
        )

    zero = jnp.zeros((1, D), jnp.float32)
    gain_sum, shift_sum, embed_sum, class_sum, distill_sum = lax.fori_loop(
        0, row_count // CHUNK, step, (zero,) * 5
    )
    patch_out[...] = matmul_tn(patches_ref[...], embed[...])
    small_out[0:POS, :] = matmul_tn(onehot[...], embed[...])
    by_column = matmul_tn(scores[...], first_ref[...])
    by_pair = jnp.sum(by_column.reshape(images, PAIR, D), 0)
    grad_query = collect_pairs(matmul(by_pair.astype(low), key_weight_ref[...])) * HD ** (-0.5)
    eight = jnp.concatenate([grad_query, jnp.zeros((6, D), jnp.float32)], 0)
    token_grad = matmul_nt(eight.astype(low), query_weight_ref[...])
    _, token_normed, token_inverse = norm_forward(
        token_rows(small_ref), gain, vector(small_ref, 4)
    )
    token_in = norm_in(token_grad, token_normed, token_inverse, gain)
    once = jnp.where(seq_index == 0, 1.0, 0.0)
    leader = jnp.where((dp_index == 0) & (seq_index == 0), 1.0, 0.0)
    middle_even = jnp.sum(jnp.where(odd_row((per, D)), 0.0, grad_middle), 0, keepdims=True)
    middle_odd = jnp.sum(jnp.where(odd_row((per, D)), grad_middle, 0.0), 0, keepdims=True)
    class_sum = class_sum + token_in[0:1] + once * middle_even
    distill_sum = distill_sum + token_in[1:2] + once * middle_odd
    small_out[0:1, :] = class_sum
    small_out[1:2, :] = distill_sum
    vector_rows = (
        embed_sum,
        class_sum,
        distill_sum,
        gain_sum + jnp.sum(token_grad * token_normed, 0, keepdims=True),
        shift_sum + jnp.sum(token_grad, 0, keepdims=True),
        jnp.sum(grad_query, 0, keepdims=True),
        once * jnp.sum(att_float, 0, keepdims=True),
        once * jnp.sum(grad_attn.astype(jnp.float32), 0, keepdims=True),
        once * jnp.sum(grad_second * normed2, 0, keepdims=True),
        once * jnp.sum(grad_second, 0, keepdims=True),
        leader * sums_ref[0:1, :],
        leader * sums_ref[1:2, :],
        leader * sums_ref[2:3, :],
    )
    for index, row in enumerate(vector_rows):
        small_out[POS + index : POS + index + 1, :] = row
    small_count = small_out.shape[0]
    small_out[POS + 13 : small_count, :] = jnp.zeros((small_count - POS - 13, D), jnp.float32)
    query_rows = jnp.concatenate(
        [grad_query[i : i + 1, h * HD : (h + 1) * HD] for i in range(2) for h in range(HEADS)], 0
    )
    key_side = jnp.concatenate([by_pair, jnp.zeros((64 - PAIR, D), jnp.float32)], 0)
    pooled_grad[...] = jnp.concatenate([key_side, jnp.zeros((64, D), jnp.float32)], 0).T
    own = 2 * HEADS
    query_side = jnp.concatenate([jnp.zeros((own, 64), jnp.float32), query_rows], 1)
    attn_half = jnp.where(
        seq_index == 0,
        grad_attn[:, : D // 2].astype(jnp.float32),
        grad_attn[:, D // 2 :].astype(jnp.float32),
    )
    share = small_count // (2 * mine_ref.shape[0])
    for block in range(mine_ref.shape[0]):
        for ref, core in ((mine_ref, seq_index), (theirs_ref, 1 - seq_index)):
            start = pl.multiple_of((block * 2 + core) * own, 8)
            ref[block, 0:own, :] = patch_out[pl.ds(start, own), :].astype(ref.dtype)
            small = pl.multiple_of((block * 2 + core) * share, 8)
            ref[block, own : own + share, :] = small_out[pl.ds(small, share), :].astype(ref.dtype)
            keys = pooled_grad[pl.ds(start, own), :] + query_side
            pieces = [keys[8 * j : 8 * (j + 1)] for j in range(own // 8)]
            if ref is mine_ref:
                pieces.append(attn_half)
            else:
                pieces.append(jnp.zeros((8, D // 2), jnp.float32))
            ref[block, own + share :, :] = jnp.concatenate(pieces, 1).astype(ref.dtype)


def owned_kernel(
    index_ref, received_ref, other_attn_ref, out_weight_ref, pooled_ref, turned_ref,
    query_ref, small_ref, up_own_ref, up_other_ref, heads_ref, down_ref, up_bias_ref,
    patch_ref, block_ref, final_ref,
):
    low = jnp.bfloat16
    first_core = index_ref[1] == 0
    blocks = received_ref.shape[0]
    own = patch_ref.shape[0]
    share = final_ref.shape[1]
    half = D // 2
    total = jnp.sum(received_ref[:, :, :half].astype(jnp.float32), 0)
    right = jnp.sum(received_ref[:, : own + share, half:].astype(jnp.float32), 0)
    patch = jnp.concatenate([total[0:own], right[0:own]], 1)
    small = jnp.concatenate([total[own : own + share], right[own : own + share]], 1)
    keys = jnp.concatenate(
        [total[own + share :, 128 * j : 128 * (j + 1)] for j in range(own // 8)], 0
    )
    patch_ref[...] = patch
    square = jnp.sum(patch * patch) + jnp.sum(small * small)
    token_out, _, _ = norm_forward(token_rows(small_ref), vector(small_ref, 3), vector(small_ref, 4))
    token_own = matmul_nt(own_selector(index_ref[0], own), token_out.astype(low))
    part = jnp.zeros((own, D), jnp.float32)
    for i in range(2):
        row = jnp.concatenate(
            [keys[i * HEADS + h : i * HEADS + h + 1, 64:128] for h in range(HEADS)], 1
        )
        part = part + token_own[:, i : i + 1] * row
    block_ref[:, 0:D] = part
    square = square + jnp.sum(part * part)
    key_high, key_rest = split_low(keys[:, 0:PAIR])
    query_blocks = query_ref[...].astype(low)
    part = (matmul(key_high, query_blocks) + matmul(key_rest, query_blocks)) * HD ** (-0.5)
    block_ref[:, D : 2 * D] = part
    square = square + jnp.sum(part * part)
    here = received_ref[:, own + share :, half:].astype(jnp.float32).reshape(blocks * 8, half)
    there = other_attn_ref[...].astype(jnp.float32).reshape(blocks * 8, half)
    attn = jnp.concatenate(
        [jnp.where(first_core, here, there), jnp.where(first_core, there, here)], 1
    ).astype(low)
    att = matmul_nt(attn, out_weight_ref[...]).astype(low).astype(jnp.float32)
    part = jnp.zeros((own, D), jnp.float32)
    for block in range(blocks):
        spread = spread_pairs(att[block * 8 : (block + 1) * 8]).astype(low)
        part = part + matmul(pooled_ref[block], spread)
    block_ref[:, 2 * D : 3 * D] = part
    square = square + jnp.sum(part * part)
    part = matmul(turned_ref[...], attn)
    block_ref[:, 3 * D : 4 * D] = part
    square = square + jnp.sum(part * part)
    hidden = down_ref.shape[0]
    columns = []
    for block in range(blocks):
        mine = up_own_ref[block].astype(jnp.float32)
        theirs = up_other_ref[block].astype(jnp.float32)
        for pick in (jnp.where(first_core, mine, theirs), jnp.where(first_core, theirs, mine)):
            columns.append(
                jnp.concatenate(
                    [pick[:, 128 * j : 128 * j + hidden] for j in range(own // 8)], 0
                )
            )
    part = jnp.concatenate(columns, 1)
    block_ref[:, 4 * D :] = part
    square = square + jnp.sum(part * part)
    for side in range(2):
        square = square + jnp.sum(heads_ref[side] * heads_ref[side])
    square = square + jnp.sum(down_ref[...] * down_ref[...])
    bias = up_bias_ref[0:1, :]
    square = jnp.broadcast_to(square + jnp.sum(bias * bias), (1, 128))
    high, rest = split_low(square)
    middle, last = split_low(square - high.astype(jnp.float32))
    side = jnp.concatenate(
        [
            high.astype(jnp.float32),
            middle.astype(jnp.float32),
            last.astype(jnp.float32),
            jnp.concatenate([bias, jnp.zeros((1, 128 - hidden), jnp.float32)], 1),
            jnp.zeros((4, 128), jnp.float32),
        ],
        0,
    )
    final = jnp.concatenate([small, side], 1).astype(low)
    final_ref[...] = jnp.broadcast_to(final[None], final_ref.shape)


def final_kernel(
    seq_ref, own_ref, other_ref, small_ref, mean_ref, square_ref, bias_ref,
    new_ref, mean_new_ref, square_new_ref, vectors_ref, scalar_ref, up_bias_ref, rows,
):
    first_core = seq_ref[0] == 0
    share = own_ref.shape[1]
    square = jnp.zeros((1, 128), jnp.float32)
    for block in range(own_ref.shape[0]):
        here = own_ref[block].astype(jnp.float32)
        there = other_ref[block].astype(jnp.float32)
        for core, pick in enumerate(
            (jnp.where(first_core, here, there), jnp.where(first_core, there, here))
        ):
            index = block * 2 + core
            rows[index * share : (index + 1) * share, :] = pick[:, :D]
            side = pick[:, D:]
            square = square + (side[0:1] + side[1:2] + side[2:3])
            up_bias_ref[index : index + 1, :] = side[3:4]
    bias = bias_ref[...]
    total = square[:, 0:1] + jnp.sum(jnp.sum(bias * bias, 0, keepdims=True), 1, keepdims=True)
    norm = jnp.sqrt(total)
    factor = jnp.minimum(1.0, CLIP_NORM / (norm + 1e-06))
    scalar_ref[...] = jnp.broadcast_to(norm, scalar_ref.shape)
    scalar_ref[0:1, :] = jnp.broadcast_to(factor, (1, scalar_ref.shape[1]))
    count = new_ref.shape[0]
    gradient = rows[0:count, :]
    new, first, second = adam_update(
        small_ref[...], mean_ref[...], square_ref[...], gradient, factor, 0.0, SMALL_RATE
    )
    new_ref[...] = new
    mean_new_ref[...] = first
    square_new_ref[...] = second
    vectors_ref[...] = rows[POS:count, :] * factor


def shards_tiled(
    patches,
    pos_index,
    valid,
    classes,
    mixing,
    image_weight,
    drop_keep,
    patch_weight,
    patch_mean,
    patch_square,
    block_weight,
    block_mean,
    block_square,
    down_weight,
    down_mean,
    down_square,
    heads_weight,
    heads_mean,
    heads_square,
    small_rows,
    rows_mean,
    rows_square,
    small_long,
    long_mean,
    long_square,
):
    low = jnp.bfloat16
    f32 = jnp.float32
    images, local_slots, patch_dim = patches.shape
    row_count = images * local_slots
    dp_size = lax.axis_size("dp")
    seq_size = lax.axis_size("seq")
    devices = dp_size * seq_size
    dp_index = lax.axis_index("dp").astype(jnp.int32)
    seq_index = lax.axis_index("seq").astype(jnp.int32)
    device = dp_index * seq_size + seq_index
    own_rows = patch_weight.shape[0]
    own_hidden = down_weight.shape[0]
    all_images = dp_size * images
    rows = all_images * 2
    per_chip = images * 2
    columns = images * PAIR
    half = D // 2
    device_scalar = device[None]
    seq_scalar = seq_index[None]
    device_seq = jnp.stack([device, seq_index])
    dp_seq = jnp.stack([dp_index, seq_index])

    pad = jnp.zeros((own_rows, 1024 - CLS), f32)
    gathered_late = lax.all_gather(
        jnp.concatenate(
            [block_weight[:, 2 * D : 4 * D], heads_weight[:, :CLS], pad, heads_weight[:, CLS:], pad],
            1,
        ).astype(low),
        ALL,
        axis=0,
        tiled=True,
    )
    gathered_query_key = lax.all_gather(
        lax.optimization_barrier((block_weight[:, : 2 * D].astype(low), gathered_late[:8, :128]))[0],
        ALL,
        axis=0,
        tiled=True,
    )

    meta = jnp.concatenate(
        [classes // 32, classes % 32, mixing[:, None], image_weight[:, None], drop_keep], 1
    )
    meta_width = meta.shape[1]
    meta_count = images * meta_width
    meta = jnp.pad(meta.reshape(1, meta_count).astype(f32), ((0, 7), (0, 128 - meta_count)))
    (asked,) = kernel_call(
        prepare_kernel,
        [((devices, 8, half + 128), low)],
        [device_scalar, small_rows, block_weight, meta],
        {2: whole((own_rows, D), 0)},
    )
    asked = exchange(asked)
    early, query_blocks = kernel_call(
        query_kernel,
        [((dp_size, own_rows, D + columns), low), ((PAIR, D), f32)],
        [asked, block_weight, patch_weight, small_rows],
        {1: whole((own_rows, D), 1)},
    )
    early = exchange(early, "dp")
    early_other = swap_cores(early)
    metas = asked.reshape(dp_size, seq_size, 8, half + 128)[:, 0, 0, half : half + meta_count]
    metas = metas.astype(f32).reshape(all_images, meta_width)
    labels = metas[:, 0:3] * 32.0 + metas[:, 3:6]
    share = metas[:, 6:7] / 16.0
    weight_keep = jnp.concatenate([metas[:, 7:8], metas[:, 8:10] * DROP_SCALE], 1)
    ones = jnp.ones_like(share)
    info_even = jnp.concatenate([labels[:, 0:2], share, 1.0 - share, weight_keep, ones], 1)
    info_odd = jnp.concatenate(
        [labels[:, 2:3], labels[:, 2:3], ones, 0.0 * ones, weight_keep, ones], 1
    )
    info = jnp.stack([info_even, info_odd], 1).reshape(rows, 8)

    flat_patches = patches.transpose(1, 0, 2).reshape(row_count, patch_dim)
    flat_pos = pos_index.T.reshape(row_count, 1)
    valid_columns = jnp.repeat(valid, PAIR)[None]
    packed, exponent, first, normed, inverse, keys = kernel_call(
        slots_kernel,
        [
            ((columns + 8, D), f32),
            ((row_count, columns), f32),
            ((row_count, D), low),
            ((row_count, D), f32),
            ((row_count, 1), f32),
            ((D, columns), low),
        ],
        [seq_scalar, early, early_other, flat_patches, flat_pos, valid_columns, small_rows],
        scratch=[
            pltpu.VMEM((D, D + columns), low),
            pltpu.VMEM((POS, D), low),
            pltpu.VMEM((POS, D), low),
        ],
    )
    packed_other = swap_cores(packed)
    pooled, scale, pooled_turned = kernel_call(
        combine_kernel,
        [((columns, D), f32), ((8, columns), f32), ((dp_size, own_rows, columns), low)],
        [seq_scalar, packed, packed_other],
        scratch=[pltpu.VMEM((D, columns), f32)],
    )

    up_blocks = (
        block_weight[:, 4 * D :]
        .astype(low)
        .reshape(own_rows, devices, own_hidden)
        .transpose(1, 0, 2)
    )
    pooled_turned = exchange(pooled_turned, "dp")
    up_blocks, _ = lax.optimization_barrier((up_blocks, packed_other[:8, :128]))
    up_own = exchange(up_blocks).reshape(D, own_hidden)

    (attended,) = kernel_call(
        attend_kernel,
        [((dp_size, per_chip, D), low)],
        [pooled, gathered_late, small_rows],
        {1: whole((D, D), 0)},
    )
    attended = exchange(attended, "dp").reshape(rows, D)
    up_shift = lax.dynamic_slice_in_dim(small_long, device * own_hidden, own_hidden, 0)[None]
    partial, second, second_normed, second_inverse, slope, act, middle, attended_turned = (
        kernel_call(
            mlp_kernel,
            [
                ((rows, D), low),
                ((rows, D), low),
                ((rows, D), f32),
                ((rows, 1), f32),
                ((rows, own_hidden), f32),
                ((rows, own_hidden), low),
                ((rows, D), f32),
                ((own_rows, rows), low),
            ],
            [
                device_scalar, attended, gathered_late, up_own, down_weight, small_rows, info,
                up_shift,
            ],
            {2: whole((D, D), 1)},
        )
    )

    def chip_sum(blocks):
        summed = jnp.sum(blocks.astype(f32), 0)
        return summed, swap_cores(summed)

    here, there = chip_sum(exchange(partial.reshape(dp_size, per_chip, D), "dp"))
    mlp_rows = gather_blocks((here + there).astype(low), "dp").reshape(rows, D)
    long_pad = jnp.zeros((1, 1024 - CLS), f32)
    head_shift = jnp.concatenate(
        [
            jnp.concatenate([small_long[None, FF : FF + CLS], long_pad], 1),
            jnp.concatenate([small_long[None, FF + CLS :], long_pad], 1),
        ],
        0,
    )
    head_blocks = {k: whole((D, 512), k - 2) for k in range(5, 9)}
    sent, grad_result, heads_grad, sums, head_bias, owned_down, up_bias, loss = kernel_call(
        heads_kernel,
        [
            ((dp_size, 2 * per_chip, D), low),
            ((rows, D), f32),
            ((2, own_rows, 1024), f32),
            ((8, D), f32),
            ((2, 1024), f32),
            ((own_hidden, D), f32),
            ((8, own_hidden), f32),
            ((8, 128), f32),
        ],
        [
            device_scalar, mlp_rows, middle, info, small_rows,
            gathered_late, gathered_late, gathered_late, gathered_late, head_shift,
            act, slope, second, up_own, down_weight,
        ],
        head_blocks,
    )
    received = exchange(sent, "dp")
    second_here, second_there = chip_sum(received[:, :per_chip])
    up_left, up_right = received[:, per_chip:, :half], received[:, per_chip:, half:]
    up_here = jnp.where(seq_index == 0, up_left, up_right)
    up_there = swap_cores(jnp.where(seq_index == 0, up_right, up_left))

    small_share = 8
    share_rows = own_rows + small_share + 8
    mine, theirs = kernel_call(
        back_kernel,
        [((dp_size, share_rows, D), f32), ((dp_size, share_rows, D), low)],
        [
            dp_seq, second_here, second_there, second_normed, second_inverse, grad_result, info,
            small_rows, gathered_late, gathered_late, gathered_query_key, gathered_query_key,
            pooled, scale, exponent, first, normed, inverse, keys, flat_patches, flat_pos, sums,
        ],
        {
            8: whole((D, D), 1),
            9: whole((D, D), 0),
            10: whole((D, D), 0),
            11: whole((D, D), 1),
        },
        scratch=[
            pltpu.VMEM((columns, D), low),
            pltpu.VMEM((columns, D), low),
            pltpu.VMEM((row_count, D), low),
            pltpu.VMEM((row_count, columns), low),
            pltpu.VMEM((row_count, POS), low),
            pltpu.VMEM((patch_dim, D), f32),
            pltpu.VMEM((devices * small_share, D), f32),
            pltpu.VMEM((D, 128), f32),
        ],
    )
    chip_terms = (mine + swap_cores(theirs).astype(f32)).astype(low)
    received = exchange(chip_terms, "dp")
    attn_other = swap_cores(received[:, own_rows + small_share :, half:])
    owned_patch, owned_block, final = kernel_call(
        owned_kernel,
        [
            ((own_rows, D), f32),
            ((own_rows, 4 * D + FF), f32),
            ((dp_size, small_share, D + 128), low),
        ],
        [
            device_seq, received, attn_other, gathered_late, pooled_turned, attended_turned,
            query_blocks, small_rows, up_here, up_there, heads_grad, owned_down, up_bias,
        ],
        {3: whole((D, D), 1)},
    )
    final = exchange(final, "dp")
    final_other = swap_cores(final)
    small_count = POS + 13
    (
        rows_new, rows_mean_new, rows_square_new, vectors_grad, scalars, up_bias_all,
    ) = kernel_call(
        final_kernel,
        [
            ((small_count, D), f32),
            ((small_count, D), f32),
            ((small_count, D), f32),
            ((13, D), f32),
            ((8, 128), f32),
            ((devices, 128), f32),
        ],
        [seq_scalar, final, final_other, small_rows, rows_mean, rows_square, head_bias],
        scratch=[pltpu.VMEM((devices * small_share, D), f32)],
    )
    loss = loss[0, 0]
    factor = scalars[0, 0]
    grad_norm = scalars[1, 0]
    summed_long = jnp.concatenate(
        [up_bias_all[:, :own_hidden].reshape(FF), head_bias[0, :CLS], head_bias[1, :CLS]]
    )
    owned_heads = jnp.concatenate([heads_grad[0, :, :CLS], heads_grad[1, :, :CLS]], 1)
    patch_new, patch_mean_new, patch_square_new = adam_update(
        patch_weight, patch_mean, patch_square, owned_patch, factor, DECAY_RATE, LEARN_RATE
    )
    block_new, block_mean_new, block_square_new = adam_update(
        block_weight, block_mean, block_square, owned_block, factor, DECAY_RATE, LEARN_RATE
    )
    down_new, down_mean_new, down_square_new = adam_update(
        down_weight, down_mean, down_square, owned_down, factor, DECAY_RATE, LEARN_RATE
    )
    heads_new, heads_mean_new, heads_square_new = adam_update(
        heads_weight, heads_mean, heads_square, owned_heads, factor, DECAY_RATE, LEARN_RATE
    )
    long_new, long_mean_new, long_square_new = adam_update(
        small_long, long_mean, long_square, summed_long, factor, 0.0, SMALL_RATE
    )
    return (
        loss,
        grad_norm,
        patch_new,
        patch_mean_new,
        patch_square_new,
        block_new,
        block_mean_new,
        block_square_new,
        down_new,
        down_mean_new,
        down_square_new,
        heads_new,
        heads_mean_new,
        heads_square_new,
        rows_new,
        rows_mean_new,
        rows_square_new,
        long_new,
        long_mean_new,
        long_square_new,
        vectors_grad,
    )


def shards_plain(
    patches,
    pos_index,
    valid,
    classes,
    mixing,
    image_weight,
    drop_keep,
    patch_weight,
    patch_mean,
    patch_square,
    block_weight,
    block_mean,
    block_square,
    down_weight,
    down_mean,
    down_square,
    heads_weight,
    heads_mean,
    heads_square,
    small_rows,
    rows_mean,
    rows_square,
    small_long,
    long_mean,
    long_square,
):
    low = jnp.bfloat16
    f32 = jnp.float32
    images, local_slots, patch_dim = patches.shape
    row_count = images * local_slots
    dp_size = lax.axis_size("dp")
    seq_size = lax.axis_size("seq")
    devices = dp_size * seq_size
    seq_index = lax.axis_index("seq")
    device = lax.axis_index("dp") * seq_size + seq_index
    own_rows = patch_weight.shape[0]
    own_hidden = down_weight.shape[0]
    own_images = images // seq_size
    all_images = dp_size * images
    pairs = 2 * HEADS
    table = small_rows[:POS]
    vectors = small_rows[POS:]

    gathered_late = lax.all_gather(
        jnp.concatenate([block_weight[:, 2 * D : 4 * D], heads_weight], 1).astype(low),
        ALL,
        axis=0,
        tiled=True,
    )
    gathered_query_key = lax.all_gather(
        lax.optimization_barrier((block_weight[:, : 2 * D].astype(low), gathered_late[:8, :128]))[0],
        ALL,
        axis=0,
        tiled=True,
    )

    tokens = vectors[1:3] + table[0:2]
    token_out, token_normed, token_inverse = norm_forward(tokens, vectors[3], vectors[4])
    token_low = token_out.astype(low)
    select_own = (
        lax.broadcasted_iota(jnp.int32, (own_rows, D), 0) + device * own_rows
        == lax.broadcasted_iota(jnp.int32, (own_rows, D), 1)
    ).astype(low)
    token_own = matmul_nt(token_low, select_own).astype(low)
    query_partial = matmul(token_own, block_weight[:, :D].astype(low))
    query = jnp.sum(gather_blocks(query_partial), 0) + vectors[5]
    query_low = query.astype(low)
    head_of = lax.broadcasted_iota(jnp.int32, (HEADS, D), 1) // HD
    head_mask = head_of == lax.broadcasted_iota(jnp.int32, (HEADS, D), 0)
    query_blocks = jnp.where(head_mask[None], query_low[:, None, :], 0).reshape(pairs, D)
    key_own = matmul_nt(block_weight[:, D : 2 * D].astype(low), query_blocks.astype(low)) * HD ** (
        -0.5
    )
    meta = jnp.concatenate(
        [
            (classes // 32),
            (classes % 32),
            mixing[:, None],
            image_weight[:, None],
            drop_keep,
        ],
        1,
    )
    meta_width = meta.shape[1]
    meta_columns = -(-images * meta_width // own_rows)
    meta = jnp.pad(meta.reshape(-1), (0, own_rows * meta_columns - images * meta_width))
    meta = meta.reshape(own_rows, meta_columns).astype(low)
    extra = -(-(pairs + meta_columns) // 128) * 128
    early = jnp.concatenate(
        [
            patch_weight.astype(low),
            key_own.astype(low),
            meta,
            jnp.zeros((own_rows, extra - pairs - meta_columns), low),
        ],
        1,
    )
    early = gather_blocks(early, "dp").reshape(dp_size, own_rows, D + extra)
    early = join_cores(early, seq_index, 1)
    metas = early[:, 0, :, D + pairs : D + pairs + meta_columns].astype(f32)
    metas = metas.reshape(dp_size, own_rows * meta_columns)[:, : images * meta_width]
    metas = metas.reshape(all_images, meta_width)
    early = early.reshape(D, D + extra)
    full_patch = early[:, :D]
    key_vectors = early[:, D : D + pairs]

    slot_global = seq_index * local_slots + lax.broadcasted_iota(jnp.int32, (1, local_slots, 1), 1)
    is_class = slot_global == 0
    is_distill = slot_global == 1
    special = is_class | is_distill
    key_mask = slot_global < valid[:, None, None]
    flat_patches = patches.reshape(row_count, patch_dim)
    onehot_pos = (
        pos_index.reshape(row_count)[:, None]
        == lax.broadcasted_iota(jnp.int32, (1, POS), 1)
    ).astype(low)
    table_high, table_rest = split_low(table)
    embedded = matmul(flat_patches, full_patch)
    positions = matmul(onehot_pos, table_high) + matmul(onehot_pos, table_rest)
    embedded = (embedded + positions + vectors[0]).reshape(images, local_slots, D)
    stream = jnp.where(is_class, tokens[0], jnp.where(is_distill, tokens[1], embedded))
    first_out, first_normed, first_inverse = norm_forward(stream, vectors[3], vectors[4])
    first_low = first_out.astype(low)
    flat_first = first_low.reshape(row_count, D)
    scores = matmul(flat_first, key_vectors).reshape(images, local_slots, pairs)
    scores = jnp.where(key_mask, scores, MASK_FILL)
    local_peak = jnp.max(scores, 1, keepdims=True)
    exponent = jnp.exp(scores - local_peak)
    local_total = jnp.sum(exponent, 1, keepdims=True)
    local_pooled = jnp.einsum(
        "nlm,nld->nmd", exponent.astype(low), first_low, preferred_element_type=f32
    )
    packed = jnp.concatenate(
        [
            local_pooled,
            jnp.broadcast_to(local_peak.transpose(0, 2, 1), (images, pairs, 64)),
            jnp.broadcast_to(local_total.transpose(0, 2, 1), (images, pairs, 64)),
        ],
        2,
    )
    other = swap_cores(packed)
    other_pooled = other[:, :, :D]
    peak_here = local_peak.transpose(0, 2, 1)
    peak_there = other[:, :, D : D + 1]
    peak = jnp.maximum(peak_here, peak_there)
    scale_here = jnp.exp(peak_here - peak)
    scale_there = jnp.exp(peak_there - peak)
    total = (
        scale_here * local_total.transpose(0, 2, 1) + scale_there * other[:, :, D + 64 : D + 65]
    )
    pooled = (scale_here * local_pooled + scale_there * other_pooled) / total
    probs = exponent * (scale_here / total).transpose(0, 2, 1)
    pooled_low = pooled.astype(low)
    own_pooled = lax.dynamic_slice_in_dim(pooled_low, seq_index * own_images, own_images, 0)

    up_blocks = (
        block_weight[:, 4 * D :]
        .astype(low)
        .reshape(own_rows, devices, own_hidden)
        .transpose(1, 0, 2)
        .reshape(devices, own_rows * own_hidden)
    )
    pooled_blocks = (
        own_pooled.reshape(own_images * pairs, devices, own_rows)
        .transpose(1, 0, 2)
        .reshape(devices, own_images * pairs * own_rows)
    )
    received = exchange(jnp.concatenate([up_blocks, pooled_blocks], 1))
    up_own = received[:, : own_rows * own_hidden].reshape(D, own_hidden)
    pooled_own = received[:, own_rows * own_hidden :].reshape(all_images, 2, HEADS, own_rows)

    full_value = gathered_late[:, :D]
    full_out = gathered_late[:, D : 2 * D]
    full_heads = gathered_late[:, 2 * D :]
    mixed = matmul(own_pooled.reshape(own_images * pairs, D), full_value)
    attended = jnp.sum(
        jnp.where(head_mask, mixed.reshape(own_images * 2, HEADS, D), 0.0), 1
    ) + vectors[6]
    attended = attended.astype(low)
    rows = all_images * 2
    attended = gather_blocks(attended).reshape(rows, D)
    keep_float = metas[:, 8:10] * DROP_SCALE
    keep_rows = jnp.repeat(keep_float, 2, axis=0)
    keep_first = keep_rows[:, 0:1]
    keep_second = keep_rows[:, 1:2]
    middle = jnp.tile(tokens, (all_images, 1)) + keep_first * (
        matmul(attended, full_out) + vectors[7]
    )
    second_out, second_normed, second_inverse = norm_forward(middle, vectors[8], vectors[9])
    second_low = second_out.astype(low)
    hidden_bias = lax.dynamic_slice_in_dim(small_long, device * own_hidden, own_hidden, 0)
    hidden = matmul(second_low, up_own) + hidden_bias
    activated, gelu_slope = gelu_parts(hidden)
    activated = activated.astype(low)
    down_low = down_weight.astype(low)
    mlp_partial = matmul(activated, down_low).astype(low)
    row_share = own_images * 2
    mlp_own = jnp.sum(
        exchange(mlp_partial.reshape(devices, row_share, D)).astype(f32), 0
    )
    mlp_rows = gather_blocks(mlp_own.astype(low)).reshape(rows, D).astype(f32)
    result = middle + keep_second * (mlp_rows + vectors[10])

    head_out, head_normed, head_inverse = norm_forward(result, vectors[11], vectors[12])
    head_low = head_out.astype(low).reshape(all_images, 2, D)
    logits_class = matmul(head_low[:, 0], full_heads[:, :CLS]) + small_long[FF : FF + CLS]
    logits_distill = matmul(head_low[:, 1], full_heads[:, CLS:]) + small_long[FF + CLS :]
    columns = lax.broadcasted_iota(jnp.int32, (1, CLS), 1)
    labels = (metas[:, 0:3] * 32.0 + metas[:, 3:6]).astype(jnp.int32)
    share = metas[:, 6:7] / 16.0
    weights = metas[:, 7]
    weight_sum = jnp.sum(weights)
    target = share * (labels[:, 0:1] == columns).astype(f32) + (1.0 - share) * (
        labels[:, 1:2] == columns
    ).astype(f32)
    teacher = (labels[:, 2:3] == columns).astype(f32)
    log_class = jax.nn.log_softmax(logits_class, -1)
    log_distill = jax.nn.log_softmax(logits_distill, -1)
    terms = -0.5 * (jnp.sum(target * log_class, -1) + jnp.sum(teacher * log_distill, -1))
    loss = jnp.sum(weights * terms) / weight_sum
    scale_rows = (weights * 0.5 / weight_sum)[:, None]
    grad_class = (scale_rows * (jnp.exp(log_class) - target)).astype(low)
    grad_distill = (scale_rows * (jnp.exp(log_distill) - teacher)).astype(low)
    head_own = matmul_nt(select_own, head_low.reshape(rows, D)).astype(low)
    head_own = head_own.reshape(own_rows, all_images, 2)
    owned_heads = jnp.concatenate(
        [matmul(head_own[:, :, 0], grad_class), matmul(head_own[:, :, 1], grad_distill)], 1
    )
    head_bias = jnp.concatenate(
        [jnp.sum(grad_class.astype(f32), 0), jnp.sum(grad_distill.astype(f32), 0)]
    )
    grad_head_rows = jnp.stack(
        [matmul_nt(grad_class, full_heads[:, :CLS]), matmul_nt(grad_distill, full_heads[:, CLS:])],
        1,
    ).reshape(rows, D)
    grad_result, final_gain, final_shift = norm_backward(
        grad_head_rows, head_normed, head_inverse, vectors[11]
    )

    grad_mlp = (keep_second * grad_result).astype(low)
    owned_down = matmul_tn(activated, grad_mlp)
    down_bias = jnp.sum(grad_mlp.astype(f32), 0)
    grad_hidden = (matmul_nt(grad_mlp, down_low) * gelu_slope).astype(low)
    up_bias = jnp.sum(grad_hidden.astype(f32), 0)
    grad_up = matmul_tn(second_low, grad_hidden).astype(low)
    grad_second_partial = matmul_nt(grad_hidden, up_own).astype(low)
    received = exchange(
        jnp.concatenate(
            [
                grad_second_partial.reshape(devices, row_share * D),
                grad_up.reshape(devices, own_rows * own_hidden),
            ],
            1,
        )
    )
    grad_second = jnp.sum(
        received[:, : row_share * D].astype(f32).reshape(devices, row_share, D), 0
    )
    owned_up = (
        received[:, row_share * D :]
        .reshape(devices, own_rows, own_hidden)
        .transpose(1, 0, 2)
        .reshape(own_rows, FF)
        .astype(f32)
    )
    row_start = device * row_share
    own_normed = lax.dynamic_slice_in_dim(second_normed, row_start, row_share, 0)
    own_inverse = lax.dynamic_slice_in_dim(second_inverse, row_start, row_share, 0)
    own_result = lax.dynamic_slice_in_dim(grad_result, row_start, row_share, 0)
    own_keep = lax.dynamic_slice_in_dim(keep_first, row_start, row_share, 0)
    grad_second_in, second_gain, second_shift = norm_backward(
        grad_second, own_normed, own_inverse, vectors[8]
    )
    grad_middle = own_result + grad_second_in
    grad_attn_own = (own_keep * grad_middle).astype(low)
    out_bias = jnp.sum(grad_attn_own.astype(f32), 0)
    grad_attn = join_cores(grad_attn_own, seq_index, 0).reshape(images * 2, D)
    grad_att = matmul_nt(grad_attn, full_out).astype(low)
    value_bias = jnp.sum(
        lax.dynamic_slice_in_dim(grad_att, seq_index * row_share, row_share, 0).astype(f32), 0
    )
    grad_att_blocks = jnp.where(
        head_mask, grad_att.reshape(images * 2, 1, D), jnp.zeros((), low)
    ).reshape(images * pairs, D)
    value_vectors = matmul_nt(grad_att_blocks, full_value).astype(low)
    value_const = jnp.sum(grad_att_blocks.astype(f32) * vectors[6], -1).reshape(images, pairs)
    value_vectors = value_vectors.reshape(images, pairs, D)
    mean_grad = jnp.sum(pooled * value_vectors.astype(f32), -1) + value_const
    grad_probs = (
        jnp.einsum("nld,nmd->nlm", first_low, value_vectors, preferred_element_type=f32)
        + value_const[:, None, :]
    )
    grad_scores = (probs * (grad_probs - mean_grad[:, None, :])).astype(low)
    key_rows = jnp.broadcast_to(key_vectors.T[None], (images, pairs, D))
    grad_first = jnp.einsum(
        "nlk,nkd->nld",
        jnp.concatenate([grad_scores, probs.astype(low)], 2),
        jnp.concatenate([key_rows, value_vectors], 1),
        preferred_element_type=f32,
    )
    grad_stream, first_gain, first_shift = norm_backward(
        grad_first, first_normed, first_inverse, vectors[3]
    )
    pooled_grad = matmul_tn(grad_scores.reshape(row_count, pairs), flat_first)
    query_grad_blocks = matmul(pooled_grad.astype(low), gathered_query_key[:, D:]) * HD ** (-0.5)
    grad_query = jnp.sum(
        jnp.where(head_mask, query_grad_blocks.reshape(2, HEADS, D), 0.0), 1
    )
    token_grad = matmul_nt(grad_query.astype(low), gathered_query_key[:, :D])
    token_grad_in, token_gain, token_shift = norm_backward(
        token_grad, token_normed, token_inverse, vectors[3]
    )
    grad_tokens = (
        token_grad_in
        + jnp.sum(grad_middle.reshape(own_images, 2, D), 0)
        + jnp.stack(
            [
                jnp.sum(jnp.where(is_class, grad_stream, 0.0), (0, 1)),
                jnp.sum(jnp.where(is_distill, grad_stream, 0.0), (0, 1)),
            ]
        )
    )
    grad_embed = jnp.where(special, 0.0, grad_stream)
    embed_low = grad_embed.astype(low).reshape(row_count, D)
    grad_patch = matmul_tn(flat_patches, embed_low)
    grad_table = matmul_tn(onehot_pos, embed_low)
    patch_bias = jnp.sum(grad_embed, (0, 1))
    leader = (device == 0).astype(f32)
    small_terms = jnp.concatenate(
        [
            grad_tokens,
            grad_table[2:],
            patch_bias[None],
            grad_tokens,
            (first_gain + token_gain)[None],
            (first_shift + token_shift)[None],
            jnp.sum(grad_query, 0)[None],
            value_bias[None],
            out_bias[None],
            second_gain[None],
            second_shift[None],
            leader * down_bias[None],
            leader * final_gain[None],
            leader * final_shift[None],
        ],
        0,
    )
    small_count = POS + 13
    small_share = -(-small_count // devices)
    small_terms = jnp.pad(small_terms, ((0, small_share * devices - small_count), (0, 0)))

    key_terms = (
        pooled_grad.reshape(pairs, devices, own_rows)
        .transpose(1, 0, 2)
        .reshape(devices, pairs * own_rows)
    )
    key_share = -(-pairs * own_rows // D)
    key_terms = jnp.pad(key_terms, ((0, 0), (0, key_share * D - pairs * own_rows)))
    terms_rows = jnp.concatenate(
        [
            grad_patch.reshape(dp_size, seq_size, own_rows, D),
            small_terms.reshape(dp_size, seq_size, small_share, D),
            key_terms.reshape(dp_size, seq_size, key_share, D),
            jnp.broadcast_to(grad_query, (dp_size, seq_size, 2, D)),
        ],
        2,
    )
    mine = lax.dynamic_index_in_dim(terms_rows, seq_index, 1, keepdims=False)
    theirs = lax.dynamic_index_in_dim(terms_rows, 1 - seq_index, 1, keepdims=False)
    chip_terms = mine + swap_cores(theirs.astype(low)).astype(f32)
    pair_share = 2 * row_share
    grad_att_own = lax.dynamic_slice_in_dim(grad_att, seq_index * row_share, row_share, 0)
    pair_own = jnp.concatenate([grad_attn_own, grad_att_own], 0)
    sent = jnp.concatenate(
        [chip_terms.astype(low), jnp.broadcast_to(pair_own, (dp_size, pair_share, D))], 1
    )
    received = exchange(sent, "dp")
    summed_share = chip_terms.shape[1]
    reduced = jnp.sum(received[:, :summed_share].astype(f32), 0)
    pair_rows = join_cores(received[:, summed_share:], seq_index, 1)
    pair_rows = pair_rows.reshape(devices, 2, row_share, D)
    owned_patch = reduced[:own_rows]
    owned_small = reduced[own_rows : own_rows + small_share]
    key_start = own_rows + small_share
    key_reduced = reduced[key_start : key_start + key_share].reshape(-1)[: pairs * own_rows]
    key_reduced = key_reduced.reshape(2, HEADS, own_rows)
    query_reduced = reduced[key_start + key_share :]

    owned_query = matmul_tn(token_own, query_reduced.astype(low))
    key_left = jnp.repeat(
        key_reduced.transpose(2, 0, 1), HD, axis=2
    )
    owned_key = jnp.sum(key_left * query_low.astype(f32)[None], 1) * HD ** (-0.5)
    grad_attn_rows = pair_rows[:, 0].reshape(rows, D)
    grad_att_rows = pair_rows[:, 1].reshape(all_images, 2, HEADS, HD)
    owned_value = jnp.einsum(
        "nihd,nihc->dhc", pooled_own, grad_att_rows, preferred_element_type=f32
    ).reshape(own_rows, D)
    attended_own = matmul_nt(select_own, attended).astype(low)
    owned_out = matmul(attended_own, grad_attn_rows)
    owned_block = jnp.concatenate([owned_query, owned_key, owned_value, owned_out, owned_up], 1)

    shard_square = (
        jnp.sum(owned_patch * owned_patch)
        + jnp.sum(owned_block * owned_block)
        + jnp.sum(owned_down * owned_down)
        + jnp.sum(owned_heads * owned_heads)
        + jnp.sum(owned_small * owned_small)
        + jnp.sum(up_bias * up_bias)
    )
    square_high, square_rest = split_low(shard_square)
    square_rest, square_last = split_low(shard_square - square_high.astype(f32))
    tail_row = jnp.concatenate(
        [
            jnp.stack([square_high, square_rest, square_last]),
            up_bias.astype(low),
            jnp.zeros((D - 3 - own_hidden,), low),
        ]
    )
    final = gather_blocks(
        jnp.concatenate([owned_small.astype(low), tail_row[None]], 0), "dp"
    ).reshape(dp_size, small_share + 1, D)
    final = join_cores(final, seq_index, 1).reshape(devices, small_share + 1, D)
    summed_rows = final[:, :small_share].astype(f32).reshape(devices * small_share, D)[:small_count]
    global_square = jnp.sum(final[:, small_share, 0:3].astype(f32))
    up_bias_all = final[:, small_share, 3 : 3 + own_hidden].astype(f32).reshape(FF)
    summed_long = jnp.concatenate([up_bias_all, head_bias])
    total_square = global_square + jnp.sum(head_bias * head_bias)
    grad_norm = jnp.sqrt(total_square)
    factor = jnp.minimum(1.0, CLIP_NORM / (grad_norm + 1e-06))
    vectors_grad = factor * summed_rows[POS:]
    patch_new, patch_mean_new, patch_square_new = adam_update(
        patch_weight, patch_mean, patch_square, owned_patch, factor, DECAY_RATE, LEARN_RATE
    )
    block_new, block_mean_new, block_square_new = adam_update(
        block_weight, block_mean, block_square, owned_block, factor, DECAY_RATE, LEARN_RATE
    )
    down_new, down_mean_new, down_square_new = adam_update(
        down_weight, down_mean, down_square, owned_down, factor, DECAY_RATE, LEARN_RATE
    )
    heads_new, heads_mean_new, heads_square_new = adam_update(
        heads_weight, heads_mean, heads_square, owned_heads, factor, DECAY_RATE, LEARN_RATE
    )
    rows_new, rows_mean_new, rows_square_new = adam_update(
        small_rows, rows_mean, rows_square, summed_rows, factor, 0.0, SMALL_RATE
    )
    long_new, long_mean_new, long_square_new = adam_update(
        small_long, long_mean, long_square, summed_long, factor, 0.0, SMALL_RATE
    )
    return (
        loss,
        grad_norm,
        patch_new,
        patch_mean_new,
        patch_square_new,
        block_new,
        block_mean_new,
        block_square_new,
        down_new,
        down_mean_new,
        down_square_new,
        heads_new,
        heads_mean_new,
        heads_square_new,
        rows_new,
        rows_mean_new,
        rows_square_new,
        long_new,
        long_mean_new,
        long_square_new,
        vectors_grad,
    )


def tiles(arguments):
    patches, patch_weight = arguments[0], arguments[7]
    images, local_slots, _ = patches.shape
    return images * PAIR == 128 and (images * local_slots) % CHUNK == 0 and patch_weight.shape[0] == 24


def shards(*arguments):
    return (shards_tiled if tiles(arguments) else shards_plain)(*arguments)


def solution(mesh):
    placed = (
        P("dp", "seq", None),
        P("dp", "seq"),
        P("dp"),
        P("dp", None),
        P("dp"),
        P("dp"),
        P("dp", None),
        P(("dp", "seq"), None),
        P(("dp", "seq"), None),
        P(("dp", "seq"), None),
        P(("dp", "seq"), None),
        P(("dp", "seq"), None),
        P(("dp", "seq"), None),
        P(("dp", "seq"), None),
        P(("dp", "seq"), None),
        P(("dp", "seq"), None),
        P(("dp", "seq"), None),
        P(("dp", "seq"), None),
        P(("dp", "seq"), None),
        P(),
        P(),
        P(),
        P(),
        P(),
        P(),
    )
    return jax.shard_map(
        shards,
        mesh=mesh,
        in_specs=placed,
        out_specs=(
            P(),
            P(),
            P(("dp", "seq"), None),
            P(("dp", "seq"), None),
            P(("dp", "seq"), None),
            P(("dp", "seq"), None),
            P(("dp", "seq"), None),
            P(("dp", "seq"), None),
            P(("dp", "seq"), None),
            P(("dp", "seq"), None),
            P(("dp", "seq"), None),
            P(("dp", "seq"), None),
            P(("dp", "seq"), None),
            P(("dp", "seq"), None),
            P(),
            P(),
            P(),
            P(),
            P(),
            P(),
            P(),
        ),
        check_vma=False,
    )
```

```python
import math

import jax
import jax.numpy as jnp
from jax import lax
from jax.experimental import pallas as pl
from jax.experimental.pallas import tpu as pltpu
from jax.sharding import PartitionSpec as P

D = 768
HEADS = 12
HD = 64
FF = 3072
CLS = 1000
POS = 198
STEP = 7


NORM_EPS = 1e-06
DROP_SCALE = 1.0 / 0.9
CLIP_NORM = 0.02
LEARN_RATE = 0.02
SMALL_RATE = 0.15
BETA_FIRST = 0.9
BETA_SECOND = 0.999
ADAM_EPS = 1e-08
DECAY_RATE = 0.05
MASK_FILL = -1e30
highest = lax.Precision.HIGHEST


def matmul(left, right):
    return jnp.dot(left, right, preferred_element_type=jnp.float32)


def matmul_tn(left, right):
    return lax.dot_general(
        left, right, (((0,), (0,)), ((), ())), preferred_element_type=jnp.float32
    )


def matmul_nt(left, right):
    return lax.dot_general(
        left, right, (((1,), (1,)), ((), ())), preferred_element_type=jnp.float32
    )


def norm_forward(values, gain, shift):
    centered = values - jnp.mean(values, -1, keepdims=True)
    inverse = lax.rsqrt(jnp.mean(centered * centered, -1, keepdims=True) + NORM_EPS)
    normed = centered * inverse
    return (normed * gain + shift, normed, inverse)


def norm_backward(grad_out, normed, inverse, gain):
    scaled = grad_out * gain
    grad_in = inverse * (
        scaled
        - jnp.mean(scaled, -1, keepdims=True)
        - normed * jnp.mean(scaled * normed, -1, keepdims=True)
    )
    leading = tuple(range(grad_out.ndim - 1))
    return (grad_in, jnp.sum(grad_out * normed, leading), jnp.sum(grad_out, leading))


def gelu_parts(values):
    cumulative = 0.5 * (1.0 + jax.scipy.special.erf(values * 0.7071067811865476))
    density = 0.3989422804014327 * jnp.exp(-0.5 * values * values)
    return (values * cumulative, cumulative + values * density)


def adam_update(weight, first, second, gradient, factor, decay, rate):
    clipped = gradient * factor
    first_new = BETA_FIRST * first + (1.0 - BETA_FIRST) * clipped
    second_new = BETA_SECOND * second + (1.0 - BETA_SECOND) * clipped * clipped
    first_hat = first_new / (1.0 - BETA_FIRST**STEP)
    second_hat = second_new / (1.0 - BETA_SECOND**STEP)
    weight_new = weight - rate * (first_hat / (jnp.sqrt(second_hat) + ADAM_EPS) + decay * weight)
    return (weight_new, first_new, second_new)


ALL = ("dp", "seq")


def exchange(blocks, axes=ALL):
    return lax.all_to_all(blocks, axes, 0, 0, tiled=True)


def gather_blocks(block, axes=ALL):
    count = lax.axis_size(axes)
    return exchange(jnp.broadcast_to(block[None], (count,) + block.shape), axes)


def swap_cores(value):
    return lax.ppermute(value, "seq", [(0, 1), (1, 0)])


def join_cores(value, seq_index, axis):
    other = swap_cores(value)
    first = jnp.where(seq_index == 0, value, other)
    second = jnp.where(seq_index == 0, other, value)
    return jnp.stack([first, second], axis)


def split_low(value):
    high = value.astype(jnp.bfloat16)
    rest = (value - high.astype(jnp.float32)).astype(jnp.bfloat16)
    return high, rest


PADDED = 16
PAIR = 2 * PADDED
CHUNK = 112


class Fetched:
    def __init__(self, value, source, semaphore, columns):
        if columns is not None:
            source = source.at[(slice(None),) * (len(source.shape) - 1) + (columns,)]
        self.copy = pltpu.make_async_copy(source, value, semaphore)
        self.value = value
        self.copy.start()
        self.waiting = True

    def ready(self):
        if self.waiting:
            self.copy.wait()
            self.waiting = False

    @property
    def shape(self):
        return self.value.shape

    @property
    def dtype(self):
        return self.value.dtype

    def __getitem__(self, index):
        self.ready()
        return self.value[index]


class Stored:
    def __init__(self, value, out, semaphore):
        self.copy = pltpu.make_async_copy(value, out, semaphore)
        self.value = value
        self.sent = False

    def send(self):
        if not self.sent:
            self.copy.start()
            self.sent = True

    @property
    def shape(self):
        return self.value.shape

    @property
    def dtype(self):
        return self.value.dtype

    def __getitem__(self, index):
        return self.value[index]

    def __setitem__(self, index, value):
        self.value[index] = value


def ready(*operands):
    for operand in operands:
        operand.ready()


def kernel_call(body, outputs, inputs, windows=None, scratch=(), flops=1_000_000, limit=48, loose=()):
    windows = windows or {}
    places, buffers = [], []
    moved = 0
    for position, value in enumerate(inputs):
        if value.ndim == 1:
            places.append(pl.BlockSpec(memory_space=pltpu.SMEM))
            continue
        places.append(pl.BlockSpec(memory_space=pltpu.HBM))
        shape = value.shape
        if position in windows:
            shape = shape[:-1] + (windows[position].stop - windows[position].start,)
        buffers.append(pltpu.VMEM(shape, value.dtype))
        moved += math.prod(shape) * value.dtype.itemsize
    moved += sum(math.prod(shape) * jnp.dtype(kind).itemsize for shape, kind in outputs)
    fetches = len(buffers)
    buffers += [pltpu.VMEM(shape, kind) for shape, kind in outputs]
    buffers += [pltpu.SemaphoreType.DMA((fetches + len(outputs),))]

    def run(*refs):
        ins, refs = refs[: len(inputs)], refs[len(inputs) :]
        outs, refs = refs[: len(outputs)], refs[len(outputs) :]
        stores, copies, semaphores = refs[fetches:][: len(outputs)], refs[:fetches], None
        semaphores = refs[fetches + len(outputs)]
        rest = refs[fetches + len(outputs) + 1 :]
        operands, used = [], 0
        for position, (value, ref) in enumerate(zip(inputs, ins)):
            if value.ndim == 1:
                operands.append(ref)
                continue
            operands.append(
                Fetched(copies[used], ref, semaphores.at[used], windows.get(position))
            )
            used += 1
        stores = [
            Stored(store, out, semaphores.at[fetches + index])
            for index, (store, out) in enumerate(zip(stores, outs))
        ]
        body(*operands, *stores, *rest)
        ready(*[operand for operand in operands if isinstance(operand, Fetched)])
        for store in stores:
            store.send()
        for store in stores:
            store.copy.wait()

    return pl.pallas_call(
        run,
        name=body.__name__,
        in_specs=places,
        out_specs=[pl.BlockSpec(memory_space=pltpu.HBM) for _ in outputs],
        out_shape=[pltpu.HBM(shape, kind) for shape, kind in outputs],
        scratch_shapes=buffers + list(scratch),
        cost_estimate=pl.CostEstimate(flops=flops, bytes_accessed=moved, transcendentals=0),
        compiler_params=pltpu.CompilerParams(vmem_limit_bytes=limit * 1024 * 1024),
    )(
        *[
            value
            if value.ndim == 1 or position in loose
            else pltpu.with_memory_space_constraint(value, pltpu.HBM)
            for position, value in enumerate(inputs)
        ]
    )


def iota(shape, axis):
    return lax.broadcasted_iota(jnp.int32, shape, axis)


def own_selector(device, count):
    return jnp.where(
        iota((count, D), 0) + device * count == iota((count, D), 1), 1.0, 0.0
    ).astype(jnp.bfloat16)


def pair_mask(rows):
    return (iota((rows, D), 0) & (PADDED - 1)) == (iota((rows, D), 1) >> 6)


def token_rows(small_ref):
    tokens = small_ref[POS + 1 : POS + 3, :] + small_ref[0:2, :]
    return jnp.concatenate([tokens, jnp.zeros((6, D), jnp.float32)], 0)


def vector(small_ref, index):
    return small_ref[POS + index : POS + index + 1, :]


def norm_in(grad_out, normed, inverse, gain):
    scaled = grad_out * gain
    return inverse * (
        scaled
        - jnp.mean(scaled, -1, keepdims=True)
        - normed * jnp.mean(scaled * normed, -1, keepdims=True)
    )


def spread_pairs(values):
    count = values.shape[0]
    spread = jnp.broadcast_to(values[:, None, :], (count, PADDED, D)).reshape(count * PADDED, D)
    return jnp.where(pair_mask(count * PADDED), spread, 0.0)


def collect_pairs(values):
    count = values.shape[0] // PADDED
    kept = jnp.where(pair_mask(values.shape[0]), values, 0.0)
    return jnp.sum(kept.reshape(count, PADDED, D), 1)


def prepare_kernel(
    device_ref, small_ref, query_weight_ref, value_out_ref, patch_ref, first_ref, late_ref
):
    low = jnp.bfloat16
    own = patch_ref.shape[0]
    late_ref[...] = value_out_ref[...].astype(low)
    query_weight = query_weight_ref[...].astype(low)
    token_out, _, _ = norm_forward(token_rows(small_ref), vector(small_ref, 3), vector(small_ref, 4))
    token_own = matmul_nt(token_out.astype(low), own_selector(device_ref[0], own))
    partial = matmul(token_own.astype(low), query_weight)
    high, rest = split_low(partial)
    pieces = [
        part[i : i + 1, 128 * j : 128 * (j + 1)].astype(jnp.float32)
        for part in (high, rest)
        for i in range(2)
        for j in range(D // 128)
    ]
    block = jnp.concatenate(
        [patch_ref[...], jnp.concatenate(pieces, 0)], 1
    ).astype(low)
    first_ref[...] = jnp.broadcast_to(block[None], first_ref.shape)


def query_kernel(
    own_ref, other_ref, key_weight_ref, up_ref, small_ref, meta_ref, heads_ref,
    out_ref, query_ref, late_ref,
):
    total = jnp.sum(own_ref[...].astype(jnp.float32), 0) + jnp.sum(
        other_ref[...].astype(jnp.float32), 0
    )
    count = D // 128
    both = total[0 : 2 * count] + total[2 * count :]
    query = jnp.concatenate(
        [
            jnp.concatenate([both[i * count + j : i * count + j + 1] for j in range(count)], 1)
            for i in range(2)
        ],
        0,
    ) + vector(small_ref, 5)
    query = query.astype(jnp.bfloat16).astype(jnp.float32)
    blocks = spread_pairs(jnp.concatenate([query] * 4, 0))
    query_ref[...] = blocks[:PAIR]
    keys = matmul_nt(key_weight_ref[...].astype(jnp.bfloat16), blocks.astype(jnp.bfloat16))
    keys = keys * HD ** (-0.5)
    low = jnp.bfloat16
    late_ref[...] = jnp.zeros(late_ref.shape, low)
    late_ref[:, 0:CLS] = heads_ref[:, 0:CLS].astype(low)
    late_ref[:, 1024 : 1024 + CLS] = heads_ref[:, CLS:].astype(low)
    up = up_ref[...]
    width = up.shape[1] // out_ref.shape[0]
    for block in range(out_ref.shape[0]):
        out_ref[block] = jnp.concatenate(
            [keys, up[:, block * width : (block + 1) * width], meta_ref[...]], 1
        ).astype(jnp.bfloat16)


def row_ids(start, rows, images, local_slots, seq_index):
    ids = iota((rows, 1), 0) + start
    shift = images.bit_length() - 1
    return ids & (images - 1), (ids >> shift) + seq_index * local_slots


def join_weights(seq_index, own_ref, other_ref, weights):
    count = own_ref.shape[1]
    first_core = seq_index == 0
    for block in range(own_ref.shape[0]):
        here = own_ref[block].astype(jnp.float32)
        there = other_ref[block].astype(jnp.float32)
        start = block * 2 * count
        weights[start : start + count, :] = jnp.where(first_core, here, there).astype(jnp.bfloat16)
        weights[start + count : start + 2 * count, :] = jnp.where(first_core, there, here).astype(
            jnp.bfloat16
        )


def embed_kernel(
    seq_ref, own_ref, other_ref, patches_ref, pos_ref, small_ref,
    first_ref, normed_ref, inverse_ref, weights, high, rest,
):
    row_count = patches_ref.shape[0]
    images = 128 // PAIR
    local_slots = row_count // images
    seq_index = seq_ref[0]
    join_weights(seq_index, own_ref, other_ref, weights)
    tokens = token_rows(small_ref)
    table_high, table_rest = split_low(small_ref[0:POS, :])
    high[...] = table_high
    rest[...] = table_rest
    ready(patches_ref, pos_ref, small_ref)

    def step(index, carry):
        rows = pl.ds(pl.multiple_of(index * CHUNK, CHUNK), CHUNK)
        onehot = jnp.where(pos_ref[rows, :] == iota((CHUNK, POS), 1), 1.0, 0.0).astype(jnp.bfloat16)
        embedded = (
            matmul(patches_ref[rows, :], weights[...])
            + matmul(onehot, high[...])
            + matmul(onehot, rest[...])
            + vector(small_ref, 0)
        )
        _, slot = row_ids(index * CHUNK, CHUNK, images, local_slots, seq_index)
        stream = jnp.where(slot == 0, tokens[0:1], jnp.where(slot == 1, tokens[1:2], embedded))
        out, normed, inverse = norm_forward(stream, vector(small_ref, 3), vector(small_ref, 4))
        first_ref[rows, :] = out.astype(jnp.bfloat16)
        normed_ref[rows, :] = normed
        inverse_ref[rows, :] = inverse
        return carry

    lax.fori_loop(0, row_count // CHUNK, step, 0)


def scores_kernel(
    seq_ref, own_ref, other_ref, first_ref, valid_ref, query_weight_ref,
    packed_ref, exponent_ref, keys_ref, up_ref, late_ref,
):
    late_ref[...] = query_weight_ref[...].astype(jnp.bfloat16)
    row_count, columns = exponent_ref.shape
    images = columns // PAIR
    seq_index = seq_ref[0]
    first_core = seq_index == 0
    count = own_ref.shape[1]
    hidden = up_ref.shape[1]
    for block in range(own_ref.shape[0]):
        here = own_ref[block].astype(jnp.float32)
        there = other_ref[block].astype(jnp.float32)
        start = block * 2 * count
        for core, pick in enumerate(
            (jnp.where(first_core, here, there), jnp.where(first_core, there, here))
        ):
            place = slice(start + core * count, start + (core + 1) * count)
            keys_ref[place, :] = pick[:, 0:columns].astype(jnp.bfloat16)
            up_ref[place, :] = jnp.where(
                first_core,
                pick[:, columns : columns + hidden],
                pick[:, columns + hidden : columns + 2 * hidden],
            ).astype(jnp.bfloat16)
    scores = matmul(first_ref[...], keys_ref[...])
    image, slot = row_ids(0, row_count, images, row_count // images, seq_index)
    kept = ((iota((row_count, columns), 1) >> 5) == image) & (slot < valid_ref[...])
    scores = jnp.where(kept, scores, MASK_FILL)
    peak = jnp.max(scores, 0, keepdims=True)
    exponent = jnp.exp(scores - peak)
    exponent_ref[...] = exponent
    packed_ref[0:columns, :] = matmul_tn(exponent.astype(jnp.bfloat16), first_ref[...])
    packed_ref[columns : columns + 8, :] = jnp.zeros((8, D), jnp.float32)
    packed_ref[columns : columns + 1, 0:columns] = peak
    packed_ref[columns + 1 : columns + 2, 0:columns] = jnp.sum(exponent, 0, keepdims=True)


def attend_kernel(
    seq_ref, own_ref, other_ref, value_weight_ref, small_ref, pooled_ref, scale_ref, out_ref, turned
):
    columns = pooled_ref.shape[0]
    peak_here = own_ref[columns : columns + 1, 0:columns]
    peak_there = other_ref[columns : columns + 1, 0:columns]
    peak = jnp.maximum(peak_here, peak_there)
    here = jnp.exp(peak_here - peak)
    there = jnp.exp(peak_there - peak)
    total = (
        here * own_ref[columns + 1 : columns + 2, 0:columns]
        + there * other_ref[columns + 1 : columns + 2, 0:columns]
    )
    here = here / total
    there = there / total
    scale_ref[...] = jnp.broadcast_to(here, (8, columns))
    here_rows = jnp.broadcast_to(here, (columns, columns)).T[:, 0:1]
    there_rows = jnp.broadcast_to(there, (columns, columns)).T[:, 0:1]
    pooled = own_ref[0:columns, :] * here_rows + other_ref[0:columns, :] * there_rows
    pooled_ref[...] = pooled
    mixed = matmul(pooled.astype(jnp.bfloat16), value_weight_ref[...])
    attended = collect_pairs(mixed) + vector(small_ref, 6)
    turned[...] = pooled.T
    own = 2 * HEADS
    for block in range(out_ref.shape[0]):
        start = pl.multiple_of(block * 2 * own + seq_ref[0] * own, 8)
        mine = turned[pl.ds(start, own), :]
        pieces = [mine[8 * j : 8 * (j + 1)] for j in range(own // 8)]
        out_ref[block] = jnp.concatenate([attended] + pieces, 1).astype(jnp.bfloat16)


def odd_row(shape):
    return (iota(shape, 0) & 1) == 1


def mlp_kernel(
    device_ref, attended_ref, out_weight_ref, up_ref, down_ref, small_ref, info_ref, bias_ref,
    partial_ref, second_ref, normed_ref, inverse_ref, slope_ref, act_ref, middle_ref, turned_ref,
):
    attended = attended_ref[...].astype(jnp.float32)
    attended = attended.reshape(info_ref.shape[0], D).astype(jnp.bfloat16)
    own = turned_ref.shape[0]
    turned_ref[...] = matmul_nt(own_selector(device_ref[0], own), attended).astype(jnp.bfloat16)
    tokens = token_rows(small_ref)
    stream = jnp.where(odd_row(attended.shape), tokens[1:2], tokens[0:1])
    middle = stream + info_ref[:, 5:6] * (
        matmul(attended, out_weight_ref[...]) + vector(small_ref, 7)
    )
    middle_ref[...] = middle
    out, normed, inverse = norm_forward(middle, vector(small_ref, 8), vector(small_ref, 9))
    second = out.astype(jnp.bfloat16)
    second_ref[...] = second
    normed_ref[...] = normed
    inverse_ref[...] = inverse
    hidden = matmul(second, up_ref[...]) + bias_ref[...]
    act, slope = gelu_parts(hidden)
    act = act.astype(jnp.bfloat16)
    act_ref[...] = act
    slope_ref[...] = slope
    partial_ref[...] = matmul(act, down_ref[...].astype(jnp.bfloat16)).astype(jnp.bfloat16)


def heads_kernel(
    device_ref, mlp_ref, middle_ref, info_ref, small_ref,
    late_ref, bias_ref,
    act_ref, slope_ref, second_ref, up_ref, down_ref,
    partial_ref, result_ref, heads_ref, sums_ref, bias_out_ref, down_out_ref, up_bias_ref, loss_ref,
):
    rows = mlp_ref.shape[0]
    half = 512
    low = jnp.bfloat16
    result = middle_ref[...] + info_ref[:, 6:7] * (
        mlp_ref[...].astype(jnp.float32) + vector(small_ref, 10)
    )
    out, normed, inverse = norm_forward(result, vector(small_ref, 11), vector(small_ref, 12))
    head = out.astype(low)
    columns = iota((rows, half), 1)
    odd = odd_row((rows, half))
    left, right, share_a, share_b = (info_ref[:, k : k + 1] for k in range(4))
    weight = info_ref[:, 4:5]
    logits, targets = [], []
    for part in range(2):
        start = part * half
        class_columns = slice(start, start + half)
        distill_columns = slice(1024 + start, 1024 + start + half)
        piece = jnp.where(
            odd,
            matmul(head, late_ref[:, distill_columns]) + bias_ref[1:2, start : start + half],
            matmul(head, late_ref[:, class_columns]) + bias_ref[0:1, start : start + half],
        )
        where = (columns + start).astype(jnp.float32)
        logits.append(jnp.where(columns + start < CLS, piece, MASK_FILL))
        targets.append(
            share_a * jnp.where(where == left, 1.0, 0.0)
            + share_b * jnp.where(where == right, 1.0, 0.0)
        )
    peak = jnp.maximum(
        jnp.max(logits[0], -1, keepdims=True), jnp.max(logits[1], -1, keepdims=True)
    )
    exponents = [jnp.exp(piece - peak) for piece in logits]
    total = jnp.sum(exponents[0], -1, keepdims=True) + jnp.sum(exponents[1], -1, keepdims=True)
    log_total = peak + jnp.log(total)
    weight_sum = 0.5 * jnp.sum(weight, 0, keepdims=True)
    terms = jnp.zeros((rows, 1), jnp.float32)
    for piece, target in zip(logits, targets):
        terms = terms - 0.5 * jnp.sum(
            target * (piece - log_total), -1, keepdims=True
        )
    loss = jnp.sum(weight * terms, 0, keepdims=True) / weight_sum
    loss_ref[...] = jnp.broadcast_to(loss, loss_ref.shape)
    scale = weight * 0.5 / weight_sum
    head_own = matmul_nt(own_selector(device_ref[0], heads_ref.shape[1]), head).astype(low)
    grad_head = jnp.zeros((rows, D), jnp.float32)
    for part in range(2):
        start = part * half
        class_columns = slice(start, start + half)
        distill_columns = slice(1024 + start, 1024 + start + half)
        grad = scale * (exponents[part] / total - targets[part])
        grad = grad.astype(low).astype(jnp.float32)
        for side, weight_columns in ((0, class_columns), (1, distill_columns)):
            mine = jnp.where(odd == (side == 1), grad, 0.0)
            bias_out_ref[side : side + 1, start : start + half] = jnp.sum(mine, 0, keepdims=True)
            mine = mine.astype(low)
            heads_ref[side, :, start : start + half] = matmul(head_own, mine)
            grad_head = grad_head + matmul_nt(mine, late_ref[:, weight_columns])
    grad_result = norm_in(grad_head, normed, inverse, vector(small_ref, 11))
    result_ref[...] = grad_result
    grad_mlp = (info_ref[:, 6:7] * grad_result).astype(low)
    sums_ref[...] = jnp.zeros(sums_ref.shape, jnp.float32)
    sums_ref[0:1, :] = jnp.sum(grad_mlp.astype(jnp.float32), 0, keepdims=True)
    sums_ref[1:2, :] = jnp.sum(grad_head * normed, 0, keepdims=True)
    sums_ref[2:3, :] = jnp.sum(grad_head, 0, keepdims=True)
    down_out_ref[...] = matmul_tn(act_ref[...], grad_mlp)
    grad_hidden = (
        matmul_nt(grad_mlp, down_ref[...].astype(low)) * slope_ref[...]
    ).astype(low)
    up_bias_ref[...] = jnp.broadcast_to(
        jnp.sum(grad_hidden.astype(jnp.float32), 0, keepdims=True), up_bias_ref.shape
    )
    partial = matmul_nt(grad_hidden, up_ref[...])
    grad_up = matmul_tn(second_ref[...], grad_hidden)
    blocks = partial_ref.shape[0]
    per = rows // blocks
    own = D // blocks
    hidden = grad_up.shape[1]
    pad = jnp.zeros((D, 128 - hidden), jnp.float32)
    grad_up = jnp.concatenate([grad_up, pad], 1)
    for block in range(blocks):
        partial_ref[block, 0:per, :] = partial[block * per : (block + 1) * per].astype(low)
        pieces = [
            grad_up[block * own + 8 * j : block * own + 8 * (j + 1)] for j in range(own // 8)
        ]
        partial_ref[block, per : 2 * per, :] = jnp.concatenate(pieces, 1).astype(low)


def back_kernel(
    index_ref, second_ref, other_ref, normed2_ref, inverse2_ref, result_ref, info_ref, small_ref,
    out_weight_ref, value_weight_ref,
    pooled_ref, scale_ref, exponent_ref, first_ref, normed_ref, inverse_ref, keys_ref,
    patches_ref, pos_ref, sums_ref,
    mine_ref, theirs_ref,
    values, turned_keys, embed, scores, onehot, patch_out, small_out, pooled_grad,
):
    low = jnp.bfloat16
    columns = pooled_ref.shape[0]
    images = columns // PAIR
    row_count = patches_ref.shape[0]
    local_slots = row_count // images
    dp_index, seq_index = index_ref[0], index_ref[1]
    per = 2 * images
    own_rows = pl.ds(pl.multiple_of(dp_index * per, 8), per)
    grad_second = second_ref[...] + other_ref[...]
    normed2 = normed2_ref[own_rows, :]
    grad_middle = result_ref[own_rows, :] + norm_in(
        grad_second, normed2, inverse2_ref[own_rows, :], vector(small_ref, 8)
    )
    grad_attn = (info_ref[own_rows, 5:6] * grad_middle).astype(low)
    grad_att = matmul_nt(grad_attn, out_weight_ref[...]).astype(low)
    att_float = grad_att.astype(jnp.float32)
    att_blocks = spread_pairs(att_float)
    value_rows = matmul_nt(att_blocks.astype(low), value_weight_ref[...]).astype(low)
    values[...] = value_rows
    turned_keys[...] = keys_ref[...].astype(jnp.float32).T.astype(low)
    const = jnp.sum(att_blocks * vector(small_ref, 6), -1, keepdims=True)
    mean = jnp.sum(pooled_ref[...] * value_rows.astype(jnp.float32), -1, keepdims=True) + const
    const = jnp.broadcast_to(const, (columns, columns)).T[0:1, :]
    mean = jnp.broadcast_to(mean, (columns, columns)).T[0:1, :]
    gain = vector(small_ref, 3)

    ready(scale_ref, exponent_ref, first_ref, normed_ref, inverse_ref, pos_ref, patches_ref)

    def step(index, sums):
        gain_sum, shift_sum, embed_sum, class_sum, distill_sum = sums
        rows = pl.ds(pl.multiple_of(index * CHUNK, CHUNK), CHUNK)
        first = first_ref[rows, :]
        probs = exponent_ref[rows, :] * scale_ref[0:1, :]
        grad_probs = matmul_nt(first, values[...]) + const
        grad_scores = (probs * (grad_probs - mean)).astype(low)
        scores[rows, :] = grad_scores
        grad_first = matmul(grad_scores, turned_keys[...]) + matmul(probs.astype(low), values[...])
        normed = normed_ref[rows, :]
        grad_stream = norm_in(grad_first, normed, inverse_ref[rows, :], gain)
        _, slot = row_ids(index * CHUNK, CHUNK, images, local_slots, seq_index)
        grad_embed = jnp.where(slot < 2, 0.0, grad_stream)
        embed[rows, :] = grad_embed.astype(low)
        onehot[rows, :] = jnp.where(pos_ref[rows, :] == iota((CHUNK, POS), 1), 1.0, 0.0).astype(low)
        return (
            gain_sum + jnp.sum(grad_first * normed, 0, keepdims=True),
            shift_sum + jnp.sum(grad_first, 0, keepdims=True),
            embed_sum + jnp.sum(grad_embed, 0, keepdims=True),
            class_sum + jnp.sum(jnp.where(slot == 0, grad_stream, 0.0), 0, keepdims=True),
            distill_sum + jnp.sum(jnp.where(slot == 1, grad_stream, 0.0), 0, keepdims=True),
        )

    zero = jnp.zeros((1, D), jnp.float32)
    gain_sum, shift_sum, embed_sum, class_sum, distill_sum = lax.fori_loop(
        0, row_count // CHUNK, step, (zero,) * 5
    )
    patch_out[...] = matmul_tn(patches_ref[...], embed[...])
    small_out[0:POS, :] = matmul_tn(onehot[...], embed[...])
    by_column = matmul_tn(scores[...], first_ref[...])
    by_pair = jnp.sum(by_column.reshape(images, PAIR, D), 0)
    once = jnp.where(seq_index == 0, 1.0, 0.0)
    leader = jnp.where((dp_index == 0) & (seq_index == 0), 1.0, 0.0)
    middle_even = jnp.sum(jnp.where(odd_row((per, D)), 0.0, grad_middle), 0, keepdims=True)
    middle_odd = jnp.sum(jnp.where(odd_row((per, D)), grad_middle, 0.0), 0, keepdims=True)
    class_sum = class_sum + once * middle_even
    distill_sum = distill_sum + once * middle_odd
    small_out[0:1, :] = class_sum
    small_out[1:2, :] = distill_sum
    vector_rows = (
        embed_sum,
        class_sum,
        distill_sum,
        gain_sum,
        shift_sum,
        zero,
        once * jnp.sum(att_float, 0, keepdims=True),
        once * jnp.sum(grad_attn.astype(jnp.float32), 0, keepdims=True),
        once * jnp.sum(grad_second * normed2, 0, keepdims=True),
        once * jnp.sum(grad_second, 0, keepdims=True),
        leader * sums_ref[0:1, :],
        leader * sums_ref[1:2, :],
        leader * sums_ref[2:3, :],
    )
    for index, row in enumerate(vector_rows):
        small_out[POS + index : POS + index + 1, :] = row
    small_count = small_out.shape[0]
    small_out[POS + 13 : small_count, :] = jnp.zeros((small_count - POS - 13, D), jnp.float32)
    pooled_grad[...] = jnp.concatenate([by_pair, jnp.zeros((128 - PAIR, D), jnp.float32)], 0).T
    own = 2 * HEADS
    attn_half = jnp.where(
        seq_index == 0,
        grad_attn[:, : D // 2].astype(jnp.float32),
        grad_attn[:, D // 2 :].astype(jnp.float32),
    )
    share = small_count // (2 * mine_ref.shape[0])
    for block in range(mine_ref.shape[0]):
        for ref, core in ((mine_ref, seq_index), (theirs_ref, 1 - seq_index)):
            start = pl.multiple_of((block * 2 + core) * own, 8)
            ref[block, 0:own, :] = patch_out[pl.ds(start, own), :].astype(ref.dtype)
            small = pl.multiple_of((block * 2 + core) * share, 8)
            ref[block, own : own + share, :] = small_out[pl.ds(small, share), :].astype(ref.dtype)
            keys = pooled_grad[pl.ds(start, own), :]
            pieces = [keys[8 * j : 8 * (j + 1)] for j in range(own // 8)]
            if ref is mine_ref:
                pieces.append(attn_half)
            else:
                pieces.append(jnp.zeros((8, D // 2), jnp.float32))
            ref[block, own + share :, :] = jnp.concatenate(pieces, 1).astype(ref.dtype)


def known_kernel(
    index_ref, up_own_ref, up_other_ref, heads_ref, down_ref, up_bias_ref, up_ref, known_ref
):
    first_core = index_ref[1] == 0
    blocks = up_own_ref.shape[0]
    own = up_ref.shape[0]
    hidden = down_ref.shape[0]
    columns = []
    for block in range(blocks):
        mine = up_own_ref[block].astype(jnp.float32)
        theirs = up_other_ref[block].astype(jnp.float32)
        for pick in (jnp.where(first_core, mine, theirs), jnp.where(first_core, theirs, mine)):
            columns.append(
                jnp.concatenate(
                    [pick[:, 128 * j : 128 * j + hidden] for j in range(own // 8)], 0
                )
            )
    part = jnp.concatenate(columns, 1)
    up_ref[...] = part
    square = jnp.sum(part * part)
    for side in range(2):
        square = square + jnp.sum(heads_ref[side] * heads_ref[side])
    square = square + jnp.sum(down_ref[...] * down_ref[...])
    bias = up_bias_ref[0:1, :]
    known_ref[...] = jnp.broadcast_to(square + jnp.sum(bias * bias), known_ref.shape)


def owned_kernel(
    index_ref, received_ref, other_attn_ref, out_weight_ref, pooled_ref, turned_ref,
    query_ref, key_weight_ref, known_ref, up_bias_ref,
    patch_ref, block_ref, final_ref,
):
    low = jnp.bfloat16
    first_core = index_ref[1] == 0
    blocks = received_ref.shape[0]
    own = patch_ref.shape[0]
    share = final_ref.shape[1]
    half = D // 2
    total = jnp.sum(received_ref[:, :, :half].astype(jnp.float32), 0)
    right = jnp.sum(received_ref[:, : own + share, half:].astype(jnp.float32), 0)
    patch = jnp.concatenate([total[0:own], right[0:own]], 1)
    small = jnp.concatenate([total[own : own + share], right[own : own + share]], 1)
    keys = jnp.concatenate(
        [total[own + share :, 128 * j : 128 * (j + 1)] for j in range(own // 8)], 0
    )
    patch_ref[...] = patch
    row = iota((share, 1), 0) + index_ref[0] * share
    open_row = (row < 2) | ((row > POS) & (row < POS + 6))
    square = jnp.sum(patch * patch) + jnp.sum(jnp.where(open_row, 0.0, small * small))
    key_high, key_rest = split_low(keys[:, 0:PAIR])
    query_blocks = query_ref[...].astype(low)
    part = (matmul(key_high, query_blocks) + matmul(key_rest, query_blocks)) * HD ** (-0.5)
    block_ref[:, 0:D] = part
    square = square + jnp.sum(part * part)
    key_weight = key_weight_ref[...].astype(low)
    query_sums = collect_pairs(
        matmul_tn(key_high, key_weight) + matmul_tn(key_rest, key_weight)
    ) * HD ** (-0.5)
    here = received_ref[:, own + share :, half:].astype(jnp.float32).reshape(blocks * 8, half)
    there = other_attn_ref[...].astype(jnp.float32).reshape(blocks * 8, half)
    attn = jnp.concatenate(
        [jnp.where(first_core, here, there), jnp.where(first_core, there, here)], 1
    ).astype(low)
    att = matmul_nt(attn, out_weight_ref[...]).astype(low).astype(jnp.float32)
    part = jnp.zeros((own, D), jnp.float32)
    for block in range(blocks):
        spread = spread_pairs(att[block * 8 : (block + 1) * 8]).astype(low)
        turned = pooled_ref[block].astype(jnp.float32)
        turned = jnp.concatenate([turned[:, 128 * j : 128 * (j + 1)] for j in range(own // 8)], 0)
        part = part + matmul(turned.astype(low), spread)
    block_ref[:, D : 2 * D] = part
    square = square + jnp.sum(part * part)
    part = matmul(turned_ref[...], attn)
    block_ref[:, 2 * D : 3 * D] = part
    square = square + jnp.sum(part * part)
    hidden = up_bias_ref.shape[1]
    bias = up_bias_ref[0:1, :]
    square = known_ref[0:1, :] + jnp.broadcast_to(square, (1, 128))
    high, rest = split_low(square)
    middle, last = split_low(square - high.astype(jnp.float32))
    side = jnp.concatenate(
        [
            high.astype(jnp.float32),
            middle.astype(jnp.float32),
            last.astype(jnp.float32),
            jnp.concatenate([bias, jnp.zeros((1, 128 - hidden), jnp.float32)], 1),
            jnp.zeros((4, 128), jnp.float32),
        ],
        0,
    )
    pieces = [
        query_sums[i : i + 1, 128 * j : 128 * (j + 1)] for i in range(2) for j in range(D // 128)
    ] + [jnp.zeros((4, 128), jnp.float32)]
    sums = jnp.concatenate(pieces, 0)
    final = jnp.concatenate([small, side, sums[0:8], sums[8:16]], 1).astype(low)
    final_ref[...] = jnp.broadcast_to(final[None], final_ref.shape)


def final_kernel(
    index_ref, own_ref, other_ref, query_weight_ref, small_ref, mean_ref, square_ref, bias_ref,
    long_ref, long_mean_ref, long_square_ref, *refs,
):
    weights, refs = refs[:17], refs[17:]
    (
        new_ref, mean_new_ref, square_new_ref, vectors_ref, scalar_ref,
        long_new_ref, long_mean_new_ref, long_square_new_ref,
    ), refs = refs[:8], refs[8:]
    results, rows = refs[:12], refs[12]
    low = jnp.bfloat16
    first_core = index_ref[1] == 0
    share = own_ref.shape[1]
    hidden = weights[8].shape[0]
    count = new_ref.shape[0]
    square = jnp.zeros((1, 128), jnp.float32)
    sums = jnp.zeros((8, 256), jnp.float32)
    biases = []
    for block in range(own_ref.shape[0]):
        here = own_ref[block].astype(jnp.float32)
        there = other_ref[block].astype(jnp.float32)
        for core, pick in enumerate(
            (jnp.where(first_core, here, there), jnp.where(first_core, there, here))
        ):
            index = block * 2 + core
            rows[index * share : (index + 1) * share, :] = pick[:, :D]
            side = pick[:, D : D + 128]
            square = square + (side[0:1] + side[1:2] + side[2:3])
            biases.append(side[3:4, :hidden])
            sums = sums + pick[:, D + 128 :]
    pieces = [sums[k : k + 1, 0:128] for k in range(8)] + [sums[k : k + 1, 128:] for k in range(4)]
    grad_query = jnp.concatenate(
        [jnp.concatenate(pieces[0:6], 1), jnp.concatenate(pieces[6:12], 1)], 0
    )
    gain = vector(small_ref, 3)
    token_out, token_normed, token_inverse = norm_forward(
        token_rows(small_ref), gain, vector(small_ref, 4)
    )
    eight = jnp.concatenate([grad_query, jnp.zeros((6, D), jnp.float32)], 0)
    token_grad = matmul_nt(eight.astype(low), query_weight_ref[...])
    token_in = norm_in(token_grad, token_normed, token_inverse, gain)
    rows[0:2, :] = rows[0:2, :] + token_in[0:2]
    opened = rows[POS + 1 : POS + 6, :] + jnp.concatenate(
        [
            token_in[0:2],
            jnp.sum(token_grad * token_normed, 0, keepdims=True),
            jnp.sum(token_grad, 0, keepdims=True),
            jnp.sum(grad_query, 0, keepdims=True),
        ],
        0,
    )
    rows[POS + 1 : POS + 6, :] = opened
    token_low = token_out.astype(low)
    own = weights[0].shape[0]
    token_own = matmul_nt(own_selector(index_ref[0], own), token_low)
    owned_query = token_own[:, 0:1] * grad_query[0:1] + token_own[:, 1:2] * grad_query[1:2]
    token_float = token_low.astype(jnp.float32)

    def product(left, right):
        return jnp.sum(left * right, -1, keepdims=True)

    cross = product(token_float[0:1], token_float[1:2]) * product(grad_query[0:1], grad_query[1:2])
    query_square = 2.0 * cross
    for i in range(2):
        query_square = query_square + product(
            token_float[i : i + 1], token_float[i : i + 1]
        ) * product(grad_query[i : i + 1], grad_query[i : i + 1])
    bias = bias_ref[...]
    table = rows[0:2, :]
    total = square[:, 0:1] + query_square
    for value in (bias, table, opened):
        total = total + jnp.sum(jnp.sum(value * value, 0, keepdims=True), 1, keepdims=True)
    norm = jnp.sqrt(total)
    factor = jnp.minimum(1.0, CLIP_NORM / (norm + 1e-06))
    scalar_ref[...] = jnp.broadcast_to(norm, scalar_ref.shape)
    gradient = rows[0:count, :]
    vectors_ref[...] = rows[POS:count, :] * factor

    def update(targets, weight, first, second, gradient, decay, rate):
        new = adam_update(weight[...], first[...], second[...], gradient, factor, decay, rate)
        for target, value in zip(targets, new):
            target[...] = value
            target.send()

    update(
        (new_ref, mean_new_ref, square_new_ref), small_ref, mean_ref, square_ref, gradient,
        0.0, SMALL_RATE,
    )
    long_gradient = jnp.concatenate(biases + [bias[0:1, :CLS], bias[1:2, :CLS]], 1)
    update(
        (long_new_ref, long_mean_new_ref, long_square_new_ref),
        long_ref, long_mean_ref, long_square_ref, long_gradient, 0.0, SMALL_RATE,
    )
    gradients = (
        weights[3][...],
        jnp.concatenate([owned_query, weights[7][...], weights[16][...]], 1),
        weights[11][...],
        jnp.concatenate([weights[15][0, :, :CLS], weights[15][1, :, :CLS]], 1),
    )
    for group, gradient in enumerate(gradients):
        update(
            results[3 * group : 3 * group + 3], *weights[4 * group : 4 * group + 3], gradient,
            DECAY_RATE, LEARN_RATE,
        )


def chip_sum_kernel(mine_ref, theirs_ref, out_ref):
    total = mine_ref[...].astype(jnp.float32) + theirs_ref[...].astype(jnp.float32)
    out_ref[...] = total.astype(jnp.bfloat16)


def shards_tiled(
    patches,
    pos_index,
    valid,
    classes,
    mixing,
    image_weight,
    drop_keep,
    patch_weight,
    patch_mean,
    patch_square,
    block_weight,
    block_mean,
    block_square,
    down_weight,
    down_mean,
    down_square,
    heads_weight,
    heads_mean,
    heads_square,
    small_rows,
    rows_mean,
    rows_square,
    small_long,
    long_mean,
    long_square,
):
    low = jnp.bfloat16
    f32 = jnp.float32
    images, local_slots, patch_dim = patches.shape
    row_count = images * local_slots
    dp_size = lax.axis_size("dp")
    seq_size = lax.axis_size("seq")
    devices = dp_size * seq_size
    dp_index = lax.axis_index("dp").astype(jnp.int32)
    seq_index = lax.axis_index("seq").astype(jnp.int32)
    device = dp_index * seq_size + seq_index
    own_rows = patch_weight.shape[0]
    own_hidden = down_weight.shape[0]
    all_images = dp_size * images
    rows = all_images * 2
    per_chip = images * 2
    columns = images * PAIR
    half = D // 2
    device_scalar = device[None]
    seq_scalar = seq_index[None]
    device_seq = jnp.stack([device, seq_index])
    dp_seq = jnp.stack([dp_index, seq_index])

    early, late = kernel_call(
        prepare_kernel,
        [((dp_size, own_rows, D + 128), low), ((own_rows, 2 * D), low)],
        [device_scalar, small_rows, block_weight, block_weight, patch_weight],
        {2: slice(0, D), 3: slice(2 * D, 4 * D)},
    )
    gathered_late = lax.all_gather(late, ALL, axis=0, tiled=True)
    flat_patches = patches.transpose(1, 0, 2).reshape(row_count, patch_dim)
    flat_pos = pos_index.T.reshape(row_count, 1)
    valid_columns = jnp.repeat(valid, PAIR)[None]
    up_shift = lax.dynamic_slice_in_dim(small_long, device * own_hidden, own_hidden, 0)[None]
    meta = jnp.concatenate(
        [classes // 32, classes % 32, mixing[:, None], image_weight[:, None], drop_keep], 1
    )
    meta_width = meta.shape[1]
    meta_count = images * meta_width
    pair_hidden = 2 * own_hidden
    key_width = columns + pair_hidden + 64
    meta = meta.reshape(1, meta_count).astype(f32)
    meta = jnp.pad(meta, ((0, own_rows - 1), (0, 64 - meta_count)))
    early = exchange(early, "dp")
    early, flat_patches, flat_pos, valid_columns, up_shift, meta = lax.optimization_barrier(
        (early, flat_patches, flat_pos, valid_columns, up_shift, meta)
    )
    early_other = swap_cores(early)

    query_lanes = slice(D, D + 128)
    keyed, query_blocks, late = kernel_call(
        query_kernel,
        [((dp_size, own_rows, key_width), low), ((PAIR, D), f32), ((own_rows, 2048), low)],
        [early, early_other, block_weight, block_weight, small_rows, meta, heads_weight],
        {0: query_lanes, 1: query_lanes, 2: slice(D, 2 * D), 3: slice(4 * D, 4 * D + FF)},
        loose=(0, 1),
    )
    gathered_heads = lax.all_gather(late, ALL, axis=0, tiled=True)
    keyed = exchange(keyed, "dp")
    keyed_other = swap_cores(keyed)
    metas = keyed[:, 0, key_width - 64 : key_width - 64 + meta_count]
    metas = metas.astype(f32).reshape(all_images, meta_width)
    labels = metas[:, 0:3] * 32.0 + metas[:, 3:6]
    share = metas[:, 6:7] / 16.0
    weight_keep = jnp.concatenate([metas[:, 7:8], metas[:, 8:10] * DROP_SCALE], 1)
    ones = jnp.ones_like(share)
    info_even = jnp.concatenate([labels[:, 0:2], share, 1.0 - share, weight_keep, ones], 1)
    info_odd = jnp.concatenate(
        [labels[:, 2:3], labels[:, 2:3], ones, 0.0 * ones, weight_keep, ones], 1
    )
    info = jnp.stack([info_even, info_odd], 1).reshape(rows, 8)

    first, normed, inverse = kernel_call(
        embed_kernel,
        [
            ((row_count, D), low),
            ((row_count, D), f32),
            ((row_count, 1), f32),
        ],
        [seq_scalar, early, early_other, flat_patches, flat_pos, small_rows],
        {1: slice(0, D), 2: slice(0, D)},
        scratch=[
            pltpu.VMEM((D, D), low),
            pltpu.VMEM((POS, D), low),
            pltpu.VMEM((POS, D), low),
        ],
        loose=(1, 2),
        flops=2_000_000_000,
    )
    packed, exponent, keys, up_own, late = kernel_call(
        scores_kernel,
        [
            ((columns + 8, D), f32),
            ((row_count, columns), f32),
            ((D, columns), low),
            ((D, own_hidden), low),
            ((own_rows, D), low),
        ],
        [seq_scalar, keyed, keyed_other, first, valid_columns, block_weight],
        {5: slice(0, D)},
        loose=(1, 2),
    )
    gathered_query = lax.all_gather(late, ALL, axis=0, tiled=True)
    packed_other = swap_cores(packed)
    pooled, scale, asked = kernel_call(
        attend_kernel,
        [
            ((columns, D), f32),
            ((8, columns), f32),
            ((dp_size, per_chip, D + own_rows // 8 * columns), low),
        ],
        [seq_scalar, packed, packed_other, gathered_late, small_rows],
        {3: slice(0, D)},
        scratch=[pltpu.VMEM((D, columns), f32)],
        loose=(2,),
    )
    asked = exchange(asked, "dp")

    partial, second, second_normed, second_inverse, slope, act, middle, attended_turned = (
        kernel_call(
            mlp_kernel,
            [
                ((rows, D), low),
                ((rows, D), low),
                ((rows, D), f32),
                ((rows, 1), f32),
                ((rows, own_hidden), f32),
                ((rows, own_hidden), low),
                ((rows, D), f32),
                ((own_rows, rows), low),
            ],
            [
                device_scalar, asked, gathered_late, up_own, down_weight, small_rows, info,
                up_shift,
            ],
            {1: slice(0, D), 2: slice(D, 2 * D)},
            loose=(1,),
        )
    )

    def chip_sum(blocks):
        summed = jnp.sum(blocks.astype(f32), 0)
        return summed, swap_cores(summed)

    here, there = chip_sum(exchange(partial.reshape(dp_size, per_chip, D), "dp"))
    mlp_rows = gather_blocks((here + there).astype(low), "dp").reshape(rows, D)
    long_pad = jnp.zeros((1, 1024 - CLS), f32)
    head_shift = jnp.concatenate(
        [
            jnp.concatenate([small_long[None, FF : FF + CLS], long_pad], 1),
            jnp.concatenate([small_long[None, FF + CLS :], long_pad], 1),
        ],
        0,
    )
    sent, grad_result, heads_grad, sums, head_bias, owned_down, up_bias, loss = kernel_call(
        heads_kernel,
        [
            ((dp_size, 2 * per_chip, D), low),
            ((rows, D), f32),
            ((2, own_rows, 1024), f32),
            ((8, D), f32),
            ((2, 1024), f32),
            ((own_hidden, D), f32),
            ((8, own_hidden), f32),
            ((8, 128), f32),
        ],
        [
            device_scalar, mlp_rows, middle, info, small_rows,
            gathered_heads, head_shift,
            act, slope, second, up_own, down_weight,
        ],
        loose=(1,),
    )
    received = exchange(sent, "dp")
    second_here, second_there = chip_sum(received[:, :per_chip])
    up_left, up_right = received[:, per_chip:, :half], received[:, per_chip:, half:]
    up_here = jnp.where(seq_index == 0, up_left, up_right)
    up_there = swap_cores(jnp.where(seq_index == 0, up_right, up_left))

    small_share = 8
    share_rows = own_rows + small_share + 8
    mine, theirs = kernel_call(
        back_kernel,
        [((dp_size, share_rows, D), low), ((dp_size, share_rows, D), low)],
        [
            dp_seq, second_here, second_there, second_normed, second_inverse, grad_result, info,
            small_rows, gathered_late, gathered_late,
            pooled, scale, exponent, first, normed, inverse, keys, flat_patches, flat_pos, sums,
        ],
        scratch=[
            pltpu.VMEM((columns, D), low),
            pltpu.VMEM((columns, D), low),
            pltpu.VMEM((row_count, D), low),
            pltpu.VMEM((row_count, columns), low),
            pltpu.VMEM((row_count, POS), low),
            pltpu.VMEM((patch_dim, D), f32),
            pltpu.VMEM((devices * small_share, D), f32),
            pltpu.VMEM((D, 128), f32),
        ],
        windows={8: slice(D, 2 * D), 9: slice(0, D)},
        loose=(1, 2),
        flops=4_000_000_000,
    )
    (chip_terms,) = kernel_call(
        chip_sum_kernel, [(mine.shape, low)], [mine, swap_cores(theirs)], loose=(1,)
    )
    received = exchange(chip_terms, "dp")
    attn_other = swap_cores(received[:, own_rows + small_share :, half:])
    owned_up, known = kernel_call(
        known_kernel,
        [((own_rows, FF), f32), ((8, 128), f32)],
        [device_seq, up_here, up_there, heads_grad, owned_down, up_bias],
    )
    final_width = D + 128 + 256
    owned_patch, owned_block, final = kernel_call(
        owned_kernel,
        [
            ((own_rows, D), f32),
            ((own_rows, 3 * D), f32),
            ((dp_size, small_share, final_width), low),
        ],
        [
            device_seq, received, attn_other, gathered_late, asked, attended_turned,
            query_blocks, block_weight, known, up_bias,
        ],
        {3: slice(D, 2 * D), 4: slice(D, D + own_rows // 8 * columns), 7: slice(D, 2 * D)},
        loose=(1, 2),
    )
    final = exchange(final, "dp")
    final_other = swap_cores(final)
    small_count = POS + 13
    long_count = small_long.shape[0]
    (
        rows_new, rows_mean_new, rows_square_new, vectors_grad, scalars,
        long_new, long_mean_new, long_square_new,
        patch_new, patch_mean_new, patch_square_new,
        block_new, block_mean_new, block_square_new,
        down_new, down_mean_new, down_square_new,
        heads_new, heads_mean_new, heads_square_new,
    ) = kernel_call(
        final_kernel,
        [((small_count, D), f32)] * 3
        + [((13, D), f32), ((8, 128), f32)]
        + [((1, long_count), f32)] * 3
        + [
            (weight.shape, f32)
            for weight in (patch_weight, block_weight, down_weight, heads_weight)
            for _ in range(3)
        ],
        [
            device_seq, final, final_other, gathered_query,
            small_rows, rows_mean, rows_square, head_bias,
            small_long[None], long_mean[None], long_square[None],
            patch_weight, patch_mean, patch_square, owned_patch,
            block_weight, block_mean, block_square, owned_block,
            down_weight, down_mean, down_square, owned_down,
            heads_weight, heads_mean, heads_square, heads_grad, owned_up,
        ],
        scratch=[pltpu.VMEM((devices * small_share, D), f32)],
        loose=(1, 2),
    )
    loss = loss[0, 0]
    grad_norm = scalars[0, 0]
    long_new, long_mean_new, long_square_new = (
        value.reshape(long_count) for value in (long_new, long_mean_new, long_square_new)
    )
    return (
        loss,
        grad_norm,
        patch_new,
        patch_mean_new,
        patch_square_new,
        block_new,
        block_mean_new,
        block_square_new,
        down_new,
        down_mean_new,
        down_square_new,
        heads_new,
        heads_mean_new,
        heads_square_new,
        rows_new,
        rows_mean_new,
        rows_square_new,
        long_new,
        long_mean_new,
        long_square_new,
        vectors_grad,
    )


def shards_plain(
    patches,
    pos_index,
    valid,
    classes,
    mixing,
    image_weight,
    drop_keep,
    patch_weight,
    patch_mean,
    patch_square,
    block_weight,
    block_mean,
    block_square,
    down_weight,
    down_mean,
    down_square,
    heads_weight,
    heads_mean,
    heads_square,
    small_rows,
    rows_mean,
    rows_square,
    small_long,
    long_mean,
    long_square,
):
    low = jnp.bfloat16
    f32 = jnp.float32
    images, local_slots, patch_dim = patches.shape
    row_count = images * local_slots
    dp_size = lax.axis_size("dp")
    seq_size = lax.axis_size("seq")
    devices = dp_size * seq_size
    seq_index = lax.axis_index("seq")
    device = lax.axis_index("dp") * seq_size + seq_index
    own_rows = patch_weight.shape[0]
    own_hidden = down_weight.shape[0]
    own_images = images // seq_size
    all_images = dp_size * images
    pairs = 2 * HEADS
    table = small_rows[:POS]
    vectors = small_rows[POS:]

    gathered_late = lax.all_gather(
        jnp.concatenate([block_weight[:, 2 * D : 4 * D], heads_weight], 1).astype(low),
        ALL,
        axis=0,
        tiled=True,
    )
    gathered_query_key = lax.all_gather(
        lax.optimization_barrier((block_weight[:, : 2 * D].astype(low), gathered_late[:8, :128]))[0],
        ALL,
        axis=0,
        tiled=True,
    )

    tokens = vectors[1:3] + table[0:2]
    token_out, token_normed, token_inverse = norm_forward(tokens, vectors[3], vectors[4])
    token_low = token_out.astype(low)
    select_own = (
        lax.broadcasted_iota(jnp.int32, (own_rows, D), 0) + device * own_rows
        == lax.broadcasted_iota(jnp.int32, (own_rows, D), 1)
    ).astype(low)
    token_own = matmul_nt(token_low, select_own).astype(low)
    query_partial = matmul(token_own, block_weight[:, :D].astype(low))
    query = jnp.sum(gather_blocks(query_partial), 0) + vectors[5]
    query_low = query.astype(low)
    head_of = lax.broadcasted_iota(jnp.int32, (HEADS, D), 1) // HD
    head_mask = head_of == lax.broadcasted_iota(jnp.int32, (HEADS, D), 0)
    query_blocks = jnp.where(head_mask[None], query_low[:, None, :], 0).reshape(pairs, D)
    key_own = matmul_nt(block_weight[:, D : 2 * D].astype(low), query_blocks.astype(low)) * HD ** (
        -0.5
    )
    meta = jnp.concatenate(
        [
            (classes // 32),
            (classes % 32),
            mixing[:, None],
            image_weight[:, None],
            drop_keep,
        ],
        1,
    )
    meta_width = meta.shape[1]
    meta_columns = -(-images * meta_width // own_rows)
    meta = jnp.pad(meta.reshape(-1), (0, own_rows * meta_columns - images * meta_width))
    meta = meta.reshape(own_rows, meta_columns).astype(low)
    extra = -(-(pairs + meta_columns) // 128) * 128
    early = jnp.concatenate(
        [
            patch_weight.astype(low),
            key_own.astype(low),
            meta,
            jnp.zeros((own_rows, extra - pairs - meta_columns), low),
        ],
        1,
    )
    early = gather_blocks(early, "dp").reshape(dp_size, own_rows, D + extra)
    early = join_cores(early, seq_index, 1)
    metas = early[:, 0, :, D + pairs : D + pairs + meta_columns].astype(f32)
    metas = metas.reshape(dp_size, own_rows * meta_columns)[:, : images * meta_width]
    metas = metas.reshape(all_images, meta_width)
    early = early.reshape(D, D + extra)
    full_patch = early[:, :D]
    key_vectors = early[:, D : D + pairs]

    slot_global = seq_index * local_slots + lax.broadcasted_iota(jnp.int32, (1, local_slots, 1), 1)
    is_class = slot_global == 0
    is_distill = slot_global == 1
    special = is_class | is_distill
    key_mask = slot_global < valid[:, None, None]
    flat_patches = patches.reshape(row_count, patch_dim)
    onehot_pos = (
        pos_index.reshape(row_count)[:, None]
        == lax.broadcasted_iota(jnp.int32, (1, POS), 1)
    ).astype(low)
    table_high, table_rest = split_low(table)
    embedded = matmul(flat_patches, full_patch)
    positions = matmul(onehot_pos, table_high) + matmul(onehot_pos, table_rest)
    embedded = (embedded + positions + vectors[0]).reshape(images, local_slots, D)
    stream = jnp.where(is_class, tokens[0], jnp.where(is_distill, tokens[1], embedded))
    first_out, first_normed, first_inverse = norm_forward(stream, vectors[3], vectors[4])
    first_low = first_out.astype(low)
    flat_first = first_low.reshape(row_count, D)
    scores = matmul(flat_first, key_vectors).reshape(images, local_slots, pairs)
    scores = jnp.where(key_mask, scores, MASK_FILL)
    local_peak = jnp.max(scores, 1, keepdims=True)
    exponent = jnp.exp(scores - local_peak)
    local_total = jnp.sum(exponent, 1, keepdims=True)
    local_pooled = jnp.einsum(
        "nlm,nld->nmd", exponent.astype(low), first_low, preferred_element_type=f32
    )
    packed = jnp.concatenate(
        [
            local_pooled,
            jnp.broadcast_to(local_peak.transpose(0, 2, 1), (images, pairs, 64)),
            jnp.broadcast_to(local_total.transpose(0, 2, 1), (images, pairs, 64)),
        ],
        2,
    )
    other = swap_cores(packed)
    other_pooled = other[:, :, :D]
    peak_here = local_peak.transpose(0, 2, 1)
    peak_there = other[:, :, D : D + 1]
    peak = jnp.maximum(peak_here, peak_there)
    scale_here = jnp.exp(peak_here - peak)
    scale_there = jnp.exp(peak_there - peak)
    total = (
        scale_here * local_total.transpose(0, 2, 1) + scale_there * other[:, :, D + 64 : D + 65]
    )
    pooled = (scale_here * local_pooled + scale_there * other_pooled) / total
    probs = exponent * (scale_here / total).transpose(0, 2, 1)
    pooled_low = pooled.astype(low)
    own_pooled = lax.dynamic_slice_in_dim(pooled_low, seq_index * own_images, own_images, 0)

    up_blocks = (
        block_weight[:, 4 * D :]
        .astype(low)
        .reshape(own_rows, devices, own_hidden)
        .transpose(1, 0, 2)
        .reshape(devices, own_rows * own_hidden)
    )
    pooled_blocks = (
        own_pooled.reshape(own_images * pairs, devices, own_rows)
        .transpose(1, 0, 2)
        .reshape(devices, own_images * pairs * own_rows)
    )
    received = exchange(jnp.concatenate([up_blocks, pooled_blocks], 1))
    up_own = received[:, : own_rows * own_hidden].reshape(D, own_hidden)
    pooled_own = received[:, own_rows * own_hidden :].reshape(all_images, 2, HEADS, own_rows)

    full_value = gathered_late[:, :D]
    full_out = gathered_late[:, D : 2 * D]
    full_heads = gathered_late[:, 2 * D :]
    mixed = matmul(own_pooled.reshape(own_images * pairs, D), full_value)
    attended = jnp.sum(
        jnp.where(head_mask, mixed.reshape(own_images * 2, HEADS, D), 0.0), 1
    ) + vectors[6]
    attended = attended.astype(low)
    rows = all_images * 2
    attended = gather_blocks(attended).reshape(rows, D)
    keep_float = metas[:, 8:10] * DROP_SCALE
    keep_rows = jnp.repeat(keep_float, 2, axis=0)
    keep_first = keep_rows[:, 0:1]
    keep_second = keep_rows[:, 1:2]
    middle = jnp.tile(tokens, (all_images, 1)) + keep_first * (
        matmul(attended, full_out) + vectors[7]
    )
    second_out, second_normed, second_inverse = norm_forward(middle, vectors[8], vectors[9])
    second_low = second_out.astype(low)
    hidden_bias = lax.dynamic_slice_in_dim(small_long, device * own_hidden, own_hidden, 0)
    hidden = matmul(second_low, up_own) + hidden_bias
    activated, gelu_slope = gelu_parts(hidden)
    activated = activated.astype(low)
    down_low = down_weight.astype(low)
    mlp_partial = matmul(activated, down_low).astype(low)
    row_share = own_images * 2
    mlp_own = jnp.sum(
        exchange(mlp_partial.reshape(devices, row_share, D)).astype(f32), 0
    )
    mlp_rows = gather_blocks(mlp_own.astype(low)).reshape(rows, D).astype(f32)
    result = middle + keep_second * (mlp_rows + vectors[10])

    head_out, head_normed, head_inverse = norm_forward(result, vectors[11], vectors[12])
    head_low = head_out.astype(low).reshape(all_images, 2, D)
    logits_class = matmul(head_low[:, 0], full_heads[:, :CLS]) + small_long[FF : FF + CLS]
    logits_distill = matmul(head_low[:, 1], full_heads[:, CLS:]) + small_long[FF + CLS :]
    columns = lax.broadcasted_iota(jnp.int32, (1, CLS), 1)
    labels = (metas[:, 0:3] * 32.0 + metas[:, 3:6]).astype(jnp.int32)
    share = metas[:, 6:7] / 16.0
    weights = metas[:, 7]
    weight_sum = jnp.sum(weights)
    target = share * (labels[:, 0:1] == columns).astype(f32) + (1.0 - share) * (
        labels[:, 1:2] == columns
    ).astype(f32)
    teacher = (labels[:, 2:3] == columns).astype(f32)
    log_class = jax.nn.log_softmax(logits_class, -1)
    log_distill = jax.nn.log_softmax(logits_distill, -1)
    terms = -0.5 * (jnp.sum(target * log_class, -1) + jnp.sum(teacher * log_distill, -1))
    loss = jnp.sum(weights * terms) / weight_sum
    scale_rows = (weights * 0.5 / weight_sum)[:, None]
    grad_class = (scale_rows * (jnp.exp(log_class) - target)).astype(low)
    grad_distill = (scale_rows * (jnp.exp(log_distill) - teacher)).astype(low)
    head_own = matmul_nt(select_own, head_low.reshape(rows, D)).astype(low)
    head_own = head_own.reshape(own_rows, all_images, 2)
    owned_heads = jnp.concatenate(
        [matmul(head_own[:, :, 0], grad_class), matmul(head_own[:, :, 1], grad_distill)], 1
    )
    head_bias = jnp.concatenate(
        [jnp.sum(grad_class.astype(f32), 0), jnp.sum(grad_distill.astype(f32), 0)]
    )
    grad_head_rows = jnp.stack(
        [matmul_nt(grad_class, full_heads[:, :CLS]), matmul_nt(grad_distill, full_heads[:, CLS:])],
        1,
    ).reshape(rows, D)
    grad_result, final_gain, final_shift = norm_backward(
        grad_head_rows, head_normed, head_inverse, vectors[11]
    )

    grad_mlp = (keep_second * grad_result).astype(low)
    owned_down = matmul_tn(activated, grad_mlp)
    down_bias = jnp.sum(grad_mlp.astype(f32), 0)
    grad_hidden = (matmul_nt(grad_mlp, down_low) * gelu_slope).astype(low)
    up_bias = jnp.sum(grad_hidden.astype(f32), 0)
    grad_up = matmul_tn(second_low, grad_hidden).astype(low)
    grad_second_partial = matmul_nt(grad_hidden, up_own).astype(low)
    received = exchange(
        jnp.concatenate(
            [
                grad_second_partial.reshape(devices, row_share * D),
                grad_up.reshape(devices, own_rows * own_hidden),
            ],
            1,
        )
    )
    grad_second = jnp.sum(
        received[:, : row_share * D].astype(f32).reshape(devices, row_share, D), 0
    )
    owned_up = (
        received[:, row_share * D :]
        .reshape(devices, own_rows, own_hidden)
        .transpose(1, 0, 2)
        .reshape(own_rows, FF)
        .astype(f32)
    )
    row_start = device * row_share
    own_normed = lax.dynamic_slice_in_dim(second_normed, row_start, row_share, 0)
    own_inverse = lax.dynamic_slice_in_dim(second_inverse, row_start, row_share, 0)
    own_result = lax.dynamic_slice_in_dim(grad_result, row_start, row_share, 0)
    own_keep = lax.dynamic_slice_in_dim(keep_first, row_start, row_share, 0)
    grad_second_in, second_gain, second_shift = norm_backward(
        grad_second, own_normed, own_inverse, vectors[8]
    )
    grad_middle = own_result + grad_second_in
    grad_attn_own = (own_keep * grad_middle).astype(low)
    out_bias = jnp.sum(grad_attn_own.astype(f32), 0)
    grad_attn = join_cores(grad_attn_own, seq_index, 0).reshape(images * 2, D)
    grad_att = matmul_nt(grad_attn, full_out).astype(low)
    value_bias = jnp.sum(
        lax.dynamic_slice_in_dim(grad_att, seq_index * row_share, row_share, 0).astype(f32), 0
    )
    grad_att_blocks = jnp.where(
        head_mask, grad_att.reshape(images * 2, 1, D), jnp.zeros((), low)
    ).reshape(images * pairs, D)
    value_vectors = matmul_nt(grad_att_blocks, full_value).astype(low)
    value_const = jnp.sum(grad_att_blocks.astype(f32) * vectors[6], -1).reshape(images, pairs)
    value_vectors = value_vectors.reshape(images, pairs, D)
    mean_grad = jnp.sum(pooled * value_vectors.astype(f32), -1) + value_const
    grad_probs = (
        jnp.einsum("nld,nmd->nlm", first_low, value_vectors, preferred_element_type=f32)
        + value_const[:, None, :]
    )
    grad_scores = (probs * (grad_probs - mean_grad[:, None, :])).astype(low)
    key_rows = jnp.broadcast_to(key_vectors.T[None], (images, pairs, D))
    grad_first = jnp.einsum(
        "nlk,nkd->nld",
        jnp.concatenate([grad_scores, probs.astype(low)], 2),
        jnp.concatenate([key_rows, value_vectors], 1),
        preferred_element_type=f32,
    )
    grad_stream, first_gain, first_shift = norm_backward(
        grad_first, first_normed, first_inverse, vectors[3]
    )
    pooled_grad = matmul_tn(grad_scores.reshape(row_count, pairs), flat_first)
    query_grad_blocks = matmul(pooled_grad.astype(low), gathered_query_key[:, D:]) * HD ** (-0.5)
    grad_query = jnp.sum(
        jnp.where(head_mask, query_grad_blocks.reshape(2, HEADS, D), 0.0), 1
    )
    token_grad = matmul_nt(grad_query.astype(low), gathered_query_key[:, :D])
    token_grad_in, token_gain, token_shift = norm_backward(
        token_grad, token_normed, token_inverse, vectors[3]
    )
    grad_tokens = (
        token_grad_in
        + jnp.sum(grad_middle.reshape(own_images, 2, D), 0)
        + jnp.stack(
            [
                jnp.sum(jnp.where(is_class, grad_stream, 0.0), (0, 1)),
                jnp.sum(jnp.where(is_distill, grad_stream, 0.0), (0, 1)),
            ]
        )
    )
    grad_embed = jnp.where(special, 0.0, grad_stream)
    embed_low = grad_embed.astype(low).reshape(row_count, D)
    grad_patch = matmul_tn(flat_patches, embed_low)
    grad_table = matmul_tn(onehot_pos, embed_low)
    patch_bias = jnp.sum(grad_embed, (0, 1))
    leader = (device == 0).astype(f32)
    small_terms = jnp.concatenate(
        [
            grad_tokens,
            grad_table[2:],
            patch_bias[None],
            grad_tokens,
            (first_gain + token_gain)[None],
            (first_shift + token_shift)[None],
            jnp.sum(grad_query, 0)[None],
            value_bias[None],
            out_bias[None],
            second_gain[None],
            second_shift[None],
            leader * down_bias[None],
            leader * final_gain[None],
            leader * final_shift[None],
        ],
        0,
    )
    small_count = POS + 13
    small_share = -(-small_count // devices)
    small_terms = jnp.pad(small_terms, ((0, small_share * devices - small_count), (0, 0)))

    key_terms = (
        pooled_grad.reshape(pairs, devices, own_rows)
        .transpose(1, 0, 2)
        .reshape(devices, pairs * own_rows)
    )
    key_share = -(-pairs * own_rows // D)
    key_terms = jnp.pad(key_terms, ((0, 0), (0, key_share * D - pairs * own_rows)))
    terms_rows = jnp.concatenate(
        [
            grad_patch.reshape(dp_size, seq_size, own_rows, D),
            small_terms.reshape(dp_size, seq_size, small_share, D),
            key_terms.reshape(dp_size, seq_size, key_share, D),
            jnp.broadcast_to(grad_query, (dp_size, seq_size, 2, D)),
        ],
        2,
    )
    mine = lax.dynamic_index_in_dim(terms_rows, seq_index, 1, keepdims=False)
    theirs = lax.dynamic_index_in_dim(terms_rows, 1 - seq_index, 1, keepdims=False)
    chip_terms = mine + swap_cores(theirs.astype(low)).astype(f32)
    pair_share = 2 * row_share
    grad_att_own = lax.dynamic_slice_in_dim(grad_att, seq_index * row_share, row_share, 0)
    pair_own = jnp.concatenate([grad_attn_own, grad_att_own], 0)
    sent = jnp.concatenate(
        [chip_terms.astype(low), jnp.broadcast_to(pair_own, (dp_size, pair_share, D))], 1
    )
    received = exchange(sent, "dp")
    summed_share = chip_terms.shape[1]
    reduced = jnp.sum(received[:, :summed_share].astype(f32), 0)
    pair_rows = join_cores(received[:, summed_share:], seq_index, 1)
    pair_rows = pair_rows.reshape(devices, 2, row_share, D)
    owned_patch = reduced[:own_rows]
    owned_small = reduced[own_rows : own_rows + small_share]
    key_start = own_rows + small_share
    key_reduced = reduced[key_start : key_start + key_share].reshape(-1)[: pairs * own_rows]
    key_reduced = key_reduced.reshape(2, HEADS, own_rows)
    query_reduced = reduced[key_start + key_share :]

    owned_query = matmul_tn(token_own, query_reduced.astype(low))
    key_left = jnp.repeat(
        key_reduced.transpose(2, 0, 1), HD, axis=2
    )
    owned_key = jnp.sum(key_left * query_low.astype(f32)[None], 1) * HD ** (-0.5)
    grad_attn_rows = pair_rows[:, 0].reshape(rows, D)
    grad_att_rows = pair_rows[:, 1].reshape(all_images, 2, HEADS, HD)
    owned_value = jnp.einsum(
        "nihd,nihc->dhc", pooled_own, grad_att_rows, preferred_element_type=f32
    ).reshape(own_rows, D)
    attended_own = matmul_nt(select_own, attended).astype(low)
    owned_out = matmul(attended_own, grad_attn_rows)
    owned_block = jnp.concatenate([owned_query, owned_key, owned_value, owned_out, owned_up], 1)

    shard_square = (
        jnp.sum(owned_patch * owned_patch)
        + jnp.sum(owned_block * owned_block)
        + jnp.sum(owned_down * owned_down)
        + jnp.sum(owned_heads * owned_heads)
        + jnp.sum(owned_small * owned_small)
        + jnp.sum(up_bias * up_bias)
    )
    square_high, square_rest = split_low(shard_square)
    square_rest, square_last = split_low(shard_square - square_high.astype(f32))
    tail_row = jnp.concatenate(
        [
            jnp.stack([square_high, square_rest, square_last]),
            up_bias.astype(low),
            jnp.zeros((D - 3 - own_hidden,), low),
        ]
    )
    final = gather_blocks(
        jnp.concatenate([owned_small.astype(low), tail_row[None]], 0), "dp"
    ).reshape(dp_size, small_share + 1, D)
    final = join_cores(final, seq_index, 1).reshape(devices, small_share + 1, D)
    summed_rows = final[:, :small_share].astype(f32).reshape(devices * small_share, D)[:small_count]
    global_square = jnp.sum(final[:, small_share, 0:3].astype(f32))
    up_bias_all = final[:, small_share, 3 : 3 + own_hidden].astype(f32).reshape(FF)
    summed_long = jnp.concatenate([up_bias_all, head_bias])
    total_square = global_square + jnp.sum(head_bias * head_bias)
    grad_norm = jnp.sqrt(total_square)
    factor = jnp.minimum(1.0, CLIP_NORM / (grad_norm + 1e-06))
    vectors_grad = factor * summed_rows[POS:]
    patch_new, patch_mean_new, patch_square_new = adam_update(
        patch_weight, patch_mean, patch_square, owned_patch, factor, DECAY_RATE, LEARN_RATE
    )
    block_new, block_mean_new, block_square_new = adam_update(
        block_weight, block_mean, block_square, owned_block, factor, DECAY_RATE, LEARN_RATE
    )
    down_new, down_mean_new, down_square_new = adam_update(
        down_weight, down_mean, down_square, owned_down, factor, DECAY_RATE, LEARN_RATE
    )
    heads_new, heads_mean_new, heads_square_new = adam_update(
        heads_weight, heads_mean, heads_square, owned_heads, factor, DECAY_RATE, LEARN_RATE
    )
    rows_new, rows_mean_new, rows_square_new = adam_update(
        small_rows, rows_mean, rows_square, summed_rows, factor, 0.0, SMALL_RATE
    )
    long_new, long_mean_new, long_square_new = adam_update(
        small_long, long_mean, long_square, summed_long, factor, 0.0, SMALL_RATE
    )
    return (
        loss,
        grad_norm,
        patch_new,
        patch_mean_new,
        patch_square_new,
        block_new,
        block_mean_new,
        block_square_new,
        down_new,
        down_mean_new,
        down_square_new,
        heads_new,
        heads_mean_new,
        heads_square_new,
        rows_new,
        rows_mean_new,
        rows_square_new,
        long_new,
        long_mean_new,
        long_square_new,
        vectors_grad,
    )


def tiles(arguments):
    patches, patch_weight = arguments[0], arguments[7]
    images, local_slots, _ = patches.shape
    return images * PAIR == 128 and (images * local_slots) % CHUNK == 0 and patch_weight.shape[0] == 24


def shards(*arguments):
    return (shards_tiled if tiles(arguments) else shards_plain)(*arguments)


def solution(mesh):
    placed = (
        P("dp", "seq", None),
        P("dp", "seq"),
        P("dp"),
        P("dp", None),
        P("dp"),
        P("dp"),
        P("dp", None),
        P(("dp", "seq"), None),
        P(("dp", "seq"), None),
        P(("dp", "seq"), None),
        P(("dp", "seq"), None),
        P(("dp", "seq"), None),
        P(("dp", "seq"), None),
        P(("dp", "seq"), None),
        P(("dp", "seq"), None),
        P(("dp", "seq"), None),
        P(("dp", "seq"), None),
        P(("dp", "seq"), None),
        P(("dp", "seq"), None),
        P(),
        P(),
        P(),
        P(),
        P(),
        P(),
    )
    return jax.shard_map(
        shards,
        mesh=mesh,
        in_specs=placed,
        out_specs=(
            P(),
            P(),
            P(("dp", "seq"), None),
            P(("dp", "seq"), None),
            P(("dp", "seq"), None),
            P(("dp", "seq"), None),
            P(("dp", "seq"), None),
            P(("dp", "seq"), None),
            P(("dp", "seq"), None),
            P(("dp", "seq"), None),
            P(("dp", "seq"), None),
            P(("dp", "seq"), None),
            P(("dp", "seq"), None),
            P(("dp", "seq"), None),
            P(),
            P(),
            P(),
            P(),
            P(),
            P(),
            P(),
        ),
        check_vma=False,
    )
```

```python
import math

import jax
import jax.numpy as jnp
from jax import lax
from jax.experimental import pallas as pl
from jax.experimental.pallas import tpu as pltpu
from jax.sharding import PartitionSpec as P

D = 768
HEADS = 12
HD = 64
FF = 3072
CLS = 1000
POS = 198
STEP = 7


NORM_EPS = 1e-06
DROP_SCALE = 1.0 / 0.9
CLIP_NORM = 0.02
LEARN_RATE = 0.02
SMALL_RATE = 0.15
BETA_FIRST = 0.9
BETA_SECOND = 0.999
ADAM_EPS = 1e-08
DECAY_RATE = 0.05
MASK_FILL = -1e30
highest = lax.Precision.HIGHEST


def matmul(left, right):
    return jnp.dot(left, right, preferred_element_type=jnp.float32)


def matmul_tn(left, right):
    return lax.dot_general(
        left, right, (((0,), (0,)), ((), ())), preferred_element_type=jnp.float32
    )


def matmul_nt(left, right):
    return lax.dot_general(
        left, right, (((1,), (1,)), ((), ())), preferred_element_type=jnp.float32
    )


def norm_forward(values, gain, shift):
    centered = values - jnp.mean(values, -1, keepdims=True)
    inverse = lax.rsqrt(jnp.mean(centered * centered, -1, keepdims=True) + NORM_EPS)
    normed = centered * inverse
    return (normed * gain + shift, normed, inverse)


def norm_backward(grad_out, normed, inverse, gain):
    scaled = grad_out * gain
    grad_in = inverse * (
        scaled
        - jnp.mean(scaled, -1, keepdims=True)
        - normed * jnp.mean(scaled * normed, -1, keepdims=True)
    )
    leading = tuple(range(grad_out.ndim - 1))
    return (grad_in, jnp.sum(grad_out * normed, leading), jnp.sum(grad_out, leading))


def gelu_parts(values):
    cumulative = 0.5 * (1.0 + jax.scipy.special.erf(values * 0.7071067811865476))
    density = 0.3989422804014327 * jnp.exp(-0.5 * values * values)
    return (values * cumulative, cumulative + values * density)


def adam_update(weight, first, second, gradient, factor, decay, rate):
    clipped = gradient * factor
    first_new = BETA_FIRST * first + (1.0 - BETA_FIRST) * clipped
    second_new = BETA_SECOND * second + (1.0 - BETA_SECOND) * clipped * clipped
    first_hat = first_new / (1.0 - BETA_FIRST**STEP)
    second_hat = second_new / (1.0 - BETA_SECOND**STEP)
    weight_new = weight - rate * (first_hat / (jnp.sqrt(second_hat) + ADAM_EPS) + decay * weight)
    return (weight_new, first_new, second_new)


ALL = ("dp", "seq")


def exchange(blocks, axes=ALL):
    return lax.all_to_all(blocks, axes, 0, 0, tiled=True)


def gather_blocks(block, axes=ALL):
    count = lax.axis_size(axes)
    return exchange(jnp.broadcast_to(block[None], (count,) + block.shape), axes)


def swap_cores(value):
    return lax.ppermute(value, "seq", [(0, 1), (1, 0)])


def join_cores(value, seq_index, axis):
    other = swap_cores(value)
    first = jnp.where(seq_index == 0, value, other)
    second = jnp.where(seq_index == 0, other, value)
    return jnp.stack([first, second], axis)


def split_low(value):
    high = value.astype(jnp.bfloat16)
    rest = (value - high.astype(jnp.float32)).astype(jnp.bfloat16)
    return high, rest


PADDED = 16
PAIR = 2 * PADDED
CHUNK = 112


class Fetched:
    def __init__(self, value, source, semaphore, columns):
        if columns is not None:
            source = source.at[(slice(None),) * (len(source.shape) - 1) + (columns,)]
        self.copy = pltpu.make_async_copy(source, value, semaphore)
        self.value = value
        self.copy.start()
        self.waiting = True

    def ready(self):
        if self.waiting:
            self.copy.wait()
            self.waiting = False

    @property
    def shape(self):
        return self.value.shape

    @property
    def dtype(self):
        return self.value.dtype

    def __getitem__(self, index):
        self.ready()
        return self.value[index]


class Stored:
    def __init__(self, value, out, semaphore):
        self.copy = pltpu.make_async_copy(value, out, semaphore)
        self.value = value
        self.sent = False

    def send(self):
        if not self.sent:
            self.copy.start()
            self.sent = True

    @property
    def shape(self):
        return self.value.shape

    @property
    def dtype(self):
        return self.value.dtype

    def __getitem__(self, index):
        return self.value[index]

    def __setitem__(self, index, value):
        self.value[index] = value


def ready(*operands):
    for operand in operands:
        operand.ready()


def kernel_call(body, outputs, inputs, windows=None, scratch=(), flops=1_000_000, limit=48, loose=()):
    windows = windows or {}
    places, buffers = [], []
    moved = 0
    for position, value in enumerate(inputs):
        if value.ndim == 1:
            places.append(pl.BlockSpec(memory_space=pltpu.SMEM))
            continue
        places.append(pl.BlockSpec(memory_space=pltpu.HBM))
        shape = value.shape
        if position in windows:
            shape = shape[:-1] + (windows[position].stop - windows[position].start,)
        buffers.append(pltpu.VMEM(shape, value.dtype))
        moved += math.prod(shape) * value.dtype.itemsize
    moved += sum(math.prod(shape) * jnp.dtype(kind).itemsize for shape, kind in outputs)
    fetches = len(buffers)
    buffers += [pltpu.VMEM(shape, kind) for shape, kind in outputs]
    buffers += [pltpu.SemaphoreType.DMA((fetches + len(outputs),))]

    def run(*refs):
        ins, refs = refs[: len(inputs)], refs[len(inputs) :]
        outs, refs = refs[: len(outputs)], refs[len(outputs) :]
        stores, copies, semaphores = refs[fetches:][: len(outputs)], refs[:fetches], None
        semaphores = refs[fetches + len(outputs)]
        rest = refs[fetches + len(outputs) + 1 :]
        operands, used = [], 0
        for position, (value, ref) in enumerate(zip(inputs, ins)):
            if value.ndim == 1:
                operands.append(ref)
                continue
            operands.append(
                Fetched(copies[used], ref, semaphores.at[used], windows.get(position))
            )
            used += 1
        stores = [
            Stored(store, out, semaphores.at[fetches + index])
            for index, (store, out) in enumerate(zip(stores, outs))
        ]
        body(*operands, *stores, *rest)
        ready(*[operand for operand in operands if isinstance(operand, Fetched)])
        for store in stores:
            store.send()
        for store in stores:
            store.copy.wait()

    return pl.pallas_call(
        run,
        name=body.__name__,
        in_specs=places,
        out_specs=[pl.BlockSpec(memory_space=pltpu.HBM) for _ in outputs],
        out_shape=[pltpu.HBM(shape, kind) for shape, kind in outputs],
        scratch_shapes=buffers + list(scratch),
        cost_estimate=pl.CostEstimate(flops=flops, bytes_accessed=moved, transcendentals=0),
        compiler_params=pltpu.CompilerParams(vmem_limit_bytes=limit * 1024 * 1024),
    )(
        *[
            value
            if value.ndim == 1 or position in loose
            else pltpu.with_memory_space_constraint(value, pltpu.HBM)
            for position, value in enumerate(inputs)
        ]
    )


def iota(shape, axis):
    return lax.broadcasted_iota(jnp.int32, shape, axis)


def own_selector(device, count):
    return jnp.where(
        iota((count, D), 0) + device * count == iota((count, D), 1), 1.0, 0.0
    ).astype(jnp.bfloat16)


def pair_mask(rows):
    return (iota((rows, D), 0) & (PADDED - 1)) == (iota((rows, D), 1) >> 6)


def token_rows(small_ref):
    tokens = small_ref[POS + 1 : POS + 3, :] + small_ref[0:2, :]
    return jnp.concatenate([tokens, jnp.zeros((6, D), jnp.float32)], 0)


def vector(small_ref, index):
    return small_ref[POS + index : POS + index + 1, :]


def norm_in(grad_out, normed, inverse, gain):
    scaled = grad_out * gain
    return inverse * (
        scaled
        - jnp.mean(scaled, -1, keepdims=True)
        - normed * jnp.mean(scaled * normed, -1, keepdims=True)
    )


def spread_pairs(values):
    count = values.shape[0]
    spread = jnp.broadcast_to(values[:, None, :], (count, PADDED, D)).reshape(count * PADDED, D)
    return jnp.where(pair_mask(count * PADDED), spread, 0.0)


def collect_pairs(values):
    count = values.shape[0] // PADDED
    kept = jnp.where(pair_mask(values.shape[0]), values, 0.0)
    return jnp.sum(kept.reshape(count, PADDED, D), 1)


def late_kernel(value_out_ref, heads_ref, late_ref):
    low = jnp.bfloat16
    late_ref[:, 0 : 2 * D] = value_out_ref[...].astype(low)
    late_ref[:, 2 * D :] = jnp.zeros((late_ref.shape[0], 2048), low)
    late_ref[:, 2 * D : 2 * D + CLS] = heads_ref[:, 0:CLS].astype(low)
    late_ref[:, 2 * D + 1024 : 2 * D + 1024 + CLS] = heads_ref[:, CLS:].astype(low)


def prepare_kernel(
    device_ref, small_ref, query_weight_ref, patch_ref, first_ref, last_ref
):
    low = jnp.bfloat16
    own = patch_ref.shape[0]
    last_ref[...] = query_weight_ref[...].astype(low)
    query_weight = query_weight_ref[...].astype(low)
    token_out, _, _ = norm_forward(token_rows(small_ref), vector(small_ref, 3), vector(small_ref, 4))
    token_own = matmul_nt(token_out.astype(low), own_selector(device_ref[0], own))
    partial = matmul(token_own.astype(low), query_weight)
    high, rest = split_low(partial)
    pieces = [
        part[i : i + 1, 128 * j : 128 * (j + 1)].astype(jnp.float32)
        for part in (high, rest)
        for i in range(2)
        for j in range(D // 128)
    ]
    block = jnp.concatenate(
        [patch_ref[...], jnp.concatenate(pieces, 0)], 1
    ).astype(low)
    first_ref[...] = jnp.broadcast_to(block[None], first_ref.shape)


def query_kernel(
    own_ref, other_ref, key_weight_ref, up_ref, small_ref, meta_ref,
    out_ref, query_ref,
):
    total = jnp.sum(own_ref[...].astype(jnp.float32), 0) + jnp.sum(
        other_ref[...].astype(jnp.float32), 0
    )
    count = D // 128
    both = total[0 : 2 * count] + total[2 * count :]
    query = jnp.concatenate(
        [
            jnp.concatenate([both[i * count + j : i * count + j + 1] for j in range(count)], 1)
            for i in range(2)
        ],
        0,
    ) + vector(small_ref, 5)
    query = query.astype(jnp.bfloat16).astype(jnp.float32)
    blocks = spread_pairs(jnp.concatenate([query] * 4, 0))
    query_ref[...] = blocks[:PAIR]
    keys = matmul_nt(key_weight_ref[...].astype(jnp.bfloat16), blocks.astype(jnp.bfloat16))
    keys = keys * HD ** (-0.5)
    up = up_ref[...]
    width = up.shape[1] // out_ref.shape[0]
    for block in range(out_ref.shape[0]):
        out_ref[block] = jnp.concatenate(
            [keys, up[:, block * width : (block + 1) * width], meta_ref[...]], 1
        ).astype(jnp.bfloat16)


def row_ids(start, rows, images, local_slots, seq_index):
    ids = iota((rows, 1), 0) + start
    shift = images.bit_length() - 1
    return ids & (images - 1), (ids >> shift) + seq_index * local_slots


def join_weights(seq_index, own_ref, other_ref, weights):
    count = own_ref.shape[1]
    first_core = seq_index == 0
    for block in range(own_ref.shape[0]):
        here = own_ref[block].astype(jnp.float32)
        there = other_ref[block].astype(jnp.float32)
        start = block * 2 * count
        weights[start : start + count, :] = jnp.where(first_core, here, there).astype(jnp.bfloat16)
        weights[start + count : start + 2 * count, :] = jnp.where(first_core, there, here).astype(
            jnp.bfloat16
        )


def embed_kernel(
    seq_ref, own_ref, other_ref, patches_ref, pos_ref, small_ref,
    first_ref, normed_ref, inverse_ref, weights, high, rest,
):
    row_count = patches_ref.shape[0]
    images = 128 // PAIR
    local_slots = row_count // images
    seq_index = seq_ref[0]
    join_weights(seq_index, own_ref, other_ref, weights)
    tokens = token_rows(small_ref)
    table_high, table_rest = split_low(small_ref[0:POS, :])
    high[...] = table_high
    rest[...] = table_rest
    ready(patches_ref, pos_ref, small_ref)

    def step(index, carry):
        rows = pl.ds(pl.multiple_of(index * CHUNK, CHUNK), CHUNK)
        onehot = jnp.where(pos_ref[rows, :] == iota((CHUNK, POS), 1), 1.0, 0.0).astype(jnp.bfloat16)
        embedded = (
            matmul(patches_ref[rows, :], weights[...])
            + matmul(onehot, high[...])
            + matmul(onehot, rest[...])
            + vector(small_ref, 0)
        )
        _, slot = row_ids(index * CHUNK, CHUNK, images, local_slots, seq_index)
        stream = jnp.where(slot == 0, tokens[0:1], jnp.where(slot == 1, tokens[1:2], embedded))
        out, normed, inverse = norm_forward(stream, vector(small_ref, 3), vector(small_ref, 4))
        first_ref[rows, :] = out.astype(jnp.bfloat16)
        normed_ref[rows, :] = normed
        inverse_ref[rows, :] = inverse
        return carry

    lax.fori_loop(0, row_count // CHUNK, step, 0)


def scores_kernel(
    seq_ref, own_ref, other_ref, first_ref, valid_ref,
    packed_ref, exponent_ref, keys_ref, up_ref,
):
    row_count, columns = exponent_ref.shape
    images = columns // PAIR
    seq_index = seq_ref[0]
    first_core = seq_index == 0
    count = own_ref.shape[1]
    hidden = up_ref.shape[1]
    for block in range(own_ref.shape[0]):
        here = own_ref[block].astype(jnp.float32)
        there = other_ref[block].astype(jnp.float32)
        start = block * 2 * count
        for core, pick in enumerate(
            (jnp.where(first_core, here, there), jnp.where(first_core, there, here))
        ):
            place = slice(start + core * count, start + (core + 1) * count)
            keys_ref[place, :] = pick[:, 0:columns].astype(jnp.bfloat16)
            up_ref[place, :] = jnp.where(
                first_core,
                pick[:, columns : columns + hidden],
                pick[:, columns + hidden : columns + 2 * hidden],
            ).astype(jnp.bfloat16)
    scores = matmul(first_ref[...], keys_ref[...])
    image, slot = row_ids(0, row_count, images, row_count // images, seq_index)
    kept = ((iota((row_count, columns), 1) >> 5) == image) & (slot < valid_ref[...])
    scores = jnp.where(kept, scores, MASK_FILL)
    peak = jnp.max(scores, 0, keepdims=True)
    exponent = jnp.exp(scores - peak)
    exponent_ref[...] = exponent
    packed_ref[0:columns, :] = matmul_tn(exponent.astype(jnp.bfloat16), first_ref[...])
    packed_ref[columns : columns + 8, :] = jnp.zeros((8, D), jnp.float32)
    packed_ref[columns : columns + 1, 0:columns] = peak
    packed_ref[columns + 1 : columns + 2, 0:columns] = jnp.sum(exponent, 0, keepdims=True)


def attend_kernel(
    seq_ref, own_ref, other_ref, value_weight_ref, small_ref, pooled_ref, scale_ref, out_ref, turned
):
    columns = pooled_ref.shape[0]
    peak_here = own_ref[columns : columns + 1, 0:columns]
    peak_there = other_ref[columns : columns + 1, 0:columns]
    peak = jnp.maximum(peak_here, peak_there)
    here = jnp.exp(peak_here - peak)
    there = jnp.exp(peak_there - peak)
    total = (
        here * own_ref[columns + 1 : columns + 2, 0:columns]
        + there * other_ref[columns + 1 : columns + 2, 0:columns]
    )
    here = here / total
    there = there / total
    scale_ref[...] = jnp.broadcast_to(here, (8, columns))
    here_rows = jnp.broadcast_to(here, (columns, columns)).T[:, 0:1]
    there_rows = jnp.broadcast_to(there, (columns, columns)).T[:, 0:1]
    pooled = own_ref[0:columns, :] * here_rows + other_ref[0:columns, :] * there_rows
    pooled_ref[...] = pooled
    mixed = matmul(pooled.astype(jnp.bfloat16), value_weight_ref[...])
    attended = collect_pairs(mixed) + vector(small_ref, 6)
    turned[...] = pooled.T
    own = 2 * HEADS
    for block in range(out_ref.shape[0]):
        start = pl.multiple_of(block * 2 * own + seq_ref[0] * own, 8)
        mine = turned[pl.ds(start, own), :]
        pieces = [mine[8 * j : 8 * (j + 1)] for j in range(own // 8)]
        out_ref[block] = jnp.concatenate([attended] + pieces, 1).astype(jnp.bfloat16)


def odd_row(shape):
    return (iota(shape, 0) & 1) == 1


def mlp_kernel(
    device_ref, attended_ref, out_weight_ref, up_ref, down_ref, small_ref, info_ref, bias_ref,
    partial_ref, second_ref, normed_ref, inverse_ref, slope_ref, act_ref, middle_ref, turned_ref,
):
    attended = attended_ref[...].astype(jnp.float32)
    attended = attended.reshape(info_ref.shape[0], D).astype(jnp.bfloat16)
    own = turned_ref.shape[0]
    turned_ref[...] = matmul_nt(own_selector(device_ref[0], own), attended).astype(jnp.bfloat16)
    tokens = token_rows(small_ref)
    stream = jnp.where(odd_row(attended.shape), tokens[1:2], tokens[0:1])
    middle = stream + info_ref[:, 5:6] * (
        matmul(attended, out_weight_ref[...]) + vector(small_ref, 7)
    )
    middle_ref[...] = middle
    out, normed, inverse = norm_forward(middle, vector(small_ref, 8), vector(small_ref, 9))
    second = out.astype(jnp.bfloat16)
    second_ref[...] = second
    normed_ref[...] = normed
    inverse_ref[...] = inverse
    hidden = matmul(second, up_ref[...]) + bias_ref[...]
    act, slope = gelu_parts(hidden)
    act = act.astype(jnp.bfloat16)
    act_ref[...] = act
    slope_ref[...] = slope
    partial_ref[...] = matmul(act, down_ref[...].astype(jnp.bfloat16)).astype(jnp.bfloat16)


def heads_kernel(
    device_ref, mlp_ref, middle_ref, info_ref, small_ref,
    late_ref, bias_ref,
    act_ref, slope_ref, second_ref, up_ref, down_ref,
    partial_ref, result_ref, heads_ref, sums_ref, bias_out_ref, down_out_ref, up_bias_ref, loss_ref,
):
    rows = mlp_ref.shape[0]
    half = 512
    low = jnp.bfloat16
    result = middle_ref[...] + info_ref[:, 6:7] * (
        mlp_ref[...].astype(jnp.float32) + vector(small_ref, 10)
    )
    out, normed, inverse = norm_forward(result, vector(small_ref, 11), vector(small_ref, 12))
    head = out.astype(low)
    columns = iota((rows, half), 1)
    odd = odd_row((rows, half))
    left, right, share_a, share_b = (info_ref[:, k : k + 1] for k in range(4))
    weight = info_ref[:, 4:5]
    logits, targets = [], []
    for part in range(2):
        start = part * half
        class_columns = slice(start, start + half)
        distill_columns = slice(1024 + start, 1024 + start + half)
        piece = jnp.where(
            odd,
            matmul(head, late_ref[:, distill_columns]) + bias_ref[1:2, start : start + half],
            matmul(head, late_ref[:, class_columns]) + bias_ref[0:1, start : start + half],
        )
        where = (columns + start).astype(jnp.float32)
        logits.append(jnp.where(columns + start < CLS, piece, MASK_FILL))
        targets.append(
            share_a * jnp.where(where == left, 1.0, 0.0)
            + share_b * jnp.where(where == right, 1.0, 0.0)
        )
    peak = jnp.maximum(
        jnp.max(logits[0], -1, keepdims=True), jnp.max(logits[1], -1, keepdims=True)
    )
    exponents = [jnp.exp(piece - peak) for piece in logits]
    total = jnp.sum(exponents[0], -1, keepdims=True) + jnp.sum(exponents[1], -1, keepdims=True)
    log_total = peak + jnp.log(total)
    weight_sum = 0.5 * jnp.sum(weight, 0, keepdims=True)
    terms = jnp.zeros((rows, 1), jnp.float32)
    for piece, target in zip(logits, targets):
        terms = terms - 0.5 * jnp.sum(
            target * (piece - log_total), -1, keepdims=True
        )
    loss = jnp.sum(weight * terms, 0, keepdims=True) / weight_sum
    loss_ref[...] = jnp.broadcast_to(loss, loss_ref.shape)
    scale = weight * 0.5 / weight_sum
    head_own = matmul_nt(own_selector(device_ref[0], heads_ref.shape[1]), head).astype(low)
    grad_head = jnp.zeros((rows, D), jnp.float32)
    for part in range(2):
        start = part * half
        class_columns = slice(start, start + half)
        distill_columns = slice(1024 + start, 1024 + start + half)
        grad = scale * (exponents[part] / total - targets[part])
        grad = grad.astype(low).astype(jnp.float32)
        for side, weight_columns in ((0, class_columns), (1, distill_columns)):
            mine = jnp.where(odd == (side == 1), grad, 0.0)
            bias_out_ref[side : side + 1, start : start + half] = jnp.sum(mine, 0, keepdims=True)
            mine = mine.astype(low)
            heads_ref[side, :, start : start + half] = matmul(head_own, mine)
            grad_head = grad_head + matmul_nt(mine, late_ref[:, weight_columns])
    grad_result = norm_in(grad_head, normed, inverse, vector(small_ref, 11))
    result_ref[...] = grad_result
    grad_mlp = (info_ref[:, 6:7] * grad_result).astype(low)
    sums_ref[...] = jnp.zeros(sums_ref.shape, jnp.float32)
    sums_ref[0:1, :] = jnp.sum(grad_mlp.astype(jnp.float32), 0, keepdims=True)
    sums_ref[1:2, :] = jnp.sum(grad_head * normed, 0, keepdims=True)
    sums_ref[2:3, :] = jnp.sum(grad_head, 0, keepdims=True)
    down_out_ref[...] = matmul_tn(act_ref[...], grad_mlp)
    grad_hidden = (
        matmul_nt(grad_mlp, down_ref[...].astype(low)) * slope_ref[...]
    ).astype(low)
    up_bias_ref[...] = jnp.broadcast_to(
        jnp.sum(grad_hidden.astype(jnp.float32), 0, keepdims=True), up_bias_ref.shape
    )
    partial = matmul_nt(grad_hidden, up_ref[...])
    grad_up = matmul_tn(second_ref[...], grad_hidden)
    blocks = partial_ref.shape[0]
    per = rows // blocks
    own = D // blocks
    hidden = grad_up.shape[1]
    pad = jnp.zeros((D, 128 - hidden), jnp.float32)
    grad_up = jnp.concatenate([grad_up, pad], 1)
    for block in range(blocks):
        partial_ref[block, 0:per, :] = partial[block * per : (block + 1) * per].astype(low)
        pieces = [
            grad_up[block * own + 8 * j : block * own + 8 * (j + 1)] for j in range(own // 8)
        ]
        partial_ref[block, per : 2 * per, :] = jnp.concatenate(pieces, 1).astype(low)


def back_kernel(
    index_ref, second_ref, other_ref, normed2_ref, inverse2_ref, result_ref, info_ref, small_ref,
    out_weight_ref, value_weight_ref,
    pooled_ref, scale_ref, exponent_ref, first_ref, normed_ref, inverse_ref, keys_ref,
    patches_ref, pos_ref, sums_ref,
    mine_ref, theirs_ref,
    values, turned_keys, embed, scores, onehot, patch_out, small_out, pooled_grad,
):
    low = jnp.bfloat16
    columns = pooled_ref.shape[0]
    images = columns // PAIR
    row_count = patches_ref.shape[0]
    local_slots = row_count // images
    dp_index, seq_index = index_ref[0], index_ref[1]
    per = 2 * images
    own_rows = pl.ds(pl.multiple_of(dp_index * per, 8), per)
    grad_second = second_ref[...] + other_ref[...]
    normed2 = normed2_ref[own_rows, :]
    grad_middle = result_ref[own_rows, :] + norm_in(
        grad_second, normed2, inverse2_ref[own_rows, :], vector(small_ref, 8)
    )
    grad_attn = (info_ref[own_rows, 5:6] * grad_middle).astype(low)
    grad_att = matmul_nt(grad_attn, out_weight_ref[...]).astype(low)
    att_float = grad_att.astype(jnp.float32)
    att_blocks = spread_pairs(att_float)
    value_rows = matmul_nt(att_blocks.astype(low), value_weight_ref[...]).astype(low)
    values[...] = value_rows
    turned_keys[...] = keys_ref[...].astype(jnp.float32).T.astype(low)
    const = jnp.sum(att_blocks * vector(small_ref, 6), -1, keepdims=True)
    mean = jnp.sum(pooled_ref[...] * value_rows.astype(jnp.float32), -1, keepdims=True) + const
    const = jnp.broadcast_to(const, (columns, columns)).T[0:1, :]
    mean = jnp.broadcast_to(mean, (columns, columns)).T[0:1, :]
    gain = vector(small_ref, 3)

    ready(scale_ref, exponent_ref, first_ref, normed_ref, inverse_ref, pos_ref, patches_ref)

    def step(index, sums):
        gain_sum, shift_sum, embed_sum, class_sum, distill_sum = sums
        rows = pl.ds(pl.multiple_of(index * CHUNK, CHUNK), CHUNK)
        first = first_ref[rows, :]
        probs = exponent_ref[rows, :] * scale_ref[0:1, :]
        grad_probs = matmul_nt(first, values[...]) + const
        grad_scores = (probs * (grad_probs - mean)).astype(low)
        scores[rows, :] = grad_scores
        grad_first = matmul(grad_scores, turned_keys[...]) + matmul(probs.astype(low), values[...])
        normed = normed_ref[rows, :]
        grad_stream = norm_in(grad_first, normed, inverse_ref[rows, :], gain)
        _, slot = row_ids(index * CHUNK, CHUNK, images, local_slots, seq_index)
        grad_embed = jnp.where(slot < 2, 0.0, grad_stream)
        embed[rows, :] = grad_embed.astype(low)
        onehot[rows, :] = jnp.where(pos_ref[rows, :] == iota((CHUNK, POS), 1), 1.0, 0.0).astype(low)
        return (
            gain_sum + jnp.sum(grad_first * normed, 0, keepdims=True),
            shift_sum + jnp.sum(grad_first, 0, keepdims=True),
            embed_sum + jnp.sum(grad_embed, 0, keepdims=True),
            class_sum + jnp.sum(jnp.where(slot == 0, grad_stream, 0.0), 0, keepdims=True),
            distill_sum + jnp.sum(jnp.where(slot == 1, grad_stream, 0.0), 0, keepdims=True),
        )

    zero = jnp.zeros((1, D), jnp.float32)
    gain_sum, shift_sum, embed_sum, class_sum, distill_sum = lax.fori_loop(
        0, row_count // CHUNK, step, (zero,) * 5
    )
    patch_out[...] = matmul_tn(patches_ref[...], embed[...])
    small_out[0:POS, :] = matmul_tn(onehot[...], embed[...])
    by_column = matmul_tn(scores[...], first_ref[...])
    by_pair = jnp.sum(by_column.reshape(images, PAIR, D), 0)
    once = jnp.where(seq_index == 0, 1.0, 0.0)
    leader = jnp.where((dp_index == 0) & (seq_index == 0), 1.0, 0.0)
    middle_even = jnp.sum(jnp.where(odd_row((per, D)), 0.0, grad_middle), 0, keepdims=True)
    middle_odd = jnp.sum(jnp.where(odd_row((per, D)), grad_middle, 0.0), 0, keepdims=True)
    class_sum = class_sum + once * middle_even
    distill_sum = distill_sum + once * middle_odd
    small_out[0:1, :] = class_sum
    small_out[1:2, :] = distill_sum
    vector_rows = (
        embed_sum,
        class_sum,
        distill_sum,
        gain_sum,
        shift_sum,
        zero,
        once * jnp.sum(att_float, 0, keepdims=True),
        once * jnp.sum(grad_attn.astype(jnp.float32), 0, keepdims=True),
        once * jnp.sum(grad_second * normed2, 0, keepdims=True),
        once * jnp.sum(grad_second, 0, keepdims=True),
        leader * sums_ref[0:1, :],
        leader * sums_ref[1:2, :],
        leader * sums_ref[2:3, :],
    )
    for index, row in enumerate(vector_rows):
        small_out[POS + index : POS + index + 1, :] = row
    small_count = small_out.shape[0]
    small_out[POS + 13 : small_count, :] = jnp.zeros((small_count - POS - 13, D), jnp.float32)
    pooled_grad[...] = jnp.concatenate([by_pair, jnp.zeros((128 - PAIR, D), jnp.float32)], 0).T
    own = 2 * HEADS
    attn_half = jnp.where(
        seq_index == 0,
        grad_attn[:, : D // 2].astype(jnp.float32),
        grad_attn[:, D // 2 :].astype(jnp.float32),
    )
    share = small_count // (2 * mine_ref.shape[0])
    for block in range(mine_ref.shape[0]):
        for ref, core in ((mine_ref, seq_index), (theirs_ref, 1 - seq_index)):
            start = pl.multiple_of((block * 2 + core) * own, 8)
            ref[block, 0:own, :] = patch_out[pl.ds(start, own), :].astype(ref.dtype)
            small = pl.multiple_of((block * 2 + core) * share, 8)
            ref[block, own : own + share, :] = small_out[pl.ds(small, share), :].astype(ref.dtype)
            keys = pooled_grad[pl.ds(start, own), :]
            pieces = [keys[8 * j : 8 * (j + 1)] for j in range(own // 8)]
            if ref is mine_ref:
                pieces.append(attn_half)
            else:
                pieces.append(jnp.zeros((8, D // 2), jnp.float32))
            ref[block, own + share :, :] = jnp.concatenate(pieces, 1).astype(ref.dtype)


def known_kernel(
    index_ref, up_own_ref, up_other_ref, heads_ref, down_ref, up_bias_ref, up_ref, known_ref
):
    first_core = index_ref[1] == 0
    blocks = up_own_ref.shape[0]
    own = up_ref.shape[0]
    hidden = down_ref.shape[0]
    columns = []
    for block in range(blocks):
        mine = up_own_ref[block].astype(jnp.float32)
        theirs = up_other_ref[block].astype(jnp.float32)
        for pick in (jnp.where(first_core, mine, theirs), jnp.where(first_core, theirs, mine)):
            columns.append(
                jnp.concatenate(
                    [pick[:, 128 * j : 128 * j + hidden] for j in range(own // 8)], 0
                )
            )
    part = jnp.concatenate(columns, 1)
    up_ref[...] = part
    square = jnp.sum(part * part)
    for side in range(2):
        square = square + jnp.sum(heads_ref[side] * heads_ref[side])
    square = square + jnp.sum(down_ref[...] * down_ref[...])
    bias = up_bias_ref[0:1, :]
    known_ref[...] = jnp.broadcast_to(square + jnp.sum(bias * bias), known_ref.shape)


def owned_kernel(
    index_ref, received_ref, other_attn_ref, out_weight_ref, pooled_ref, turned_ref,
    query_ref, key_weight_ref, known_ref, up_bias_ref,
    patch_ref, block_ref, final_ref,
):
    low = jnp.bfloat16
    first_core = index_ref[1] == 0
    blocks = received_ref.shape[0]
    own = patch_ref.shape[0]
    share = final_ref.shape[1]
    half = D // 2
    total = jnp.sum(received_ref[:, :, :half].astype(jnp.float32), 0)
    right = jnp.sum(received_ref[:, : own + share, half:].astype(jnp.float32), 0)
    patch = jnp.concatenate([total[0:own], right[0:own]], 1)
    small = jnp.concatenate([total[own : own + share], right[own : own + share]], 1)
    keys = jnp.concatenate(
        [total[own + share :, 128 * j : 128 * (j + 1)] for j in range(own // 8)], 0
    )
    patch_ref[...] = patch
    row = iota((share, 1), 0) + index_ref[0] * share
    open_row = (row < 2) | ((row > POS) & (row < POS + 6))
    square = jnp.sum(patch * patch) + jnp.sum(jnp.where(open_row, 0.0, small * small))
    key_high, key_rest = split_low(keys[:, 0:PAIR])
    query_blocks = query_ref[...].astype(low)
    part = (matmul(key_high, query_blocks) + matmul(key_rest, query_blocks)) * HD ** (-0.5)
    block_ref[:, 0:D] = part
    square = square + jnp.sum(part * part)
    key_weight = key_weight_ref[...].astype(low)
    query_sums = collect_pairs(
        matmul_tn(key_high, key_weight) + matmul_tn(key_rest, key_weight)
    ) * HD ** (-0.5)
    here = received_ref[:, own + share :, half:].astype(jnp.float32).reshape(blocks * 8, half)
    there = other_attn_ref[...].astype(jnp.float32).reshape(blocks * 8, half)
    attn = jnp.concatenate(
        [jnp.where(first_core, here, there), jnp.where(first_core, there, here)], 1
    ).astype(low)
    att = matmul_nt(attn, out_weight_ref[...]).astype(low).astype(jnp.float32)
    part = jnp.zeros((own, D), jnp.float32)
    for block in range(blocks):
        spread = spread_pairs(att[block * 8 : (block + 1) * 8]).astype(low)
        turned = pooled_ref[block].astype(jnp.float32)
        turned = jnp.concatenate([turned[:, 128 * j : 128 * (j + 1)] for j in range(own // 8)], 0)
        part = part + matmul(turned.astype(low), spread)
    block_ref[:, D : 2 * D] = part
    square = square + jnp.sum(part * part)
    part = matmul(turned_ref[...], attn)
    block_ref[:, 2 * D : 3 * D] = part
    square = square + jnp.sum(part * part)
    hidden = up_bias_ref.shape[1]
    bias = up_bias_ref[0:1, :]
    square = known_ref[0:1, :] + jnp.broadcast_to(square, (1, 128))
    high, rest = split_low(square)
    middle, last = split_low(square - high.astype(jnp.float32))
    side = jnp.concatenate(
        [
            high.astype(jnp.float32),
            middle.astype(jnp.float32),
            last.astype(jnp.float32),
            jnp.concatenate([bias, jnp.zeros((1, 128 - hidden), jnp.float32)], 1),
            jnp.zeros((4, 128), jnp.float32),
        ],
        0,
    )
    pieces = [
        query_sums[i : i + 1, 128 * j : 128 * (j + 1)] for i in range(2) for j in range(D // 128)
    ] + [jnp.zeros((4, 128), jnp.float32)]
    sums = jnp.concatenate(pieces, 0)
    final = jnp.concatenate([small, side, sums[0:8], sums[8:16]], 1).astype(low)
    final_ref[...] = jnp.broadcast_to(final[None], final_ref.shape)


def final_kernel(
    index_ref, own_ref, other_ref, query_weight_ref, small_ref, mean_ref, square_ref, bias_ref,
    long_ref, long_mean_ref, long_square_ref, *refs,
):
    weights, refs = refs[:17], refs[17:]
    (
        new_ref, mean_new_ref, square_new_ref, vectors_ref, scalar_ref,
        long_new_ref, long_mean_new_ref, long_square_new_ref,
    ), refs = refs[:8], refs[8:]
    results, rows = refs[:12], refs[12]
    low = jnp.bfloat16
    first_core = index_ref[1] == 0
    share = own_ref.shape[1]
    hidden = weights[8].shape[0]
    count = new_ref.shape[0]
    square = jnp.zeros((1, 128), jnp.float32)
    sums = jnp.zeros((8, 256), jnp.float32)
    biases = []
    for block in range(own_ref.shape[0]):
        here = own_ref[block].astype(jnp.float32)
        there = other_ref[block].astype(jnp.float32)
        for core, pick in enumerate(
            (jnp.where(first_core, here, there), jnp.where(first_core, there, here))
        ):
            index = block * 2 + core
            rows[index * share : (index + 1) * share, :] = pick[:, :D]
            side = pick[:, D : D + 128]
            square = square + (side[0:1] + side[1:2] + side[2:3])
            biases.append(side[3:4, :hidden])
            sums = sums + pick[:, D + 128 :]
    pieces = [sums[k : k + 1, 0:128] for k in range(8)] + [sums[k : k + 1, 128:] for k in range(4)]
    grad_query = jnp.concatenate(
        [jnp.concatenate(pieces[0:6], 1), jnp.concatenate(pieces[6:12], 1)], 0
    )
    gain = vector(small_ref, 3)
    token_out, token_normed, token_inverse = norm_forward(
        token_rows(small_ref), gain, vector(small_ref, 4)
    )
    eight = jnp.concatenate([grad_query, jnp.zeros((6, D), jnp.float32)], 0)
    token_grad = matmul_nt(eight.astype(low), query_weight_ref[...])
    token_in = norm_in(token_grad, token_normed, token_inverse, gain)
    rows[0:2, :] = rows[0:2, :] + token_in[0:2]
    opened = rows[POS + 1 : POS + 6, :] + jnp.concatenate(
        [
            token_in[0:2],
            jnp.sum(token_grad * token_normed, 0, keepdims=True),
            jnp.sum(token_grad, 0, keepdims=True),
            jnp.sum(grad_query, 0, keepdims=True),
        ],
        0,
    )
    rows[POS + 1 : POS + 6, :] = opened
    token_low = token_out.astype(low)
    own = weights[0].shape[0]
    token_own = matmul_nt(own_selector(index_ref[0], own), token_low)
    owned_query = token_own[:, 0:1] * grad_query[0:1] + token_own[:, 1:2] * grad_query[1:2]
    token_float = token_low.astype(jnp.float32)

    def product(left, right):
        return jnp.sum(left * right, -1, keepdims=True)

    cross = product(token_float[0:1], token_float[1:2]) * product(grad_query[0:1], grad_query[1:2])
    query_square = 2.0 * cross
    for i in range(2):
        query_square = query_square + product(
            token_float[i : i + 1], token_float[i : i + 1]
        ) * product(grad_query[i : i + 1], grad_query[i : i + 1])
    bias = bias_ref[...]
    table = rows[0:2, :]
    total = square[:, 0:1] + query_square
    for value in (bias, table, opened):
        total = total + jnp.sum(jnp.sum(value * value, 0, keepdims=True), 1, keepdims=True)
    norm = jnp.sqrt(total)
    factor = jnp.minimum(1.0, CLIP_NORM / (norm + 1e-06))
    scalar_ref[...] = norm
    gradient = rows[0:count, :]
    vectors_ref[...] = rows[POS:count, :] * factor

    def update(targets, weight, first, second, gradient, decay, rate):
        new = adam_update(weight[...], first[...], second[...], gradient, factor, decay, rate)
        for target, value in zip(targets, new):
            target[...] = value
            target.send()

    update(
        (new_ref, mean_new_ref, square_new_ref), small_ref, mean_ref, square_ref, gradient,
        0.0, SMALL_RATE,
    )
    long_gradient = jnp.concatenate(biases + [bias[0:1, :CLS], bias[1:2, :CLS]], 1)
    update(
        (long_new_ref, long_mean_new_ref, long_square_new_ref),
        long_ref, long_mean_ref, long_square_ref, long_gradient, 0.0, SMALL_RATE,
    )
    gradients = (
        weights[3][...],
        jnp.concatenate([owned_query, weights[7][...], weights[16][...]], 1),
        weights[11][...],
        jnp.concatenate([weights[15][0, :, :CLS], weights[15][1, :, :CLS]], 1),
    )
    for group, gradient in enumerate(gradients):
        update(
            results[3 * group : 3 * group + 3], *weights[4 * group : 4 * group + 3], gradient,
            DECAY_RATE, LEARN_RATE,
        )


def chip_sum_kernel(mine_ref, theirs_ref, out_ref):
    total = mine_ref[...].astype(jnp.float32) + theirs_ref[...].astype(jnp.float32)
    out_ref[...] = total.astype(jnp.bfloat16)


def shards_tiled(
    patches,
    pos_index,
    valid,
    classes,
    mixing,
    image_weight,
    drop_keep,
    patch_weight,
    patch_mean,
    patch_square,
    block_weight,
    block_mean,
    block_square,
    down_weight,
    down_mean,
    down_square,
    heads_weight,
    heads_mean,
    heads_square,
    small_rows,
    rows_mean,
    rows_square,
    small_long,
    long_mean,
    long_square,
):
    low = jnp.bfloat16
    f32 = jnp.float32
    images, local_slots, patch_dim = patches.shape
    row_count = images * local_slots
    dp_size = lax.axis_size("dp")
    seq_size = lax.axis_size("seq")
    devices = dp_size * seq_size
    dp_index = lax.axis_index("dp").astype(jnp.int32)
    seq_index = lax.axis_index("seq").astype(jnp.int32)
    device = dp_index * seq_size + seq_index
    own_rows = patch_weight.shape[0]
    own_hidden = down_weight.shape[0]
    all_images = dp_size * images
    rows = all_images * 2
    per_chip = images * 2
    columns = images * PAIR
    half = D // 2
    device_scalar = device[None]
    seq_scalar = seq_index[None]
    device_seq = jnp.stack([device, seq_index])
    dp_seq = jnp.stack([dp_index, seq_index])

    late_width = 2 * D + 2048
    (late,) = kernel_call(
        late_kernel,
        [((own_rows, late_width), low)],
        [block_weight, heads_weight],
        {0: slice(2 * D, 4 * D)},
    )
    device_scalar, late = lax.optimization_barrier((device_scalar, late))
    gathered_late = lax.all_gather(late, ALL, axis=0, tiled=True)
    value_lanes, out_lanes = slice(0, D), slice(D, 2 * D)
    head_lanes = slice(2 * D, late_width)
    early, last = kernel_call(
        prepare_kernel,
        [((dp_size, own_rows, D + 128), low), ((own_rows, D), low)],
        [device_scalar, small_rows, block_weight, patch_weight],
        {2: slice(0, D)},
    )
    gathered_last = lax.all_gather(last, ALL, axis=0, tiled=True)
    flat_patches = patches.transpose(1, 0, 2).reshape(row_count, patch_dim)
    flat_pos = pos_index.T.reshape(row_count, 1)
    valid_columns = jnp.repeat(valid, PAIR)[None]
    up_shift = lax.dynamic_slice_in_dim(small_long, device * own_hidden, own_hidden, 0)[None]
    meta = jnp.concatenate(
        [classes // 32, classes % 32, mixing[:, None], image_weight[:, None], drop_keep], 1
    )
    meta_width = meta.shape[1]
    meta_count = images * meta_width
    pair_hidden = 2 * own_hidden
    key_width = columns + pair_hidden + 64
    meta = meta.reshape(1, meta_count).astype(f32)
    meta = jnp.pad(meta, ((0, own_rows - 1), (0, 64 - meta_count)))
    early = exchange(early, "dp")
    early, flat_patches, flat_pos, valid_columns, up_shift, meta = lax.optimization_barrier(
        (early, flat_patches, flat_pos, valid_columns, up_shift, meta)
    )
    early_other = swap_cores(early)

    query_lanes = slice(D, D + 128)
    keyed, query_blocks = kernel_call(
        query_kernel,
        [((dp_size, own_rows, key_width), low), ((PAIR, D), f32)],
        [early, early_other, block_weight, block_weight, small_rows, meta],
        {0: query_lanes, 1: query_lanes, 2: slice(D, 2 * D), 3: slice(4 * D, 4 * D + FF)},
        loose=(0, 1),
    )
    keyed = exchange(keyed, "dp")
    keyed_other = swap_cores(keyed)
    metas = keyed[:, 0, key_width - 64 : key_width - 64 + meta_count]
    metas = metas.astype(f32).reshape(all_images, meta_width)
    labels = metas[:, 0:3] * 32.0 + metas[:, 3:6]
    share = metas[:, 6:7] / 16.0
    weight_keep = jnp.concatenate([metas[:, 7:8], metas[:, 8:10] * DROP_SCALE], 1)
    ones = jnp.ones_like(share)
    info_even = jnp.concatenate([labels[:, 0:2], share, 1.0 - share, weight_keep, ones], 1)
    info_odd = jnp.concatenate(
        [labels[:, 2:3], labels[:, 2:3], ones, 0.0 * ones, weight_keep, ones], 1
    )
    info = jnp.stack([info_even, info_odd], 1).reshape(rows, 8)

    first, normed, inverse = kernel_call(
        embed_kernel,
        [
            ((row_count, D), low),
            ((row_count, D), f32),
            ((row_count, 1), f32),
        ],
        [seq_scalar, early, early_other, flat_patches, flat_pos, small_rows],
        {1: slice(0, D), 2: slice(0, D)},
        scratch=[
            pltpu.VMEM((D, D), low),
            pltpu.VMEM((POS, D), low),
            pltpu.VMEM((POS, D), low),
        ],
        loose=(1, 2),
        flops=2_000_000_000,
    )
    packed, exponent, keys, up_own = kernel_call(
        scores_kernel,
        [
            ((columns + 8, D), f32),
            ((row_count, columns), f32),
            ((D, columns), low),
            ((D, own_hidden), low),
        ],
        [seq_scalar, keyed, keyed_other, first, valid_columns],
        loose=(1, 2),
    )
    packed_other = swap_cores(packed)
    pooled, scale, asked = kernel_call(
        attend_kernel,
        [
            ((columns, D), f32),
            ((8, columns), f32),
            ((dp_size, per_chip, D + own_rows // 8 * columns), low),
        ],
        [seq_scalar, packed, packed_other, gathered_late, small_rows],
        {3: value_lanes},
        scratch=[pltpu.VMEM((D, columns), f32)],
        loose=(2,),
    )
    asked = exchange(asked, "dp")

    partial, second, second_normed, second_inverse, slope, act, middle, attended_turned = (
        kernel_call(
            mlp_kernel,
            [
                ((rows, D), low),
                ((rows, D), low),
                ((rows, D), f32),
                ((rows, 1), f32),
                ((rows, own_hidden), f32),
                ((rows, own_hidden), low),
                ((rows, D), f32),
                ((own_rows, rows), low),
            ],
            [
                device_scalar, asked, gathered_late, up_own, down_weight, small_rows, info,
                up_shift,
            ],
            {1: slice(0, D), 2: out_lanes},
            loose=(1,),
        )
    )

    def chip_sum(blocks):
        summed = jnp.sum(blocks.astype(f32), 0)
        return summed, swap_cores(summed)

    here, there = chip_sum(exchange(partial.reshape(dp_size, per_chip, D), "dp"))
    mlp_rows = gather_blocks((here + there).astype(low), "dp").reshape(rows, D)
    long_pad = jnp.zeros((1, 1024 - CLS), f32)
    head_shift = jnp.concatenate(
        [
            jnp.concatenate([small_long[None, FF : FF + CLS], long_pad], 1),
            jnp.concatenate([small_long[None, FF + CLS :], long_pad], 1),
        ],
        0,
    )
    sent, grad_result, heads_grad, sums, head_bias, owned_down, up_bias, loss = kernel_call(
        heads_kernel,
        [
            ((dp_size, 2 * per_chip, D), low),
            ((rows, D), f32),
            ((2, own_rows, 1024), f32),
            ((8, D), f32),
            ((2, 1024), f32),
            ((own_hidden, D), f32),
            ((8, own_hidden), f32),
            ((8, 128), f32),
        ],
        [
            device_scalar, mlp_rows, middle, info, small_rows,
            gathered_late, head_shift,
            act, slope, second, up_own, down_weight,
        ],
        {5: head_lanes},
        loose=(1,),
    )
    received = exchange(sent, "dp")
    second_here, second_there = chip_sum(received[:, :per_chip])
    up_left, up_right = received[:, per_chip:, :half], received[:, per_chip:, half:]
    up_here = jnp.where(seq_index == 0, up_left, up_right)
    up_there = swap_cores(jnp.where(seq_index == 0, up_right, up_left))

    second_here, gathered_last = lax.optimization_barrier((second_here, gathered_last))

    small_share = 8
    share_rows = own_rows + small_share + 8
    mine, theirs = kernel_call(
        back_kernel,
        [((dp_size, share_rows, D), low), ((dp_size, share_rows, D), low)],
        [
            dp_seq, second_here, second_there, second_normed, second_inverse, grad_result, info,
            small_rows, gathered_late, gathered_late,
            pooled, scale, exponent, first, normed, inverse, keys, flat_patches, flat_pos, sums,
        ],
        scratch=[
            pltpu.VMEM((columns, D), low),
            pltpu.VMEM((columns, D), low),
            pltpu.VMEM((row_count, D), low),
            pltpu.VMEM((row_count, columns), low),
            pltpu.VMEM((row_count, POS), low),
            pltpu.VMEM((patch_dim, D), f32),
            pltpu.VMEM((devices * small_share, D), f32),
            pltpu.VMEM((D, 128), f32),
        ],
        windows={8: out_lanes, 9: value_lanes},
        loose=(1, 2),
        flops=4_000_000_000,
    )
    (chip_terms,) = kernel_call(
        chip_sum_kernel, [(mine.shape, low)], [mine, swap_cores(theirs)], loose=(1,)
    )
    received = exchange(chip_terms, "dp")
    owned_up, known = kernel_call(
        known_kernel,
        [((own_rows, FF), f32), ((8, 128), f32)],
        [device_seq, up_here, up_there, heads_grad, owned_down, up_bias],
    )
    loss = loss[0, 0]
    received, owned_up, known, loss = lax.optimization_barrier((received, owned_up, known, loss))
    attn_other = swap_cores(received[:, own_rows + small_share :, half:])
    final_width = D + 128 + 256
    owned_patch, owned_block, final = kernel_call(
        owned_kernel,
        [
            ((own_rows, D), f32),
            ((own_rows, 3 * D), f32),
            ((dp_size, small_share, final_width), low),
        ],
        [
            device_seq, received, attn_other, gathered_late, asked, attended_turned,
            query_blocks, block_weight, known, up_bias,
        ],
        {3: out_lanes, 4: slice(D, D + own_rows // 8 * columns), 7: slice(D, 2 * D)},
        loose=(1, 2),
    )
    final = exchange(final, "dp")
    final_other = swap_cores(final)
    small_count = POS + 13
    long_count = small_long.shape[0]
    (
        rows_new, rows_mean_new, rows_square_new, vectors_grad, scalars,
        long_new, long_mean_new, long_square_new,
        patch_new, patch_mean_new, patch_square_new,
        block_new, block_mean_new, block_square_new,
        down_new, down_mean_new, down_square_new,
        heads_new, heads_mean_new, heads_square_new,
    ) = kernel_call(
        final_kernel,
        [((small_count, D), f32)] * 3
        + [((13, D), f32), ((1, 1), f32)]
        + [((1, long_count), f32)] * 3
        + [
            (weight.shape, f32)
            for weight in (patch_weight, block_weight, down_weight, heads_weight)
            for _ in range(3)
        ],
        [
            device_seq, final, final_other, gathered_last,
            small_rows, rows_mean, rows_square, head_bias,
            small_long[None], long_mean[None], long_square[None],
            patch_weight, patch_mean, patch_square, owned_patch,
            block_weight, block_mean, block_square, owned_block,
            down_weight, down_mean, down_square, owned_down,
            heads_weight, heads_mean, heads_square, heads_grad, owned_up,
        ],
        scratch=[pltpu.VMEM((devices * small_share, D), f32)],
        loose=(1, 2),
    )
    grad_norm = scalars.reshape(())
    long_new, long_mean_new, long_square_new = (
        value.reshape(long_count) for value in (long_new, long_mean_new, long_square_new)
    )
    return (
        loss,
        grad_norm,
        patch_new,
        patch_mean_new,
        patch_square_new,
        block_new,
        block_mean_new,
        block_square_new,
        down_new,
        down_mean_new,
        down_square_new,
        heads_new,
        heads_mean_new,
        heads_square_new,
        rows_new,
        rows_mean_new,
        rows_square_new,
        long_new,
        long_mean_new,
        long_square_new,
        vectors_grad,
    )


def shards_plain(
    patches,
    pos_index,
    valid,
    classes,
    mixing,
    image_weight,
    drop_keep,
    patch_weight,
    patch_mean,
    patch_square,
    block_weight,
    block_mean,
    block_square,
    down_weight,
    down_mean,
    down_square,
    heads_weight,
    heads_mean,
    heads_square,
    small_rows,
    rows_mean,
    rows_square,
    small_long,
    long_mean,
    long_square,
):
    low = jnp.bfloat16
    f32 = jnp.float32
    images, local_slots, patch_dim = patches.shape
    row_count = images * local_slots
    dp_size = lax.axis_size("dp")
    seq_size = lax.axis_size("seq")
    devices = dp_size * seq_size
    seq_index = lax.axis_index("seq")
    device = lax.axis_index("dp") * seq_size + seq_index
    own_rows = patch_weight.shape[0]
    own_hidden = down_weight.shape[0]
    own_images = images // seq_size
    all_images = dp_size * images
    pairs = 2 * HEADS
    table = small_rows[:POS]
    vectors = small_rows[POS:]

    gathered_late = lax.all_gather(
        jnp.concatenate([block_weight[:, 2 * D : 4 * D], heads_weight], 1).astype(low),
        ALL,
        axis=0,
        tiled=True,
    )
    gathered_query_key = lax.all_gather(
        lax.optimization_barrier((block_weight[:, : 2 * D].astype(low), gathered_late[:8, :128]))[0],
        ALL,
        axis=0,
        tiled=True,
    )

    tokens = vectors[1:3] + table[0:2]
    token_out, token_normed, token_inverse = norm_forward(tokens, vectors[3], vectors[4])
    token_low = token_out.astype(low)
    select_own = (
        lax.broadcasted_iota(jnp.int32, (own_rows, D), 0) + device * own_rows
        == lax.broadcasted_iota(jnp.int32, (own_rows, D), 1)
    ).astype(low)
    token_own = matmul_nt(token_low, select_own).astype(low)
    query_partial = matmul(token_own, block_weight[:, :D].astype(low))
    query = jnp.sum(gather_blocks(query_partial), 0) + vectors[5]
    query_low = query.astype(low)
    head_of = lax.broadcasted_iota(jnp.int32, (HEADS, D), 1) // HD
    head_mask = head_of == lax.broadcasted_iota(jnp.int32, (HEADS, D), 0)
    query_blocks = jnp.where(head_mask[None], query_low[:, None, :], 0).reshape(pairs, D)
    key_own = matmul_nt(block_weight[:, D : 2 * D].astype(low), query_blocks.astype(low)) * HD ** (
        -0.5
    )
    meta = jnp.concatenate(
        [
            (classes // 32),
            (classes % 32),
            mixing[:, None],
            image_weight[:, None],
            drop_keep,
        ],
        1,
    )
    meta_width = meta.shape[1]
    meta_columns = -(-images * meta_width // own_rows)
    meta = jnp.pad(meta.reshape(-1), (0, own_rows * meta_columns - images * meta_width))
    meta = meta.reshape(own_rows, meta_columns).astype(low)
    extra = -(-(pairs + meta_columns) // 128) * 128
    early = jnp.concatenate(
        [
            patch_weight.astype(low),
            key_own.astype(low),
            meta,
            jnp.zeros((own_rows, extra - pairs - meta_columns), low),
        ],
        1,
    )
    early = gather_blocks(early, "dp").reshape(dp_size, own_rows, D + extra)
    early = join_cores(early, seq_index, 1)
    metas = early[:, 0, :, D + pairs : D + pairs + meta_columns].astype(f32)
    metas = metas.reshape(dp_size, own_rows * meta_columns)[:, : images * meta_width]
    metas = metas.reshape(all_images, meta_width)
    early = early.reshape(D, D + extra)
    full_patch = early[:, :D]
    key_vectors = early[:, D : D + pairs]

    slot_global = seq_index * local_slots + lax.broadcasted_iota(jnp.int32, (1, local_slots, 1), 1)
    is_class = slot_global == 0
    is_distill = slot_global == 1
    special = is_class | is_distill
    key_mask = slot_global < valid[:, None, None]
    flat_patches = patches.reshape(row_count, patch_dim)
    onehot_pos = (
        pos_index.reshape(row_count)[:, None]
        == lax.broadcasted_iota(jnp.int32, (1, POS), 1)
    ).astype(low)
    table_high, table_rest = split_low(table)
    embedded = matmul(flat_patches, full_patch)
    positions = matmul(onehot_pos, table_high) + matmul(onehot_pos, table_rest)
    embedded = (embedded + positions + vectors[0]).reshape(images, local_slots, D)
    stream = jnp.where(is_class, tokens[0], jnp.where(is_distill, tokens[1], embedded))
    first_out, first_normed, first_inverse = norm_forward(stream, vectors[3], vectors[4])
    first_low = first_out.astype(low)
    flat_first = first_low.reshape(row_count, D)
    scores = matmul(flat_first, key_vectors).reshape(images, local_slots, pairs)
    scores = jnp.where(key_mask, scores, MASK_FILL)
    local_peak = jnp.max(scores, 1, keepdims=True)
    exponent = jnp.exp(scores - local_peak)
    local_total = jnp.sum(exponent, 1, keepdims=True)
    local_pooled = jnp.einsum(
        "nlm,nld->nmd", exponent.astype(low), first_low, preferred_element_type=f32
    )
    packed = jnp.concatenate(
        [
            local_pooled,
            jnp.broadcast_to(local_peak.transpose(0, 2, 1), (images, pairs, 64)),
            jnp.broadcast_to(local_total.transpose(0, 2, 1), (images, pairs, 64)),
        ],
        2,
    )
    other = swap_cores(packed)
    other_pooled = other[:, :, :D]
    peak_here = local_peak.transpose(0, 2, 1)
    peak_there = other[:, :, D : D + 1]
    peak = jnp.maximum(peak_here, peak_there)
    scale_here = jnp.exp(peak_here - peak)
    scale_there = jnp.exp(peak_there - peak)
    total = (
        scale_here * local_total.transpose(0, 2, 1) + scale_there * other[:, :, D + 64 : D + 65]
    )
    pooled = (scale_here * local_pooled + scale_there * other_pooled) / total
    probs = exponent * (scale_here / total).transpose(0, 2, 1)
    pooled_low = pooled.astype(low)
    own_pooled = lax.dynamic_slice_in_dim(pooled_low, seq_index * own_images, own_images, 0)

    up_blocks = (
        block_weight[:, 4 * D :]
        .astype(low)
        .reshape(own_rows, devices, own_hidden)
        .transpose(1, 0, 2)
        .reshape(devices, own_rows * own_hidden)
    )
    pooled_blocks = (
        own_pooled.reshape(own_images * pairs, devices, own_rows)
        .transpose(1, 0, 2)
        .reshape(devices, own_images * pairs * own_rows)
    )
    received = exchange(jnp.concatenate([up_blocks, pooled_blocks], 1))
    up_own = received[:, : own_rows * own_hidden].reshape(D, own_hidden)
    pooled_own = received[:, own_rows * own_hidden :].reshape(all_images, 2, HEADS, own_rows)

    full_value = gathered_late[:, :D]
    full_out = gathered_late[:, D : 2 * D]
    full_heads = gathered_late[:, 2 * D :]
    mixed = matmul(own_pooled.reshape(own_images * pairs, D), full_value)
    attended = jnp.sum(
        jnp.where(head_mask, mixed.reshape(own_images * 2, HEADS, D), 0.0), 1
    ) + vectors[6]
    attended = attended.astype(low)
    rows = all_images * 2
    attended = gather_blocks(attended).reshape(rows, D)
    keep_float = metas[:, 8:10] * DROP_SCALE
    keep_rows = jnp.repeat(keep_float, 2, axis=0)
    keep_first = keep_rows[:, 0:1]
    keep_second = keep_rows[:, 1:2]
    middle = jnp.tile(tokens, (all_images, 1)) + keep_first * (
        matmul(attended, full_out) + vectors[7]
    )
    second_out, second_normed, second_inverse = norm_forward(middle, vectors[8], vectors[9])
    second_low = second_out.astype(low)
    hidden_bias = lax.dynamic_slice_in_dim(small_long, device * own_hidden, own_hidden, 0)
    hidden = matmul(second_low, up_own) + hidden_bias
    activated, gelu_slope = gelu_parts(hidden)
    activated = activated.astype(low)
    down_low = down_weight.astype(low)
    mlp_partial = matmul(activated, down_low).astype(low)
    row_share = own_images * 2
    mlp_own = jnp.sum(
        exchange(mlp_partial.reshape(devices, row_share, D)).astype(f32), 0
    )
    mlp_rows = gather_blocks(mlp_own.astype(low)).reshape(rows, D).astype(f32)
    result = middle + keep_second * (mlp_rows + vectors[10])

    head_out, head_normed, head_inverse = norm_forward(result, vectors[11], vectors[12])
    head_low = head_out.astype(low).reshape(all_images, 2, D)
    logits_class = matmul(head_low[:, 0], full_heads[:, :CLS]) + small_long[FF : FF + CLS]
    logits_distill = matmul(head_low[:, 1], full_heads[:, CLS:]) + small_long[FF + CLS :]
    columns = lax.broadcasted_iota(jnp.int32, (1, CLS), 1)
    labels = (metas[:, 0:3] * 32.0 + metas[:, 3:6]).astype(jnp.int32)
    share = metas[:, 6:7] / 16.0
    weights = metas[:, 7]
    weight_sum = jnp.sum(weights)
    target = share * (labels[:, 0:1] == columns).astype(f32) + (1.0 - share) * (
        labels[:, 1:2] == columns
    ).astype(f32)
    teacher = (labels[:, 2:3] == columns).astype(f32)
    log_class = jax.nn.log_softmax(logits_class, -1)
    log_distill = jax.nn.log_softmax(logits_distill, -1)
    terms = -0.5 * (jnp.sum(target * log_class, -1) + jnp.sum(teacher * log_distill, -1))
    loss = jnp.sum(weights * terms) / weight_sum
    scale_rows = (weights * 0.5 / weight_sum)[:, None]
    grad_class = (scale_rows * (jnp.exp(log_class) - target)).astype(low)
    grad_distill = (scale_rows * (jnp.exp(log_distill) - teacher)).astype(low)
    head_own = matmul_nt(select_own, head_low.reshape(rows, D)).astype(low)
    head_own = head_own.reshape(own_rows, all_images, 2)
    owned_heads = jnp.concatenate(
        [matmul(head_own[:, :, 0], grad_class), matmul(head_own[:, :, 1], grad_distill)], 1
    )
    head_bias = jnp.concatenate(
        [jnp.sum(grad_class.astype(f32), 0), jnp.sum(grad_distill.astype(f32), 0)]
    )
    grad_head_rows = jnp.stack(
        [matmul_nt(grad_class, full_heads[:, :CLS]), matmul_nt(grad_distill, full_heads[:, CLS:])],
        1,
    ).reshape(rows, D)
    grad_result, final_gain, final_shift = norm_backward(
        grad_head_rows, head_normed, head_inverse, vectors[11]
    )

    grad_mlp = (keep_second * grad_result).astype(low)
    owned_down = matmul_tn(activated, grad_mlp)
    down_bias = jnp.sum(grad_mlp.astype(f32), 0)
    grad_hidden = (matmul_nt(grad_mlp, down_low) * gelu_slope).astype(low)
    up_bias = jnp.sum(grad_hidden.astype(f32), 0)
    grad_up = matmul_tn(second_low, grad_hidden).astype(low)
    grad_second_partial = matmul_nt(grad_hidden, up_own).astype(low)
    received = exchange(
        jnp.concatenate(
            [
                grad_second_partial.reshape(devices, row_share * D),
                grad_up.reshape(devices, own_rows * own_hidden),
            ],
            1,
        )
    )
    grad_second = jnp.sum(
        received[:, : row_share * D].astype(f32).reshape(devices, row_share, D), 0
    )
    owned_up = (
        received[:, row_share * D :]
        .reshape(devices, own_rows, own_hidden)
        .transpose(1, 0, 2)
        .reshape(own_rows, FF)
        .astype(f32)
    )
    row_start = device * row_share
    own_normed = lax.dynamic_slice_in_dim(second_normed, row_start, row_share, 0)
    own_inverse = lax.dynamic_slice_in_dim(second_inverse, row_start, row_share, 0)
    own_result = lax.dynamic_slice_in_dim(grad_result, row_start, row_share, 0)
    own_keep = lax.dynamic_slice_in_dim(keep_first, row_start, row_share, 0)
    grad_second_in, second_gain, second_shift = norm_backward(
        grad_second, own_normed, own_inverse, vectors[8]
    )
    grad_middle = own_result + grad_second_in
    grad_attn_own = (own_keep * grad_middle).astype(low)
    out_bias = jnp.sum(grad_attn_own.astype(f32), 0)
    grad_attn = join_cores(grad_attn_own, seq_index, 0).reshape(images * 2, D)
    grad_att = matmul_nt(grad_attn, full_out).astype(low)
    value_bias = jnp.sum(
        lax.dynamic_slice_in_dim(grad_att, seq_index * row_share, row_share, 0).astype(f32), 0
    )
    grad_att_blocks = jnp.where(
        head_mask, grad_att.reshape(images * 2, 1, D), jnp.zeros((), low)
    ).reshape(images * pairs, D)
    value_vectors = matmul_nt(grad_att_blocks, full_value).astype(low)
    value_const = jnp.sum(grad_att_blocks.astype(f32) * vectors[6], -1).reshape(images, pairs)
    value_vectors = value_vectors.reshape(images, pairs, D)
    mean_grad = jnp.sum(pooled * value_vectors.astype(f32), -1) + value_const
    grad_probs = (
        jnp.einsum("nld,nmd->nlm", first_low, value_vectors, preferred_element_type=f32)
        + value_const[:, None, :]
    )
    grad_scores = (probs * (grad_probs - mean_grad[:, None, :])).astype(low)
    key_rows = jnp.broadcast_to(key_vectors.T[None], (images, pairs, D))
    grad_first = jnp.einsum(
        "nlk,nkd->nld",
        jnp.concatenate([grad_scores, probs.astype(low)], 2),
        jnp.concatenate([key_rows, value_vectors], 1),
        preferred_element_type=f32,
    )
    grad_stream, first_gain, first_shift = norm_backward(
        grad_first, first_normed, first_inverse, vectors[3]
    )
    pooled_grad = matmul_tn(grad_scores.reshape(row_count, pairs), flat_first)
    query_grad_blocks = matmul(pooled_grad.astype(low), gathered_query_key[:, D:]) * HD ** (-0.5)
    grad_query = jnp.sum(
        jnp.where(head_mask, query_grad_blocks.reshape(2, HEADS, D), 0.0), 1
    )
    token_grad = matmul_nt(grad_query.astype(low), gathered_query_key[:, :D])
    token_grad_in, token_gain, token_shift = norm_backward(
        token_grad, token_normed, token_inverse, vectors[3]
    )
    grad_tokens = (
        token_grad_in
        + jnp.sum(grad_middle.reshape(own_images, 2, D), 0)
        + jnp.stack(
            [
                jnp.sum(jnp.where(is_class, grad_stream, 0.0), (0, 1)),
                jnp.sum(jnp.where(is_distill, grad_stream, 0.0), (0, 1)),
            ]
        )
    )
    grad_embed = jnp.where(special, 0.0, grad_stream)
    embed_low = grad_embed.astype(low).reshape(row_count, D)
    grad_patch = matmul_tn(flat_patches, embed_low)
    grad_table = matmul_tn(onehot_pos, embed_low)
    patch_bias = jnp.sum(grad_embed, (0, 1))
    leader = (device == 0).astype(f32)
    small_terms = jnp.concatenate(
        [
            grad_tokens,
            grad_table[2:],
            patch_bias[None],
            grad_tokens,
            (first_gain + token_gain)[None],
            (first_shift + token_shift)[None],
            jnp.sum(grad_query, 0)[None],
            value_bias[None],
            out_bias[None],
            second_gain[None],
            second_shift[None],
            leader * down_bias[None],
            leader * final_gain[None],
            leader * final_shift[None],
        ],
        0,
    )
    small_count = POS + 13
    small_share = -(-small_count // devices)
    small_terms = jnp.pad(small_terms, ((0, small_share * devices - small_count), (0, 0)))

    key_terms = (
        pooled_grad.reshape(pairs, devices, own_rows)
        .transpose(1, 0, 2)
        .reshape(devices, pairs * own_rows)
    )
    key_share = -(-pairs * own_rows // D)
    key_terms = jnp.pad(key_terms, ((0, 0), (0, key_share * D - pairs * own_rows)))
    terms_rows = jnp.concatenate(
        [
            grad_patch.reshape(dp_size, seq_size, own_rows, D),
            small_terms.reshape(dp_size, seq_size, small_share, D),
            key_terms.reshape(dp_size, seq_size, key_share, D),
            jnp.broadcast_to(grad_query, (dp_size, seq_size, 2, D)),
        ],
        2,
    )
    mine = lax.dynamic_index_in_dim(terms_rows, seq_index, 1, keepdims=False)
    theirs = lax.dynamic_index_in_dim(terms_rows, 1 - seq_index, 1, keepdims=False)
    chip_terms = mine + swap_cores(theirs.astype(low)).astype(f32)
    pair_share = 2 * row_share
    grad_att_own = lax.dynamic_slice_in_dim(grad_att, seq_index * row_share, row_share, 0)
    pair_own = jnp.concatenate([grad_attn_own, grad_att_own], 0)
    sent = jnp.concatenate(
        [chip_terms.astype(low), jnp.broadcast_to(pair_own, (dp_size, pair_share, D))], 1
    )
    received = exchange(sent, "dp")
    summed_share = chip_terms.shape[1]
    reduced = jnp.sum(received[:, :summed_share].astype(f32), 0)
    pair_rows = join_cores(received[:, summed_share:], seq_index, 1)
    pair_rows = pair_rows.reshape(devices, 2, row_share, D)
    owned_patch = reduced[:own_rows]
    owned_small = reduced[own_rows : own_rows + small_share]
    key_start = own_rows + small_share
    key_reduced = reduced[key_start : key_start + key_share].reshape(-1)[: pairs * own_rows]
    key_reduced = key_reduced.reshape(2, HEADS, own_rows)
    query_reduced = reduced[key_start + key_share :]

    owned_query = matmul_tn(token_own, query_reduced.astype(low))
    key_left = jnp.repeat(
        key_reduced.transpose(2, 0, 1), HD, axis=2
    )
    owned_key = jnp.sum(key_left * query_low.astype(f32)[None], 1) * HD ** (-0.5)
    grad_attn_rows = pair_rows[:, 0].reshape(rows, D)
    grad_att_rows = pair_rows[:, 1].reshape(all_images, 2, HEADS, HD)
    owned_value = jnp.einsum(
        "nihd,nihc->dhc", pooled_own, grad_att_rows, preferred_element_type=f32
    ).reshape(own_rows, D)
    attended_own = matmul_nt(select_own, attended).astype(low)
    owned_out = matmul(attended_own, grad_attn_rows)
    owned_block = jnp.concatenate([owned_query, owned_key, owned_value, owned_out, owned_up], 1)

    shard_square = (
        jnp.sum(owned_patch * owned_patch)
        + jnp.sum(owned_block * owned_block)
        + jnp.sum(owned_down * owned_down)
        + jnp.sum(owned_heads * owned_heads)
        + jnp.sum(owned_small * owned_small)
        + jnp.sum(up_bias * up_bias)
    )
    square_high, square_rest = split_low(shard_square)
    square_rest, square_last = split_low(shard_square - square_high.astype(f32))
    tail_row = jnp.concatenate(
        [
            jnp.stack([square_high, square_rest, square_last]),
            up_bias.astype(low),
            jnp.zeros((D - 3 - own_hidden,), low),
        ]
    )
    final = gather_blocks(
        jnp.concatenate([owned_small.astype(low), tail_row[None]], 0), "dp"
    ).reshape(dp_size, small_share + 1, D)
    final = join_cores(final, seq_index, 1).reshape(devices, small_share + 1, D)
    summed_rows = final[:, :small_share].astype(f32).reshape(devices * small_share, D)[:small_count]
    global_square = jnp.sum(final[:, small_share, 0:3].astype(f32))
    up_bias_all = final[:, small_share, 3 : 3 + own_hidden].astype(f32).reshape(FF)
    summed_long = jnp.concatenate([up_bias_all, head_bias])
    total_square = global_square + jnp.sum(head_bias * head_bias)
    grad_norm = jnp.sqrt(total_square)
    factor = jnp.minimum(1.0, CLIP_NORM / (grad_norm + 1e-06))
    vectors_grad = factor * summed_rows[POS:]
    patch_new, patch_mean_new, patch_square_new = adam_update(
        patch_weight, patch_mean, patch_square, owned_patch, factor, DECAY_RATE, LEARN_RATE
    )
    block_new, block_mean_new, block_square_new = adam_update(
        block_weight, block_mean, block_square, owned_block, factor, DECAY_RATE, LEARN_RATE
    )
    down_new, down_mean_new, down_square_new = adam_update(
        down_weight, down_mean, down_square, owned_down, factor, DECAY_RATE, LEARN_RATE
    )
    heads_new, heads_mean_new, heads_square_new = adam_update(
        heads_weight, heads_mean, heads_square, owned_heads, factor, DECAY_RATE, LEARN_RATE
    )
    rows_new, rows_mean_new, rows_square_new = adam_update(
        small_rows, rows_mean, rows_square, summed_rows, factor, 0.0, SMALL_RATE
    )
    long_new, long_mean_new, long_square_new = adam_update(
        small_long, long_mean, long_square, summed_long, factor, 0.0, SMALL_RATE
    )
    return (
        loss,
        grad_norm,
        patch_new,
        patch_mean_new,
        patch_square_new,
        block_new,
        block_mean_new,
        block_square_new,
        down_new,
        down_mean_new,
        down_square_new,
        heads_new,
        heads_mean_new,
        heads_square_new,
        rows_new,
        rows_mean_new,
        rows_square_new,
        long_new,
        long_mean_new,
        long_square_new,
        vectors_grad,
    )


def tiles(arguments):
    patches, patch_weight = arguments[0], arguments[7]
    images, local_slots, _ = patches.shape
    return images * PAIR == 128 and (images * local_slots) % CHUNK == 0 and patch_weight.shape[0] == 24


def shards(*arguments):
    return (shards_tiled if tiles(arguments) else shards_plain)(*arguments)


def solution(mesh):
    placed = (
        P("dp", "seq", None),
        P("dp", "seq"),
        P("dp"),
        P("dp", None),
        P("dp"),
        P("dp"),
        P("dp", None),
        P(("dp", "seq"), None),
        P(("dp", "seq"), None),
        P(("dp", "seq"), None),
        P(("dp", "seq"), None),
        P(("dp", "seq"), None),
        P(("dp", "seq"), None),
        P(("dp", "seq"), None),
        P(("dp", "seq"), None),
        P(("dp", "seq"), None),
        P(("dp", "seq"), None),
        P(("dp", "seq"), None),
        P(("dp", "seq"), None),
        P(),
        P(),
        P(),
        P(),
        P(),
        P(),
    )
    return jax.shard_map(
        shards,
        mesh=mesh,
        in_specs=placed,
        out_specs=(
            P(),
            P(),
            P(("dp", "seq"), None),
            P(("dp", "seq"), None),
            P(("dp", "seq"), None),
            P(("dp", "seq"), None),
            P(("dp", "seq"), None),
            P(("dp", "seq"), None),
            P(("dp", "seq"), None),
            P(("dp", "seq"), None),
            P(("dp", "seq"), None),
            P(("dp", "seq"), None),
            P(("dp", "seq"), None),
            P(("dp", "seq"), None),
            P(),
            P(),
            P(),
            P(),
            P(),
            P(),
            P(),
        ),
        check_vma=False,
    )
```

```python
import math

import jax
import jax.numpy as jnp
from jax import lax
from jax.experimental import pallas as pl
from jax.experimental.pallas import tpu as pltpu
from jax.sharding import PartitionSpec as P

D = 768
HEADS = 12
HD = 64
FF = 3072
CLS = 1000
POS = 198
STEP = 7


NORM_EPS = 1e-06
DROP_SCALE = 1.0 / 0.9
CLIP_NORM = 0.02
LEARN_RATE = 0.02
SMALL_RATE = 0.15
BETA_FIRST = 0.9
BETA_SECOND = 0.999
ADAM_EPS = 1e-08
DECAY_RATE = 0.05
MASK_FILL = -1e30
highest = lax.Precision.HIGHEST


def matmul(left, right):
    return jnp.dot(left, right, preferred_element_type=jnp.float32)


def matmul_tn(left, right):
    return lax.dot_general(
        left, right, (((0,), (0,)), ((), ())), preferred_element_type=jnp.float32
    )


def matmul_nt(left, right):
    return lax.dot_general(
        left, right, (((1,), (1,)), ((), ())), preferred_element_type=jnp.float32
    )


def norm_forward(values, gain, shift):
    centered = values - jnp.mean(values, -1, keepdims=True)
    inverse = lax.rsqrt(jnp.mean(centered * centered, -1, keepdims=True) + NORM_EPS)
    normed = centered * inverse
    return (normed * gain + shift, normed, inverse)


def norm_backward(grad_out, normed, inverse, gain):
    scaled = grad_out * gain
    grad_in = inverse * (
        scaled
        - jnp.mean(scaled, -1, keepdims=True)
        - normed * jnp.mean(scaled * normed, -1, keepdims=True)
    )
    leading = tuple(range(grad_out.ndim - 1))
    return (grad_in, jnp.sum(grad_out * normed, leading), jnp.sum(grad_out, leading))


def gelu_parts(values):
    cumulative = 0.5 * (1.0 + jax.scipy.special.erf(values * 0.7071067811865476))
    density = 0.3989422804014327 * jnp.exp(-0.5 * values * values)
    return (values * cumulative, cumulative + values * density)


def adam_update(weight, first, second, gradient, factor, decay, rate):
    clipped = gradient * factor
    first_new = BETA_FIRST * first + (1.0 - BETA_FIRST) * clipped
    second_new = BETA_SECOND * second + (1.0 - BETA_SECOND) * clipped * clipped
    first_hat = first_new / (1.0 - BETA_FIRST**STEP)
    second_hat = second_new / (1.0 - BETA_SECOND**STEP)
    weight_new = weight - rate * (first_hat / (jnp.sqrt(second_hat) + ADAM_EPS) + decay * weight)
    return (weight_new, first_new, second_new)


ALL = ("dp", "seq")


def exchange(blocks, axes=ALL):
    return lax.all_to_all(blocks, axes, 0, 0, tiled=True)


def gather_blocks(block, axes=ALL):
    count = lax.axis_size(axes)
    return exchange(jnp.broadcast_to(block[None], (count,) + block.shape), axes)


def swap_cores(value):
    return lax.ppermute(value, "seq", [(0, 1), (1, 0)])


def join_cores(value, seq_index, axis):
    other = swap_cores(value)
    first = jnp.where(seq_index == 0, value, other)
    second = jnp.where(seq_index == 0, other, value)
    return jnp.stack([first, second], axis)


def split_low(value):
    high = value.astype(jnp.bfloat16)
    rest = (value - high.astype(jnp.float32)).astype(jnp.bfloat16)
    return high, rest


PADDED = 16
PAIR = 2 * PADDED
CHUNK = 112


class Fetched:
    def __init__(self, value, source, semaphore, columns):
        if columns is not None:
            source = source.at[(slice(None),) * (len(source.shape) - 1) + (columns,)]
        self.copy = pltpu.make_async_copy(source, value, semaphore)
        self.value = value
        self.copy.start()
        self.waiting = True

    def ready(self):
        if self.waiting:
            self.copy.wait()
            self.waiting = False

    @property
    def shape(self):
        return self.value.shape

    @property
    def dtype(self):
        return self.value.dtype

    def __getitem__(self, index):
        self.ready()
        return self.value[index]


class Stored:
    def __init__(self, value, out, semaphore):
        self.copy = pltpu.make_async_copy(value, out, semaphore)
        self.value = value
        self.sent = False

    def send(self):
        if not self.sent:
            self.copy.start()
            self.sent = True

    @property
    def shape(self):
        return self.value.shape

    @property
    def dtype(self):
        return self.value.dtype

    def __getitem__(self, index):
        return self.value[index]

    def __setitem__(self, index, value):
        self.value[index] = value


def ready(*operands):
    for operand in operands:
        operand.ready()


def kernel_call(body, outputs, inputs, windows=None, scratch=(), flops=1_000_000, limit=48, loose=(), near=()):
    windows = windows or {}
    places, buffers = [], []
    moved = 0
    for position, value in enumerate(inputs):
        if value.ndim == 1:
            places.append(pl.BlockSpec(memory_space=pltpu.SMEM))
            continue
        if position in near:
            places.append(pl.BlockSpec(memory_space=pltpu.VMEM))
            continue
        places.append(pl.BlockSpec(memory_space=pltpu.HBM))
        shape = value.shape
        if position in windows:
            shape = shape[:-1] + (windows[position].stop - windows[position].start,)
        buffers.append(pltpu.VMEM(shape, value.dtype))
        moved += math.prod(shape) * value.dtype.itemsize
    moved += sum(math.prod(shape) * jnp.dtype(kind).itemsize for shape, kind in outputs)
    fetches = len(buffers)
    buffers += [pltpu.VMEM(shape, kind) for shape, kind in outputs]
    buffers += [pltpu.SemaphoreType.DMA((fetches + len(outputs),))]

    def run(*refs):
        ins, refs = refs[: len(inputs)], refs[len(inputs) :]
        outs, refs = refs[: len(outputs)], refs[len(outputs) :]
        stores, copies, semaphores = refs[fetches:][: len(outputs)], refs[:fetches], None
        semaphores = refs[fetches + len(outputs)]
        rest = refs[fetches + len(outputs) + 1 :]
        operands, used = [], 0
        for position, (value, ref) in enumerate(zip(inputs, ins)):
            if value.ndim == 1 or position in near:
                operands.append(ref)
                continue
            operands.append(
                Fetched(copies[used], ref, semaphores.at[used], windows.get(position))
            )
            used += 1
        stores = [
            Stored(store, out, semaphores.at[fetches + index])
            for index, (store, out) in enumerate(zip(stores, outs))
        ]
        body(*operands, *stores, *rest)
        ready(*[operand for operand in operands if isinstance(operand, Fetched)])
        for store in stores:
            store.send()
        for store in stores:
            store.copy.wait()

    return pl.pallas_call(
        run,
        name=body.__name__,
        in_specs=places,
        out_specs=[pl.BlockSpec(memory_space=pltpu.HBM) for _ in outputs],
        out_shape=[pltpu.HBM(shape, kind) for shape, kind in outputs],
        scratch_shapes=buffers + list(scratch),
        cost_estimate=pl.CostEstimate(flops=flops, bytes_accessed=moved, transcendentals=0),
        compiler_params=pltpu.CompilerParams(vmem_limit_bytes=limit * 1024 * 1024),
    )(
        *[
            value
            if value.ndim == 1 or position in loose or position in near
            else pltpu.with_memory_space_constraint(value, pltpu.HBM)
            for position, value in enumerate(inputs)
        ]
    )


def iota(shape, axis):
    return lax.broadcasted_iota(jnp.int32, shape, axis)


def own_selector(device, count):
    return jnp.where(
        iota((count, D), 0) + device * count == iota((count, D), 1), 1.0, 0.0
    ).astype(jnp.bfloat16)


def pair_mask(rows):
    return (iota((rows, D), 0) & (PADDED - 1)) == (iota((rows, D), 1) >> 6)


def token_rows(small_ref):
    tokens = small_ref[POS + 1 : POS + 3, :] + small_ref[0:2, :]
    return jnp.concatenate([tokens, jnp.zeros((6, D), jnp.float32)], 0)


def vector(small_ref, index):
    return small_ref[POS + index : POS + index + 1, :]


def norm_in(grad_out, normed, inverse, gain):
    scaled = grad_out * gain
    return inverse * (
        scaled
        - jnp.mean(scaled, -1, keepdims=True)
        - normed * jnp.mean(scaled * normed, -1, keepdims=True)
    )


def spread_pairs(values):
    count = values.shape[0]
    spread = jnp.broadcast_to(values[:, None, :], (count, PADDED, D)).reshape(count * PADDED, D)
    return jnp.where(pair_mask(count * PADDED), spread, 0.0)


def collect_pairs(values):
    count = values.shape[0] // PADDED
    kept = jnp.where(pair_mask(values.shape[0]), values, 0.0)
    return jnp.sum(kept.reshape(count, PADDED, D), 1)


def late_kernel(value_out_ref, heads_ref, late_ref):
    low = jnp.bfloat16
    late_ref[:, 0 : 2 * D] = value_out_ref[...].astype(low)
    late_ref[:, 2 * D :] = jnp.zeros((late_ref.shape[0], 2048), low)
    late_ref[:, 2 * D : 2 * D + CLS] = heads_ref[:, 0:CLS].astype(low)
    late_ref[:, 2 * D + 1024 : 2 * D + 1024 + CLS] = heads_ref[:, CLS:].astype(low)


def prepare_kernel(
    device_ref, small_ref, query_weight_ref, patch_ref, first_ref, last_ref
):
    low = jnp.bfloat16
    own = patch_ref.shape[0]
    last_ref[...] = query_weight_ref[...].astype(low)
    query_weight = query_weight_ref[...].astype(low)
    token_out, _, _ = norm_forward(token_rows(small_ref), vector(small_ref, 3), vector(small_ref, 4))
    token_own = matmul_nt(token_out.astype(low), own_selector(device_ref[0], own))
    partial = matmul(token_own.astype(low), query_weight)
    high, rest = split_low(partial)
    pieces = [
        part[i : i + 1, 128 * j : 128 * (j + 1)].astype(jnp.float32)
        for part in (high, rest)
        for i in range(2)
        for j in range(D // 128)
    ]
    block = jnp.concatenate(
        [patch_ref[...], jnp.concatenate(pieces, 0)], 1
    ).astype(low)
    first_ref[...] = jnp.broadcast_to(block[None], first_ref.shape)


def query_kernel(
    own_ref, other_ref, key_weight_ref, up_ref, small_ref, meta_ref,
    out_ref, query_ref,
):
    total = jnp.sum(own_ref[...].astype(jnp.float32), 0) + jnp.sum(
        other_ref[...].astype(jnp.float32), 0
    )
    count = D // 128
    both = total[0 : 2 * count] + total[2 * count :]
    query = jnp.concatenate(
        [
            jnp.concatenate([both[i * count + j : i * count + j + 1] for j in range(count)], 1)
            for i in range(2)
        ],
        0,
    ) + vector(small_ref, 5)
    query = query.astype(jnp.bfloat16).astype(jnp.float32)
    blocks = spread_pairs(jnp.concatenate([query] * 4, 0))
    query_ref[...] = blocks[:PAIR]
    keys = matmul_nt(key_weight_ref[...].astype(jnp.bfloat16), blocks.astype(jnp.bfloat16))
    keys = keys * HD ** (-0.5)
    up = up_ref[...]
    width = up.shape[1] // out_ref.shape[0]
    for block in range(out_ref.shape[0]):
        out_ref[block] = jnp.concatenate(
            [keys, up[:, block * width : (block + 1) * width], meta_ref[...]], 1
        ).astype(jnp.bfloat16)


def row_ids(start, rows, images, local_slots, seq_index):
    ids = iota((rows, 1), 0) + start
    shift = images.bit_length() - 1
    return ids & (images - 1), (ids >> shift) + seq_index * local_slots


def join_weights(seq_index, own_ref, other_ref, weights):
    count = own_ref.shape[1]
    first_core = seq_index == 0
    for block in range(own_ref.shape[0]):
        here = own_ref[block].astype(jnp.float32)
        there = other_ref[block].astype(jnp.float32)
        start = block * 2 * count
        weights[start : start + count, :] = jnp.where(first_core, here, there).astype(jnp.bfloat16)
        weights[start + count : start + 2 * count, :] = jnp.where(first_core, there, here).astype(
            jnp.bfloat16
        )


def embed_kernel(
    seq_ref, own_ref, other_ref, patches_ref, pos_ref, small_ref,
    first_ref, normed_ref, inverse_ref, weights, high, rest,
):
    row_count = patches_ref.shape[0]
    images = 128 // PAIR
    local_slots = row_count // images
    seq_index = seq_ref[0]
    join_weights(seq_index, own_ref, other_ref, weights)
    tokens = token_rows(small_ref)
    table_high, table_rest = split_low(small_ref[0:POS, :])
    high[...] = table_high
    rest[...] = table_rest
    ready(patches_ref, pos_ref, small_ref)

    def step(index, carry):
        rows = pl.ds(pl.multiple_of(index * CHUNK, CHUNK), CHUNK)
        onehot = jnp.where(pos_ref[rows, :] == iota((CHUNK, POS), 1), 1.0, 0.0).astype(jnp.bfloat16)
        embedded = (
            matmul(patches_ref[rows, :], weights[...])
            + matmul(onehot, high[...])
            + matmul(onehot, rest[...])
            + vector(small_ref, 0)
        )
        _, slot = row_ids(index * CHUNK, CHUNK, images, local_slots, seq_index)
        stream = jnp.where(slot == 0, tokens[0:1], jnp.where(slot == 1, tokens[1:2], embedded))
        out, normed, inverse = norm_forward(stream, vector(small_ref, 3), vector(small_ref, 4))
        first_ref[rows, :] = out.astype(jnp.bfloat16)
        normed_ref[rows, :] = normed
        inverse_ref[rows, :] = inverse
        return carry

    lax.fori_loop(0, row_count // CHUNK, step, 0)


def scores_kernel(
    seq_ref, own_ref, other_ref, first_ref, valid_ref,
    packed_ref, exponent_ref, keys_ref, up_ref,
):
    row_count, columns = exponent_ref.shape
    images = columns // PAIR
    seq_index = seq_ref[0]
    first_core = seq_index == 0
    count = own_ref.shape[1]
    hidden = up_ref.shape[1]
    for block in range(own_ref.shape[0]):
        here = own_ref[block].astype(jnp.float32)
        there = other_ref[block].astype(jnp.float32)
        start = block * 2 * count
        for core, pick in enumerate(
            (jnp.where(first_core, here, there), jnp.where(first_core, there, here))
        ):
            place = slice(start + core * count, start + (core + 1) * count)
            keys_ref[place, :] = pick[:, 0:columns].astype(jnp.bfloat16)
            up_ref[place, :] = jnp.where(
                first_core,
                pick[:, columns : columns + hidden],
                pick[:, columns + hidden : columns + 2 * hidden],
            ).astype(jnp.bfloat16)
    scores = matmul(first_ref[...], keys_ref[...])
    image, slot = row_ids(0, row_count, images, row_count // images, seq_index)
    kept = ((iota((row_count, columns), 1) >> 5) == image) & (slot < valid_ref[...])
    scores = jnp.where(kept, scores, MASK_FILL)
    peak = jnp.max(scores, 0, keepdims=True)
    exponent = jnp.exp(scores - peak)
    exponent_ref[...] = exponent
    packed_ref[0:columns, :] = matmul_tn(exponent.astype(jnp.bfloat16), first_ref[...])
    packed_ref[columns : columns + 8, :] = jnp.zeros((8, D), jnp.float32)
    packed_ref[columns : columns + 1, 0:columns] = peak
    packed_ref[columns + 1 : columns + 2, 0:columns] = jnp.sum(exponent, 0, keepdims=True)


def attend_kernel(
    seq_ref, own_ref, other_ref, value_weight_ref, small_ref, pooled_ref, scale_ref, out_ref, turned
):
    columns = pooled_ref.shape[0]
    peak_here = own_ref[columns : columns + 1, 0:columns]
    peak_there = other_ref[columns : columns + 1, 0:columns]
    peak = jnp.maximum(peak_here, peak_there)
    here = jnp.exp(peak_here - peak)
    there = jnp.exp(peak_there - peak)
    total = (
        here * own_ref[columns + 1 : columns + 2, 0:columns]
        + there * other_ref[columns + 1 : columns + 2, 0:columns]
    )
    here = here / total
    there = there / total
    scale_ref[...] = jnp.broadcast_to(here, (8, columns))
    here_rows = jnp.broadcast_to(here, (columns, columns)).T[:, 0:1]
    there_rows = jnp.broadcast_to(there, (columns, columns)).T[:, 0:1]
    pooled = own_ref[0:columns, :] * here_rows + other_ref[0:columns, :] * there_rows
    pooled_ref[...] = pooled
    mixed = matmul(pooled.astype(jnp.bfloat16), value_weight_ref[...])
    attended = collect_pairs(mixed) + vector(small_ref, 6)
    turned[...] = pooled.T
    own = 2 * HEADS
    for block in range(out_ref.shape[0]):
        start = pl.multiple_of(block * 2 * own + seq_ref[0] * own, 8)
        mine = turned[pl.ds(start, own), :]
        pieces = [mine[8 * j : 8 * (j + 1)] for j in range(own // 8)]
        out_ref[block] = jnp.concatenate([attended] + pieces, 1).astype(jnp.bfloat16)


def odd_row(shape):
    return (iota(shape, 0) & 1) == 1


def mlp_kernel(
    device_ref, attended_ref, out_weight_ref, up_ref, down_ref, small_ref, info_ref, bias_ref,
    partial_ref, second_ref, normed_ref, inverse_ref, slope_ref, act_ref, middle_ref, turned_ref,
):
    attended = attended_ref[...].astype(jnp.float32)
    attended = attended.reshape(info_ref.shape[0], D).astype(jnp.bfloat16)
    own = turned_ref.shape[0]
    turned_ref[...] = matmul_nt(own_selector(device_ref[0], own), attended).astype(jnp.bfloat16)
    tokens = token_rows(small_ref)
    stream = jnp.where(odd_row(attended.shape), tokens[1:2], tokens[0:1])
    middle = stream + info_ref[:, 5:6] * (
        matmul(attended, out_weight_ref[...]) + vector(small_ref, 7)
    )
    middle_ref[...] = middle
    out, normed, inverse = norm_forward(middle, vector(small_ref, 8), vector(small_ref, 9))
    second = out.astype(jnp.bfloat16)
    second_ref[...] = second
    normed_ref[...] = normed
    inverse_ref[...] = inverse
    hidden = matmul(second, up_ref[...]) + bias_ref[...]
    act, slope = gelu_parts(hidden)
    act = act.astype(jnp.bfloat16)
    act_ref[...] = act
    slope_ref[...] = slope
    partial_ref[...] = matmul(act, down_ref[...].astype(jnp.bfloat16)).astype(jnp.bfloat16)


def heads_kernel(
    device_ref, mlp_ref, middle_ref, info_ref, small_ref,
    late_ref, bias_ref,
    act_ref, slope_ref, second_ref, up_ref, down_ref,
    partial_ref, result_ref, heads_ref, sums_ref, bias_out_ref, down_out_ref, up_bias_ref, loss_ref,
):
    rows = mlp_ref.shape[0]
    half = 512
    low = jnp.bfloat16
    result = middle_ref[...] + info_ref[:, 6:7] * (
        mlp_ref[...].astype(jnp.float32) + vector(small_ref, 10)
    )
    out, normed, inverse = norm_forward(result, vector(small_ref, 11), vector(small_ref, 12))
    head = out.astype(low)
    columns = iota((rows, half), 1)
    odd = odd_row((rows, half))
    left, right, share_a, share_b = (info_ref[:, k : k + 1] for k in range(4))
    weight = info_ref[:, 4:5]
    logits, targets = [], []
    for part in range(2):
        start = part * half
        class_columns = slice(start, start + half)
        distill_columns = slice(1024 + start, 1024 + start + half)
        piece = jnp.where(
            odd,
            matmul(head, late_ref[:, distill_columns]) + bias_ref[1:2, start : start + half],
            matmul(head, late_ref[:, class_columns]) + bias_ref[0:1, start : start + half],
        )
        where = (columns + start).astype(jnp.float32)
        logits.append(jnp.where(columns + start < CLS, piece, MASK_FILL))
        targets.append(
            share_a * jnp.where(where == left, 1.0, 0.0)
            + share_b * jnp.where(where == right, 1.0, 0.0)
        )
    peak = jnp.maximum(
        jnp.max(logits[0], -1, keepdims=True), jnp.max(logits[1], -1, keepdims=True)
    )
    exponents = [jnp.exp(piece - peak) for piece in logits]
    total = jnp.sum(exponents[0], -1, keepdims=True) + jnp.sum(exponents[1], -1, keepdims=True)
    log_total = peak + jnp.log(total)
    weight_sum = 0.5 * jnp.sum(weight, 0, keepdims=True)
    terms = jnp.zeros((rows, 1), jnp.float32)
    for piece, target in zip(logits, targets):
        terms = terms - 0.5 * jnp.sum(
            target * (piece - log_total), -1, keepdims=True
        )
    loss = jnp.sum(weight * terms, 0, keepdims=True) / weight_sum
    loss_ref[...] = jnp.broadcast_to(loss, loss_ref.shape)
    scale = weight * 0.5 / weight_sum
    head_own = matmul_nt(own_selector(device_ref[0], heads_ref.shape[1]), head).astype(low)
    grad_head = jnp.zeros((rows, D), jnp.float32)
    for part in range(2):
        start = part * half
        class_columns = slice(start, start + half)
        distill_columns = slice(1024 + start, 1024 + start + half)
        grad = scale * (exponents[part] / total - targets[part])
        grad = grad.astype(low).astype(jnp.float32)
        for side, weight_columns in ((0, class_columns), (1, distill_columns)):
            mine = jnp.where(odd == (side == 1), grad, 0.0)
            bias_out_ref[side : side + 1, start : start + half] = jnp.sum(mine, 0, keepdims=True)
            mine = mine.astype(low)
            heads_ref[side, :, start : start + half] = matmul(head_own, mine)
            grad_head = grad_head + matmul_nt(mine, late_ref[:, weight_columns])
    grad_result = norm_in(grad_head, normed, inverse, vector(small_ref, 11))
    result_ref[...] = grad_result
    grad_mlp = (info_ref[:, 6:7] * grad_result).astype(low)
    sums_ref[...] = jnp.zeros(sums_ref.shape, jnp.float32)
    sums_ref[0:1, :] = jnp.sum(grad_mlp.astype(jnp.float32), 0, keepdims=True)
    sums_ref[1:2, :] = jnp.sum(grad_head * normed, 0, keepdims=True)
    sums_ref[2:3, :] = jnp.sum(grad_head, 0, keepdims=True)
    down_out_ref[...] = matmul_tn(act_ref[...], grad_mlp)
    grad_hidden = (
        matmul_nt(grad_mlp, down_ref[...].astype(low)) * slope_ref[...]
    ).astype(low)
    up_bias_ref[...] = jnp.broadcast_to(
        jnp.sum(grad_hidden.astype(jnp.float32), 0, keepdims=True), up_bias_ref.shape
    )
    partial = matmul_nt(grad_hidden, up_ref[...])
    grad_up = matmul_tn(second_ref[...], grad_hidden)
    blocks = partial_ref.shape[0]
    per = rows // blocks
    own = D // blocks
    hidden = grad_up.shape[1]
    pad = jnp.zeros((D, 128 - hidden), jnp.float32)
    grad_up = jnp.concatenate([grad_up, pad], 1)
    for block in range(blocks):
        partial_ref[block, 0:per, :] = partial[block * per : (block + 1) * per].astype(low)
        pieces = [
            grad_up[block * own + 8 * j : block * own + 8 * (j + 1)] for j in range(own // 8)
        ]
        partial_ref[block, per : 2 * per, :] = jnp.concatenate(pieces, 1).astype(low)


def back_kernel(
    index_ref, second_ref, other_ref, normed2_ref, inverse2_ref, result_ref, info_ref, small_ref,
    out_weight_ref, value_weight_ref,
    pooled_ref, scale_ref, exponent_ref, first_ref, normed_ref, inverse_ref, keys_ref,
    patches_ref, pos_ref, sums_ref,
    mine_ref, theirs_ref,
    values, turned_keys, embed, scores, onehot, patch_out, small_out, pooled_grad,
):
    low = jnp.bfloat16
    columns = pooled_ref.shape[0]
    images = columns // PAIR
    row_count = patches_ref.shape[0]
    local_slots = row_count // images
    dp_index, seq_index = index_ref[0], index_ref[1]
    per = 2 * images
    own_rows = pl.ds(pl.multiple_of(dp_index * per, 8), per)
    grad_second = second_ref[...] + other_ref[...]
    normed2 = normed2_ref[own_rows, :]
    grad_middle = result_ref[own_rows, :] + norm_in(
        grad_second, normed2, inverse2_ref[own_rows, :], vector(small_ref, 8)
    )
    grad_attn = (info_ref[own_rows, 5:6] * grad_middle).astype(low)
    grad_att = matmul_nt(grad_attn, out_weight_ref[...]).astype(low)
    att_float = grad_att.astype(jnp.float32)
    att_blocks = spread_pairs(att_float)
    value_rows = matmul_nt(att_blocks.astype(low), value_weight_ref[...]).astype(low)
    values[...] = value_rows
    turned_keys[...] = keys_ref[...].astype(jnp.float32).T.astype(low)
    const = jnp.sum(att_blocks * vector(small_ref, 6), -1, keepdims=True)
    mean = jnp.sum(pooled_ref[...] * value_rows.astype(jnp.float32), -1, keepdims=True) + const
    const = jnp.broadcast_to(const, (columns, columns)).T[0:1, :]
    mean = jnp.broadcast_to(mean, (columns, columns)).T[0:1, :]
    gain = vector(small_ref, 3)

    ready(scale_ref, exponent_ref, first_ref, normed_ref, inverse_ref, pos_ref, patches_ref)

    def step(index, sums):
        gain_sum, shift_sum, embed_sum, class_sum, distill_sum = sums
        rows = pl.ds(pl.multiple_of(index * CHUNK, CHUNK), CHUNK)
        first = first_ref[rows, :]
        probs = exponent_ref[rows, :] * scale_ref[0:1, :]
        grad_probs = matmul_nt(first, values[...]) + const
        grad_scores = (probs * (grad_probs - mean)).astype(low)
        scores[rows, :] = grad_scores
        grad_first = matmul(grad_scores, turned_keys[...]) + matmul(probs.astype(low), values[...])
        normed = normed_ref[rows, :]
        grad_stream = norm_in(grad_first, normed, inverse_ref[rows, :], gain)
        _, slot = row_ids(index * CHUNK, CHUNK, images, local_slots, seq_index)
        grad_embed = jnp.where(slot < 2, 0.0, grad_stream)
        embed[rows, :] = grad_embed.astype(low)
        onehot[rows, :] = jnp.where(pos_ref[rows, :] == iota((CHUNK, POS), 1), 1.0, 0.0).astype(low)
        return (
            gain_sum + jnp.sum(grad_first * normed, 0, keepdims=True),
            shift_sum + jnp.sum(grad_first, 0, keepdims=True),
            embed_sum + jnp.sum(grad_embed, 0, keepdims=True),
            class_sum + jnp.sum(jnp.where(slot == 0, grad_stream, 0.0), 0, keepdims=True),
            distill_sum + jnp.sum(jnp.where(slot == 1, grad_stream, 0.0), 0, keepdims=True),
        )

    zero = jnp.zeros((1, D), jnp.float32)
    gain_sum, shift_sum, embed_sum, class_sum, distill_sum = lax.fori_loop(
        0, row_count // CHUNK, step, (zero,) * 5
    )
    patch_out[...] = matmul_tn(patches_ref[...], embed[...])
    small_out[0:POS, :] = matmul_tn(onehot[...], embed[...])
    by_column = matmul_tn(scores[...], first_ref[...])
    by_pair = jnp.sum(by_column.reshape(images, PAIR, D), 0)
    once = jnp.where(seq_index == 0, 1.0, 0.0)
    leader = jnp.where((dp_index == 0) & (seq_index == 0), 1.0, 0.0)
    middle_even = jnp.sum(jnp.where(odd_row((per, D)), 0.0, grad_middle), 0, keepdims=True)
    middle_odd = jnp.sum(jnp.where(odd_row((per, D)), grad_middle, 0.0), 0, keepdims=True)
    class_sum = class_sum + once * middle_even
    distill_sum = distill_sum + once * middle_odd
    small_out[0:1, :] = class_sum
    small_out[1:2, :] = distill_sum
    vector_rows = (
        embed_sum,
        class_sum,
        distill_sum,
        gain_sum,
        shift_sum,
        zero,
        once * jnp.sum(att_float, 0, keepdims=True),
        once * jnp.sum(grad_attn.astype(jnp.float32), 0, keepdims=True),
        once * jnp.sum(grad_second * normed2, 0, keepdims=True),
        once * jnp.sum(grad_second, 0, keepdims=True),
        leader * sums_ref[0:1, :],
        leader * sums_ref[1:2, :],
        leader * sums_ref[2:3, :],
    )
    for index, row in enumerate(vector_rows):
        small_out[POS + index : POS + index + 1, :] = row
    small_count = small_out.shape[0]
    small_out[POS + 13 : small_count, :] = jnp.zeros((small_count - POS - 13, D), jnp.float32)
    pooled_grad[...] = jnp.concatenate([by_pair, jnp.zeros((128 - PAIR, D), jnp.float32)], 0).T
    own = 2 * HEADS
    attn_half = jnp.where(
        seq_index == 0,
        grad_attn[:, : D // 2].astype(jnp.float32),
        grad_attn[:, D // 2 :].astype(jnp.float32),
    )
    share = small_count // (2 * mine_ref.shape[0])
    for block in range(mine_ref.shape[0]):
        for ref, core in ((mine_ref, seq_index), (theirs_ref, 1 - seq_index)):
            start = pl.multiple_of((block * 2 + core) * own, 8)
            ref[block, 0:own, :] = patch_out[pl.ds(start, own), :].astype(ref.dtype)
            small = pl.multiple_of((block * 2 + core) * share, 8)
            ref[block, own : own + share, :] = small_out[pl.ds(small, share), :].astype(ref.dtype)
            keys = pooled_grad[pl.ds(start, own), :]
            pieces = [keys[8 * j : 8 * (j + 1)] for j in range(own // 8)]
            if ref is mine_ref:
                pieces.append(attn_half)
            else:
                pieces.append(jnp.zeros((8, D // 2), jnp.float32))
            ref[block, own + share :, :] = jnp.concatenate(pieces, 1).astype(ref.dtype)


def known_kernel(
    index_ref, up_own_ref, up_other_ref, heads_ref, down_ref, up_bias_ref, up_ref, known_ref
):
    first_core = index_ref[1] == 0
    blocks = up_own_ref.shape[0]
    own = up_ref.shape[0]
    hidden = down_ref.shape[0]
    columns = []
    for block in range(blocks):
        mine = up_own_ref[block].astype(jnp.float32)
        theirs = up_other_ref[block].astype(jnp.float32)
        for pick in (jnp.where(first_core, mine, theirs), jnp.where(first_core, theirs, mine)):
            columns.append(
                jnp.concatenate(
                    [pick[:, 128 * j : 128 * j + hidden] for j in range(own // 8)], 0
                )
            )
    part = jnp.concatenate(columns, 1)
    up_ref[...] = part
    square = jnp.sum(part * part)
    for side in range(2):
        square = square + jnp.sum(heads_ref[side] * heads_ref[side])
    square = square + jnp.sum(down_ref[...] * down_ref[...])
    bias = up_bias_ref[0:1, :]
    known_ref[...] = jnp.broadcast_to(square + jnp.sum(bias * bias), known_ref.shape)


def owned_kernel(
    index_ref, received_ref, other_attn_ref, out_weight_ref, pooled_ref, turned_ref,
    query_ref, key_weight_ref, known_ref, up_bias_ref,
    patch_ref, block_ref, final_ref,
):
    low = jnp.bfloat16
    first_core = index_ref[1] == 0
    blocks = received_ref.shape[0]
    own = patch_ref.shape[0]
    share = final_ref.shape[1]
    half = D // 2
    total = jnp.sum(received_ref[:, :, :half].astype(jnp.float32), 0)
    right = jnp.sum(received_ref[:, : own + share, half:].astype(jnp.float32), 0)
    patch = jnp.concatenate([total[0:own], right[0:own]], 1)
    small = jnp.concatenate([total[own : own + share], right[own : own + share]], 1)
    keys = jnp.concatenate(
        [total[own + share :, 128 * j : 128 * (j + 1)] for j in range(own // 8)], 0
    )
    patch_ref[...] = patch
    row = iota((share, 1), 0) + index_ref[0] * share
    open_row = (row < 2) | ((row > POS) & (row < POS + 6))
    square = jnp.sum(patch * patch) + jnp.sum(jnp.where(open_row, 0.0, small * small))
    key_high, key_rest = split_low(keys[:, 0:PAIR])
    query_blocks = query_ref[...].astype(low)
    part = (matmul(key_high, query_blocks) + matmul(key_rest, query_blocks)) * HD ** (-0.5)
    block_ref[:, 0:D] = part
    square = square + jnp.sum(part * part)
    key_weight = key_weight_ref[...].astype(low)
    query_sums = collect_pairs(
        matmul_tn(key_high, key_weight) + matmul_tn(key_rest, key_weight)
    ) * HD ** (-0.5)
    here = received_ref[:, own + share :, half:].astype(jnp.float32).reshape(blocks * 8, half)
    there = other_attn_ref[...].astype(jnp.float32).reshape(blocks * 8, half)
    attn = jnp.concatenate(
        [jnp.where(first_core, here, there), jnp.where(first_core, there, here)], 1
    ).astype(low)
    att = matmul_nt(attn, out_weight_ref[...]).astype(low).astype(jnp.float32)
    part = jnp.zeros((own, D), jnp.float32)
    for block in range(blocks):
        spread = spread_pairs(att[block * 8 : (block + 1) * 8]).astype(low)
        turned = pooled_ref[block].astype(jnp.float32)
        turned = jnp.concatenate([turned[:, 128 * j : 128 * (j + 1)] for j in range(own // 8)], 0)
        part = part + matmul(turned.astype(low), spread)
    block_ref[:, D : 2 * D] = part
    square = square + jnp.sum(part * part)
    part = matmul(turned_ref[...], attn)
    block_ref[:, 2 * D : 3 * D] = part
    square = square + jnp.sum(part * part)
    hidden = up_bias_ref.shape[1]
    bias = up_bias_ref[0:1, :]
    square = known_ref[0:1, :] + jnp.broadcast_to(square, (1, 128))
    high, rest = split_low(square)
    middle, last = split_low(square - high.astype(jnp.float32))
    side = jnp.concatenate(
        [
            high.astype(jnp.float32),
            middle.astype(jnp.float32),
            last.astype(jnp.float32),
            jnp.concatenate([bias, jnp.zeros((1, 128 - hidden), jnp.float32)], 1),
            jnp.zeros((4, 128), jnp.float32),
        ],
        0,
    )
    pieces = [
        query_sums[i : i + 1, 128 * j : 128 * (j + 1)] for i in range(2) for j in range(D // 128)
    ] + [jnp.zeros((4, 128), jnp.float32)]
    sums = jnp.concatenate(pieces, 0)
    final = jnp.concatenate([small, side, sums[0:8], sums[8:16]], 1).astype(low)
    final_ref[...] = jnp.broadcast_to(final[None], final_ref.shape)


def final_kernel(
    index_ref, own_ref, other_ref, query_weight_ref, small_ref, mean_ref, square_ref, bias_ref,
    long_ref, long_mean_ref, long_square_ref, *refs,
):
    weights, refs = refs[:17], refs[17:]
    (
        new_ref, mean_new_ref, square_new_ref, vectors_ref, scalar_ref,
        long_new_ref, long_mean_new_ref, long_square_new_ref,
    ), refs = refs[:8], refs[8:]
    results, rows = refs[:12], refs[12]
    low = jnp.bfloat16
    first_core = index_ref[1] == 0
    share = own_ref.shape[1]
    hidden = weights[8].shape[0]
    count = new_ref.shape[0]
    square = jnp.zeros((1, 128), jnp.float32)
    sums = jnp.zeros((8, 256), jnp.float32)
    biases = []
    for block in range(own_ref.shape[0]):
        here = own_ref[block].astype(jnp.float32)
        there = other_ref[block].astype(jnp.float32)
        for core, pick in enumerate(
            (jnp.where(first_core, here, there), jnp.where(first_core, there, here))
        ):
            index = block * 2 + core
            rows[index * share : (index + 1) * share, :] = pick[:, :D]
            side = pick[:, D : D + 128]
            square = square + (side[0:1] + side[1:2] + side[2:3])
            biases.append(side[3:4, :hidden])
            sums = sums + pick[:, D + 128 :]
    pieces = [sums[k : k + 1, 0:128] for k in range(8)] + [sums[k : k + 1, 128:] for k in range(4)]
    grad_query = jnp.concatenate(
        [jnp.concatenate(pieces[0:6], 1), jnp.concatenate(pieces[6:12], 1)], 0
    )
    gain = vector(small_ref, 3)
    token_out, token_normed, token_inverse = norm_forward(
        token_rows(small_ref), gain, vector(small_ref, 4)
    )
    eight = jnp.concatenate([grad_query, jnp.zeros((6, D), jnp.float32)], 0)
    token_grad = matmul_nt(eight.astype(low), query_weight_ref[...])
    token_in = norm_in(token_grad, token_normed, token_inverse, gain)
    rows[0:2, :] = rows[0:2, :] + token_in[0:2]
    opened = rows[POS + 1 : POS + 6, :] + jnp.concatenate(
        [
            token_in[0:2],
            jnp.sum(token_grad * token_normed, 0, keepdims=True),
            jnp.sum(token_grad, 0, keepdims=True),
            jnp.sum(grad_query, 0, keepdims=True),
        ],
        0,
    )
    rows[POS + 1 : POS + 6, :] = opened
    token_low = token_out.astype(low)
    own = weights[0].shape[0]
    token_own = matmul_nt(own_selector(index_ref[0], own), token_low)
    owned_query = token_own[:, 0:1] * grad_query[0:1] + token_own[:, 1:2] * grad_query[1:2]
    token_float = token_low.astype(jnp.float32)

    def product(left, right):
        return jnp.sum(left * right, -1, keepdims=True)

    cross = product(token_float[0:1], token_float[1:2]) * product(grad_query[0:1], grad_query[1:2])
    query_square = 2.0 * cross
    for i in range(2):
        query_square = query_square + product(
            token_float[i : i + 1], token_float[i : i + 1]
        ) * product(grad_query[i : i + 1], grad_query[i : i + 1])
    bias = bias_ref[...]
    table = rows[0:2, :]
    total = square[:, 0:1] + query_square
    for value in (bias, table, opened):
        total = total + jnp.sum(jnp.sum(value * value, 0, keepdims=True), 1, keepdims=True)
    norm = jnp.sqrt(total)
    factor = jnp.minimum(1.0, CLIP_NORM / (norm + 1e-06))
    scalar_ref[...] = norm
    gradient = rows[0:count, :]
    vectors_ref[...] = rows[POS:count, :] * factor

    def update(targets, weight, first, second, gradient, decay, rate):
        new = adam_update(weight[...], first[...], second[...], gradient, factor, decay, rate)
        for target, value in zip(targets, new):
            target[...] = value
            target.send()

    update(
        (new_ref, mean_new_ref, square_new_ref), small_ref, mean_ref, square_ref, gradient,
        0.0, SMALL_RATE,
    )
    long_gradient = jnp.concatenate(biases + [bias[0:1, :CLS], bias[1:2, :CLS]], 1)
    update(
        (long_new_ref, long_mean_new_ref, long_square_new_ref),
        long_ref, long_mean_ref, long_square_ref, long_gradient, 0.0, SMALL_RATE,
    )
    gradients = (
        weights[3][...],
        jnp.concatenate([owned_query, weights[7][...], weights[16][...]], 1),
        weights[11][...],
        jnp.concatenate([weights[15][0, :, :CLS], weights[15][1, :, :CLS]], 1),
    )
    for group, gradient in enumerate(gradients):
        update(
            results[3 * group : 3 * group + 3], *weights[4 * group : 4 * group + 3], gradient,
            DECAY_RATE, LEARN_RATE,
        )


def chip_sum_kernel(mine_ref, theirs_ref, out_ref):
    total = mine_ref[...].astype(jnp.float32) + theirs_ref[...].astype(jnp.float32)
    out_ref[...] = total.astype(jnp.bfloat16)


def shards_tiled(
    patches,
    pos_index,
    valid,
    classes,
    mixing,
    image_weight,
    drop_keep,
    patch_weight,
    patch_mean,
    patch_square,
    block_weight,
    block_mean,
    block_square,
    down_weight,
    down_mean,
    down_square,
    heads_weight,
    heads_mean,
    heads_square,
    small_rows,
    rows_mean,
    rows_square,
    small_long,
    long_mean,
    long_square,
):
    low = jnp.bfloat16
    f32 = jnp.float32
    images, local_slots, patch_dim = patches.shape
    row_count = images * local_slots
    dp_size = lax.axis_size("dp")
    seq_size = lax.axis_size("seq")
    devices = dp_size * seq_size
    dp_index = lax.axis_index("dp").astype(jnp.int32)
    seq_index = lax.axis_index("seq").astype(jnp.int32)
    device = dp_index * seq_size + seq_index
    own_rows = patch_weight.shape[0]
    own_hidden = down_weight.shape[0]
    all_images = dp_size * images
    rows = all_images * 2
    per_chip = images * 2
    columns = images * PAIR
    half = D // 2
    device_scalar = device[None]
    seq_scalar = seq_index[None]
    device_seq = jnp.stack([device, seq_index])
    dp_seq = jnp.stack([dp_index, seq_index])

    late_width = 2 * D + 2048
    (late,) = kernel_call(
        late_kernel,
        [((own_rows, late_width), low)],
        [block_weight, heads_weight],
        {0: slice(2 * D, 4 * D)},
    )
    device_scalar, late = lax.optimization_barrier((device_scalar, late))
    gathered_late = lax.all_gather(late, ALL, axis=0, tiled=True)
    value_lanes, out_lanes = slice(0, D), slice(D, 2 * D)
    head_lanes = slice(2 * D, late_width)
    early, last = kernel_call(
        prepare_kernel,
        [((dp_size, own_rows, D + 128), low), ((own_rows, D), low)],
        [device_scalar, small_rows, block_weight, patch_weight],
        {2: slice(0, D)},
    )
    gathered_last = lax.all_gather(last, ALL, axis=0, tiled=True)
    flat_patches = patches.transpose(1, 0, 2).reshape(row_count, patch_dim)
    flat_pos = pos_index.T.reshape(row_count, 1)
    valid_columns = jnp.repeat(valid, PAIR)[None]
    up_shift = lax.dynamic_slice_in_dim(small_long, device * own_hidden, own_hidden, 0)[None]
    meta = jnp.concatenate(
        [classes // 32, classes % 32, mixing[:, None], image_weight[:, None], drop_keep], 1
    )
    meta_width = meta.shape[1]
    meta_count = images * meta_width
    pair_hidden = 2 * own_hidden
    key_width = columns + pair_hidden + 64
    meta = meta.reshape(1, meta_count).astype(f32)
    meta = jnp.pad(meta, ((0, own_rows - 1), (0, 64 - meta_count)))
    early = exchange(early, "dp")
    early, flat_patches, flat_pos, valid_columns, up_shift, meta = lax.optimization_barrier(
        (early, flat_patches, flat_pos, valid_columns, up_shift, meta)
    )
    early_other = swap_cores(early)

    query_lanes = slice(D, D + 128)
    keyed, query_blocks = kernel_call(
        query_kernel,
        [((dp_size, own_rows, key_width), low), ((PAIR, D), f32)],
        [early, early_other, block_weight, block_weight, small_rows, meta],
        {0: query_lanes, 1: query_lanes, 2: slice(D, 2 * D), 3: slice(4 * D, 4 * D + FF)},
        loose=(0, 1),
    )
    keyed = exchange(keyed, "dp")
    keyed_other = swap_cores(keyed)
    metas = keyed[:, 0, key_width - 64 : key_width - 64 + meta_count]
    metas = metas.astype(f32).reshape(all_images, meta_width)
    labels = metas[:, 0:3] * 32.0 + metas[:, 3:6]
    share = metas[:, 6:7] / 16.0
    weight_keep = jnp.concatenate([metas[:, 7:8], metas[:, 8:10] * DROP_SCALE], 1)
    ones = jnp.ones_like(share)
    info_even = jnp.concatenate([labels[:, 0:2], share, 1.0 - share, weight_keep, ones], 1)
    info_odd = jnp.concatenate(
        [labels[:, 2:3], labels[:, 2:3], ones, 0.0 * ones, weight_keep, ones], 1
    )
    info = jnp.stack([info_even, info_odd], 1).reshape(rows, 8)

    first, normed, inverse = kernel_call(
        embed_kernel,
        [
            ((row_count, D), low),
            ((row_count, D), f32),
            ((row_count, 1), f32),
        ],
        [seq_scalar, early, early_other, flat_patches, flat_pos, small_rows],
        {1: slice(0, D), 2: slice(0, D)},
        scratch=[
            pltpu.VMEM((D, D), low),
            pltpu.VMEM((POS, D), low),
            pltpu.VMEM((POS, D), low),
        ],
        loose=(1, 2),
        flops=2_000_000_000,
    )
    packed, exponent, keys, up_own = kernel_call(
        scores_kernel,
        [
            ((columns + 8, D), f32),
            ((row_count, columns), f32),
            ((D, columns), low),
            ((D, own_hidden), low),
        ],
        [seq_scalar, keyed, keyed_other, first, valid_columns],
        loose=(1, 2),
    )
    packed_other = swap_cores(packed)
    pooled, scale, asked = kernel_call(
        attend_kernel,
        [
            ((columns, D), f32),
            ((8, columns), f32),
            ((dp_size, per_chip, D + own_rows // 8 * columns), low),
        ],
        [seq_scalar, packed, packed_other, gathered_late, small_rows],
        {3: value_lanes},
        scratch=[pltpu.VMEM((D, columns), f32)],
        loose=(2,),
    )
    asked = exchange(asked, "dp")

    partial, second, second_normed, second_inverse, slope, act, middle, attended_turned = (
        kernel_call(
            mlp_kernel,
            [
                ((rows, D), low),
                ((rows, D), low),
                ((rows, D), f32),
                ((rows, 1), f32),
                ((rows, own_hidden), f32),
                ((rows, own_hidden), low),
                ((rows, D), f32),
                ((own_rows, rows), low),
            ],
            [
                device_scalar, asked, gathered_late, up_own, down_weight, small_rows, info,
                up_shift,
            ],
            {1: slice(0, D), 2: out_lanes},
            loose=(1,),
        )
    )

    def chip_sum(blocks):
        summed = jnp.sum(blocks.astype(f32), 0)
        return summed, swap_cores(summed)

    here, there = chip_sum(exchange(partial.reshape(dp_size, per_chip, D), "dp"))
    mlp_rows = gather_blocks((here + there).astype(low), "dp").reshape(rows, D)
    long_pad = jnp.zeros((1, 1024 - CLS), f32)
    head_shift = jnp.concatenate(
        [
            jnp.concatenate([small_long[None, FF : FF + CLS], long_pad], 1),
            jnp.concatenate([small_long[None, FF + CLS :], long_pad], 1),
        ],
        0,
    )
    sent, grad_result, heads_grad, sums, head_bias, owned_down, up_bias, loss = kernel_call(
        heads_kernel,
        [
            ((dp_size, 2 * per_chip, D), low),
            ((rows, D), f32),
            ((2, own_rows, 1024), f32),
            ((8, D), f32),
            ((2, 1024), f32),
            ((own_hidden, D), f32),
            ((8, own_hidden), f32),
            ((8, 128), f32),
        ],
        [
            device_scalar, mlp_rows, middle, info, small_rows,
            gathered_late, head_shift,
            act, slope, second, up_own, down_weight,
        ],
        {5: head_lanes},
        loose=(1,),
    )
    received = exchange(sent, "dp")
    second_here, second_there = chip_sum(received[:, :per_chip])
    up_left, up_right = received[:, per_chip:, :half], received[:, per_chip:, half:]
    up_here = jnp.where(seq_index == 0, up_left, up_right)
    up_there = swap_cores(jnp.where(seq_index == 0, up_right, up_left))

    second_here, gathered_last = lax.optimization_barrier((second_here, gathered_last))

    small_share = 8
    share_rows = own_rows + small_share + 8
    mine, theirs = kernel_call(
        back_kernel,
        [((dp_size, share_rows, D), low), ((dp_size, share_rows, D), low)],
        [
            dp_seq, second_here, second_there, second_normed, second_inverse, grad_result, info,
            small_rows, gathered_late, gathered_late,
            pooled, scale, exponent, first, normed, inverse, keys, flat_patches, flat_pos, sums,
        ],
        scratch=[
            pltpu.VMEM((columns, D), low),
            pltpu.VMEM((columns, D), low),
            pltpu.VMEM((row_count, D), low),
            pltpu.VMEM((row_count, columns), low),
            pltpu.VMEM((row_count, POS), low),
            pltpu.VMEM((patch_dim, D), f32),
            pltpu.VMEM((devices * small_share, D), f32),
            pltpu.VMEM((D, 128), f32),
        ],
        windows={8: out_lanes, 9: value_lanes},
        loose=(1, 2),
        flops=4_000_000_000,
    )
    (chip_terms,) = kernel_call(
        chip_sum_kernel, [(mine.shape, low)], [mine, swap_cores(theirs)], loose=(1,)
    )
    received = exchange(chip_terms, "dp")
    owned_up, known = kernel_call(
        known_kernel,
        [((own_rows, FF), f32), ((8, 128), f32)],
        [device_seq, up_here, up_there, heads_grad, owned_down, up_bias],
    )
    loss = loss[0, 0]
    received, owned_up, known, loss = lax.optimization_barrier((received, owned_up, known, loss))
    attn_other = swap_cores(received[:, own_rows + small_share :, half:])
    final_width = D + 128 + 256
    owned_patch, owned_block, final = kernel_call(
        owned_kernel,
        [
            ((own_rows, D), f32),
            ((own_rows, 3 * D), f32),
            ((dp_size, small_share, final_width), low),
        ],
        [
            device_seq, received, attn_other, gathered_late, asked, attended_turned,
            query_blocks, block_weight, known, up_bias,
        ],
        {3: out_lanes, 4: slice(D, D + own_rows // 8 * columns), 7: slice(D, 2 * D)},
        loose=(1, 2),
    )
    final = exchange(final, "dp")
    final_other = swap_cores(final)
    small_count = POS + 13
    long_count = small_long.shape[0]
    (
        rows_new, rows_mean_new, rows_square_new, vectors_grad, scalars,
        long_new, long_mean_new, long_square_new,
        patch_new, patch_mean_new, patch_square_new,
        block_new, block_mean_new, block_square_new,
        down_new, down_mean_new, down_square_new,
        heads_new, heads_mean_new, heads_square_new,
    ) = kernel_call(
        final_kernel,
        [((small_count, D), f32)] * 3
        + [((13, D), f32), ((1, 1), f32)]
        + [((1, long_count), f32)] * 3
        + [
            (weight.shape, f32)
            for weight in (patch_weight, block_weight, down_weight, heads_weight)
            for _ in range(3)
        ],
        [
            device_seq, final, final_other, gathered_last,
            small_rows, rows_mean, rows_square, head_bias,
            small_long[None], long_mean[None], long_square[None],
            patch_weight, patch_mean, patch_square, owned_patch,
            block_weight, block_mean, block_square, owned_block,
            down_weight, down_mean, down_square, owned_down,
            heads_weight, heads_mean, heads_square, heads_grad, owned_up,
        ],
        scratch=[pltpu.VMEM((devices * small_share, D), f32)],
        limit=24,
        loose=(1, 2),
        near=(3, 4, 5, 6, 15, 16, 17, 19, 20, 21, 23, 24, 25),
    )
    grad_norm = scalars.reshape(())
    long_new, long_mean_new, long_square_new = (
        value.reshape(long_count) for value in (long_new, long_mean_new, long_square_new)
    )
    return (
        loss,
        grad_norm,
        patch_new,
        patch_mean_new,
        patch_square_new,
        block_new,
        block_mean_new,
        block_square_new,
        down_new,
        down_mean_new,
        down_square_new,
        heads_new,
        heads_mean_new,
        heads_square_new,
        rows_new,
        rows_mean_new,
        rows_square_new,
        long_new,
        long_mean_new,
        long_square_new,
        vectors_grad,
    )


def shards_plain(
    patches,
    pos_index,
    valid,
    classes,
    mixing,
    image_weight,
    drop_keep,
    patch_weight,
    patch_mean,
    patch_square,
    block_weight,
    block_mean,
    block_square,
    down_weight,
    down_mean,
    down_square,
    heads_weight,
    heads_mean,
    heads_square,
    small_rows,
    rows_mean,
    rows_square,
    small_long,
    long_mean,
    long_square,
):
    low = jnp.bfloat16
    f32 = jnp.float32
    images, local_slots, patch_dim = patches.shape
    row_count = images * local_slots
    dp_size = lax.axis_size("dp")
    seq_size = lax.axis_size("seq")
    devices = dp_size * seq_size
    seq_index = lax.axis_index("seq")
    device = lax.axis_index("dp") * seq_size + seq_index
    own_rows = patch_weight.shape[0]
    own_hidden = down_weight.shape[0]
    own_images = images // seq_size
    all_images = dp_size * images
    pairs = 2 * HEADS
    table = small_rows[:POS]
    vectors = small_rows[POS:]

    gathered_late = lax.all_gather(
        jnp.concatenate([block_weight[:, 2 * D : 4 * D], heads_weight], 1).astype(low),
        ALL,
        axis=0,
        tiled=True,
    )
    gathered_query_key = lax.all_gather(
        lax.optimization_barrier((block_weight[:, : 2 * D].astype(low), gathered_late[:8, :128]))[0],
        ALL,
        axis=0,
        tiled=True,
    )

    tokens = vectors[1:3] + table[0:2]
    token_out, token_normed, token_inverse = norm_forward(tokens, vectors[3], vectors[4])
    token_low = token_out.astype(low)
    select_own = (
        lax.broadcasted_iota(jnp.int32, (own_rows, D), 0) + device * own_rows
        == lax.broadcasted_iota(jnp.int32, (own_rows, D), 1)
    ).astype(low)
    token_own = matmul_nt(token_low, select_own).astype(low)
    query_partial = matmul(token_own, block_weight[:, :D].astype(low))
    query = jnp.sum(gather_blocks(query_partial), 0) + vectors[5]
    query_low = query.astype(low)
    head_of = lax.broadcasted_iota(jnp.int32, (HEADS, D), 1) // HD
    head_mask = head_of == lax.broadcasted_iota(jnp.int32, (HEADS, D), 0)
    query_blocks = jnp.where(head_mask[None], query_low[:, None, :], 0).reshape(pairs, D)
    key_own = matmul_nt(block_weight[:, D : 2 * D].astype(low), query_blocks.astype(low)) * HD ** (
        -0.5
    )
    meta = jnp.concatenate(
        [
            (classes // 32),
            (classes % 32),
            mixing[:, None],
            image_weight[:, None],
            drop_keep,
        ],
        1,
    )
    meta_width = meta.shape[1]
    meta_columns = -(-images * meta_width // own_rows)
    meta = jnp.pad(meta.reshape(-1), (0, own_rows * meta_columns - images * meta_width))
    meta = meta.reshape(own_rows, meta_columns).astype(low)
    extra = -(-(pairs + meta_columns) // 128) * 128
    early = jnp.concatenate(
        [
            patch_weight.astype(low),
            key_own.astype(low),
            meta,
            jnp.zeros((own_rows, extra - pairs - meta_columns), low),
        ],
        1,
    )
    early = gather_blocks(early, "dp").reshape(dp_size, own_rows, D + extra)
    early = join_cores(early, seq_index, 1)
    metas = early[:, 0, :, D + pairs : D + pairs + meta_columns].astype(f32)
    metas = metas.reshape(dp_size, own_rows * meta_columns)[:, : images * meta_width]
    metas = metas.reshape(all_images, meta_width)
    early = early.reshape(D, D + extra)
    full_patch = early[:, :D]
    key_vectors = early[:, D : D + pairs]

    slot_global = seq_index * local_slots + lax.broadcasted_iota(jnp.int32, (1, local_slots, 1), 1)
    is_class = slot_global == 0
    is_distill = slot_global == 1
    special = is_class | is_distill
    key_mask = slot_global < valid[:, None, None]
    flat_patches = patches.reshape(row_count, patch_dim)
    onehot_pos = (
        pos_index.reshape(row_count)[:, None]
        == lax.broadcasted_iota(jnp.int32, (1, POS), 1)
    ).astype(low)
    table_high, table_rest = split_low(table)
    embedded = matmul(flat_patches, full_patch)
    positions = matmul(onehot_pos, table_high) + matmul(onehot_pos, table_rest)
    embedded = (embedded + positions + vectors[0]).reshape(images, local_slots, D)
    stream = jnp.where(is_class, tokens[0], jnp.where(is_distill, tokens[1], embedded))
    first_out, first_normed, first_inverse = norm_forward(stream, vectors[3], vectors[4])
    first_low = first_out.astype(low)
    flat_first = first_low.reshape(row_count, D)
    scores = matmul(flat_first, key_vectors).reshape(images, local_slots, pairs)
    scores = jnp.where(key_mask, scores, MASK_FILL)
    local_peak = jnp.max(scores, 1, keepdims=True)
    exponent = jnp.exp(scores - local_peak)
    local_total = jnp.sum(exponent, 1, keepdims=True)
    local_pooled = jnp.einsum(
        "nlm,nld->nmd", exponent.astype(low), first_low, preferred_element_type=f32
    )
    packed = jnp.concatenate(
        [
            local_pooled,
            jnp.broadcast_to(local_peak.transpose(0, 2, 1), (images, pairs, 64)),
            jnp.broadcast_to(local_total.transpose(0, 2, 1), (images, pairs, 64)),
        ],
        2,
    )
    other = swap_cores(packed)
    other_pooled = other[:, :, :D]
    peak_here = local_peak.transpose(0, 2, 1)
    peak_there = other[:, :, D : D + 1]
    peak = jnp.maximum(peak_here, peak_there)
    scale_here = jnp.exp(peak_here - peak)
    scale_there = jnp.exp(peak_there - peak)
    total = (
        scale_here * local_total.transpose(0, 2, 1) + scale_there * other[:, :, D + 64 : D + 65]
    )
    pooled = (scale_here * local_pooled + scale_there * other_pooled) / total
    probs = exponent * (scale_here / total).transpose(0, 2, 1)
    pooled_low = pooled.astype(low)
    own_pooled = lax.dynamic_slice_in_dim(pooled_low, seq_index * own_images, own_images, 0)

    up_blocks = (
        block_weight[:, 4 * D :]
        .astype(low)
        .reshape(own_rows, devices, own_hidden)
        .transpose(1, 0, 2)
        .reshape(devices, own_rows * own_hidden)
    )
    pooled_blocks = (
        own_pooled.reshape(own_images * pairs, devices, own_rows)
        .transpose(1, 0, 2)
        .reshape(devices, own_images * pairs * own_rows)
    )
    received = exchange(jnp.concatenate([up_blocks, pooled_blocks], 1))
    up_own = received[:, : own_rows * own_hidden].reshape(D, own_hidden)
    pooled_own = received[:, own_rows * own_hidden :].reshape(all_images, 2, HEADS, own_rows)

    full_value = gathered_late[:, :D]
    full_out = gathered_late[:, D : 2 * D]
    full_heads = gathered_late[:, 2 * D :]
    mixed = matmul(own_pooled.reshape(own_images * pairs, D), full_value)
    attended = jnp.sum(
        jnp.where(head_mask, mixed.reshape(own_images * 2, HEADS, D), 0.0), 1
    ) + vectors[6]
    attended = attended.astype(low)
    rows = all_images * 2
    attended = gather_blocks(attended).reshape(rows, D)
    keep_float = metas[:, 8:10] * DROP_SCALE
    keep_rows = jnp.repeat(keep_float, 2, axis=0)
    keep_first = keep_rows[:, 0:1]
    keep_second = keep_rows[:, 1:2]
    middle = jnp.tile(tokens, (all_images, 1)) + keep_first * (
        matmul(attended, full_out) + vectors[7]
    )
    second_out, second_normed, second_inverse = norm_forward(middle, vectors[8], vectors[9])
    second_low = second_out.astype(low)
    hidden_bias = lax.dynamic_slice_in_dim(small_long, device * own_hidden, own_hidden, 0)
    hidden = matmul(second_low, up_own) + hidden_bias
    activated, gelu_slope = gelu_parts(hidden)
    activated = activated.astype(low)
    down_low = down_weight.astype(low)
    mlp_partial = matmul(activated, down_low).astype(low)
    row_share = own_images * 2
    mlp_own = jnp.sum(
        exchange(mlp_partial.reshape(devices, row_share, D)).astype(f32), 0
    )
    mlp_rows = gather_blocks(mlp_own.astype(low)).reshape(rows, D).astype(f32)
    result = middle + keep_second * (mlp_rows + vectors[10])

    head_out, head_normed, head_inverse = norm_forward(result, vectors[11], vectors[12])
    head_low = head_out.astype(low).reshape(all_images, 2, D)
    logits_class = matmul(head_low[:, 0], full_heads[:, :CLS]) + small_long[FF : FF + CLS]
    logits_distill = matmul(head_low[:, 1], full_heads[:, CLS:]) + small_long[FF + CLS :]
    columns = lax.broadcasted_iota(jnp.int32, (1, CLS), 1)
    labels = (metas[:, 0:3] * 32.0 + metas[:, 3:6]).astype(jnp.int32)
    share = metas[:, 6:7] / 16.0
    weights = metas[:, 7]
    weight_sum = jnp.sum(weights)
    target = share * (labels[:, 0:1] == columns).astype(f32) + (1.0 - share) * (
        labels[:, 1:2] == columns
    ).astype(f32)
    teacher = (labels[:, 2:3] == columns).astype(f32)
    log_class = jax.nn.log_softmax(logits_class, -1)
    log_distill = jax.nn.log_softmax(logits_distill, -1)
    terms = -0.5 * (jnp.sum(target * log_class, -1) + jnp.sum(teacher * log_distill, -1))
    loss = jnp.sum(weights * terms) / weight_sum
    scale_rows = (weights * 0.5 / weight_sum)[:, None]
    grad_class = (scale_rows * (jnp.exp(log_class) - target)).astype(low)
    grad_distill = (scale_rows * (jnp.exp(log_distill) - teacher)).astype(low)
    head_own = matmul_nt(select_own, head_low.reshape(rows, D)).astype(low)
    head_own = head_own.reshape(own_rows, all_images, 2)
    owned_heads = jnp.concatenate(
        [matmul(head_own[:, :, 0], grad_class), matmul(head_own[:, :, 1], grad_distill)], 1
    )
    head_bias = jnp.concatenate(
        [jnp.sum(grad_class.astype(f32), 0), jnp.sum(grad_distill.astype(f32), 0)]
    )
    grad_head_rows = jnp.stack(
        [matmul_nt(grad_class, full_heads[:, :CLS]), matmul_nt(grad_distill, full_heads[:, CLS:])],
        1,
    ).reshape(rows, D)
    grad_result, final_gain, final_shift = norm_backward(
        grad_head_rows, head_normed, head_inverse, vectors[11]
    )

    grad_mlp = (keep_second * grad_result).astype(low)
    owned_down = matmul_tn(activated, grad_mlp)
    down_bias = jnp.sum(grad_mlp.astype(f32), 0)
    grad_hidden = (matmul_nt(grad_mlp, down_low) * gelu_slope).astype(low)
    up_bias = jnp.sum(grad_hidden.astype(f32), 0)
    grad_up = matmul_tn(second_low, grad_hidden).astype(low)
    grad_second_partial = matmul_nt(grad_hidden, up_own).astype(low)
    received = exchange(
        jnp.concatenate(
            [
                grad_second_partial.reshape(devices, row_share * D),
                grad_up.reshape(devices, own_rows * own_hidden),
            ],
            1,
        )
    )
    grad_second = jnp.sum(
        received[:, : row_share * D].astype(f32).reshape(devices, row_share, D), 0
    )
    owned_up = (
        received[:, row_share * D :]
        .reshape(devices, own_rows, own_hidden)
        .transpose(1, 0, 2)
        .reshape(own_rows, FF)
        .astype(f32)
    )
    row_start = device * row_share
    own_normed = lax.dynamic_slice_in_dim(second_normed, row_start, row_share, 0)
    own_inverse = lax.dynamic_slice_in_dim(second_inverse, row_start, row_share, 0)
    own_result = lax.dynamic_slice_in_dim(grad_result, row_start, row_share, 0)
    own_keep = lax.dynamic_slice_in_dim(keep_first, row_start, row_share, 0)
    grad_second_in, second_gain, second_shift = norm_backward(
        grad_second, own_normed, own_inverse, vectors[8]
    )
    grad_middle = own_result + grad_second_in
    grad_attn_own = (own_keep * grad_middle).astype(low)
    out_bias = jnp.sum(grad_attn_own.astype(f32), 0)
    grad_attn = join_cores(grad_attn_own, seq_index, 0).reshape(images * 2, D)
    grad_att = matmul_nt(grad_attn, full_out).astype(low)
    value_bias = jnp.sum(
        lax.dynamic_slice_in_dim(grad_att, seq_index * row_share, row_share, 0).astype(f32), 0
    )
    grad_att_blocks = jnp.where(
        head_mask, grad_att.reshape(images * 2, 1, D), jnp.zeros((), low)
    ).reshape(images * pairs, D)
    value_vectors = matmul_nt(grad_att_blocks, full_value).astype(low)
    value_const = jnp.sum(grad_att_blocks.astype(f32) * vectors[6], -1).reshape(images, pairs)
    value_vectors = value_vectors.reshape(images, pairs, D)
    mean_grad = jnp.sum(pooled * value_vectors.astype(f32), -1) + value_const
    grad_probs = (
        jnp.einsum("nld,nmd->nlm", first_low, value_vectors, preferred_element_type=f32)
        + value_const[:, None, :]
    )
    grad_scores = (probs * (grad_probs - mean_grad[:, None, :])).astype(low)
    key_rows = jnp.broadcast_to(key_vectors.T[None], (images, pairs, D))
    grad_first = jnp.einsum(
        "nlk,nkd->nld",
        jnp.concatenate([grad_scores, probs.astype(low)], 2),
        jnp.concatenate([key_rows, value_vectors], 1),
        preferred_element_type=f32,
    )
    grad_stream, first_gain, first_shift = norm_backward(
        grad_first, first_normed, first_inverse, vectors[3]
    )
    pooled_grad = matmul_tn(grad_scores.reshape(row_count, pairs), flat_first)
    query_grad_blocks = matmul(pooled_grad.astype(low), gathered_query_key[:, D:]) * HD ** (-0.5)
    grad_query = jnp.sum(
        jnp.where(head_mask, query_grad_blocks.reshape(2, HEADS, D), 0.0), 1
    )
    token_grad = matmul_nt(grad_query.astype(low), gathered_query_key[:, :D])
    token_grad_in, token_gain, token_shift = norm_backward(
        token_grad, token_normed, token_inverse, vectors[3]
    )
    grad_tokens = (
        token_grad_in
        + jnp.sum(grad_middle.reshape(own_images, 2, D), 0)
        + jnp.stack(
            [
                jnp.sum(jnp.where(is_class, grad_stream, 0.0), (0, 1)),
                jnp.sum(jnp.where(is_distill, grad_stream, 0.0), (0, 1)),
            ]
        )
    )
    grad_embed = jnp.where(special, 0.0, grad_stream)
    embed_low = grad_embed.astype(low).reshape(row_count, D)
    grad_patch = matmul_tn(flat_patches, embed_low)
    grad_table = matmul_tn(onehot_pos, embed_low)
    patch_bias = jnp.sum(grad_embed, (0, 1))
    leader = (device == 0).astype(f32)
    small_terms = jnp.concatenate(
        [
            grad_tokens,
            grad_table[2:],
            patch_bias[None],
            grad_tokens,
            (first_gain + token_gain)[None],
            (first_shift + token_shift)[None],
            jnp.sum(grad_query, 0)[None],
            value_bias[None],
            out_bias[None],
            second_gain[None],
            second_shift[None],
            leader * down_bias[None],
            leader * final_gain[None],
            leader * final_shift[None],
        ],
        0,
    )
    small_count = POS + 13
    small_share = -(-small_count // devices)
    small_terms = jnp.pad(small_terms, ((0, small_share * devices - small_count), (0, 0)))

    key_terms = (
        pooled_grad.reshape(pairs, devices, own_rows)
        .transpose(1, 0, 2)
        .reshape(devices, pairs * own_rows)
    )
    key_share = -(-pairs * own_rows // D)
    key_terms = jnp.pad(key_terms, ((0, 0), (0, key_share * D - pairs * own_rows)))
    terms_rows = jnp.concatenate(
        [
            grad_patch.reshape(dp_size, seq_size, own_rows, D),
            small_terms.reshape(dp_size, seq_size, small_share, D),
            key_terms.reshape(dp_size, seq_size, key_share, D),
            jnp.broadcast_to(grad_query, (dp_size, seq_size, 2, D)),
        ],
        2,
    )
    mine = lax.dynamic_index_in_dim(terms_rows, seq_index, 1, keepdims=False)
    theirs = lax.dynamic_index_in_dim(terms_rows, 1 - seq_index, 1, keepdims=False)
    chip_terms = mine + swap_cores(theirs.astype(low)).astype(f32)
    pair_share = 2 * row_share
    grad_att_own = lax.dynamic_slice_in_dim(grad_att, seq_index * row_share, row_share, 0)
    pair_own = jnp.concatenate([grad_attn_own, grad_att_own], 0)
    sent = jnp.concatenate(
        [chip_terms.astype(low), jnp.broadcast_to(pair_own, (dp_size, pair_share, D))], 1
    )
    received = exchange(sent, "dp")
    summed_share = chip_terms.shape[1]
    reduced = jnp.sum(received[:, :summed_share].astype(f32), 0)
    pair_rows = join_cores(received[:, summed_share:], seq_index, 1)
    pair_rows = pair_rows.reshape(devices, 2, row_share, D)
    owned_patch = reduced[:own_rows]
    owned_small = reduced[own_rows : own_rows + small_share]
    key_start = own_rows + small_share
    key_reduced = reduced[key_start : key_start + key_share].reshape(-1)[: pairs * own_rows]
    key_reduced = key_reduced.reshape(2, HEADS, own_rows)
    query_reduced = reduced[key_start + key_share :]

    owned_query = matmul_tn(token_own, query_reduced.astype(low))
    key_left = jnp.repeat(
        key_reduced.transpose(2, 0, 1), HD, axis=2
    )
    owned_key = jnp.sum(key_left * query_low.astype(f32)[None], 1) * HD ** (-0.5)
    grad_attn_rows = pair_rows[:, 0].reshape(rows, D)
    grad_att_rows = pair_rows[:, 1].reshape(all_images, 2, HEADS, HD)
    owned_value = jnp.einsum(
        "nihd,nihc->dhc", pooled_own, grad_att_rows, preferred_element_type=f32
    ).reshape(own_rows, D)
    attended_own = matmul_nt(select_own, attended).astype(low)
    owned_out = matmul(attended_own, grad_attn_rows)
    owned_block = jnp.concatenate([owned_query, owned_key, owned_value, owned_out, owned_up], 1)

    shard_square = (
        jnp.sum(owned_patch * owned_patch)
        + jnp.sum(owned_block * owned_block)
        + jnp.sum(owned_down * owned_down)
        + jnp.sum(owned_heads * owned_heads)
        + jnp.sum(owned_small * owned_small)
        + jnp.sum(up_bias * up_bias)
    )
    square_high, square_rest = split_low(shard_square)
    square_rest, square_last = split_low(shard_square - square_high.astype(f32))
    tail_row = jnp.concatenate(
        [
            jnp.stack([square_high, square_rest, square_last]),
            up_bias.astype(low),
            jnp.zeros((D - 3 - own_hidden,), low),
        ]
    )
    final = gather_blocks(
        jnp.concatenate([owned_small.astype(low), tail_row[None]], 0), "dp"
    ).reshape(dp_size, small_share + 1, D)
    final = join_cores(final, seq_index, 1).reshape(devices, small_share + 1, D)
    summed_rows = final[:, :small_share].astype(f32).reshape(devices * small_share, D)[:small_count]
    global_square = jnp.sum(final[:, small_share, 0:3].astype(f32))
    up_bias_all = final[:, small_share, 3 : 3 + own_hidden].astype(f32).reshape(FF)
    summed_long = jnp.concatenate([up_bias_all, head_bias])
    total_square = global_square + jnp.sum(head_bias * head_bias)
    grad_norm = jnp.sqrt(total_square)
    factor = jnp.minimum(1.0, CLIP_NORM / (grad_norm + 1e-06))
    vectors_grad = factor * summed_rows[POS:]
    patch_new, patch_mean_new, patch_square_new = adam_update(
        patch_weight, patch_mean, patch_square, owned_patch, factor, DECAY_RATE, LEARN_RATE
    )
    block_new, block_mean_new, block_square_new = adam_update(
        block_weight, block_mean, block_square, owned_block, factor, DECAY_RATE, LEARN_RATE
    )
    down_new, down_mean_new, down_square_new = adam_update(
        down_weight, down_mean, down_square, owned_down, factor, DECAY_RATE, LEARN_RATE
    )
    heads_new, heads_mean_new, heads_square_new = adam_update(
        heads_weight, heads_mean, heads_square, owned_heads, factor, DECAY_RATE, LEARN_RATE
    )
    rows_new, rows_mean_new, rows_square_new = adam_update(
        small_rows, rows_mean, rows_square, summed_rows, factor, 0.0, SMALL_RATE
    )
    long_new, long_mean_new, long_square_new = adam_update(
        small_long, long_mean, long_square, summed_long, factor, 0.0, SMALL_RATE
    )
    return (
        loss,
        grad_norm,
        patch_new,
        patch_mean_new,
        patch_square_new,
        block_new,
        block_mean_new,
        block_square_new,
        down_new,
        down_mean_new,
        down_square_new,
        heads_new,
        heads_mean_new,
        heads_square_new,
        rows_new,
        rows_mean_new,
        rows_square_new,
        long_new,
        long_mean_new,
        long_square_new,
        vectors_grad,
    )


def tiles(arguments):
    patches, patch_weight = arguments[0], arguments[7]
    images, local_slots, _ = patches.shape
    return images * PAIR == 128 and (images * local_slots) % CHUNK == 0 and patch_weight.shape[0] == 24


def shards(*arguments):
    return (shards_tiled if tiles(arguments) else shards_plain)(*arguments)


def solution(mesh):
    placed = (
        P("dp", "seq", None),
        P("dp", "seq"),
        P("dp"),
        P("dp", None),
        P("dp"),
        P("dp"),
        P("dp", None),
        P(("dp", "seq"), None),
        P(("dp", "seq"), None),
        P(("dp", "seq"), None),
        P(("dp", "seq"), None),
        P(("dp", "seq"), None),
        P(("dp", "seq"), None),
        P(("dp", "seq"), None),
        P(("dp", "seq"), None),
        P(("dp", "seq"), None),
        P(("dp", "seq"), None),
        P(("dp", "seq"), None),
        P(("dp", "seq"), None),
        P(),
        P(),
        P(),
        P(),
        P(),
        P(),
    )
    return jax.shard_map(
        shards,
        mesh=mesh,
        in_specs=placed,
        out_specs=(
            P(),
            P(),
            P(("dp", "seq"), None),
            P(("dp", "seq"), None),
            P(("dp", "seq"), None),
            P(("dp", "seq"), None),
            P(("dp", "seq"), None),
            P(("dp", "seq"), None),
            P(("dp", "seq"), None),
            P(("dp", "seq"), None),
            P(("dp", "seq"), None),
            P(("dp", "seq"), None),
            P(("dp", "seq"), None),
            P(("dp", "seq"), None),
            P(),
            P(),
            P(),
            P(),
            P(),
            P(),
            P(),
        ),
        check_vma=False,
    )
```

```python
import math

import jax
import jax.numpy as jnp
from jax import lax
from jax.experimental import pallas as pl
from jax.experimental.pallas import tpu as pltpu
from jax.sharding import PartitionSpec as P

D = 768
HEADS = 12
HD = 64
FF = 3072
CLS = 1000
POS = 198
STEP = 7


NORM_EPS = 1e-06
DROP_SCALE = 1.0 / 0.9
CLIP_NORM = 0.02
LEARN_RATE = 0.02
SMALL_RATE = 0.15
BETA_FIRST = 0.9
BETA_SECOND = 0.999
ADAM_EPS = 1e-08
DECAY_RATE = 0.05
MASK_FILL = -1e30
highest = lax.Precision.HIGHEST


def matmul(left, right):
    return jnp.dot(left, right, preferred_element_type=jnp.float32)


def matmul_tn(left, right):
    return lax.dot_general(
        left, right, (((0,), (0,)), ((), ())), preferred_element_type=jnp.float32
    )


def matmul_nt(left, right):
    return lax.dot_general(
        left, right, (((1,), (1,)), ((), ())), preferred_element_type=jnp.float32
    )


def norm_forward(values, gain, shift):
    centered = values - jnp.mean(values, -1, keepdims=True)
    inverse = lax.rsqrt(jnp.mean(centered * centered, -1, keepdims=True) + NORM_EPS)
    normed = centered * inverse
    return (normed * gain + shift, normed, inverse)


def norm_backward(grad_out, normed, inverse, gain):
    scaled = grad_out * gain
    grad_in = inverse * (
        scaled
        - jnp.mean(scaled, -1, keepdims=True)
        - normed * jnp.mean(scaled * normed, -1, keepdims=True)
    )
    leading = tuple(range(grad_out.ndim - 1))
    return (grad_in, jnp.sum(grad_out * normed, leading), jnp.sum(grad_out, leading))


def gelu_parts(values):
    cumulative = 0.5 * (1.0 + jax.scipy.special.erf(values * 0.7071067811865476))
    density = 0.3989422804014327 * jnp.exp(-0.5 * values * values)
    return (values * cumulative, cumulative + values * density)


def adam_update(weight, first, second, gradient, factor, decay, rate):
    clipped = gradient * factor
    first_new = BETA_FIRST * first + (1.0 - BETA_FIRST) * clipped
    second_new = BETA_SECOND * second + (1.0 - BETA_SECOND) * clipped * clipped
    first_hat = first_new / (1.0 - BETA_FIRST**STEP)
    second_hat = second_new / (1.0 - BETA_SECOND**STEP)
    weight_new = weight - rate * (first_hat / (jnp.sqrt(second_hat) + ADAM_EPS) + decay * weight)
    return (weight_new, first_new, second_new)


ALL = ("dp", "seq")


def exchange(blocks, axes=ALL):
    return lax.all_to_all(blocks, axes, 0, 0, tiled=True)


def gather_blocks(block, axes=ALL):
    count = lax.axis_size(axes)
    return exchange(jnp.broadcast_to(block[None], (count,) + block.shape), axes)


def swap_cores(value):
    return lax.ppermute(value, "seq", [(0, 1), (1, 0)])


def join_cores(value, seq_index, axis):
    other = swap_cores(value)
    first = jnp.where(seq_index == 0, value, other)
    second = jnp.where(seq_index == 0, other, value)
    return jnp.stack([first, second], axis)


def split_low(value):
    high = value.astype(jnp.bfloat16)
    rest = (value - high.astype(jnp.float32)).astype(jnp.bfloat16)
    return high, rest


PADDED = 16
PAIR = 2 * PADDED
CHUNK = 112


class Fetched:
    def __init__(self, value, source, semaphore, columns):
        if columns is not None:
            source = source.at[(slice(None),) * (len(source.shape) - 1) + (columns,)]
        self.copy = pltpu.make_async_copy(source, value, semaphore)
        self.value = value
        self.copy.start()
        self.waiting = True

    def ready(self):
        if self.waiting:
            self.copy.wait()
            self.waiting = False

    @property
    def shape(self):
        return self.value.shape

    @property
    def dtype(self):
        return self.value.dtype

    def __getitem__(self, index):
        self.ready()
        return self.value[index]


class Stored:
    def __init__(self, value, out, semaphore):
        self.copy = pltpu.make_async_copy(value, out, semaphore)
        self.value = value
        self.sent = False

    def send(self):
        if not self.sent:
            self.copy.start()
            self.sent = True

    @property
    def shape(self):
        return self.value.shape

    @property
    def dtype(self):
        return self.value.dtype

    def __getitem__(self, index):
        return self.value[index]

    def __setitem__(self, index, value):
        self.value[index] = value


def ready(*operands):
    for operand in operands:
        operand.ready()


def kernel_call(body, outputs, inputs, windows=None, scratch=(), flops=1_000_000, limit=24, loose=(), near=()):
    windows = windows or {}
    places, buffers = [], []
    moved = 0
    for position, value in enumerate(inputs):
        if value.ndim == 1:
            places.append(pl.BlockSpec(memory_space=pltpu.SMEM))
            continue
        if position in near:
            places.append(pl.BlockSpec(memory_space=pltpu.VMEM))
            continue
        places.append(pl.BlockSpec(memory_space=pltpu.HBM))
        shape = value.shape
        if position in windows:
            shape = shape[:-1] + (windows[position].stop - windows[position].start,)
        buffers.append(pltpu.VMEM(shape, value.dtype))
        moved += math.prod(shape) * value.dtype.itemsize
    moved += sum(math.prod(shape) * jnp.dtype(kind).itemsize for shape, kind in outputs)
    fetches = len(buffers)
    buffers += [pltpu.VMEM(shape, kind) for shape, kind in outputs]
    buffers += [pltpu.SemaphoreType.DMA((fetches + len(outputs),))]

    def run(*refs):
        ins, refs = refs[: len(inputs)], refs[len(inputs) :]
        outs, refs = refs[: len(outputs)], refs[len(outputs) :]
        stores, copies, semaphores = refs[fetches:][: len(outputs)], refs[:fetches], None
        semaphores = refs[fetches + len(outputs)]
        rest = refs[fetches + len(outputs) + 1 :]
        operands, used = [], 0
        for position, (value, ref) in enumerate(zip(inputs, ins)):
            if value.ndim == 1 or position in near:
                operands.append(ref)
                continue
            operands.append(
                Fetched(copies[used], ref, semaphores.at[used], windows.get(position))
            )
            used += 1
        stores = [
            Stored(store, out, semaphores.at[fetches + index])
            for index, (store, out) in enumerate(zip(stores, outs))
        ]
        body(*operands, *stores, *rest)
        ready(*[operand for operand in operands if isinstance(operand, Fetched)])
        for store in stores:
            store.send()
        for store in stores:
            store.copy.wait()

    return pl.pallas_call(
        run,
        name=body.__name__,
        in_specs=places,
        out_specs=[pl.BlockSpec(memory_space=pltpu.HBM) for _ in outputs],
        out_shape=[pltpu.HBM(shape, kind) for shape, kind in outputs],
        scratch_shapes=buffers + list(scratch),
        cost_estimate=pl.CostEstimate(flops=flops, bytes_accessed=moved, transcendentals=0),
        compiler_params=pltpu.CompilerParams(vmem_limit_bytes=limit * 1024 * 1024),
    )(
        *[
            value
            if value.ndim == 1 or position in loose or position in near
            else pltpu.with_memory_space_constraint(value, pltpu.HBM)
            for position, value in enumerate(inputs)
        ]
    )


def iota(shape, axis):
    return lax.broadcasted_iota(jnp.int32, shape, axis)


def own_selector(device, count):
    return jnp.where(
        iota((count, D), 0) + device * count == iota((count, D), 1), 1.0, 0.0
    ).astype(jnp.bfloat16)


def pair_mask(rows):
    return (iota((rows, D), 0) & (PADDED - 1)) == (iota((rows, D), 1) >> 6)


def token_rows(small_ref):
    tokens = small_ref[POS + 1 : POS + 3, :] + small_ref[0:2, :]
    return jnp.concatenate([tokens, jnp.zeros((6, D), jnp.float32)], 0)


def vector(small_ref, index):
    return small_ref[POS + index : POS + index + 1, :]


def norm_in(grad_out, normed, inverse, gain):
    scaled = grad_out * gain
    return inverse * (
        scaled
        - jnp.mean(scaled, -1, keepdims=True)
        - normed * jnp.mean(scaled * normed, -1, keepdims=True)
    )


def spread_pairs(values):
    count = values.shape[0]
    spread = jnp.broadcast_to(values[:, None, :], (count, PADDED, D)).reshape(count * PADDED, D)
    return jnp.where(pair_mask(count * PADDED), spread, 0.0)


def collect_pairs(values):
    count = values.shape[0] // PADDED
    kept = jnp.where(pair_mask(values.shape[0]), values, 0.0)
    return jnp.sum(kept.reshape(count, PADDED, D), 1)


def late_kernel(value_out_ref, heads_ref, late_ref):
    low = jnp.bfloat16
    late_ref[:, 0 : 2 * D] = value_out_ref[...].astype(low)
    late_ref[:, 2 * D :] = jnp.zeros((late_ref.shape[0], 2048), low)
    late_ref[:, 2 * D : 2 * D + CLS] = heads_ref[:, 0:CLS].astype(low)
    late_ref[:, 2 * D + 1024 : 2 * D + 1024 + CLS] = heads_ref[:, CLS:].astype(low)


def prepare_kernel(
    device_ref, small_ref, query_weight_ref, patch_ref, first_ref, last_ref
):
    low = jnp.bfloat16
    own = patch_ref.shape[0]
    last_ref[...] = query_weight_ref[...].astype(low)
    query_weight = query_weight_ref[...].astype(low)
    token_out, _, _ = norm_forward(token_rows(small_ref), vector(small_ref, 3), vector(small_ref, 4))
    token_own = matmul_nt(token_out.astype(low), own_selector(device_ref[0], own))
    partial = matmul(token_own.astype(low), query_weight)
    high, rest = split_low(partial)
    pieces = [
        part[i : i + 1, 128 * j : 128 * (j + 1)].astype(jnp.float32)
        for part in (high, rest)
        for i in range(2)
        for j in range(D // 128)
    ]
    block = jnp.concatenate(
        [patch_ref[...], jnp.concatenate(pieces, 0)], 1
    ).astype(low)
    first_ref[...] = jnp.broadcast_to(block[None], first_ref.shape)


def query_kernel(
    own_ref, other_ref, key_weight_ref, up_ref, small_ref, meta_ref,
    out_ref, query_ref,
):
    total = jnp.sum(own_ref[...].astype(jnp.float32), 0) + jnp.sum(
        other_ref[...].astype(jnp.float32), 0
    )
    count = D // 128
    both = total[0 : 2 * count] + total[2 * count :]
    query = jnp.concatenate(
        [
            jnp.concatenate([both[i * count + j : i * count + j + 1] for j in range(count)], 1)
            for i in range(2)
        ],
        0,
    ) + vector(small_ref, 5)
    query = query.astype(jnp.bfloat16).astype(jnp.float32)
    blocks = spread_pairs(jnp.concatenate([query] * 4, 0))
    query_ref[...] = blocks[:PAIR]
    keys = matmul_nt(key_weight_ref[...].astype(jnp.bfloat16), blocks.astype(jnp.bfloat16))
    keys = keys * HD ** (-0.5)
    up = up_ref[...]
    width = up.shape[1] // out_ref.shape[0]
    for block in range(out_ref.shape[0]):
        out_ref[block] = jnp.concatenate(
            [keys, up[:, block * width : (block + 1) * width], meta_ref[...]], 1
        ).astype(jnp.bfloat16)


def row_ids(start, rows, images, local_slots, seq_index):
    ids = iota((rows, 1), 0) + start
    shift = images.bit_length() - 1
    return ids & (images - 1), (ids >> shift) + seq_index * local_slots


def join_weights(seq_index, own_ref, other_ref, weights):
    count = own_ref.shape[1]
    first_core = seq_index == 0
    for block in range(own_ref.shape[0]):
        here = own_ref[block].astype(jnp.float32)
        there = other_ref[block].astype(jnp.float32)
        start = block * 2 * count
        weights[start : start + count, :] = jnp.where(first_core, here, there).astype(jnp.bfloat16)
        weights[start + count : start + 2 * count, :] = jnp.where(first_core, there, here).astype(
            jnp.bfloat16
        )


def embed_kernel(
    seq_ref, own_ref, other_ref, patches_ref, pos_ref, small_ref,
    first_ref, normed_ref, inverse_ref, weights, high, rest,
):
    row_count = patches_ref.shape[0]
    images = 128 // PAIR
    local_slots = row_count // images
    seq_index = seq_ref[0]
    join_weights(seq_index, own_ref, other_ref, weights)
    tokens = token_rows(small_ref)
    table_high, table_rest = split_low(small_ref[0:POS, :])
    high[...] = table_high
    rest[...] = table_rest
    ready(patches_ref, pos_ref, small_ref)

    def step(index, carry):
        rows = pl.ds(pl.multiple_of(index * CHUNK, CHUNK), CHUNK)
        onehot = jnp.where(pos_ref[rows, :] == iota((CHUNK, POS), 1), 1.0, 0.0).astype(jnp.bfloat16)
        embedded = (
            matmul(patches_ref[rows, :], weights[...])
            + matmul(onehot, high[...])
            + matmul(onehot, rest[...])
            + vector(small_ref, 0)
        )
        _, slot = row_ids(index * CHUNK, CHUNK, images, local_slots, seq_index)
        stream = jnp.where(slot == 0, tokens[0:1], jnp.where(slot == 1, tokens[1:2], embedded))
        out, normed, inverse = norm_forward(stream, vector(small_ref, 3), vector(small_ref, 4))
        first_ref[rows, :] = out.astype(jnp.bfloat16)
        normed_ref[rows, :] = normed
        inverse_ref[rows, :] = inverse
        return carry

    lax.fori_loop(0, row_count // CHUNK, step, 0)


def scores_kernel(
    seq_ref, own_ref, other_ref, first_ref, valid_ref,
    packed_ref, exponent_ref, keys_ref, up_ref,
):
    row_count, columns = exponent_ref.shape
    images = columns // PAIR
    seq_index = seq_ref[0]
    first_core = seq_index == 0
    count = own_ref.shape[1]
    hidden = up_ref.shape[1]
    for block in range(own_ref.shape[0]):
        here = own_ref[block].astype(jnp.float32)
        there = other_ref[block].astype(jnp.float32)
        start = block * 2 * count
        for core, pick in enumerate(
            (jnp.where(first_core, here, there), jnp.where(first_core, there, here))
        ):
            place = slice(start + core * count, start + (core + 1) * count)
            keys_ref[place, :] = pick[:, 0:columns].astype(jnp.bfloat16)
            up_ref[place, :] = jnp.where(
                first_core,
                pick[:, columns : columns + hidden],
                pick[:, columns + hidden : columns + 2 * hidden],
            ).astype(jnp.bfloat16)
    scores = matmul(first_ref[...], keys_ref[...])
    image, slot = row_ids(0, row_count, images, row_count // images, seq_index)
    kept = ((iota((row_count, columns), 1) >> 5) == image) & (slot < valid_ref[...])
    scores = jnp.where(kept, scores, MASK_FILL)
    peak = jnp.max(scores, 0, keepdims=True)
    exponent = jnp.exp(scores - peak)
    exponent_ref[...] = exponent
    packed_ref[0:columns, :] = matmul_tn(exponent.astype(jnp.bfloat16), first_ref[...])
    packed_ref[columns : columns + 8, :] = jnp.zeros((8, D), jnp.float32)
    packed_ref[columns : columns + 1, 0:columns] = peak
    packed_ref[columns + 1 : columns + 2, 0:columns] = jnp.sum(exponent, 0, keepdims=True)


def attend_kernel(
    seq_ref, own_ref, other_ref, value_weight_ref, small_ref, pooled_ref, scale_ref, out_ref, turned
):
    columns = pooled_ref.shape[0]
    peak_here = own_ref[columns : columns + 1, 0:columns]
    peak_there = other_ref[columns : columns + 1, 0:columns]
    peak = jnp.maximum(peak_here, peak_there)
    here = jnp.exp(peak_here - peak)
    there = jnp.exp(peak_there - peak)
    total = (
        here * own_ref[columns + 1 : columns + 2, 0:columns]
        + there * other_ref[columns + 1 : columns + 2, 0:columns]
    )
    here = here / total
    there = there / total
    scale_ref[...] = jnp.broadcast_to(here, (8, columns))
    here_rows = jnp.broadcast_to(here, (columns, columns)).T[:, 0:1]
    there_rows = jnp.broadcast_to(there, (columns, columns)).T[:, 0:1]
    pooled = own_ref[0:columns, :] * here_rows + other_ref[0:columns, :] * there_rows
    pooled_ref[...] = pooled
    mixed = matmul(pooled.astype(jnp.bfloat16), value_weight_ref[...])
    attended = collect_pairs(mixed) + vector(small_ref, 6)
    turned[...] = pooled.T
    own = 2 * HEADS
    for block in range(out_ref.shape[0]):
        start = pl.multiple_of(block * 2 * own + seq_ref[0] * own, 8)
        mine = turned[pl.ds(start, own), :]
        pieces = [mine[8 * j : 8 * (j + 1)] for j in range(own // 8)]
        out_ref[block] = jnp.concatenate([attended] + pieces, 1).astype(jnp.bfloat16)


def odd_row(shape):
    return (iota(shape, 0) & 1) == 1


def mlp_kernel(
    device_ref, attended_ref, out_weight_ref, up_ref, down_ref, small_ref, info_ref, bias_ref,
    partial_ref, second_ref, normed_ref, inverse_ref, slope_ref, act_ref, middle_ref, turned_ref,
):
    attended = attended_ref[...].astype(jnp.float32)
    attended = attended.reshape(info_ref.shape[0], D).astype(jnp.bfloat16)
    own = turned_ref.shape[0]
    turned_ref[...] = matmul_nt(own_selector(device_ref[0], own), attended).astype(jnp.bfloat16)
    tokens = token_rows(small_ref)
    stream = jnp.where(odd_row(attended.shape), tokens[1:2], tokens[0:1])
    middle = stream + info_ref[:, 5:6] * (
        matmul(attended, out_weight_ref[...]) + vector(small_ref, 7)
    )
    middle_ref[...] = middle
    out, normed, inverse = norm_forward(middle, vector(small_ref, 8), vector(small_ref, 9))
    second = out.astype(jnp.bfloat16)
    second_ref[...] = second
    normed_ref[...] = normed
    inverse_ref[...] = inverse
    hidden = matmul(second, up_ref[...]) + bias_ref[...]
    act, slope = gelu_parts(hidden)
    act = act.astype(jnp.bfloat16)
    act_ref[...] = act
    slope_ref[...] = slope
    partial_ref[...] = matmul(act, down_ref[...].astype(jnp.bfloat16)).astype(jnp.bfloat16)


def heads_kernel(
    device_ref, mlp_ref, middle_ref, info_ref, small_ref,
    late_ref, bias_ref,
    act_ref, slope_ref, second_ref, up_ref, down_ref,
    partial_ref, result_ref, heads_ref, sums_ref, bias_out_ref, down_out_ref, up_bias_ref, loss_ref,
):
    rows = mlp_ref.shape[0]
    half = 512
    low = jnp.bfloat16
    result = middle_ref[...] + info_ref[:, 6:7] * (
        mlp_ref[...].astype(jnp.float32) + vector(small_ref, 10)
    )
    out, normed, inverse = norm_forward(result, vector(small_ref, 11), vector(small_ref, 12))
    head = out.astype(low)
    columns = iota((rows, half), 1)
    odd = odd_row((rows, half))
    left, right, share_a, share_b = (info_ref[:, k : k + 1] for k in range(4))
    weight = info_ref[:, 4:5]
    logits, targets = [], []
    for part in range(2):
        start = part * half
        class_columns = slice(start, start + half)
        distill_columns = slice(1024 + start, 1024 + start + half)
        piece = jnp.where(
            odd,
            matmul(head, late_ref[:, distill_columns]) + bias_ref[1:2, start : start + half],
            matmul(head, late_ref[:, class_columns]) + bias_ref[0:1, start : start + half],
        )
        where = (columns + start).astype(jnp.float32)
        logits.append(jnp.where(columns + start < CLS, piece, MASK_FILL))
        targets.append(
            share_a * jnp.where(where == left, 1.0, 0.0)
            + share_b * jnp.where(where == right, 1.0, 0.0)
        )
    peak = jnp.maximum(
        jnp.max(logits[0], -1, keepdims=True), jnp.max(logits[1], -1, keepdims=True)
    )
    exponents = [jnp.exp(piece - peak) for piece in logits]
    total = jnp.sum(exponents[0], -1, keepdims=True) + jnp.sum(exponents[1], -1, keepdims=True)
    log_total = peak + jnp.log(total)
    weight_sum = 0.5 * jnp.sum(weight, 0, keepdims=True)
    terms = jnp.zeros((rows, 1), jnp.float32)
    for piece, target in zip(logits, targets):
        terms = terms - 0.5 * jnp.sum(
            target * (piece - log_total), -1, keepdims=True
        )
    loss = jnp.sum(weight * terms, 0, keepdims=True) / weight_sum
    loss_ref[...] = jnp.broadcast_to(loss, loss_ref.shape)
    scale = weight * 0.5 / weight_sum
    head_own = matmul_nt(own_selector(device_ref[0], heads_ref.shape[1]), head).astype(low)
    grad_head = jnp.zeros((rows, D), jnp.float32)
    for part in range(2):
        start = part * half
        class_columns = slice(start, start + half)
        distill_columns = slice(1024 + start, 1024 + start + half)
        grad = scale * (exponents[part] / total - targets[part])
        grad = grad.astype(low).astype(jnp.float32)
        for side, weight_columns in ((0, class_columns), (1, distill_columns)):
            mine = jnp.where(odd == (side == 1), grad, 0.0)
            bias_out_ref[side : side + 1, start : start + half] = jnp.sum(mine, 0, keepdims=True)
            mine = mine.astype(low)
            heads_ref[side, :, start : start + half] = matmul(head_own, mine)
            grad_head = grad_head + matmul_nt(mine, late_ref[:, weight_columns])
    grad_result = norm_in(grad_head, normed, inverse, vector(small_ref, 11))
    result_ref[...] = grad_result
    grad_mlp = (info_ref[:, 6:7] * grad_result).astype(low)
    sums_ref[...] = jnp.zeros(sums_ref.shape, jnp.float32)
    sums_ref[0:1, :] = jnp.sum(grad_mlp.astype(jnp.float32), 0, keepdims=True)
    sums_ref[1:2, :] = jnp.sum(grad_head * normed, 0, keepdims=True)
    sums_ref[2:3, :] = jnp.sum(grad_head, 0, keepdims=True)
    down_out_ref[...] = matmul_tn(act_ref[...], grad_mlp)
    grad_hidden = (
        matmul_nt(grad_mlp, down_ref[...].astype(low)) * slope_ref[...]
    ).astype(low)
    up_bias_ref[...] = jnp.broadcast_to(
        jnp.sum(grad_hidden.astype(jnp.float32), 0, keepdims=True), up_bias_ref.shape
    )
    partial = matmul_nt(grad_hidden, up_ref[...])
    grad_up = matmul_tn(second_ref[...], grad_hidden)
    blocks = partial_ref.shape[0]
    per = rows // blocks
    own = D // blocks
    hidden = grad_up.shape[1]
    pad = jnp.zeros((D, 128 - hidden), jnp.float32)
    grad_up = jnp.concatenate([grad_up, pad], 1)
    for block in range(blocks):
        partial_ref[block, 0:per, :] = partial[block * per : (block + 1) * per].astype(low)
        pieces = [
            grad_up[block * own + 8 * j : block * own + 8 * (j + 1)] for j in range(own // 8)
        ]
        partial_ref[block, per : 2 * per, :] = jnp.concatenate(pieces, 1).astype(low)


def back_kernel(
    index_ref, second_ref, other_ref, normed2_ref, inverse2_ref, result_ref, info_ref, small_ref,
    out_weight_ref, value_weight_ref,
    pooled_ref, scale_ref, exponent_ref, first_ref, normed_ref, inverse_ref, keys_ref,
    patches_ref, pos_ref, sums_ref,
    mine_ref, theirs_ref,
    values, turned_keys, embed, scores, onehot, patch_out, small_out, pooled_grad,
):
    low = jnp.bfloat16
    columns = pooled_ref.shape[0]
    images = columns // PAIR
    row_count = patches_ref.shape[0]
    local_slots = row_count // images
    dp_index, seq_index = index_ref[0], index_ref[1]
    per = 2 * images
    own_rows = pl.ds(pl.multiple_of(dp_index * per, 8), per)
    grad_second = second_ref[...] + other_ref[...]
    normed2 = normed2_ref[own_rows, :]
    grad_middle = result_ref[own_rows, :] + norm_in(
        grad_second, normed2, inverse2_ref[own_rows, :], vector(small_ref, 8)
    )
    grad_attn = (info_ref[own_rows, 5:6] * grad_middle).astype(low)
    grad_att = matmul_nt(grad_attn, out_weight_ref[...]).astype(low)
    att_float = grad_att.astype(jnp.float32)
    att_blocks = spread_pairs(att_float)
    value_rows = matmul_nt(att_blocks.astype(low), value_weight_ref[...]).astype(low)
    values[...] = value_rows
    turned_keys[...] = keys_ref[...].astype(jnp.float32).T.astype(low)
    const = jnp.sum(att_blocks * vector(small_ref, 6), -1, keepdims=True)
    mean = jnp.sum(pooled_ref[...] * value_rows.astype(jnp.float32), -1, keepdims=True) + const
    const = jnp.broadcast_to(const, (columns, columns)).T[0:1, :]
    mean = jnp.broadcast_to(mean, (columns, columns)).T[0:1, :]
    gain = vector(small_ref, 3)

    ready(scale_ref, exponent_ref, first_ref, normed_ref, inverse_ref, pos_ref, patches_ref)

    def step(index, sums):
        gain_sum, shift_sum, embed_sum, class_sum, distill_sum = sums
        rows = pl.ds(pl.multiple_of(index * CHUNK, CHUNK), CHUNK)
        first = first_ref[rows, :]
        probs = exponent_ref[rows, :] * scale_ref[0:1, :]
        grad_probs = matmul_nt(first, values[...]) + const
        grad_scores = (probs * (grad_probs - mean)).astype(low)
        scores[rows, :] = grad_scores
        grad_first = matmul(grad_scores, turned_keys[...]) + matmul(probs.astype(low), values[...])
        normed = normed_ref[rows, :]
        grad_stream = norm_in(grad_first, normed, inverse_ref[rows, :], gain)
        _, slot = row_ids(index * CHUNK, CHUNK, images, local_slots, seq_index)
        grad_embed = jnp.where(slot < 2, 0.0, grad_stream)
        embed[rows, :] = grad_embed.astype(low)
        onehot[rows, :] = jnp.where(pos_ref[rows, :] == iota((CHUNK, POS), 1), 1.0, 0.0).astype(low)
        return (
            gain_sum + jnp.sum(grad_first * normed, 0, keepdims=True),
            shift_sum + jnp.sum(grad_first, 0, keepdims=True),
            embed_sum + jnp.sum(grad_embed, 0, keepdims=True),
            class_sum + jnp.sum(jnp.where(slot == 0, grad_stream, 0.0), 0, keepdims=True),
            distill_sum + jnp.sum(jnp.where(slot == 1, grad_stream, 0.0), 0, keepdims=True),
        )

    zero = jnp.zeros((1, D), jnp.float32)
    gain_sum, shift_sum, embed_sum, class_sum, distill_sum = lax.fori_loop(
        0, row_count // CHUNK, step, (zero,) * 5
    )
    patch_out[...] = matmul_tn(patches_ref[...], embed[...])
    small_out[0:POS, :] = matmul_tn(onehot[...], embed[...])
    by_column = matmul_tn(scores[...], first_ref[...])
    by_pair = jnp.sum(by_column.reshape(images, PAIR, D), 0)
    once = jnp.where(seq_index == 0, 1.0, 0.0)
    leader = jnp.where((dp_index == 0) & (seq_index == 0), 1.0, 0.0)
    middle_even = jnp.sum(jnp.where(odd_row((per, D)), 0.0, grad_middle), 0, keepdims=True)
    middle_odd = jnp.sum(jnp.where(odd_row((per, D)), grad_middle, 0.0), 0, keepdims=True)
    class_sum = class_sum + once * middle_even
    distill_sum = distill_sum + once * middle_odd
    small_out[0:1, :] = class_sum
    small_out[1:2, :] = distill_sum
    vector_rows = (
        embed_sum,
        class_sum,
        distill_sum,
        gain_sum,
        shift_sum,
        zero,
        once * jnp.sum(att_float, 0, keepdims=True),
        once * jnp.sum(grad_attn.astype(jnp.float32), 0, keepdims=True),
        once * jnp.sum(grad_second * normed2, 0, keepdims=True),
        once * jnp.sum(grad_second, 0, keepdims=True),
        leader * sums_ref[0:1, :],
        leader * sums_ref[1:2, :],
        leader * sums_ref[2:3, :],
    )
    for index, row in enumerate(vector_rows):
        small_out[POS + index : POS + index + 1, :] = row
    small_count = small_out.shape[0]
    small_out[POS + 13 : small_count, :] = jnp.zeros((small_count - POS - 13, D), jnp.float32)
    pooled_grad[...] = jnp.concatenate([by_pair, jnp.zeros((128 - PAIR, D), jnp.float32)], 0).T
    own = 2 * HEADS
    attn_half = jnp.where(
        seq_index == 0,
        grad_attn[:, : D // 2].astype(jnp.float32),
        grad_attn[:, D // 2 :].astype(jnp.float32),
    )
    share = small_count // (2 * mine_ref.shape[0])
    for block in range(mine_ref.shape[0]):
        for ref, core in ((mine_ref, seq_index), (theirs_ref, 1 - seq_index)):
            start = pl.multiple_of((block * 2 + core) * own, 8)
            ref[block, 0:own, :] = patch_out[pl.ds(start, own), :].astype(ref.dtype)
            small = pl.multiple_of((block * 2 + core) * share, 8)
            ref[block, own : own + share, :] = small_out[pl.ds(small, share), :].astype(ref.dtype)
            keys = pooled_grad[pl.ds(start, own), :]
            pieces = [keys[8 * j : 8 * (j + 1)] for j in range(own // 8)]
            if ref is mine_ref:
                pieces.append(attn_half)
            else:
                pieces.append(jnp.zeros((8, D // 2), jnp.float32))
            ref[block, own + share :, :] = jnp.concatenate(pieces, 1).astype(ref.dtype)


def known_kernel(
    index_ref, up_own_ref, up_other_ref, heads_ref, down_ref, up_bias_ref, up_ref, known_ref
):
    first_core = index_ref[1] == 0
    blocks = up_own_ref.shape[0]
    own = up_ref.shape[0]
    hidden = down_ref.shape[0]
    columns = []
    for block in range(blocks):
        mine = up_own_ref[block].astype(jnp.float32)
        theirs = up_other_ref[block].astype(jnp.float32)
        for pick in (jnp.where(first_core, mine, theirs), jnp.where(first_core, theirs, mine)):
            columns.append(
                jnp.concatenate(
                    [pick[:, 128 * j : 128 * j + hidden] for j in range(own // 8)], 0
                )
            )
    part = jnp.concatenate(columns, 1)
    up_ref[...] = part
    square = jnp.sum(part * part)
    for side in range(2):
        square = square + jnp.sum(heads_ref[side] * heads_ref[side])
    square = square + jnp.sum(down_ref[...] * down_ref[...])
    bias = up_bias_ref[0:1, :]
    known_ref[...] = jnp.broadcast_to(square + jnp.sum(bias * bias), known_ref.shape)


def owned_kernel(
    index_ref, received_ref, other_attn_ref, out_weight_ref, pooled_ref, turned_ref,
    query_ref, key_weight_ref, known_ref, up_bias_ref,
    patch_ref, block_ref, final_ref,
):
    low = jnp.bfloat16
    first_core = index_ref[1] == 0
    blocks = received_ref.shape[0]
    own = patch_ref.shape[0]
    share = final_ref.shape[1]
    half = D // 2
    total = jnp.sum(received_ref[:, :, :half].astype(jnp.float32), 0)
    right = jnp.sum(received_ref[:, : own + share, half:].astype(jnp.float32), 0)
    patch = jnp.concatenate([total[0:own], right[0:own]], 1)
    small = jnp.concatenate([total[own : own + share], right[own : own + share]], 1)
    keys = jnp.concatenate(
        [total[own + share :, 128 * j : 128 * (j + 1)] for j in range(own // 8)], 0
    )
    patch_ref[...] = patch
    row = iota((share, 1), 0) + index_ref[0] * share
    open_row = (row < 2) | ((row > POS) & (row < POS + 6))
    square = jnp.sum(patch * patch) + jnp.sum(jnp.where(open_row, 0.0, small * small))
    key_high, key_rest = split_low(keys[:, 0:PAIR])
    query_blocks = query_ref[...].astype(low)
    part = (matmul(key_high, query_blocks) + matmul(key_rest, query_blocks)) * HD ** (-0.5)
    block_ref[:, 0:D] = part
    square = square + jnp.sum(part * part)
    key_weight = key_weight_ref[...].astype(low)
    query_sums = collect_pairs(
        matmul_tn(key_high, key_weight) + matmul_tn(key_rest, key_weight)
    ) * HD ** (-0.5)
    here = received_ref[:, own + share :, half:].astype(jnp.float32).reshape(blocks * 8, half)
    there = other_attn_ref[...].astype(jnp.float32).reshape(blocks * 8, half)
    attn = jnp.concatenate(
        [jnp.where(first_core, here, there), jnp.where(first_core, there, here)], 1
    ).astype(low)
    att = matmul_nt(attn, out_weight_ref[...]).astype(low).astype(jnp.float32)
    part = jnp.zeros((own, D), jnp.float32)
    for block in range(blocks):
        spread = spread_pairs(att[block * 8 : (block + 1) * 8]).astype(low)
        turned = pooled_ref[block].astype(jnp.float32)
        turned = jnp.concatenate([turned[:, 128 * j : 128 * (j + 1)] for j in range(own // 8)], 0)
        part = part + matmul(turned.astype(low), spread)
    block_ref[:, D : 2 * D] = part
    square = square + jnp.sum(part * part)
    part = matmul(turned_ref[...], attn)
    block_ref[:, 2 * D : 3 * D] = part
    square = square + jnp.sum(part * part)
    hidden = up_bias_ref.shape[1]
    bias = up_bias_ref[0:1, :]
    square = known_ref[0:1, :] + jnp.broadcast_to(square, (1, 128))
    high, rest = split_low(square)
    middle, last = split_low(square - high.astype(jnp.float32))
    pieces = [
        query_sums[i : i + 1, 128 * j : 128 * (j + 1)] for i in range(2) for j in range(D // 128)
    ]
    side = jnp.concatenate(
        [
            high.astype(jnp.float32),
            middle.astype(jnp.float32),
            last.astype(jnp.float32),
            jnp.concatenate([bias, jnp.zeros((1, 128 - hidden), jnp.float32)], 1),
        ]
        + pieces[8:],
        0,
    )
    final = jnp.concatenate([small, side, jnp.concatenate(pieces[:8], 0)], 1).astype(low)
    final_ref[...] = jnp.broadcast_to(final[None], final_ref.shape)


def final_kernel(
    index_ref, own_ref, other_ref, query_weight_ref, small_ref, mean_ref, square_ref, bias_ref,
    long_ref, long_mean_ref, long_square_ref, *refs,
):
    weights, refs = refs[:17], refs[17:]
    (
        new_ref, mean_new_ref, square_new_ref, vectors_ref, scalar_ref,
        long_new_ref, long_mean_new_ref, long_square_new_ref,
    ), refs = refs[:8], refs[8:]
    results, rows = refs[:12], refs[12]
    low = jnp.bfloat16
    first_core = index_ref[1] == 0
    share = own_ref.shape[1]
    hidden = weights[8].shape[0]
    count = new_ref.shape[0]
    square = jnp.zeros((1, 128), jnp.float32)
    sums = jnp.zeros((8, 128), jnp.float32)
    rest = jnp.zeros((8, 128), jnp.float32)
    biases = []
    for block in range(own_ref.shape[0]):
        here = own_ref[block].astype(jnp.float32)
        there = other_ref[block].astype(jnp.float32)
        for core, pick in enumerate(
            (jnp.where(first_core, here, there), jnp.where(first_core, there, here))
        ):
            index = block * 2 + core
            rows[index * share : (index + 1) * share, :] = pick[:, :D]
            side = pick[:, D : D + 128]
            square = square + (side[0:1] + side[1:2] + side[2:3])
            biases.append(side[3:4, :hidden])
            sums = sums + pick[:, D + 128 :]
            rest = rest + side
    pieces = [sums[k : k + 1] for k in range(8)] + [rest[k : k + 1] for k in range(4, 8)]
    grad_query = jnp.concatenate(
        [jnp.concatenate(pieces[0:6], 1), jnp.concatenate(pieces[6:12], 1)], 0
    )
    gain = vector(small_ref, 3)
    token_out, token_normed, token_inverse = norm_forward(
        token_rows(small_ref), gain, vector(small_ref, 4)
    )
    eight = jnp.concatenate([grad_query, jnp.zeros((6, D), jnp.float32)], 0)
    token_grad = matmul_nt(eight.astype(low), query_weight_ref[...])
    token_in = norm_in(token_grad, token_normed, token_inverse, gain)
    rows[0:2, :] = rows[0:2, :] + token_in[0:2]
    opened = rows[POS + 1 : POS + 6, :] + jnp.concatenate(
        [
            token_in[0:2],
            jnp.sum(token_grad * token_normed, 0, keepdims=True),
            jnp.sum(token_grad, 0, keepdims=True),
            jnp.sum(grad_query, 0, keepdims=True),
        ],
        0,
    )
    rows[POS + 1 : POS + 6, :] = opened
    token_low = token_out.astype(low)
    own = weights[0].shape[0]
    token_own = matmul_nt(own_selector(index_ref[0], own), token_low)
    owned_query = token_own[:, 0:1] * grad_query[0:1] + token_own[:, 1:2] * grad_query[1:2]
    token_float = token_low.astype(jnp.float32)

    def product(left, right):
        return jnp.sum(left * right, -1, keepdims=True)

    cross = product(token_float[0:1], token_float[1:2]) * product(grad_query[0:1], grad_query[1:2])
    query_square = 2.0 * cross
    for i in range(2):
        query_square = query_square + product(
            token_float[i : i + 1], token_float[i : i + 1]
        ) * product(grad_query[i : i + 1], grad_query[i : i + 1])
    bias = bias_ref[...]
    table = rows[0:2, :]
    total = square[:, 0:1] + query_square
    for value in (bias, table, opened):
        total = total + jnp.sum(jnp.sum(value * value, 0, keepdims=True), 1, keepdims=True)
    norm = jnp.sqrt(total)
    factor = jnp.minimum(1.0, CLIP_NORM / (norm + 1e-06))
    scalar_ref[...] = norm
    gradient = rows[0:count, :]
    vectors_ref[...] = rows[POS:count, :] * factor

    def update(targets, weight, first, second, gradient, decay, rate):
        new = adam_update(weight[...], first[...], second[...], gradient, factor, decay, rate)
        for target, value in zip(targets, new):
            target[...] = value
            target.send()

    update(
        (new_ref, mean_new_ref, square_new_ref), small_ref, mean_ref, square_ref, gradient,
        0.0, SMALL_RATE,
    )
    long_gradient = jnp.concatenate(biases + [bias[0:1, :CLS], bias[1:2, :CLS]], 1)
    update(
        (long_new_ref, long_mean_new_ref, long_square_new_ref),
        long_ref, long_mean_ref, long_square_ref, long_gradient, 0.0, SMALL_RATE,
    )
    gradients = (
        weights[3][...],
        jnp.concatenate([owned_query, weights[7][...], weights[16][...]], 1),
        weights[11][...],
        jnp.concatenate([weights[15][0, :, :CLS], weights[15][1, :, :CLS]], 1),
    )
    for group, gradient in enumerate(gradients):
        update(
            results[3 * group : 3 * group + 3], *weights[4 * group : 4 * group + 3], gradient,
            DECAY_RATE, LEARN_RATE,
        )


def chip_sum_kernel(mine_ref, theirs_ref, out_ref):
    total = mine_ref[...].astype(jnp.float32) + theirs_ref[...].astype(jnp.float32)
    out_ref[...] = total.astype(jnp.bfloat16)


def shards_tiled(
    patches,
    pos_index,
    valid,
    classes,
    mixing,
    image_weight,
    drop_keep,
    patch_weight,
    patch_mean,
    patch_square,
    block_weight,
    block_mean,
    block_square,
    down_weight,
    down_mean,
    down_square,
    heads_weight,
    heads_mean,
    heads_square,
    small_rows,
    rows_mean,
    rows_square,
    small_long,
    long_mean,
    long_square,
):
    low = jnp.bfloat16
    f32 = jnp.float32
    images, local_slots, patch_dim = patches.shape
    row_count = images * local_slots
    dp_size = lax.axis_size("dp")
    seq_size = lax.axis_size("seq")
    devices = dp_size * seq_size
    dp_index = lax.axis_index("dp").astype(jnp.int32)
    seq_index = lax.axis_index("seq").astype(jnp.int32)
    device = dp_index * seq_size + seq_index
    own_rows = patch_weight.shape[0]
    own_hidden = down_weight.shape[0]
    all_images = dp_size * images
    rows = all_images * 2
    per_chip = images * 2
    columns = images * PAIR
    half = D // 2
    device_scalar = device[None]
    seq_scalar = seq_index[None]
    device_seq = jnp.stack([device, seq_index])
    dp_seq = jnp.stack([dp_index, seq_index])

    late_width = 2 * D + 2048
    (late,) = kernel_call(
        late_kernel,
        [((own_rows, late_width), low)],
        [block_weight, heads_weight],
        {0: slice(2 * D, 4 * D)},
    )
    device_scalar, late = lax.optimization_barrier((device_scalar, late))
    gathered_late = lax.all_gather(late, ALL, axis=0, tiled=True)
    value_lanes, out_lanes = slice(0, D), slice(D, 2 * D)
    head_lanes = slice(2 * D, late_width)
    early, last = kernel_call(
        prepare_kernel,
        [((dp_size, own_rows, D + 128), low), ((own_rows, D), low)],
        [device_scalar, small_rows, block_weight, patch_weight],
        {2: slice(0, D)},
    )
    gathered_last = lax.all_gather(last, ALL, axis=0, tiled=True)
    flat_patches = patches.transpose(1, 0, 2).reshape(row_count, patch_dim)
    flat_pos = pos_index.T.reshape(row_count, 1)
    valid_columns = jnp.repeat(valid, PAIR)[None]
    up_shift = lax.dynamic_slice_in_dim(small_long, device * own_hidden, own_hidden, 0)[None]
    meta = jnp.concatenate(
        [classes // 32, classes % 32, mixing[:, None], image_weight[:, None], drop_keep], 1
    )
    meta_width = meta.shape[1]
    meta_count = images * meta_width
    pair_hidden = 2 * own_hidden
    key_width = columns + pair_hidden + 64
    meta = meta.reshape(1, meta_count).astype(f32)
    meta = jnp.pad(meta, ((0, own_rows - 1), (0, 64 - meta_count)))
    early = exchange(early, "dp")
    early, flat_patches, flat_pos, valid_columns, up_shift, meta = lax.optimization_barrier(
        (early, flat_patches, flat_pos, valid_columns, up_shift, meta)
    )
    early_other = swap_cores(early)

    query_lanes = slice(D, D + 128)
    keyed, query_blocks = kernel_call(
        query_kernel,
        [((dp_size, own_rows, key_width), low), ((PAIR, D), f32)],
        [early, early_other, block_weight, block_weight, small_rows, meta],
        {0: query_lanes, 1: query_lanes, 2: slice(D, 2 * D), 3: slice(4 * D, 4 * D + FF)},
        loose=(0, 1),
    )
    keyed = exchange(keyed, "dp")
    keyed_other = swap_cores(keyed)
    metas = keyed[:, 0, key_width - 64 : key_width - 64 + meta_count]
    metas = metas.astype(f32).reshape(all_images, meta_width)
    labels = metas[:, 0:3] * 32.0 + metas[:, 3:6]
    share = metas[:, 6:7] / 16.0
    weight_keep = jnp.concatenate([metas[:, 7:8], metas[:, 8:10] * DROP_SCALE], 1)
    ones = jnp.ones_like(share)
    info_even = jnp.concatenate([labels[:, 0:2], share, 1.0 - share, weight_keep, ones], 1)
    info_odd = jnp.concatenate(
        [labels[:, 2:3], labels[:, 2:3], ones, 0.0 * ones, weight_keep, ones], 1
    )
    info = jnp.stack([info_even, info_odd], 1).reshape(rows, 8)

    first, normed, inverse = kernel_call(
        embed_kernel,
        [
            ((row_count, D), low),
            ((row_count, D), f32),
            ((row_count, 1), f32),
        ],
        [seq_scalar, early, early_other, flat_patches, flat_pos, small_rows],
        {1: slice(0, D), 2: slice(0, D)},
        scratch=[
            pltpu.VMEM((D, D), low),
            pltpu.VMEM((POS, D), low),
            pltpu.VMEM((POS, D), low),
        ],
        loose=(1, 2),
        flops=2_000_000_000,
    )
    packed, exponent, keys, up_own = kernel_call(
        scores_kernel,
        [
            ((columns + 8, D), f32),
            ((row_count, columns), f32),
            ((D, columns), low),
            ((D, own_hidden), low),
        ],
        [seq_scalar, keyed, keyed_other, first, valid_columns],
        loose=(1, 2),
    )
    packed_other = swap_cores(packed)
    pooled, scale, asked = kernel_call(
        attend_kernel,
        [
            ((columns, D), f32),
            ((8, columns), f32),
            ((dp_size, per_chip, D + own_rows // 8 * columns), low),
        ],
        [seq_scalar, packed, packed_other, gathered_late, small_rows],
        {3: value_lanes},
        scratch=[pltpu.VMEM((D, columns), f32)],
        loose=(2,),
    )
    asked = exchange(asked, "dp")

    partial, second, second_normed, second_inverse, slope, act, middle, attended_turned = (
        kernel_call(
            mlp_kernel,
            [
                ((rows, D), low),
                ((rows, D), low),
                ((rows, D), f32),
                ((rows, 1), f32),
                ((rows, own_hidden), f32),
                ((rows, own_hidden), low),
                ((rows, D), f32),
                ((own_rows, rows), low),
            ],
            [
                device_scalar, asked, gathered_late, up_own, down_weight, small_rows, info,
                up_shift,
            ],
            {1: slice(0, D), 2: out_lanes},
            loose=(1,),
        )
    )

    def chip_sum(blocks):
        summed = jnp.sum(blocks.astype(f32), 0)
        return summed, swap_cores(summed)

    here, there = chip_sum(exchange(partial.reshape(dp_size, per_chip, D), "dp"))
    mlp_rows = gather_blocks((here + there).astype(low), "dp").reshape(rows, D)
    long_pad = jnp.zeros((1, 1024 - CLS), f32)
    head_shift = jnp.concatenate(
        [
            jnp.concatenate([small_long[None, FF : FF + CLS], long_pad], 1),
            jnp.concatenate([small_long[None, FF + CLS :], long_pad], 1),
        ],
        0,
    )
    sent, grad_result, heads_grad, sums, head_bias, owned_down, up_bias, loss = kernel_call(
        heads_kernel,
        [
            ((dp_size, 2 * per_chip, D), low),
            ((rows, D), f32),
            ((2, own_rows, 1024), f32),
            ((8, D), f32),
            ((2, 1024), f32),
            ((own_hidden, D), f32),
            ((8, own_hidden), f32),
            ((8, 128), f32),
        ],
        [
            device_scalar, mlp_rows, middle, info, small_rows,
            gathered_late, head_shift,
            act, slope, second, up_own, down_weight,
        ],
        {5: head_lanes},
        loose=(1,),
    )
    received = exchange(sent, "dp")
    second_here, second_there = chip_sum(received[:, :per_chip])
    up_left, up_right = received[:, per_chip:, :half], received[:, per_chip:, half:]
    up_here = jnp.where(seq_index == 0, up_left, up_right)
    up_there = swap_cores(jnp.where(seq_index == 0, up_right, up_left))

    second_here, gathered_last = lax.optimization_barrier((second_here, gathered_last))

    small_share = 8
    share_rows = own_rows + small_share + 8
    mine, theirs = kernel_call(
        back_kernel,
        [((dp_size, share_rows, D), low), ((dp_size, share_rows, D), low)],
        [
            dp_seq, second_here, second_there, second_normed, second_inverse, grad_result, info,
            small_rows, gathered_late, gathered_late,
            pooled, scale, exponent, first, normed, inverse, keys, flat_patches, flat_pos, sums,
        ],
        scratch=[
            pltpu.VMEM((columns, D), low),
            pltpu.VMEM((columns, D), low),
            pltpu.VMEM((row_count, D), low),
            pltpu.VMEM((row_count, columns), low),
            pltpu.VMEM((row_count, POS), low),
            pltpu.VMEM((patch_dim, D), f32),
            pltpu.VMEM((devices * small_share, D), f32),
            pltpu.VMEM((D, 128), f32),
        ],
        windows={8: out_lanes, 9: value_lanes},
        loose=(1, 2),
        flops=4_000_000_000,
    )
    (chip_terms,) = kernel_call(
        chip_sum_kernel, [(mine.shape, low)], [mine, swap_cores(theirs)], loose=(1,)
    )
    received = exchange(chip_terms, "dp")
    owned_up, known = kernel_call(
        known_kernel,
        [((own_rows, FF), f32), ((8, 128), f32)],
        [device_seq, up_here, up_there, heads_grad, owned_down, up_bias],
    )
    loss = loss[0, 0]
    received, owned_up, known, loss = lax.optimization_barrier((received, owned_up, known, loss))
    attn_other = swap_cores(received[:, own_rows + small_share :, half:])
    final_width = D + 256
    owned_patch, owned_block, final = kernel_call(
        owned_kernel,
        [
            ((own_rows, D), f32),
            ((own_rows, 3 * D), f32),
            ((dp_size, small_share, final_width), low),
        ],
        [
            device_seq, received, attn_other, gathered_late, asked, attended_turned,
            query_blocks, block_weight, known, up_bias,
        ],
        {3: out_lanes, 4: slice(D, D + own_rows // 8 * columns), 7: slice(D, 2 * D)},
        loose=(2,),
        near=(1,),
    )
    final = exchange(final, "dp")
    final_other = swap_cores(final)
    small_count = POS + 13
    long_count = small_long.shape[0]
    (
        rows_new, rows_mean_new, rows_square_new, vectors_grad, scalars,
        long_new, long_mean_new, long_square_new,
        patch_new, patch_mean_new, patch_square_new,
        block_new, block_mean_new, block_square_new,
        down_new, down_mean_new, down_square_new,
        heads_new, heads_mean_new, heads_square_new,
    ) = kernel_call(
        final_kernel,
        [((small_count, D), f32)] * 3
        + [((13, D), f32), ((1, 1), f32)]
        + [((1, long_count), f32)] * 3
        + [
            (weight.shape, f32)
            for weight in (patch_weight, block_weight, down_weight, heads_weight)
            for _ in range(3)
        ],
        [
            device_seq, final, final_other, gathered_last,
            small_rows, rows_mean, rows_square, head_bias,
            small_long[None], long_mean[None], long_square[None],
            patch_weight, patch_mean, patch_square, owned_patch,
            block_weight, block_mean, block_square, owned_block,
            down_weight, down_mean, down_square, owned_down,
            heads_weight, heads_mean, heads_square, heads_grad, owned_up,
        ],
        scratch=[pltpu.VMEM((devices * small_share, D), f32)],
        limit=24,
        loose=(1, 2),
        near=(3, 4, 5, 6, 15, 16, 17, 19, 20, 21, 23, 24, 25),
    )
    grad_norm = scalars.reshape(())
    long_new, long_mean_new, long_square_new = (
        value.reshape(long_count) for value in (long_new, long_mean_new, long_square_new)
    )
    return (
        loss,
        grad_norm,
        patch_new,
        patch_mean_new,
        patch_square_new,
        block_new,
        block_mean_new,
        block_square_new,
        down_new,
        down_mean_new,
        down_square_new,
        heads_new,
        heads_mean_new,
        heads_square_new,
        rows_new,
        rows_mean_new,
        rows_square_new,
        long_new,
        long_mean_new,
        long_square_new,
        vectors_grad,
    )


def shards_plain(
    patches,
    pos_index,
    valid,
    classes,
    mixing,
    image_weight,
    drop_keep,
    patch_weight,
    patch_mean,
    patch_square,
    block_weight,
    block_mean,
    block_square,
    down_weight,
    down_mean,
    down_square,
    heads_weight,
    heads_mean,
    heads_square,
    small_rows,
    rows_mean,
    rows_square,
    small_long,
    long_mean,
    long_square,
):
    low = jnp.bfloat16
    f32 = jnp.float32
    images, local_slots, patch_dim = patches.shape
    row_count = images * local_slots
    dp_size = lax.axis_size("dp")
    seq_size = lax.axis_size("seq")
    devices = dp_size * seq_size
    seq_index = lax.axis_index("seq")
    device = lax.axis_index("dp") * seq_size + seq_index
    own_rows = patch_weight.shape[0]
    own_hidden = down_weight.shape[0]
    own_images = images // seq_size
    all_images = dp_size * images
    pairs = 2 * HEADS
    table = small_rows[:POS]
    vectors = small_rows[POS:]

    gathered_late = lax.all_gather(
        jnp.concatenate([block_weight[:, 2 * D : 4 * D], heads_weight], 1).astype(low),
        ALL,
        axis=0,
        tiled=True,
    )
    gathered_query_key = lax.all_gather(
        lax.optimization_barrier((block_weight[:, : 2 * D].astype(low), gathered_late[:8, :128]))[0],
        ALL,
        axis=0,
        tiled=True,
    )

    tokens = vectors[1:3] + table[0:2]
    token_out, token_normed, token_inverse = norm_forward(tokens, vectors[3], vectors[4])
    token_low = token_out.astype(low)
    select_own = (
        lax.broadcasted_iota(jnp.int32, (own_rows, D), 0) + device * own_rows
        == lax.broadcasted_iota(jnp.int32, (own_rows, D), 1)
    ).astype(low)
    token_own = matmul_nt(token_low, select_own).astype(low)
    query_partial = matmul(token_own, block_weight[:, :D].astype(low))
    query = jnp.sum(gather_blocks(query_partial), 0) + vectors[5]
    query_low = query.astype(low)
    head_of = lax.broadcasted_iota(jnp.int32, (HEADS, D), 1) // HD
    head_mask = head_of == lax.broadcasted_iota(jnp.int32, (HEADS, D), 0)
    query_blocks = jnp.where(head_mask[None], query_low[:, None, :], 0).reshape(pairs, D)
    key_own = matmul_nt(block_weight[:, D : 2 * D].astype(low), query_blocks.astype(low)) * HD ** (
        -0.5
    )
    meta = jnp.concatenate(
        [
            (classes // 32),
            (classes % 32),
            mixing[:, None],
            image_weight[:, None],
            drop_keep,
        ],
        1,
    )
    meta_width = meta.shape[1]
    meta_columns = -(-images * meta_width // own_rows)
    meta = jnp.pad(meta.reshape(-1), (0, own_rows * meta_columns - images * meta_width))
    meta = meta.reshape(own_rows, meta_columns).astype(low)
    extra = -(-(pairs + meta_columns) // 128) * 128
    early = jnp.concatenate(
        [
            patch_weight.astype(low),
            key_own.astype(low),
            meta,
            jnp.zeros((own_rows, extra - pairs - meta_columns), low),
        ],
        1,
    )
    early = gather_blocks(early, "dp").reshape(dp_size, own_rows, D + extra)
    early = join_cores(early, seq_index, 1)
    metas = early[:, 0, :, D + pairs : D + pairs + meta_columns].astype(f32)
    metas = metas.reshape(dp_size, own_rows * meta_columns)[:, : images * meta_width]
    metas = metas.reshape(all_images, meta_width)
    early = early.reshape(D, D + extra)
    full_patch = early[:, :D]
    key_vectors = early[:, D : D + pairs]

    slot_global = seq_index * local_slots + lax.broadcasted_iota(jnp.int32, (1, local_slots, 1), 1)
    is_class = slot_global == 0
    is_distill = slot_global == 1
    special = is_class | is_distill
    key_mask = slot_global < valid[:, None, None]
    flat_patches = patches.reshape(row_count, patch_dim)
    onehot_pos = (
        pos_index.reshape(row_count)[:, None]
        == lax.broadcasted_iota(jnp.int32, (1, POS), 1)
    ).astype(low)
    table_high, table_rest = split_low(table)
    embedded = matmul(flat_patches, full_patch)
    positions = matmul(onehot_pos, table_high) + matmul(onehot_pos, table_rest)
    embedded = (embedded + positions + vectors[0]).reshape(images, local_slots, D)
    stream = jnp.where(is_class, tokens[0], jnp.where(is_distill, tokens[1], embedded))
    first_out, first_normed, first_inverse = norm_forward(stream, vectors[3], vectors[4])
    first_low = first_out.astype(low)
    flat_first = first_low.reshape(row_count, D)
    scores = matmul(flat_first, key_vectors).reshape(images, local_slots, pairs)
    scores = jnp.where(key_mask, scores, MASK_FILL)
    local_peak = jnp.max(scores, 1, keepdims=True)
    exponent = jnp.exp(scores - local_peak)
    local_total = jnp.sum(exponent, 1, keepdims=True)
    local_pooled = jnp.einsum(
        "nlm,nld->nmd", exponent.astype(low), first_low, preferred_element_type=f32
    )
    packed = jnp.concatenate(
        [
            local_pooled,
            jnp.broadcast_to(local_peak.transpose(0, 2, 1), (images, pairs, 64)),
            jnp.broadcast_to(local_total.transpose(0, 2, 1), (images, pairs, 64)),
        ],
        2,
    )
    other = swap_cores(packed)
    other_pooled = other[:, :, :D]
    peak_here = local_peak.transpose(0, 2, 1)
    peak_there = other[:, :, D : D + 1]
    peak = jnp.maximum(peak_here, peak_there)
    scale_here = jnp.exp(peak_here - peak)
    scale_there = jnp.exp(peak_there - peak)
    total = (
        scale_here * local_total.transpose(0, 2, 1) + scale_there * other[:, :, D + 64 : D + 65]
    )
    pooled = (scale_here * local_pooled + scale_there * other_pooled) / total
    probs = exponent * (scale_here / total).transpose(0, 2, 1)
    pooled_low = pooled.astype(low)
    own_pooled = lax.dynamic_slice_in_dim(pooled_low, seq_index * own_images, own_images, 0)

    up_blocks = (
        block_weight[:, 4 * D :]
        .astype(low)
        .reshape(own_rows, devices, own_hidden)
        .transpose(1, 0, 2)
        .reshape(devices, own_rows * own_hidden)
    )
    pooled_blocks = (
        own_pooled.reshape(own_images * pairs, devices, own_rows)
        .transpose(1, 0, 2)
        .reshape(devices, own_images * pairs * own_rows)
    )
    received = exchange(jnp.concatenate([up_blocks, pooled_blocks], 1))
    up_own = received[:, : own_rows * own_hidden].reshape(D, own_hidden)
    pooled_own = received[:, own_rows * own_hidden :].reshape(all_images, 2, HEADS, own_rows)

    full_value = gathered_late[:, :D]
    full_out = gathered_late[:, D : 2 * D]
    full_heads = gathered_late[:, 2 * D :]
    mixed = matmul(own_pooled.reshape(own_images * pairs, D), full_value)
    attended = jnp.sum(
        jnp.where(head_mask, mixed.reshape(own_images * 2, HEADS, D), 0.0), 1
    ) + vectors[6]
    attended = attended.astype(low)
    rows = all_images * 2
    attended = gather_blocks(attended).reshape(rows, D)
    keep_float = metas[:, 8:10] * DROP_SCALE
    keep_rows = jnp.repeat(keep_float, 2, axis=0)
    keep_first = keep_rows[:, 0:1]
    keep_second = keep_rows[:, 1:2]
    middle = jnp.tile(tokens, (all_images, 1)) + keep_first * (
        matmul(attended, full_out) + vectors[7]
    )
    second_out, second_normed, second_inverse = norm_forward(middle, vectors[8], vectors[9])
    second_low = second_out.astype(low)
    hidden_bias = lax.dynamic_slice_in_dim(small_long, device * own_hidden, own_hidden, 0)
    hidden = matmul(second_low, up_own) + hidden_bias
    activated, gelu_slope = gelu_parts(hidden)
    activated = activated.astype(low)
    down_low = down_weight.astype(low)
    mlp_partial = matmul(activated, down_low).astype(low)
    row_share = own_images * 2
    mlp_own = jnp.sum(
        exchange(mlp_partial.reshape(devices, row_share, D)).astype(f32), 0
    )
    mlp_rows = gather_blocks(mlp_own.astype(low)).reshape(rows, D).astype(f32)
    result = middle + keep_second * (mlp_rows + vectors[10])

    head_out, head_normed, head_inverse = norm_forward(result, vectors[11], vectors[12])
    head_low = head_out.astype(low).reshape(all_images, 2, D)
    logits_class = matmul(head_low[:, 0], full_heads[:, :CLS]) + small_long[FF : FF + CLS]
    logits_distill = matmul(head_low[:, 1], full_heads[:, CLS:]) + small_long[FF + CLS :]
    columns = lax.broadcasted_iota(jnp.int32, (1, CLS), 1)
    labels = (metas[:, 0:3] * 32.0 + metas[:, 3:6]).astype(jnp.int32)
    share = metas[:, 6:7] / 16.0
    weights = metas[:, 7]
    weight_sum = jnp.sum(weights)
    target = share * (labels[:, 0:1] == columns).astype(f32) + (1.0 - share) * (
        labels[:, 1:2] == columns
    ).astype(f32)
    teacher = (labels[:, 2:3] == columns).astype(f32)
    log_class = jax.nn.log_softmax(logits_class, -1)
    log_distill = jax.nn.log_softmax(logits_distill, -1)
    terms = -0.5 * (jnp.sum(target * log_class, -1) + jnp.sum(teacher * log_distill, -1))
    loss = jnp.sum(weights * terms) / weight_sum
    scale_rows = (weights * 0.5 / weight_sum)[:, None]
    grad_class = (scale_rows * (jnp.exp(log_class) - target)).astype(low)
    grad_distill = (scale_rows * (jnp.exp(log_distill) - teacher)).astype(low)
    head_own = matmul_nt(select_own, head_low.reshape(rows, D)).astype(low)
    head_own = head_own.reshape(own_rows, all_images, 2)
    owned_heads = jnp.concatenate(
        [matmul(head_own[:, :, 0], grad_class), matmul(head_own[:, :, 1], grad_distill)], 1
    )
    head_bias = jnp.concatenate(
        [jnp.sum(grad_class.astype(f32), 0), jnp.sum(grad_distill.astype(f32), 0)]
    )
    grad_head_rows = jnp.stack(
        [matmul_nt(grad_class, full_heads[:, :CLS]), matmul_nt(grad_distill, full_heads[:, CLS:])],
        1,
    ).reshape(rows, D)
    grad_result, final_gain, final_shift = norm_backward(
        grad_head_rows, head_normed, head_inverse, vectors[11]
    )

    grad_mlp = (keep_second * grad_result).astype(low)
    owned_down = matmul_tn(activated, grad_mlp)
    down_bias = jnp.sum(grad_mlp.astype(f32), 0)
    grad_hidden = (matmul_nt(grad_mlp, down_low) * gelu_slope).astype(low)
    up_bias = jnp.sum(grad_hidden.astype(f32), 0)
    grad_up = matmul_tn(second_low, grad_hidden).astype(low)
    grad_second_partial = matmul_nt(grad_hidden, up_own).astype(low)
    received = exchange(
        jnp.concatenate(
            [
                grad_second_partial.reshape(devices, row_share * D),
                grad_up.reshape(devices, own_rows * own_hidden),
            ],
            1,
        )
    )
    grad_second = jnp.sum(
        received[:, : row_share * D].astype(f32).reshape(devices, row_share, D), 0
    )
    owned_up = (
        received[:, row_share * D :]
        .reshape(devices, own_rows, own_hidden)
        .transpose(1, 0, 2)
        .reshape(own_rows, FF)
        .astype(f32)
    )
    row_start = device * row_share
    own_normed = lax.dynamic_slice_in_dim(second_normed, row_start, row_share, 0)
    own_inverse = lax.dynamic_slice_in_dim(second_inverse, row_start, row_share, 0)
    own_result = lax.dynamic_slice_in_dim(grad_result, row_start, row_share, 0)
    own_keep = lax.dynamic_slice_in_dim(keep_first, row_start, row_share, 0)
    grad_second_in, second_gain, second_shift = norm_backward(
        grad_second, own_normed, own_inverse, vectors[8]
    )
    grad_middle = own_result + grad_second_in
    grad_attn_own = (own_keep * grad_middle).astype(low)
    out_bias = jnp.sum(grad_attn_own.astype(f32), 0)
    grad_attn = join_cores(grad_attn_own, seq_index, 0).reshape(images * 2, D)
    grad_att = matmul_nt(grad_attn, full_out).astype(low)
    value_bias = jnp.sum(
        lax.dynamic_slice_in_dim(grad_att, seq_index * row_share, row_share, 0).astype(f32), 0
    )
    grad_att_blocks = jnp.where(
        head_mask, grad_att.reshape(images * 2, 1, D), jnp.zeros((), low)
    ).reshape(images * pairs, D)
    value_vectors = matmul_nt(grad_att_blocks, full_value).astype(low)
    value_const = jnp.sum(grad_att_blocks.astype(f32) * vectors[6], -1).reshape(images, pairs)
    value_vectors = value_vectors.reshape(images, pairs, D)
    mean_grad = jnp.sum(pooled * value_vectors.astype(f32), -1) + value_const
    grad_probs = (
        jnp.einsum("nld,nmd->nlm", first_low, value_vectors, preferred_element_type=f32)
        + value_const[:, None, :]
    )
    grad_scores = (probs * (grad_probs - mean_grad[:, None, :])).astype(low)
    key_rows = jnp.broadcast_to(key_vectors.T[None], (images, pairs, D))
    grad_first = jnp.einsum(
        "nlk,nkd->nld",
        jnp.concatenate([grad_scores, probs.astype(low)], 2),
        jnp.concatenate([key_rows, value_vectors], 1),
        preferred_element_type=f32,
    )
    grad_stream, first_gain, first_shift = norm_backward(
        grad_first, first_normed, first_inverse, vectors[3]
    )
    pooled_grad = matmul_tn(grad_scores.reshape(row_count, pairs), flat_first)
    query_grad_blocks = matmul(pooled_grad.astype(low), gathered_query_key[:, D:]) * HD ** (-0.5)
    grad_query = jnp.sum(
        jnp.where(head_mask, query_grad_blocks.reshape(2, HEADS, D), 0.0), 1
    )
    token_grad = matmul_nt(grad_query.astype(low), gathered_query_key[:, :D])
    token_grad_in, token_gain, token_shift = norm_backward(
        token_grad, token_normed, token_inverse, vectors[3]
    )
    grad_tokens = (
        token_grad_in
        + jnp.sum(grad_middle.reshape(own_images, 2, D), 0)
        + jnp.stack(
            [
                jnp.sum(jnp.where(is_class, grad_stream, 0.0), (0, 1)),
                jnp.sum(jnp.where(is_distill, grad_stream, 0.0), (0, 1)),
            ]
        )
    )
    grad_embed = jnp.where(special, 0.0, grad_stream)
    embed_low = grad_embed.astype(low).reshape(row_count, D)
    grad_patch = matmul_tn(flat_patches, embed_low)
    grad_table = matmul_tn(onehot_pos, embed_low)
    patch_bias = jnp.sum(grad_embed, (0, 1))
    leader = (device == 0).astype(f32)
    small_terms = jnp.concatenate(
        [
            grad_tokens,
            grad_table[2:],
            patch_bias[None],
            grad_tokens,
            (first_gain + token_gain)[None],
            (first_shift + token_shift)[None],
            jnp.sum(grad_query, 0)[None],
            value_bias[None],
            out_bias[None],
            second_gain[None],
            second_shift[None],
            leader * down_bias[None],
            leader * final_gain[None],
            leader * final_shift[None],
        ],
        0,
    )
    small_count = POS + 13
    small_share = -(-small_count // devices)
    small_terms = jnp.pad(small_terms, ((0, small_share * devices - small_count), (0, 0)))

    key_terms = (
        pooled_grad.reshape(pairs, devices, own_rows)
        .transpose(1, 0, 2)
        .reshape(devices, pairs * own_rows)
    )
    key_share = -(-pairs * own_rows // D)
    key_terms = jnp.pad(key_terms, ((0, 0), (0, key_share * D - pairs * own_rows)))
    terms_rows = jnp.concatenate(
        [
            grad_patch.reshape(dp_size, seq_size, own_rows, D),
            small_terms.reshape(dp_size, seq_size, small_share, D),
            key_terms.reshape(dp_size, seq_size, key_share, D),
            jnp.broadcast_to(grad_query, (dp_size, seq_size, 2, D)),
        ],
        2,
    )
    mine = lax.dynamic_index_in_dim(terms_rows, seq_index, 1, keepdims=False)
    theirs = lax.dynamic_index_in_dim(terms_rows, 1 - seq_index, 1, keepdims=False)
    chip_terms = mine + swap_cores(theirs.astype(low)).astype(f32)
    pair_share = 2 * row_share
    grad_att_own = lax.dynamic_slice_in_dim(grad_att, seq_index * row_share, row_share, 0)
    pair_own = jnp.concatenate([grad_attn_own, grad_att_own], 0)
    sent = jnp.concatenate(
        [chip_terms.astype(low), jnp.broadcast_to(pair_own, (dp_size, pair_share, D))], 1
    )
    received = exchange(sent, "dp")
    summed_share = chip_terms.shape[1]
    reduced = jnp.sum(received[:, :summed_share].astype(f32), 0)
    pair_rows = join_cores(received[:, summed_share:], seq_index, 1)
    pair_rows = pair_rows.reshape(devices, 2, row_share, D)
    owned_patch = reduced[:own_rows]
    owned_small = reduced[own_rows : own_rows + small_share]
    key_start = own_rows + small_share
    key_reduced = reduced[key_start : key_start + key_share].reshape(-1)[: pairs * own_rows]
    key_reduced = key_reduced.reshape(2, HEADS, own_rows)
    query_reduced = reduced[key_start + key_share :]

    owned_query = matmul_tn(token_own, query_reduced.astype(low))
    key_left = jnp.repeat(
        key_reduced.transpose(2, 0, 1), HD, axis=2
    )
    owned_key = jnp.sum(key_left * query_low.astype(f32)[None], 1) * HD ** (-0.5)
    grad_attn_rows = pair_rows[:, 0].reshape(rows, D)
    grad_att_rows = pair_rows[:, 1].reshape(all_images, 2, HEADS, HD)
    owned_value = jnp.einsum(
        "nihd,nihc->dhc", pooled_own, grad_att_rows, preferred_element_type=f32
    ).reshape(own_rows, D)
    attended_own = matmul_nt(select_own, attended).astype(low)
    owned_out = matmul(attended_own, grad_attn_rows)
    owned_block = jnp.concatenate([owned_query, owned_key, owned_value, owned_out, owned_up], 1)

    shard_square = (
        jnp.sum(owned_patch * owned_patch)
        + jnp.sum(owned_block * owned_block)
        + jnp.sum(owned_down * owned_down)
        + jnp.sum(owned_heads * owned_heads)
        + jnp.sum(owned_small * owned_small)
        + jnp.sum(up_bias * up_bias)
    )
    square_high, square_rest = split_low(shard_square)
    square_rest, square_last = split_low(shard_square - square_high.astype(f32))
    tail_row = jnp.concatenate(
        [
            jnp.stack([square_high, square_rest, square_last]),
            up_bias.astype(low),
            jnp.zeros((D - 3 - own_hidden,), low),
        ]
    )
    final = gather_blocks(
        jnp.concatenate([owned_small.astype(low), tail_row[None]], 0), "dp"
    ).reshape(dp_size, small_share + 1, D)
    final = join_cores(final, seq_index, 1).reshape(devices, small_share + 1, D)
    summed_rows = final[:, :small_share].astype(f32).reshape(devices * small_share, D)[:small_count]
    global_square = jnp.sum(final[:, small_share, 0:3].astype(f32))
    up_bias_all = final[:, small_share, 3 : 3 + own_hidden].astype(f32).reshape(FF)
    summed_long = jnp.concatenate([up_bias_all, head_bias])
    total_square = global_square + jnp.sum(head_bias * head_bias)
    grad_norm = jnp.sqrt(total_square)
    factor = jnp.minimum(1.0, CLIP_NORM / (grad_norm + 1e-06))
    vectors_grad = factor * summed_rows[POS:]
    patch_new, patch_mean_new, patch_square_new = adam_update(
        patch_weight, patch_mean, patch_square, owned_patch, factor, DECAY_RATE, LEARN_RATE
    )
    block_new, block_mean_new, block_square_new = adam_update(
        block_weight, block_mean, block_square, owned_block, factor, DECAY_RATE, LEARN_RATE
    )
    down_new, down_mean_new, down_square_new = adam_update(
        down_weight, down_mean, down_square, owned_down, factor, DECAY_RATE, LEARN_RATE
    )
    heads_new, heads_mean_new, heads_square_new = adam_update(
        heads_weight, heads_mean, heads_square, owned_heads, factor, DECAY_RATE, LEARN_RATE
    )
    rows_new, rows_mean_new, rows_square_new = adam_update(
        small_rows, rows_mean, rows_square, summed_rows, factor, 0.0, SMALL_RATE
    )
    long_new, long_mean_new, long_square_new = adam_update(
        small_long, long_mean, long_square, summed_long, factor, 0.0, SMALL_RATE
    )
    return (
        loss,
        grad_norm,
        patch_new,
        patch_mean_new,
        patch_square_new,
        block_new,
        block_mean_new,
        block_square_new,
        down_new,
        down_mean_new,
        down_square_new,
        heads_new,
        heads_mean_new,
        heads_square_new,
        rows_new,
        rows_mean_new,
        rows_square_new,
        long_new,
        long_mean_new,
        long_square_new,
        vectors_grad,
    )


def tiles(arguments):
    patches, patch_weight = arguments[0], arguments[7]
    images, local_slots, _ = patches.shape
    return images * PAIR == 128 and (images * local_slots) % CHUNK == 0 and patch_weight.shape[0] == 24


def shards(*arguments):
    return (shards_tiled if tiles(arguments) else shards_plain)(*arguments)


def solution(mesh):
    placed = (
        P("dp", "seq", None),
        P("dp", "seq"),
        P("dp"),
        P("dp", None),
        P("dp"),
        P("dp"),
        P("dp", None),
        P(("dp", "seq"), None),
        P(("dp", "seq"), None),
        P(("dp", "seq"), None),
        P(("dp", "seq"), None),
        P(("dp", "seq"), None),
        P(("dp", "seq"), None),
        P(("dp", "seq"), None),
        P(("dp", "seq"), None),
        P(("dp", "seq"), None),
        P(("dp", "seq"), None),
        P(("dp", "seq"), None),
        P(("dp", "seq"), None),
        P(),
        P(),
        P(),
        P(),
        P(),
        P(),
    )
    return jax.shard_map(
        shards,
        mesh=mesh,
        in_specs=placed,
        out_specs=(
            P(),
            P(),
            P(("dp", "seq"), None),
            P(("dp", "seq"), None),
            P(("dp", "seq"), None),
            P(("dp", "seq"), None),
            P(("dp", "seq"), None),
            P(("dp", "seq"), None),
            P(("dp", "seq"), None),
            P(("dp", "seq"), None),
            P(("dp", "seq"), None),
            P(("dp", "seq"), None),
            P(("dp", "seq"), None),
            P(("dp", "seq"), None),
            P(),
            P(),
            P(),
            P(),
            P(),
            P(),
            P(),
        ),
        check_vma=False,
    )
```
